32 devices in a mesh: dp: 8 (over z, y), seq: 4 (over x, core).
Axes of the slice: x: 2, y: 2, z: 4, core: 2. Of those that a mesh axis runs over, the one named last changes fastest.
Arguments:
- hidden_in: bfloat16 [16, 1024, 1024], P('dp', 'seq'), may hold values from -6 to 6
- attn_gain: bfloat16 [1024], P(('dp', 'seq')), may hold values from 0.25 to 1.75
- w_query: bfloat16 [1024, 2048], P(('dp', 'seq')), may hold values from -0.1875 to 0.1875
- key_weight: bfloat16 [1024, 1024], P(('dp', 'seq')), may hold values from -0.1875 to 0.1875
- value_weight: bfloat16 [1024, 1024], P(('dp', 'seq')), may hold values from -0.1875 to 0.1875
- query_gain: bfloat16 [128], replicated, may hold values from 0.25 to 1.75
- key_gain: bfloat16 [128], replicated, may hold values from 0.25 to 1.75
- w_out: bfloat16 [2048, 1024], P(('dp', 'seq')), may hold values from -1.5 to 1.5
- mlp_gain: bfloat16 [1024], P(('dp', 'seq')), may hold values from 0.25 to 1.75
- w_gate: bfloat16 [1024, 3072], P(('dp', 'seq')), may hold values from -0.1875 to 0.1875
- w_up: bfloat16 [1024, 3072], P(('dp', 'seq')), may hold values from -0.1875 to 0.1875
- w_down: bfloat16 [3072, 1024], P(('dp', 'seq')), may hold values from -0.21875 to 0.21875
- cotangent: bfloat16 [16, 1024, 1024], P('dp', 'seq'), may hold values from -6 to 6
Outputs:
- hidden_out: bfloat16 [16, 1024, 1024], P('dp', 'seq')
- grad_in: float32 [16, 1024, 1024], P('dp', 'seq')
- grad_attn_gain: float32 [1024], P(('dp', 'seq'))
- grad_query_w: float32 [1024, 2048], P(('dp', 'seq'))
- grad_key_w: float32 [1024, 1024], P(('dp', 'seq'))
- grad_value_w: float32 [1024, 1024], P(('dp', 'seq'))
- grad_query_gain: float32 [128], replicated
- grad_key_gain: float32 [128], replicated
- grad_out_w: float32 [2048, 1024], P(('dp', 'seq'))
- grad_mlp_gain: float32 [1024], P(('dp', 'seq'))
- grad_gate_w: float32 [1024, 3072], P(('dp', 'seq'))
- grad_up_w: float32 [1024, 3072], P(('dp', 'seq'))
- grad_down_w: float32 [3072, 1024], P(('dp', 'seq'))
The draws below stay inside these ranges and needn't reach their ends.
All inputs are finite; a program needn't handle non-finite values.
Results may differ from the reference program's by a relative error of at most 0.017.
Values may be sent and summed in bfloat16 or wider, within the bound.
A program may use at most 320 MiB of HBM per device.

```python
import jax
import jax.numpy as jnp
from jax import lax

MODEL_WIDTH = 1024
QUERY_HEADS = 16
KEY_VALUE_HEADS = 8
HEAD_SIZE = 128
FF = 3072
SEQUENCE_LENGTH = 1024
SEQS = 16


def strengthened(array, rng, source, target, parts, factor):
    owner, partner = [(jnp.arange(array.shape[position]) // (array.shape[position] // parts)).reshape([-1 if axis == position else 1 for axis in range(array.ndim)]) for position in (source, target)]
    chosen = jax.random.permutation(rng, parts)[partner]
    strong = (owner == chosen) | (owner == (partner + parts // 2) % parts)
    return jnp.where(strong, factor * array, array)


def shard_levels(key, dims, cuts, smallest, high):
    factor_of, own = 1.0, jax.random.fold_in(key, 6)
    for dim, blocks in cuts:
        draws = jnp.exp(jax.random.uniform(jax.random.fold_in(own, dim), (blocks,), jnp.float32, smallest / len(cuts), high / len(cuts)))
        factor_of = factor_of * jnp.repeat(draws, dims[dim] // blocks).reshape([-1 if axis == dim else 1 for axis in range(len(dims))])
    return factor_of


def centred(stream_key, shape, scale, bound, cuts=(), kind=jnp.bfloat16):
    factor_of = shard_levels(stream_key, shape, cuts, -0.22, 0.18) if cuts else 1.0
    drawn = jax.random.normal(stream_key, shape, jnp.float32) * scale * factor_of
    return jnp.minimum(jnp.maximum(drawn, -bound), bound).astype(kind)


def gaussian_with(rng, extent, spread, bound, shards, heavy, dtype=jnp.bfloat16):
    result = spread * jax.random.normal(rng, extent, jnp.float32)
    if shards:
        result = result * shard_levels(rng, extent, shards, -0.22, 0.18)
    return jnp.clip(strengthened(result, jax.random.fold_in(rng, 3), *heavy), -bound, bound).astype(dtype)


def setup_inputs(seed: int = 0) -> dict:
    key_of = jax.random.split(jax.random.key(seed), 14)
    return {
        "hidden_in": gaussian_with(key_of[0], (SEQS, SEQUENCE_LENGTH, MODEL_WIDTH), 1.0, 6.0, ((0, 8), (1, 4)), (0, 2, 8, 2.0)),
        "attn_gain": jnp.clip(1.0 + 0.15 * jax.random.normal(key_of[1], (MODEL_WIDTH,), jnp.float32), 0.25, 1.75).astype(jnp.bfloat16),
        "w_query": centred(key_of[2], (MODEL_WIDTH, QUERY_HEADS * HEAD_SIZE), MODEL_WIDTH ** -0.5, 0.1875, ((0, 32),)),
        "key_weight": centred(key_of[3], (MODEL_WIDTH, KEY_VALUE_HEADS * HEAD_SIZE), MODEL_WIDTH ** -0.5, 0.1875, ((0, 32),)),
        "value_weight": centred(key_of[4], (MODEL_WIDTH, KEY_VALUE_HEADS * HEAD_SIZE), MODEL_WIDTH ** -0.5, 0.1875, ((0, 32),)),
        "query_gain": jnp.clip(1.0 + 0.15 * jax.random.normal(key_of[5], (HEAD_SIZE,), jnp.float32), 0.25, 1.75).astype(jnp.bfloat16),
        "key_gain": jnp.clip(1.0 + 0.15 * jax.random.normal(key_of[6], (HEAD_SIZE,), jnp.float32), 0.25, 1.75).astype(jnp.bfloat16),
        "w_out": centred(key_of[7], (QUERY_HEADS * HEAD_SIZE, MODEL_WIDTH), (QUERY_HEADS * HEAD_SIZE // 128) ** -0.5, 1.5, ((0, 32),)),
        "mlp_gain": jnp.clip(1.0 + 0.15 * jax.random.normal(key_of[8], (MODEL_WIDTH,), jnp.float32), 0.25, 1.75).astype(jnp.bfloat16),
        "w_gate": centred(key_of[9], (MODEL_WIDTH, FF), MODEL_WIDTH ** -0.5, 0.1875, ((0, 32),)),
        "w_up": centred(key_of[10], (MODEL_WIDTH, FF), MODEL_WIDTH ** -0.5, 0.1875, ((0, 32),)),
        "w_down": centred(key_of[11], (FF, MODEL_WIDTH), (FF // 4) ** -0.5, 0.21875, ((0, 32),)),
        "cotangent": centred(key_of[12], (SEQS, SEQUENCE_LENGTH, MODEL_WIDTH), 1.0, 6.0, ((0, 8), (1, 4))),
    }


EPS = 1e-06
ROPE_THETA = 1000000.0
HIGHEST = lax.Precision.HIGHEST

@jax.custom_vjp
def low(v):
    return lax.optimization_barrier(v.astype(jnp.bfloat16)).astype(jnp.float32)

@jax.custom_vjp
def low_back(v):
    return v

def low_keep(v):
    return (low(v), None)

def low_pass(kept, grad):
    return (grad,)

def back_keep(v):
    return (v, None)

def back_low(kept, grad):
    return (low(grad),)
low.defvjp(low_keep, low_pass)
low_back.defvjp(back_keep, back_low)

def rms_scale(value_rows):
    return lax.rsqrt(lax.optimization_barrier(jnp.mean(value_rows * value_rows, axis=-1, keepdims=True)) + EPS)

def rope_tables(positions):
    halfway = HEAD_SIZE // 2
    inverse = jnp.power(jnp.float32(ROPE_THETA), -(jnp.arange(halfway).astype(jnp.float32) * 2.0) / HEAD_SIZE)
    angles = positions.astype(jnp.float32)[:, None] * inverse[None, :]
    angles = jnp.concatenate([angles, angles], axis=-1)
    return (jnp.cos(angles), jnp.sin(angles))

def rotate(value_rows, cosine, sine):
    halfway = value_rows.shape[-1] // 2
    turned = jnp.concatenate([-value_rows[..., halfway:], value_rows[..., :halfway]], axis=-1)
    return value_rows * cosine[:, None, :] + turned * sine[:, None, :]

def head_prep(projected, gain, cosine, sine):
    shaped = projected.reshape(projected.shape[:-1] + (-1, HEAD_SIZE))
    normed = shaped * rms_scale(shaped) * gain
    return rotate(normed, cosine, sine)

def layer(tokens, weights):
    attn_gain, w_query, key_weight, value_weight, query_gain, key_gain, w_out, mlp_gain, w_gate, w_up, w_down = weights
    head_group = tokens.shape[0]
    cosine, sine = rope_tables(jnp.arange(SEQUENCE_LENGTH))
    normed = low(tokens * rms_scale(tokens) * attn_gain)
    query_proj = low_back(jnp.einsum('bsd,de->bse', normed, w_query, precision=HIGHEST))
    key_proj = low_back(jnp.einsum('bsd,de->bse', normed, key_weight, precision=HIGHEST))
    value_rows = low(low_back(jnp.einsum('bsd,de->bse', normed, value_weight, precision=HIGHEST)))
    query_rows = low(head_prep(query_proj, query_gain, cosine, sine))
    keys = low(head_prep(key_proj, key_gain, cosine, sine))
    query_rows = query_rows.reshape(head_group, SEQUENCE_LENGTH, KEY_VALUE_HEADS, QUERY_HEADS // KEY_VALUE_HEADS, HEAD_SIZE)
    value_rows = value_rows.reshape(head_group, SEQUENCE_LENGTH, KEY_VALUE_HEADS, HEAD_SIZE)
    raw = jnp.einsum('bqkgd,btkd->bkgqt', query_rows, keys, precision=HIGHEST) * HEAD_SIZE ** (-0.5)
    scores = low_back(raw)
    places = jnp.arange(SEQUENCE_LENGTH)
    allowed = places[None, :] <= places[:, None]
    masked = jnp.where(allowed, scores, -jnp.inf)
    highest = lax.optimization_barrier(jnp.max(masked, axis=-1, keepdims=True))
    exponent = jnp.exp(masked - highest)
    probs = low(exponent / lax.optimization_barrier(jnp.sum(exponent, axis=-1, keepdims=True)))
    mixed = low(low_back(jnp.einsum('bkgqt,btkd->bqkgd', probs, value_rows, precision=HIGHEST)))
    mixed = mixed.reshape(head_group, SEQUENCE_LENGTH, QUERY_HEADS * HEAD_SIZE)
    branch = low_back(jnp.einsum('bse,ed->bsd', mixed, w_out, precision=HIGHEST))
    residual = tokens + branch
    normed_mlp = low(residual * rms_scale(residual) * mlp_gain)
    gate = low_back(jnp.einsum('bsd,df->bsf', normed_mlp, w_gate, precision=HIGHEST))
    upward = low_back(jnp.einsum('bsd,df->bsf', normed_mlp, w_up, precision=HIGHEST))
    hidden = low(jax.nn.silu(gate) * upward)
    return residual + jnp.einsum('bsf,fd->bsd', hidden, w_down, precision=HIGHEST)

def reference(hidden_in, attn_gain, w_query, key_weight, value_weight, query_gain, key_gain, w_out, mlp_gain, w_gate, w_up, w_down, cotangent):
    weights = tuple((weight.astype(jnp.float32) for weight in (attn_gain, w_query, key_weight, value_weight, query_gain, key_gain, w_out, mlp_gain, w_gate, w_up, w_down)))
    groups = SEQS // 4
    tokens = hidden_in.astype(jnp.float32).reshape(groups, 4, SEQUENCE_LENGTH, MODEL_WIDTH)
    grads_top = cotangent.astype(jnp.float32).reshape(groups, 4, SEQUENCE_LENGTH, MODEL_WIDTH)

    def step(totals, item):
        block, grad_block = item
        output, pull = jax.vjp(layer, block, weights)
        grad_block_in, grad_weights = pull(grad_block)
        totals = tuple((total + piece for total, piece in zip(totals, grad_weights)))
        return (totals, (output, grad_block_in))
    start = tuple((jnp.zeros_like(weight) for weight in weights))
    totals, (outputs, grads_in) = lax.scan(step, start, (tokens, grads_top))
    return (outputs.reshape(SEQS, SEQUENCE_LENGTH, MODEL_WIDTH).astype(jnp.bfloat16), grads_in.reshape(SEQS, SEQUENCE_LENGTH, MODEL_WIDTH), totals[0], totals[1], totals[2], totals[3], totals[4], totals[5], totals[6], totals[7], totals[8], totals[9], totals[10])
```

```python
import functools

import jax
import jax.numpy as jnp
from jax import lax
from jax.experimental import pallas as pl
from jax.experimental.pallas import tpu as pltpu
from jax.sharding import PartitionSpec as P

HEAD_SIZE = 128
EPS = 1e-06
ROPE_THETA = 1000000.0
AXES = ("dp", "seq")
SCALE = HEAD_SIZE ** (-0.5)
F32 = jnp.float32
BF16 = jnp.bfloat16


def log2(n):
    return n.bit_length() - 1


class Wires:
    def __init__(self, dp, seq):
        self.dp, self.seq, self.count = dp, seq, dp * seq
        self.dp_bits, self.seq_bits = log2(dp), log2(seq)
        self.x_count = seq // 2
        y_bits = min(log2(self.x_count), self.dp_bits)
        self.dp_order = list(range(y_bits, self.dp_bits)) + list(range(y_bits))
        self.x_bits = list(range(1, self.seq_bits))
        self.d = lax.axis_index("dp")
        self.s = lax.axis_index("seq")

    def swap(self, value, mask, only=None):
        pairs = [(i, i ^ mask) for i in range(self.count) if only is None or only(i)]
        return lax.ppermute(value, AXES, pairs)

    def dp_swap(self, value, bit, only=None):
        return self.swap(value, (1 << bit) * self.seq, only)

    def bit_d(self, bit):
        return (self.d >> bit) & 1

    def bit_s(self, bit):
        return (self.s >> bit) & 1

    def gather_dp(self, shard):
        pieces = {0: shard}
        for bit in self.dp_order:
            pieces.update({r | (1 << bit): self.dp_swap(v, bit) for r, v in list(pieces.items())})
        full = jnp.zeros((self.dp,) + shard.shape, shard.dtype)
        for r, v in pieces.items():
            full = lax.dynamic_update_index_in_dim(full, v, self.d ^ r, 0)
        return full

    def scatter_dp(self, value):
        rest = value.shape[1:]
        held = list(range(self.dp_bits - 1, -1, -1))
        value = value.reshape((2,) * self.dp_bits + rest)
        for bit in reversed(self.dp_order):
            axis = held.index(bit)
            held.pop(axis)
            mine = lax.dynamic_index_in_dim(value, self.bit_d(bit), axis, keepdims=False)
            other = lax.dynamic_index_in_dim(value, 1 - self.bit_d(bit), axis, keepdims=False)
            got = self.dp_swap(other, bit)
            value = (mine.astype(F32) + got.astype(F32)).astype(BF16)
        return value

    def exchange_seq(self, value):
        rest = value.shape[1:]
        for bit in self.x_bits + [0]:
            value = value.reshape((self.seq >> (bit + 1), 2, 1 << bit) + rest)
            me = self.bit_s(bit)
            mine = lax.dynamic_index_in_dim(value, me, 1, keepdims=False)
            other = lax.dynamic_index_in_dim(value, 1 - me, 1, keepdims=False)
            got = self.swap(other, 1 << bit)
            low = jnp.where(me == 0, mine, got)
            high = jnp.where(me == 0, got, mine)
            value = jnp.stack([low, high], axis=1).reshape((self.seq,) + rest)
        return value

    def gather_seq_relative(self, value):
        pieces = [value]
        for bit in self.x_bits:
            pieces = pieces + [self.swap(v, 1 << bit) for v in pieces]
        return pieces + [self.swap(v, 1) for v in pieces]

    def sum_x(self, value):
        n = self.x_count
        shape = value.shape
        for bit in self.x_bits:
            got = self.swap(value.astype(BF16), 1 << bit).astype(F32)
            blocks = got.reshape((n, shape[0] // n) + shape[1:])
            flip = [i ^ (1 << (bit - 1)) for i in range(n)]
            value = value + jnp.concatenate([blocks[i] for i in flip], axis=0)
        return value

    def scatter_x(self, value):
        n = self.x_count
        for bit in reversed(self.x_bits):
            half = value.shape[0] // 2
            got = self.swap(value[half:].astype(BF16), 1 << bit)
            value = value[:half] + got.astype(F32)
        return value

    def sum_all(self, value):
        for bit in range(log2(self.count)):
            value = value + self.swap(value, 1 << bit)
        return value

    def head_bits(self, heads_kv):
        low = self.dp_bits - log2(heads_kv)
        partner = {0: 1, 1: 0, 2: 2}
        matched = [(low + k, partner[k]) for k in range(self.seq_bits)]
        free = [low + k for k in range(self.seq_bits, log2(heads_kv))]
        return low, matched, free

    def heads_of(self, t, heads_kv):
        low, matched, free = self.head_bits(heads_kv)
        heads = [0]
        for bit, tbit in matched:
            heads = [h | (((t >> tbit) & 1) << (bit - low)) for h in heads]
        for bit in free:
            heads = heads + [h | (1 << (bit - low)) for h in heads]
        return heads

    def matches(self, i, pairs):
        return all(((i // self.seq) >> b) & 1 == (i >> t) & 1 for b, t in pairs)

    def gather_out(self, shard, heads_kv):
        low, matched, free = self.head_bits(heads_kv)
        value = shard
        for bit in self.x_bits + [0]:
            pass
        value = shard[None]
        for bit in [0] + self.x_bits:
            got = self.swap(value, 1 << bit)
            value = self.ordered(value, got, self.bit_s(bit))
        for bit in range(low):
            got = self.dp_swap(value, bit)
            value = self.ordered(value, got, self.bit_d(bit))
        for n, (bit, tbit) in enumerate(matched):
            got = self.dp_swap(value, bit, lambda i: self.matches(i, matched[n:]))
            value = jnp.where(self.bit_d(bit) == self.bit_s(tbit), value, got)
        for bit in free:
            got = self.dp_swap(value, bit)
            value = self.ordered(value, got, self.bit_d(bit))
        return value.reshape((-1,) + shard.shape[1:])

    def ordered(self, own, got, bit):
        return jnp.concatenate(
            [jnp.where(bit == 0, own, got), jnp.where(bit == 0, got, own)], axis=0
        )

    def halves(self, value, bit):
        half = value.shape[0] // 2
        mine = lax.dynamic_slice_in_dim(value, bit * half, half, 0)
        other = lax.dynamic_slice_in_dim(value, (1 - bit) * half, half, 0)
        return mine, other

    def scatter_out(self, value, heads_kv):
        low, matched, free = self.head_bits(heads_kv)
        for bit in reversed(free):
            mine, other = self.halves(value, self.bit_d(bit))
            got = self.dp_swap(other, bit)
            value = (mine.astype(F32) + got.astype(F32)).astype(BF16)
        for n in reversed(range(len(matched))):
            bit, tbit = matched[n]
            got = self.dp_swap(
                value,
                bit,
                lambda i: self.matches(i, matched[n + 1 :]) and not self.matches(i, [matched[n]]),
            )
            value = (value.astype(F32) + got.astype(F32)).astype(BF16)
        for bit in reversed(range(low)):
            mine, other = self.halves(value, self.bit_d(bit))
            got = self.dp_swap(other, bit, lambda i: self.matches(i, matched))
            value = (mine.astype(F32) + got.astype(F32)).astype(BF16)
        todo = dict((tbit, bit) for bit, tbit in matched)
        for tbit in reversed(self.x_bits):
            value = self.hand_out(value, tbit, todo)
        return self.hand_out(value, 0, todo)

    def hand_out(self, value, tbit, todo):
        bit = todo.pop(tbit)
        left = [(b, t) for t, b in todo.items()]
        mine, other = self.halves(value, self.bit_s(tbit))
        got = self.swap(
            other, 1 << tbit, lambda i: self.matches(i, left) and self.matches(i, [(bit, tbit)])
        )
        return jnp.where(self.bit_d(bit) == self.bit_s(tbit), mine, got)


def dot(a, b):
    return lax.dot_general(a, b, (((1,), (0,)), ((), ())), preferred_element_type=F32)


def dot_t(a, b):
    return lax.dot_general(a, b, (((1,), (1,)), ((), ())), preferred_element_type=F32)


def t_dot(a, b):
    return lax.dot_general(a, b, (((0,), (0,)), ((), ())), preferred_element_type=F32)


def rms_scale(rows):
    return lax.rsqrt(jnp.mean(rows * rows, axis=-1, keepdims=True) + EPS)


def rope_tables(length):
    halfway = HEAD_SIZE // 2
    inverse = jnp.power(F32(ROPE_THETA), -(jnp.arange(halfway).astype(F32) * 2.0) / HEAD_SIZE)
    angles = jnp.arange(length).astype(F32)[:, None] * inverse[None, :]
    cosine, sine = jnp.cos(angles), jnp.sin(angles)
    return (
        jnp.concatenate([cosine, cosine], axis=-1),
        jnp.concatenate([-sine, sine], axis=-1),
    )


def place(block, s, x_count):
    return ((block & 1) ^ (s & 1)) * x_count + ((block >> 1) ^ (s >> 1))


def project_kernel(s_ref, x_ref, w_ref, gain_ref, qg_ref, kg_ref, cos_ref, sin_ref, n_ref, qkv_ref, pre_ref):
    x = x_ref[0].astype(F32)
    normed = (x * rms_scale(x) * gain_ref[...]).astype(BF16)
    n_ref[0] = normed
    y = dot(normed, w_ref[...])
    cosine, sine = cos_ref[...], sin_ref[...]
    for j in range(y.shape[1] // (4 * HEAD_SIZE)):
        for part in range(4):
            at = slice((4 * j + part) * HEAD_SIZE, (4 * j + part + 1) * HEAD_SIZE)
            head = y[:, at]
            if part < 3:
                pre_ref[:, (3 * j + part) * HEAD_SIZE : (3 * j + part + 1) * HEAD_SIZE] = head
                gain = qg_ref[...] if part < 2 else kg_ref[...]
                head = head * rms_scale(head) * gain
                head = head * cosine + pltpu.roll(head, HEAD_SIZE // 2, 1) * sine
            qkv_ref[:, at] = head.astype(BF16)


def project(s, x_rel, w, gain, query_gain, key_gain, cosine, sine, x_count):
    blocks, piece, width = x_rel.shape
    length, columns = blocks * piece, w.shape[1]
    heads = columns // (4 * HEAD_SIZE)
    whole = lambda shape: pl.BlockSpec(shape, lambda i, s_ref: (0,) * len(shape))
    rel = pl.BlockSpec((1, piece, width), lambda i, s_ref: (place(i, s_ref[0], x_count), 0, 0))
    table = pl.BlockSpec((piece, HEAD_SIZE), lambda i, s_ref: (i, 0))
    return pl.pallas_call(
        project_kernel,
        name="project",
        out_shape=(
            jax.ShapeDtypeStruct((blocks, piece, width), BF16),
            jax.ShapeDtypeStruct((length, columns), BF16),
            jax.ShapeDtypeStruct((length, 3 * heads * HEAD_SIZE), F32),
        ),
        grid_spec=pltpu.PrefetchScalarGridSpec(
            num_scalar_prefetch=1,
            grid=(blocks,),
            in_specs=[
                rel,
                whole(w.shape),
                whole((1, width)),
                whole((1, HEAD_SIZE)),
                whole((1, HEAD_SIZE)),
                table,
                table,
            ],
            out_specs=[
                rel,
                pl.BlockSpec((piece, columns), lambda i, s_ref: (i, 0)),
                pl.BlockSpec((piece, 3 * heads * HEAD_SIZE), lambda i, s_ref: (i, 0)),
            ],
        ),
        cost_estimate=pl.CostEstimate(
            flops=2 * length * width * columns,
            bytes_accessed=2 * (2 * length * width + width * columns + 4 * length * columns),
            transcendentals=0,
        ),
    )(s, x_rel, w, gain, query_gain, key_gain, cosine, sine)


def masked_exp(k_ref, query, i, piece, offset):
    diagonal = dot_t(k_ref[i * piece : (i + 1) * piece, :], query) * SCALE
    key_at = lax.broadcasted_iota(jnp.int32, (piece, piece), 0)
    query_at = lax.broadcasted_iota(jnp.int32, (piece, piece), 1)
    diagonal = jnp.where(key_at <= query_at, diagonal, -jnp.inf)
    if i == 0:
        scores = diagonal
    else:
        scores = jnp.concatenate(
            [dot_t(k_ref[: i * piece, :], query) * SCALE, diagonal], axis=0
        )
    if offset is None:
        offset = jnp.max(scores, axis=0, keepdims=True)
    return jnp.exp(scores - offset), offset


def forward_kernel(blocks, x_count, s_ref, q_ref, k_ref, v_ref, o_ref, log_ref):
    piece = q_ref.shape[0] // blocks
    values_t = v_ref[...].T
    for i in range(blocks):
        query = q_ref[i * piece : (i + 1) * piece, :]
        exponent, highest = masked_exp(k_ref, query, i, piece, None)
        total = jnp.sum(exponent, axis=0, keepdims=True)
        probs = (exponent * (1.0 / total)).astype(BF16)
        mixed = dot(values_t[:, : (i + 1) * piece], probs)
        o_ref[place(i, s_ref[0], x_count)] = mixed.T.astype(BF16)
        log_ref[0, :, i * piece : (i + 1) * piece] = highest + jnp.log(total)


def attend(s, qkv, blocks, x_count):
    length, columns = qkv.shape
    heads = columns // (2 * HEAD_SIZE)
    piece = length // blocks
    head = lambda part: pl.BlockSpec(
        (length, HEAD_SIZE), lambda h, s_ref: (0, 4 * (h // 2) + (h % 2 if part == 0 else part))
    )
    return pl.pallas_call(
        functools.partial(forward_kernel, blocks, x_count),
        name="attend",
        out_shape=(
            jax.ShapeDtypeStruct((blocks, piece, heads * HEAD_SIZE), BF16),
            jax.ShapeDtypeStruct((heads, 1, length), F32),
        ),
        grid_spec=pltpu.PrefetchScalarGridSpec(
            num_scalar_prefetch=1,
            grid=(heads,),
            in_specs=[head(0), head(2), head(3)],
            out_specs=[
                pl.BlockSpec((blocks, piece, HEAD_SIZE), lambda h, s_ref: (0, 0, h)),
                pl.BlockSpec((1, 1, length), lambda h, s_ref: (h, 0, 0)),
            ],
        ),
        cost_estimate=pl.CostEstimate(
            flops=2 * heads * length * length * HEAD_SIZE * 2,
            bytes_accessed=2 * heads * length * HEAD_SIZE * 4,
            transcendentals=heads * length * length // 2,
        ),
    )(s, qkv, qkv, qkv)


def head_back(grad, pre, gain, cosine, sine):
    turned = grad * cosine - pltpu.roll(grad, HEAD_SIZE // 2, 1) * sine
    scale = rms_scale(pre)
    part = turned * gain
    result = scale * part - pre * (scale * scale * scale * jnp.mean(part * pre, axis=-1, keepdims=True))
    return result, jnp.sum(turned * pre * scale, axis=0, keepdims=True)


def backward_kernel(
    blocks, x_count, s_ref, q_ref, k_ref, v_ref, do_ref, log_ref, qp_ref, kp_ref, qg_ref, kg_ref,
    cos_ref, sin_ref, grad_ref, qgain_ref, kgain_ref, dk_ref, dv_ref,
):
    piece = q_ref.shape[0] // blocks
    second = pl.program_id(1)

    @pl.when((pl.program_id(0) == 0) & (second == 0))
    def _():
        qgain_ref[...] = jnp.zeros_like(qgain_ref)
        kgain_ref[...] = jnp.zeros_like(kgain_ref)

    @pl.when(second == 0)
    def _():
        dk_ref[...] = jnp.zeros_like(dk_ref)
        dv_ref[...] = jnp.zeros_like(dv_ref)

    keys_t = k_ref[...].T
    column = pl.ds(pl.multiple_of(second * HEAD_SIZE, HEAD_SIZE), HEAD_SIZE)
    for i in range(blocks):
        rows = slice(i * piece, (i + 1) * piece)
        end = (i + 1) * piece
        at = place(i, s_ref[0], x_count)
        query = q_ref[rows, :]
        grad_out = do_ref[at]
        probs, _ = masked_exp(k_ref, query, i, piece, log_ref[0, :, rows])
        dv_ref[:end, :] += dot(probs.astype(BF16), grad_out)
        grad_probs = dot_t(v_ref[:end, :], grad_out)
        inner = jnp.sum(probs * grad_probs, axis=0, keepdims=True)
        grad_scores = (probs * (grad_probs - inner)).astype(BF16)
        dk_ref[:end, :] += dot(grad_scores, query)
        grad_query = dot(keys_t[:, :end], grad_scores).T * SCALE
        result, gain = head_back(grad_query, qp_ref[rows, :], qg_ref[...], cos_ref[rows, :], sin_ref[rows, :])
        grad_ref[at, :, column] = result.astype(BF16)
        qgain_ref[...] += gain

    @pl.when(second == 1)
    def _():
        for i in range(blocks):
            rows = slice(i * piece, (i + 1) * piece)
            at = place(i, s_ref[0], x_count)
            result, gain = head_back(
                dk_ref[rows, :] * SCALE, kp_ref[rows, :], kg_ref[...], cos_ref[rows, :], sin_ref[rows, :]
            )
            grad_ref[at, :, 2 * HEAD_SIZE : 3 * HEAD_SIZE] = result.astype(BF16)
            grad_ref[at, :, 3 * HEAD_SIZE :] = dv_ref[rows, :].astype(BF16)
            kgain_ref[...] += gain


def attend_back(s, qkv, pre, log_total, grad_mixed, query_gain, key_gain, cosine, sine, blocks, x_count):
    length, columns = qkv.shape
    heads_kv = columns // (4 * HEAD_SIZE)
    piece = length // blocks
    head = lambda part: pl.BlockSpec(
        (length, HEAD_SIZE), lambda j, g, s_ref: (0, 4 * j + (g if part == 0 else part))
    )
    pre_head = lambda part: pl.BlockSpec(
        (length, HEAD_SIZE), lambda j, g, s_ref: (0, 3 * j + (g if part == 0 else part))
    )
    whole = lambda shape: pl.BlockSpec(shape, lambda j, g, s_ref: (0,) * len(shape))
    return pl.pallas_call(
        functools.partial(backward_kernel, blocks, x_count),
        name="attend_back",
        out_shape=(
            jax.ShapeDtypeStruct((blocks, piece, columns), BF16),
            jax.ShapeDtypeStruct((1, HEAD_SIZE), F32),
            jax.ShapeDtypeStruct((1, HEAD_SIZE), F32),
        ),
        grid_spec=pltpu.PrefetchScalarGridSpec(
            num_scalar_prefetch=1,
            grid=(heads_kv, 2),
            in_specs=[
                head(0),
                head(2),
                head(3),
                pl.BlockSpec((blocks, piece, HEAD_SIZE), lambda j, g, s_ref: (0, 0, 2 * j + g)),
                pl.BlockSpec((1, 1, length), lambda j, g, s_ref: (2 * j + g, 0, 0)),
                pre_head(0),
                pre_head(2),
                whole((1, HEAD_SIZE)),
                whole((1, HEAD_SIZE)),
                whole((length, HEAD_SIZE)),
                whole((length, HEAD_SIZE)),
            ],
            out_specs=[
                pl.BlockSpec((blocks, piece, 4 * HEAD_SIZE), lambda j, g, s_ref: (0, 0, j)),
                whole((1, HEAD_SIZE)),
                whole((1, HEAD_SIZE)),
            ],
            scratch_shapes=[pltpu.VMEM((length, HEAD_SIZE), F32), pltpu.VMEM((length, HEAD_SIZE), F32)],
        ),
        cost_estimate=pl.CostEstimate(
            flops=2 * 2 * heads_kv * length * length * HEAD_SIZE * 5 // 2,
            bytes_accessed=2 * heads_kv * length * HEAD_SIZE * 24,
            transcendentals=heads_kv * length * length,
        ),
    )(s, qkv, qkv, qkv, grad_mixed, log_total, pre, pre, query_gain, key_gain, cosine, sine)


def body(
    hidden_in,
    attn_gain,
    w_query,
    key_weight,
    value_weight,
    query_gain,
    key_gain,
    w_out,
    mlp_gain,
    w_gate,
    w_up,
    w_down,
    cotangent,
):
    wires = Wires(lax.axis_size("dp"), lax.axis_size("seq"))
    dp, seq, x_count = wires.dp, wires.seq, wires.x_count
    count = wires.count
    sequences, piece, width = hidden_in.shape
    length = seq * piece
    part = x_count * piece
    heads_kv = key_weight.shape[1] // HEAD_SIZE
    s_index = wires.s.reshape(1).astype(jnp.int32)
    cosine, sine = rope_tables(length)
    query_gain_row = query_gain.astype(F32).reshape(1, -1)
    key_gain_row = key_gain.astype(F32).reshape(1, -1)

    gains = jnp.zeros((2, count, width // count), BF16)
    own_gains = jnp.stack([attn_gain, mlp_gain]).reshape(2, 1, -1)
    index = wires.d * seq + wires.s
    gains = lax.dynamic_update_slice(gains, own_gains, (0, index, 0))
    gains = wires.sum_all(gains.reshape(2, width)).astype(F32)
    attn_gain_row, mlp_gain_row = gains[:1], gains[1:]

    rows = w_query.shape[0]
    by_head = jnp.concatenate(
        [
            w_query.reshape(rows, heads_kv, -1),
            key_weight.reshape(rows, heads_kv, -1),
            value_weight.reshape(rows, heads_kv, -1),
        ],
        axis=2,
    )
    order = [wires.heads_of(t, heads_kv) for t in range(seq)]
    package = jnp.stack([jnp.concatenate([by_head[:, j] for j in order[t]], axis=1) for t in range(seq)])
    package = wires.exchange_seq(package).reshape(seq * rows, -1)
    w_in = wires.gather_dp(package).reshape(width, -1)

    x_pieces = wires.gather_seq_relative(hidden_in)
    x_rel = jnp.stack(x_pieces, axis=1)

    w_o = wires.gather_out(w_out, heads_kv)

    down_rows = w_down.shape[0]

    def by_unit(w):
        return w.reshape(rows, dp, seq, down_rows).transpose(2, 0, 1, 3).reshape(seq, rows, -1)

    units = dp * down_rows
    package = jnp.concatenate([by_unit(w_gate), by_unit(w_up)], axis=2)
    package = wires.exchange_seq(package).reshape(seq * rows, -1)
    w_mlp = wires.gather_dp(package).reshape(width, -1)

    g_pieces = wires.gather_seq_relative(cotangent)
    g_rel = jnp.stack(g_pieces, axis=1)

    w_d = wires.gather_dp(w_down).reshape(units, width)

    kept = []
    outs = []
    for n in range(sequences):
        normed, qkv, pre = project(
            s_index, x_rel[n], w_in, attn_gain_row, query_gain_row, key_gain_row, cosine, sine, x_count
        )
        mixed, log_total = attend(s_index, qkv, seq, x_count)
        mixed_rows = mixed.reshape(length, -1)
        other = wires.swap(dot(mixed_rows[part:], w_o).astype(BF16), 1)
        total = wires.sum_x(dot(mixed_rows[:part], w_o) + other.astype(F32))
        residual = total + x_rel[n].reshape(length, width)[:part].astype(F32)
        scale = rms_scale(residual)
        normed_mlp = (residual * scale * mlp_gain_row).astype(BF16)
        normed_mlp = jnp.concatenate([normed_mlp, wires.swap(normed_mlp, 1)], axis=0)
        both = dot(normed_mlp, w_mlp)
        gate, upward = both[:, :units], both[:, units:]
        sigmoid = jax.nn.sigmoid(gate)
        silu = gate * sigmoid
        hidden = (silu * upward).astype(BF16)
        other = wires.swap(dot(hidden[part:], w_d).astype(BF16), 1)
        total = wires.scatter_x(dot(hidden[:part], w_d) + other.astype(F32))
        outs.append((residual[:piece] + total).astype(BF16))

        grad_top = g_rel[n].reshape(length, width)
        grad_hidden = dot_t(grad_top, w_d)
        grad_gate = (grad_hidden * upward * sigmoid * (1.0 + gate * (1.0 - sigmoid))).astype(BF16)
        grad_upward = (grad_hidden * silu).astype(BF16)
        grad_both = jnp.concatenate([grad_gate, grad_upward], axis=1)
        other = wires.swap(dot_t(grad_both[part:], w_mlp).astype(BF16), 1)
        grad_normed = wires.sum_x(dot_t(grad_both[:part], w_mlp) + other.astype(F32))
        scaled = grad_normed * mlp_gain_row
        grad_residual = (
            grad_top[:part].astype(F32)
            + scale * scaled
            - residual * (scale * scale * scale * jnp.mean(scaled * residual, axis=-1, keepdims=True))
        )
        grad_mlp_gain = jnp.sum((grad_normed * residual * scale)[:piece], axis=0)
        branch = grad_residual.astype(BF16)
        branch = jnp.concatenate([branch, wires.swap(branch, 1)], axis=0)
        grad_mixed = dot_t(branch, w_o).astype(BF16).reshape(mixed.shape)
        grad_qkv, grad_query_gain, grad_key_gain = attend_back(
            s_index, qkv, pre, log_total, grad_mixed, query_gain_row, key_gain_row, cosine, sine, seq, x_count
        )
        grad_rows = grad_qkv.reshape(length, -1)
        other = wires.swap(dot_t(grad_rows[part:], w_in).astype(BF16), 1)
        grad_first = wires.scatter_x(dot_t(grad_rows[:part], w_in) + other.astype(F32))
        tokens = hidden_in[n].astype(F32)
        scale = rms_scale(tokens)
        scaled = grad_first * attn_gain_row
        grad_tokens = (
            grad_residual[:piece]
            + scale * scaled
            - tokens * (scale * scale * scale * jnp.mean(scaled * tokens, axis=-1, keepdims=True))
        )
        grad_attn_gain = jnp.sum(grad_first * tokens * scale, axis=0)
        kept.append(
            dict(
                normed=normed.reshape(length, width),
                mixed=mixed_rows,
                normed_mlp=normed_mlp,
                hidden=hidden,
                grad_both=grad_both,
                branch=branch,
                grad_rows=grad_rows,
                grad_tokens=grad_tokens,
                gains=jnp.concatenate(
                    [grad_attn_gain, grad_mlp_gain, grad_query_gain[0], grad_key_gain[0]]
                ),
            )
        )

    def over(name):
        return jnp.concatenate([k[name] for k in kept], axis=0)

    grad_down = t_dot(over("hidden"), g_rel.reshape(-1, width)).astype(BF16)
    grad_down = wires.scatter_dp(grad_down.reshape(dp, down_rows, width)).astype(F32)

    grad_mlp = t_dot(over("normed_mlp"), over("grad_both")).astype(BF16)
    grad_mlp = wires.scatter_dp(grad_mlp.reshape(dp, seq * rows, -1))
    grad_mlp = wires.exchange_seq(grad_mlp.reshape(seq, rows, -1)).astype(F32)

    def from_unit(g):
        return g.reshape(seq, rows, dp, down_rows).transpose(1, 2, 0, 3).reshape(rows, -1)

    grad_gate, grad_up = from_unit(grad_mlp[..., :units]), from_unit(grad_mlp[..., units:])

    grad_out = t_dot(over("mixed"), over("branch")).astype(BF16)
    grad_out = wires.scatter_out(grad_out, heads_kv).astype(F32)

    grad_in = t_dot(over("normed"), over("grad_rows")).astype(BF16)
    grad_in = wires.scatter_dp(grad_in.reshape(dp, seq * rows, -1))
    grad_in = wires.exchange_seq(grad_in.reshape(seq, rows, -1)).astype(F32)
    pieces = [None] * heads_kv
    for t in range(seq):
        for m, j in enumerate(order[t]):
            pieces[j] = grad_in[t, :, m * 4 * HEAD_SIZE : (m + 1) * 4 * HEAD_SIZE]
    grad_query = jnp.concatenate([p[:, : 2 * HEAD_SIZE] for p in pieces], axis=1)
    grad_key = jnp.concatenate([p[:, 2 * HEAD_SIZE : 3 * HEAD_SIZE] for p in pieces], axis=1)
    grad_value = jnp.concatenate([p[:, 3 * HEAD_SIZE :] for p in pieces], axis=1)

    gain_sums = wires.sum_all(sum(k["gains"] for k in kept))
    own = width // count
    grad_attn_gain = lax.dynamic_slice_in_dim(gain_sums, index * own, own)
    grad_mlp_gain = lax.dynamic_slice_in_dim(gain_sums, width + index * own, own)
    return (
        jnp.stack(outs),
        jnp.stack([k["grad_tokens"] for k in kept]),
        grad_attn_gain,
        grad_query,
        grad_key,
        grad_value,
        gain_sums[2 * width : 2 * width + HEAD_SIZE],
        gain_sums[2 * width + HEAD_SIZE :],
        grad_out,
        grad_mlp_gain,
        grad_gate,
        grad_up,
        grad_down,
    )


def solution(mesh):
    rows = P(("dp", "seq"), None)
    line = P(("dp", "seq"))
    tokens = P("dp", "seq", None)
    return jax.shard_map(
        body,
        mesh=mesh,
        in_specs=(tokens, line, rows, rows, rows, P(), P(), rows, line, rows, rows, rows, tokens),
        out_specs=(tokens, tokens, line, rows, rows, rows, P(), P(), rows, line, rows, rows, rows),
        check_vma=False,
    )
```

```python
import functools

import jax
import jax.numpy as jnp
from jax import lax
from jax.experimental import pallas as pl
from jax.experimental.pallas import tpu as pltpu
from jax.sharding import PartitionSpec as P

HEAD_SIZE = 128
EPS = 1e-06
ROPE_THETA = 1000000.0
AXES = ("dp", "seq")
SCALE = HEAD_SIZE ** (-0.5)
F32 = jnp.float32
BF16 = jnp.bfloat16


def log2(n):
    return n.bit_length() - 1


class Wires:
    def __init__(self, dp, seq):
        self.dp, self.seq, self.count = dp, seq, dp * seq
        self.dp_bits, self.seq_bits = log2(dp), log2(seq)
        self.x_count = seq // 2
        y_bits = min(log2(self.x_count), self.dp_bits)
        self.dp_order = list(range(y_bits, self.dp_bits)) + list(range(y_bits))
        self.x_bits = list(range(1, self.seq_bits))
        self.d = lax.axis_index("dp")
        self.s = lax.axis_index("seq")

    def swap(self, value, mask, only=None):
        pairs = [(i, i ^ mask) for i in range(self.count) if only is None or only(i)]
        return lax.ppermute(value, AXES, pairs)

    def dp_swap(self, value, bit, only=None):
        return self.swap(value, (1 << bit) * self.seq, only)

    def bit_d(self, bit):
        return (self.d >> bit) & 1

    def bit_s(self, bit):
        return (self.s >> bit) & 1

    def gather_dp(self, shard):
        pieces = {0: shard}
        for bit in self.dp_order:
            pieces.update({r | (1 << bit): self.dp_swap(v, bit) for r, v in list(pieces.items())})
        full = jnp.zeros((self.dp,) + shard.shape, shard.dtype)
        for r, v in pieces.items():
            full = lax.dynamic_update_index_in_dim(full, v, self.d ^ r, 0)
        return full

    def scatter_dp(self, value):
        rest = value.shape[1:]
        held = list(range(self.dp_bits - 1, -1, -1))
        value = value.reshape((2,) * self.dp_bits + rest)
        for bit in reversed(self.dp_order):
            axis = held.index(bit)
            held.pop(axis)
            mine = lax.dynamic_index_in_dim(value, self.bit_d(bit), axis, keepdims=False)
            other = lax.dynamic_index_in_dim(value, 1 - self.bit_d(bit), axis, keepdims=False)
            got = self.dp_swap(other, bit)
            value = (mine.astype(F32) + got.astype(F32)).astype(BF16)
        return value

    def exchange_seq(self, value):
        rest = value.shape[1:]
        for bit in self.x_bits + [0]:
            value = value.reshape((self.seq >> (bit + 1), 2, 1 << bit) + rest)
            me = self.bit_s(bit)
            mine = lax.dynamic_index_in_dim(value, me, 1, keepdims=False)
            other = lax.dynamic_index_in_dim(value, 1 - me, 1, keepdims=False)
            got = self.swap(other, 1 << bit)
            low = jnp.where(me == 0, mine, got)
            high = jnp.where(me == 0, got, mine)
            value = jnp.stack([low, high], axis=1).reshape((self.seq,) + rest)
        return value

    def gather_seq_relative(self, value):
        pieces = [value]
        for bit in self.x_bits:
            pieces = pieces + [self.swap(v, 1 << bit) for v in pieces]
        return pieces + [self.swap(v, 1) for v in pieces]

    def sum_x(self, value):
        n = self.x_count
        shape = value.shape
        for bit in self.x_bits:
            got = self.swap(value.astype(BF16), 1 << bit).astype(F32)
            blocks = got.reshape((n, shape[0] // n) + shape[1:])
            flip = [i ^ (1 << (bit - 1)) for i in range(n)]
            value = value + jnp.concatenate([blocks[i] for i in flip], axis=0)
        return value

    def scatter_x(self, value):
        n = self.x_count
        for bit in reversed(self.x_bits):
            half = value.shape[0] // 2
            got = self.swap(value[half:].astype(BF16), 1 << bit)
            value = value[:half] + got.astype(F32)
        return value

    def sum_all(self, value):
        for bit in range(log2(self.count)):
            value = value + self.swap(value, 1 << bit)
        return value

    def head_bits(self, heads_kv):
        low = self.dp_bits - log2(heads_kv)
        partner = {0: 1, 1: 0, 2: 2}
        matched = [(low + k, partner[k]) for k in range(self.seq_bits)]
        free = [low + k for k in range(self.seq_bits, log2(heads_kv))]
        return low, matched, free

    def heads_of(self, t, heads_kv):
        low, matched, free = self.head_bits(heads_kv)
        heads = [0]
        for bit, tbit in matched:
            heads = [h | (((t >> tbit) & 1) << (bit - low)) for h in heads]
        for bit in free:
            heads = heads + [h | (1 << (bit - low)) for h in heads]
        return heads

    def matches(self, i, pairs):
        return all(((i // self.seq) >> b) & 1 == (i >> t) & 1 for b, t in pairs)

    def gather_out(self, shard, heads_kv):
        low, matched, free = self.head_bits(heads_kv)
        value = shard
        for bit in self.x_bits + [0]:
            pass
        value = shard[None]
        for bit in [0] + self.x_bits:
            got = self.swap(value, 1 << bit)
            value = self.ordered(value, got, self.bit_s(bit))
        for bit in range(low):
            got = self.dp_swap(value, bit)
            value = self.ordered(value, got, self.bit_d(bit))
        for n, (bit, tbit) in enumerate(matched):
            got = self.dp_swap(value, bit, lambda i: self.matches(i, matched[n:]))
            value = jnp.where(self.bit_d(bit) == self.bit_s(tbit), value, got)
        for bit in free:
            got = self.dp_swap(value, bit)
            value = self.ordered(value, got, self.bit_d(bit))
        return value.reshape((-1,) + shard.shape[1:])

    def ordered(self, own, got, bit):
        return jnp.concatenate(
            [jnp.where(bit == 0, own, got), jnp.where(bit == 0, got, own)], axis=0
        )

    def halves(self, value, bit):
        half = value.shape[0] // 2
        mine = lax.dynamic_slice_in_dim(value, bit * half, half, 0)
        other = lax.dynamic_slice_in_dim(value, (1 - bit) * half, half, 0)
        return mine, other

    def scatter_out(self, value, heads_kv):
        low, matched, free = self.head_bits(heads_kv)
        for bit in reversed(free):
            mine, other = self.halves(value, self.bit_d(bit))
            got = self.dp_swap(other, bit)
            value = (mine.astype(F32) + got.astype(F32)).astype(BF16)
        for n in reversed(range(len(matched))):
            bit, tbit = matched[n]
            got = self.dp_swap(
                value,
                bit,
                lambda i: self.matches(i, matched[n + 1 :]) and not self.matches(i, [matched[n]]),
            )
            value = (value.astype(F32) + got.astype(F32)).astype(BF16)
        for bit in reversed(range(low)):
            mine, other = self.halves(value, self.bit_d(bit))
            got = self.dp_swap(other, bit, lambda i: self.matches(i, matched))
            value = (mine.astype(F32) + got.astype(F32)).astype(BF16)
        todo = dict((tbit, bit) for bit, tbit in matched)
        for tbit in reversed(self.x_bits):
            value = self.hand_out(value, tbit, todo)
        return self.hand_out(value, 0, todo)

    def hand_out(self, value, tbit, todo):
        bit = todo.pop(tbit)
        left = [(b, t) for t, b in todo.items()]
        mine, other = self.halves(value, self.bit_s(tbit))
        got = self.swap(
            other, 1 << tbit, lambda i: self.matches(i, left) and self.matches(i, [(bit, tbit)])
        )
        return jnp.where(self.bit_d(bit) == self.bit_s(tbit), mine, got)


def dot(a, b):
    return lax.dot_general(a, b, (((1,), (0,)), ((), ())), preferred_element_type=F32)


def dot_t(a, b):
    return lax.dot_general(a, b, (((1,), (1,)), ((), ())), preferred_element_type=F32)


def t_dot(a, b):
    return lax.dot_general(a, b, (((0,), (0,)), ((), ())), preferred_element_type=F32)


def rms_scale(rows):
    return lax.rsqrt(jnp.mean(rows * rows, axis=-1, keepdims=True) + EPS)


def rope_tables(length):
    halfway = HEAD_SIZE // 2
    inverse = jnp.power(F32(ROPE_THETA), -(jnp.arange(halfway).astype(F32) * 2.0) / HEAD_SIZE)
    angles = jnp.arange(length).astype(F32)[:, None] * inverse[None, :]
    cosine, sine = jnp.cos(angles), jnp.sin(angles)
    return (
        jnp.concatenate([cosine, cosine], axis=-1),
        jnp.concatenate([-sine, sine], axis=-1),
    )


def place(block, s, x_count):
    return ((block & 1) ^ (s & 1)) * x_count + ((block >> 1) ^ (s >> 1))


def project_kernel(s_ref, x_ref, w_ref, gain_ref, qg_ref, kg_ref, cos_ref, sin_ref, n_ref, qkv_ref, pre_ref):
    x = x_ref[0].astype(F32)
    normed = (x * rms_scale(x) * gain_ref[...]).astype(BF16)
    n_ref[0] = normed
    y = dot(normed, w_ref[...])
    cosine, sine = cos_ref[...], sin_ref[...]
    for j in range(y.shape[1] // (4 * HEAD_SIZE)):
        for part in range(4):
            at = slice((4 * j + part) * HEAD_SIZE, (4 * j + part + 1) * HEAD_SIZE)
            head = y[:, at]
            if part < 3:
                pre_ref[:, (3 * j + part) * HEAD_SIZE : (3 * j + part + 1) * HEAD_SIZE] = head
                gain = qg_ref[...] if part < 2 else kg_ref[...]
                head = head * rms_scale(head) * gain
                head = head * cosine + pltpu.roll(head, HEAD_SIZE // 2, 1) * sine
            qkv_ref[:, at] = head.astype(BF16)


def project(s, x_rel, w, gain, query_gain, key_gain, cosine, sine, x_count):
    blocks, piece, width = x_rel.shape
    length, columns = blocks * piece, w.shape[1]
    heads = columns // (4 * HEAD_SIZE)
    whole = lambda shape: pl.BlockSpec(shape, lambda i, s_ref: (0,) * len(shape))
    rel = pl.BlockSpec((1, piece, width), lambda i, s_ref: (place(i, s_ref[0], x_count), 0, 0))
    table = pl.BlockSpec((piece, HEAD_SIZE), lambda i, s_ref: (i, 0))
    return pl.pallas_call(
        project_kernel,
        name="project",
        out_shape=(
            jax.ShapeDtypeStruct((blocks, piece, width), BF16),
            jax.ShapeDtypeStruct((length, columns), BF16),
            jax.ShapeDtypeStruct((length, 3 * heads * HEAD_SIZE), F32),
        ),
        grid_spec=pltpu.PrefetchScalarGridSpec(
            num_scalar_prefetch=1,
            grid=(blocks,),
            in_specs=[
                rel,
                whole(w.shape),
                whole((1, width)),
                whole((1, HEAD_SIZE)),
                whole((1, HEAD_SIZE)),
                table,
                table,
            ],
            out_specs=[
                rel,
                pl.BlockSpec((piece, columns), lambda i, s_ref: (i, 0)),
                pl.BlockSpec((piece, 3 * heads * HEAD_SIZE), lambda i, s_ref: (i, 0)),
            ],
        ),
        cost_estimate=pl.CostEstimate(
            flops=2 * length * width * columns,
            bytes_accessed=2 * (2 * length * width + width * columns + 4 * length * columns),
            transcendentals=0,
        ),
    )(s, x_rel, w, gain, query_gain, key_gain, cosine, sine)


def masked_exp(k_ref, query, i, piece, offset):
    diagonal = dot_t(k_ref[i * piece : (i + 1) * piece, :], query) * SCALE
    key_at = lax.broadcasted_iota(jnp.int32, (piece, piece), 0)
    query_at = lax.broadcasted_iota(jnp.int32, (piece, piece), 1)
    diagonal = jnp.where(key_at <= query_at, diagonal, -jnp.inf)
    if i == 0:
        scores = diagonal
    else:
        scores = jnp.concatenate(
            [dot_t(k_ref[: i * piece, :], query) * SCALE, diagonal], axis=0
        )
    if offset is None:
        offset = jnp.max(scores, axis=0, keepdims=True)
    return jnp.exp(scores - offset), offset


def forward_kernel(blocks, x_count, s_ref, q_ref, k_ref, v_ref, o_ref, log_ref):
    piece = q_ref.shape[0] // blocks
    values_t = v_ref[...].T
    for i in range(blocks):
        query = q_ref[i * piece : (i + 1) * piece, :]
        exponent, highest = masked_exp(k_ref, query, i, piece, None)
        total = jnp.sum(exponent, axis=0, keepdims=True)
        probs = (exponent * (1.0 / total)).astype(BF16)
        mixed = dot(values_t[:, : (i + 1) * piece], probs)
        o_ref[place(i, s_ref[0], x_count)] = mixed.T.astype(BF16)
        log_ref[0, :, i * piece : (i + 1) * piece] = highest + jnp.log(total)


def attend(s, qkv, blocks, x_count):
    length, columns = qkv.shape
    heads = columns // (2 * HEAD_SIZE)
    piece = length // blocks
    head = lambda part: pl.BlockSpec(
        (length, HEAD_SIZE), lambda h, s_ref: (0, 4 * (h // 2) + (h % 2 if part == 0 else part))
    )
    return pl.pallas_call(
        functools.partial(forward_kernel, blocks, x_count),
        name="attend",
        out_shape=(
            jax.ShapeDtypeStruct((blocks, piece, heads * HEAD_SIZE), BF16),
            jax.ShapeDtypeStruct((heads, 1, length), F32),
        ),
        grid_spec=pltpu.PrefetchScalarGridSpec(
            num_scalar_prefetch=1,
            grid=(heads,),
            in_specs=[head(0), head(2), head(3)],
            out_specs=[
                pl.BlockSpec((blocks, piece, HEAD_SIZE), lambda h, s_ref: (0, 0, h)),
                pl.BlockSpec((1, 1, length), lambda h, s_ref: (h, 0, 0)),
            ],
        ),
        cost_estimate=pl.CostEstimate(
            flops=2 * heads * length * length * HEAD_SIZE * 2,
            bytes_accessed=2 * heads * length * HEAD_SIZE * 4,
            transcendentals=heads * length * length // 2,
        ),
    )(s, qkv, qkv, qkv)


def head_back(grad, pre, gain, cosine, sine):
    turned = grad * cosine - pltpu.roll(grad, HEAD_SIZE // 2, 1) * sine
    scale = rms_scale(pre)
    part = turned * gain
    result = scale * part - pre * (scale * scale * scale * jnp.mean(part * pre, axis=-1, keepdims=True))
    return result, jnp.sum(turned * pre * scale, axis=0, keepdims=True)


def backward_kernel(
    blocks, x_count, s_ref, q_ref, k_ref, v_ref, do_ref, log_ref, qp_ref, kp_ref, qg_ref, kg_ref,
    cos_ref, sin_ref, grad_ref, qgain_ref, kgain_ref, dk_ref, dv_ref,
):
    piece = q_ref.shape[0] // blocks
    second = pl.program_id(1)

    @pl.when((pl.program_id(0) == 0) & (second == 0))
    def _():
        qgain_ref[...] = jnp.zeros_like(qgain_ref)
        kgain_ref[...] = jnp.zeros_like(kgain_ref)

    @pl.when(second == 0)
    def _():
        dk_ref[...] = jnp.zeros_like(dk_ref)
        dv_ref[...] = jnp.zeros_like(dv_ref)

    keys_t = k_ref[...].T
    column = pl.ds(pl.multiple_of(second * HEAD_SIZE, HEAD_SIZE), HEAD_SIZE)
    for i in range(blocks):
        rows = slice(i * piece, (i + 1) * piece)
        end = (i + 1) * piece
        at = place(i, s_ref[0], x_count)
        query = q_ref[rows, :]
        grad_out = do_ref[at]
        probs, _ = masked_exp(k_ref, query, i, piece, log_ref[0, :, rows])
        dv_ref[:end, :] += dot(probs.astype(BF16), grad_out)
        grad_probs = dot_t(v_ref[:end, :], grad_out)
        inner = jnp.sum(probs * grad_probs, axis=0, keepdims=True)
        grad_scores = (probs * (grad_probs - inner)).astype(BF16)
        dk_ref[:end, :] += dot(grad_scores, query)
        grad_query = dot(keys_t[:, :end], grad_scores).T * SCALE
        result, gain = head_back(grad_query, qp_ref[rows, :], qg_ref[...], cos_ref[rows, :], sin_ref[rows, :])
        grad_ref[at, :, column] = result.astype(BF16)
        qgain_ref[...] += gain

    @pl.when(second == 1)
    def _():
        for i in range(blocks):
            rows = slice(i * piece, (i + 1) * piece)
            at = place(i, s_ref[0], x_count)
            result, gain = head_back(
                dk_ref[rows, :] * SCALE, kp_ref[rows, :], kg_ref[...], cos_ref[rows, :], sin_ref[rows, :]
            )
            grad_ref[at, :, 2 * HEAD_SIZE : 3 * HEAD_SIZE] = result.astype(BF16)
            grad_ref[at, :, 3 * HEAD_SIZE :] = dv_ref[rows, :].astype(BF16)
            kgain_ref[...] += gain


def attend_back(s, qkv, pre, log_total, grad_mixed, query_gain, key_gain, cosine, sine, blocks, x_count):
    length, columns = qkv.shape
    heads_kv = columns // (4 * HEAD_SIZE)
    piece = length // blocks
    head = lambda part: pl.BlockSpec(
        (length, HEAD_SIZE), lambda j, g, s_ref: (0, 4 * j + (g if part == 0 else part))
    )
    pre_head = lambda part: pl.BlockSpec(
        (length, HEAD_SIZE), lambda j, g, s_ref: (0, 3 * j + (g if part == 0 else part))
    )
    whole = lambda shape: pl.BlockSpec(shape, lambda j, g, s_ref: (0,) * len(shape))
    return pl.pallas_call(
        functools.partial(backward_kernel, blocks, x_count),
        name="attend_back",
        out_shape=(
            jax.ShapeDtypeStruct((blocks, piece, columns), BF16),
            jax.ShapeDtypeStruct((1, HEAD_SIZE), F32),
            jax.ShapeDtypeStruct((1, HEAD_SIZE), F32),
        ),
        grid_spec=pltpu.PrefetchScalarGridSpec(
            num_scalar_prefetch=1,
            grid=(heads_kv, 2),
            in_specs=[
                head(0),
                head(2),
                head(3),
                pl.BlockSpec((blocks, piece, HEAD_SIZE), lambda j, g, s_ref: (0, 0, 2 * j + g)),
                pl.BlockSpec((1, 1, length), lambda j, g, s_ref: (2 * j + g, 0, 0)),
                pre_head(0),
                pre_head(2),
                whole((1, HEAD_SIZE)),
                whole((1, HEAD_SIZE)),
                whole((length, HEAD_SIZE)),
                whole((length, HEAD_SIZE)),
            ],
            out_specs=[
                pl.BlockSpec((blocks, piece, 4 * HEAD_SIZE), lambda j, g, s_ref: (0, 0, j)),
                whole((1, HEAD_SIZE)),
                whole((1, HEAD_SIZE)),
            ],
            scratch_shapes=[pltpu.VMEM((length, HEAD_SIZE), F32), pltpu.VMEM((length, HEAD_SIZE), F32)],
        ),
        cost_estimate=pl.CostEstimate(
            flops=2 * 2 * heads_kv * length * length * HEAD_SIZE * 5 // 2,
            bytes_accessed=2 * heads_kv * length * HEAD_SIZE * 24,
            transcendentals=heads_kv * length * length,
        ),
    )(s, qkv, qkv, qkv, grad_mixed, log_total, pre, pre, query_gain, key_gain, cosine, sine)


MESH = pl.DeviceIdType.MESH


def flip(index, bit):
    step = 1 << bit
    return index + step - 2 * step * lax.rem(lax.div(index, step), 2)


def bit_of(index, bit):
    return lax.rem(lax.div(index, 1 << bit), 2)


class Links:
    def __init__(self, send, recv):
        self.send, self.recv = send, recv
        self.d, self.s = lax.axis_index("dp"), lax.axis_index("seq")
        self.used = 0
        self.started = []

    def slots(self, n):
        self.used += n
        return self.used - n

    def copy(self, src, dst, slot, **to):
        return pltpu.make_async_remote_copy(
            src_ref=src,
            dst_ref=dst,
            send_sem=self.send.at[slot],
            recv_sem=self.recv.at[slot],
            device_id=to,
            device_id_type=MESH,
        )

    def start(self, src, dst, slot, when=None, **to):
        copy = self.copy(src, dst, slot, **to)
        self.started.append((copy, when))
        if when is None:
            copy.start()
        else:
            pl.when(when)(copy.start)
        return copy

    def finish(self):
        for copy, when in self.started:
            if when is None:
                copy.wait_send()
            else:
                pl.when(when)(copy.wait_send)

    def greet(self, dp_bits, seq_masks):
        barrier = pltpu.get_barrier_semaphore()
        for bit in dp_bits:
            pl.semaphore_signal(
                barrier, inc=1, device_id={"dp": flip(self.d, bit)}, device_id_type=MESH
            )
        for mask in seq_masks:
            pl.semaphore_signal(
                barrier, inc=1, device_id={"seq": self.seq_at(mask)}, device_id_type=MESH
            )
        pl.semaphore_wait(barrier, len(dp_bits) + len(seq_masks))

    def seq_at(self, mask):
        s = self.s
        for bit in range(2):
            if mask >> bit & 1:
                s = flip(s, bit)
        return s

    def dp_at(self, mask):
        d = self.d
        for bit in range(3):
            if mask >> bit & 1:
                d = flip(d, bit)
        return d


class Gather:
    def __init__(self, links, block, order):
        self.links, self.block, self.order = links, block, order
        self.base = links.slots(8)
        self.copies = {}

    def send(self, r, bit):
        src = self.block(self.links.dp_at(r))
        self.copies[r | 1 << bit] = self.links.start(
            src, src, self.base + (r | 1 << bit), dp=flip(self.links.d, bit)
        )

    def got(self, r):
        self.copies[r].wait_recv()

    def first(self):
        for bit in self.order:
            self.send(0, bit)

    def second(self):
        a, b, c = self.order
        self.got(1 << a)
        self.send(1 << a, b)
        self.send(1 << a, c)

    def third(self):
        a, b, c = self.order
        self.got(1 << b)
        self.send(1 << b, c)
        self.got(1 << a | 1 << b)
        self.send(1 << a | 1 << b, c)

    def last(self):
        a, b, c = self.order
        for r in (0, 1 << a, 1 << b, 1 << a | 1 << b):
            self.got(r | 1 << c)


def first_kernel(
    heads,
    a_ref, c_ref, out_ref, down_ref, x_ref, g_ref, gains_ref, qg_ref, kg_ref, cos_ref, sin_ref,
    xr_ref, gr_ref, wa_ref, wc_ref, wo_ref, wd_ref, n_ref, qkv_ref, pre_ref, o_ref, log_ref, gain_ref,
    w_v, x_v, n_v, qkv_v, pre_v, o_v, sum_v, got_v, send, recv, local,
):
    links = Links(send, recv)
    d, s = links.d, links.s
    sequences, piece, width = x_ref.shape
    blocks = xr_ref.shape[1]
    length = blocks * piece
    x_bit, core = bit_of(s, 1), bit_of(s, 0)
    z1, z0, y = bit_of(d, 2), bit_of(d, 1), bit_of(d, 0)
    place_of = lambda i: lax.rem((i & 1) + core, 2) * 2 + lax.rem((i >> 1) + x_bit, 2)
    local_used = [0]
    locals_ = {}

    def near(name, src, dst):
        copy = pltpu.make_async_copy(src, dst, local.at[local_used[0]])
        local_used[0] += 1
        copy.start()
        locals_[name] = copy

    links.greet((0, 1, 2), (1, 2, 3))

    def exchange(src, dst):
        base = links.slots(4)
        return [
            links.start(src.at[links.seq_at(k)], dst.at[d, s], base + k, seq=links.seq_at(k))
            for k in (2, 3, 1)
        ]

    a_own = exchange(a_ref, wa_ref)
    near("a", a_ref.at[s], wa_ref.at[d, s])

    gain_slots = links.slots(5)
    gain_to = [dict(seq=links.seq_at(1)), dict(seq=links.seq_at(2))] + [dict(dp=flip(d, b)) for b in range(3)]
    gain_copy = links.start(gains_ref, got_v.at[0], gain_slots, **gain_to[0])

    x_slots = links.slots(3 * sequences)
    x_far = [
        links.start(x_ref.at[n], xr_ref.at[n, 1], x_slots + 3 * n, seq=links.seq_at(2))
        for n in range(sequences)
    ]
    x_near = [
        links.start(x_ref.at[n], xr_ref.at[n, 2], x_slots + 3 * n + 1, seq=links.seq_at(1))
        for n in range(sequences)
    ]
    c_own = exchange(c_ref, wc_ref)
    near("c", c_ref.at[s], wc_ref.at[d, s])
    for n in range(sequences):
        near(f"x{n}", x_ref.at[n], xr_ref.at[n, 0])
    near("d", down_ref, wd_ref.at[d])

    across, beside = lax.rem(x_bit + y, 2), lax.rem(core + z0, 2)
    out_slots = links.slots(7)
    holder = (across == 0) & (beside == 0)
    out_first = [
        links.start(
            out_ref, wo_ref.at[z1, s], out_slots + k,
            when=(across == k >> 1) & (beside == (k & 1)), seq=links.seq_at(k),
        )
        for k in (1, 2, 3)
    ]

    for copy in a_own:
        copy.wait_recv()
    locals_["a"].wait()
    half = blocks // 2
    gathers_a = [
        Gather(links, lambda at, h=h: wa_ref.at[at, pl.ds(h * half, half)], order)
        for h, order in ((0, (1, 2, 0)), (1, (0, 2, 1)))
    ]
    for gather in gathers_a:
        gather.first()
    gather_d = Gather(links, lambda at: wd_ref.at[at], (1, 2, 0))
    gather_c = Gather(links, lambda at: wc_ref.at[at], (1, 2, 0))

    for stage in range(5):
        gain_copy.wait_recv()
        before = gains_ref[...] if stage == 0 else sum_v[stage - 1]
        if stage == 4:
            gain_ref[...] = before + got_v[4]
        else:
            sum_v[stage] = before + got_v[stage]
            gain_copy = links.start(
                sum_v.at[stage], got_v.at[stage + 1], gain_slots + stage + 1, **gain_to[stage + 1]
            )

    for gather in gathers_a:
        gather.second()

    for copy in c_own:
        copy.wait_recv()
    locals_["c"].wait()
    gather_c.first()

    x_on = []
    x_far[0].wait_recv()
    x_on.append(links.start(xr_ref.at[0, 1], xr_ref.at[0, 3], x_slots + 2, seq=links.seq_at(1)))

    @pl.when(holder)
    def _():
        own = pltpu.make_async_copy(out_ref, wo_ref.at[z1, s], local.at[local_used[0]])
        own.start()
        for copy in out_first:
            copy.wait_recv()
        own.wait()

    local_used[0] += 1
    out_y = links.start(wo_ref.at[z1], wo_ref.at[z1], out_slots + 4, when=holder, dp=flip(d, 0))

    for gather in gathers_a:
        gather.third()
    locals_["d"].wait()
    gather_d.first()

    g_slots = links.slots(3 * sequences)
    g_far = [
        links.start(g_ref.at[n], gr_ref.at[n, 1], g_slots + 3 * n, seq=links.seq_at(2))
        for n in range(sequences)
    ]
    g_near = [
        links.start(g_ref.at[n], gr_ref.at[n, 2], g_slots + 3 * n + 1, seq=links.seq_at(1))
        for n in range(sequences)
    ]
    for n in range(sequences):
        near(f"g{n}", g_ref.at[n], gr_ref.at[n, 0])
    g_on = []

    for gather in gathers_a:
        gather.last()
    near("w", wa_ref, w_v)

    def wait_x(n):
        if n:
            x_far[n].wait_recv()
            x_on.append(
                links.start(xr_ref.at[n, 1], xr_ref.at[n, 3], x_slots + 3 * n + 2, seq=links.seq_at(1))
            )
        locals_[f"x{n}"].wait()
        x_near[n].wait_recv()
        x_on[n].wait_recv()
        near(f"xv{n}", xr_ref.at[n], x_v)
        locals_[f"xv{n}"].wait()

    def project_part(n):
        def step(i, carry):
            at = place_of(i)
            x = x_v[at].astype(F32)
            normed = (x * rms_scale(x) * gain_ref[0:1, :]).astype(BF16)
            n_v[n, at] = normed
            y_rows = dot(normed, w_v[...].reshape(width, -1))
            rows = pl.ds(pl.multiple_of(i * piece, piece), piece)
            cosine, sine = cos_ref[rows, :], sin_ref[rows, :]
            for j in range(heads // 2):
                for part in range(4):
                    cut = slice((4 * j + part) * HEAD_SIZE, (4 * j + part + 1) * HEAD_SIZE)
                    head = y_rows[:, cut]
                    if part < 3:
                        pre_v[n, rows, (3 * j + part) * HEAD_SIZE : (3 * j + part + 1) * HEAD_SIZE] = head
                        gain = qg_ref[...] if part < 2 else kg_ref[...]
                        head = head * rms_scale(head) * gain
                        head = head * cosine + pltpu.roll(head, HEAD_SIZE // 2, 1) * sine
                    qkv_v[n, rows, cut] = head.astype(BF16)
            return carry

        lax.fori_loop(0, blocks, step, 0)
        near(f"n{n}", n_v.at[n], n_ref.at[n])
        near(f"qkv{n}", qkv_v.at[n], qkv_ref.at[n])
        near(f"pre{n}", pre_v.at[n], pre_ref.at[n])

    def attend_part(n, start, stop):
        def step(h, carry):
            j, g = lax.div(h, 2), lax.rem(h, 2)
            lanes = lambda at: pl.ds(pl.multiple_of(at * HEAD_SIZE, HEAD_SIZE), HEAD_SIZE)
            values_t = qkv_v[n, :, lanes(4 * j + 3)].T
            keys = qkv_v.at[n, :, lanes(4 * j + 2)]
            for i in range(blocks):
                query = qkv_v[n, i * piece : (i + 1) * piece, lanes(4 * j + g)]
                exponent, highest = masked_exp(keys, query, i, piece, None)
                total = jnp.sum(exponent, axis=0, keepdims=True)
                probs = (exponent * (1.0 / total)).astype(BF16)
                mixed = dot(values_t[:, : (i + 1) * piece], probs)
                o_v[n, place_of(i), :, lanes(h)] = mixed.T.astype(BF16)
                log_ref[n, h, :, i * piece : (i + 1) * piece] = highest + jnp.log(total)
            return carry

        lax.fori_loop(start, stop, step, 0)

    wait_x(0)
    locals_["w"].wait()
    project_part(0)
    gather_c.second()
    pl.when((across == 1) & (beside == 0))(out_y.wait_recv)
    out_z0 = links.start(wo_ref.at[z1], wo_ref.at[z1], out_slots + 5, when=beside == 0, dp=flip(d, 1))
    gather_d.second()
    attend_part(0, 0, heads // 2)
    gather_c.third()
    pl.when(beside == 1)(out_z0.wait_recv)
    out_z1 = links.start(wo_ref.at[z1], wo_ref.at[z1], out_slots + 6, dp=flip(d, 2))
    attend_part(0, heads // 2, heads)
    near("o0", o_v.at[0], o_ref.at[0])
    for n in range(1, sequences):
        wait_x(n)
        project_part(n)
        if n == 1:
            gather_d.third()
            for m in range(sequences):
                g_far[m].wait_recv()
                g_on.append(
                    links.start(gr_ref.at[m, 1], gr_ref.at[m, 3], g_slots + 3 * m + 2, seq=links.seq_at(1))
                )
        attend_part(n, 0, heads)
        near(f"o{n}", o_v.at[n], o_ref.at[n])
    gather_c.last()
    gather_d.last()
    out_z1.wait_recv()
    for copy in g_near + g_on:
        copy.wait_recv()
    for n in range(sequences):
        for name in ("g", "n", "qkv", "pre", "o"):
            locals_[f"{name}{n}"].wait()
    links.finish()


def first(a, c, w_out, w_down, x, g, gains, query_gain, key_gain, cosine, sine, dp, heads):
    blocks, rows, columns = a.shape
    sequences, piece, width = x.shape
    length = blocks * piece
    hbm = pl.BlockSpec(memory_space=pl.ANY)
    vmem = pl.BlockSpec(memory_space=pltpu.VMEM)
    shape = jax.ShapeDtypeStruct
    pre_columns = columns // 4 * 3
    slots = 96
    return pl.pallas_call(
        functools.partial(first_kernel, heads),
        name="first",
        out_shape=(
            shape((sequences, blocks, piece, width), BF16),
            shape((sequences, blocks, piece, width), BF16),
            shape((dp, blocks, rows, columns), BF16),
            shape((dp, blocks, rows, c.shape[2]), BF16),
            shape((2, blocks) + w_out.shape, BF16),
            shape((dp,) + w_down.shape, BF16),
            shape((sequences, blocks, piece, width), BF16),
            shape((sequences, length, columns), BF16),
            shape((sequences, length, pre_columns), F32),
            shape((sequences, blocks, piece, heads * HEAD_SIZE), BF16),
            shape((sequences, heads, 1, length), F32),
            shape((8, width), F32),
        ),
        in_specs=[hbm] * 6 + [vmem] * 5,
        out_specs=[hbm] * 10 + [vmem] * 2,
        scratch_shapes=[
            pltpu.VMEM((dp, blocks, rows, columns), BF16),
            pltpu.VMEM((blocks, piece, width), BF16),
            pltpu.VMEM((sequences, blocks, piece, width), BF16),
            pltpu.VMEM((sequences, length, columns), BF16),
            pltpu.VMEM((sequences, length, pre_columns), F32),
            pltpu.VMEM((sequences, blocks, piece, heads * HEAD_SIZE), BF16),
            pltpu.VMEM((4, 8, width), F32),
            pltpu.VMEM((5, 8, width), F32),
            pltpu.SemaphoreType.DMA((slots,)),
            pltpu.SemaphoreType.DMA((slots,)),
            pltpu.SemaphoreType.DMA((24,)),
        ],
        compiler_params=pltpu.CompilerParams(
            collective_id=0, has_side_effects=True, vmem_limit_bytes=60 * 1024 * 1024
        ),
    )(a, c, w_out, w_down, x, g, gains, query_gain, key_gain, cosine, sine)


def body(
    hidden_in,
    attn_gain,
    w_query,
    key_weight,
    value_weight,
    query_gain,
    key_gain,
    w_out,
    mlp_gain,
    w_gate,
    w_up,
    w_down,
    cotangent,
):
    wires = Wires(lax.axis_size("dp"), lax.axis_size("seq"))
    dp, seq, x_count = wires.dp, wires.seq, wires.x_count
    count = wires.count
    sequences, piece, width = hidden_in.shape
    length = seq * piece
    part = x_count * piece
    heads_kv = key_weight.shape[1] // HEAD_SIZE
    s_index = wires.s.reshape(1).astype(jnp.int32)
    cosine, sine = rope_tables(length)
    query_gain_row = query_gain.astype(F32).reshape(1, -1)
    key_gain_row = key_gain.astype(F32).reshape(1, -1)

    index = wires.d * seq + wires.s
    own_gains = jnp.stack([attn_gain, mlp_gain])
    rows = w_query.shape[0]
    by_head = jnp.concatenate(
        [
            w_query.reshape(rows, heads_kv, -1),
            key_weight.reshape(rows, heads_kv, -1),
            value_weight.reshape(rows, heads_kv, -1),
        ],
        axis=2,
    )
    order = [wires.heads_of(t, heads_kv) for t in range(seq)]
    package_in = jnp.stack(
        [jnp.concatenate([by_head[:, j] for j in order[t]], axis=1) for t in range(seq)]
    )
    down_rows = w_down.shape[0]

    def by_unit(w):
        return w.reshape(rows, dp, seq, down_rows).transpose(2, 0, 1, 3).reshape(seq, rows, -1)

    units = dp * down_rows
    package_mlp = jnp.concatenate([by_unit(w_gate), by_unit(w_up)], axis=2)

    fused = (dp, seq) == (8, 4) and rows % 16 == 0 and down_rows % 16 == 0
    if fused:
        gains = jnp.zeros((8, count, width // count), F32)
        gains = lax.dynamic_update_slice(gains, own_gains.astype(F32)[:, None], (0, index, 0))
        (
            x_rel, g_rel, w_in, w_mlp, w_o, w_d, all_normed, all_qkv, all_pre, all_mixed, all_log, gains
        ) = first(
            package_in, package_mlp, w_out, w_down, hidden_in, cotangent, gains.reshape(8, width),
            query_gain_row, key_gain_row, cosine, sine, dp, 2 * heads_kv // seq,
        )
        w_in, w_mlp = w_in.reshape(width, -1), w_mlp.reshape(width, -1)
        w_o, w_d = w_o.reshape(-1, width), w_d.reshape(units, width)
        attn_gain_row, mlp_gain_row = gains[:1], gains[1:2]
    else:
        gains = jnp.zeros((2, count, width // count), BF16)
        gains = lax.dynamic_update_slice(gains, own_gains[:, None], (0, index, 0))
        gains = wires.sum_all(gains.reshape(2, width)).astype(F32)
        attn_gain_row, mlp_gain_row = gains[:1], gains[1:]
        package = wires.exchange_seq(package_in).reshape(seq * rows, -1)
        w_in = wires.gather_dp(package).reshape(width, -1)
        x_rel = jnp.stack(wires.gather_seq_relative(hidden_in), axis=1)
        w_o = wires.gather_out(w_out, heads_kv)
        package = wires.exchange_seq(package_mlp).reshape(seq * rows, -1)
        w_mlp = wires.gather_dp(package).reshape(width, -1)
        g_rel = jnp.stack(wires.gather_seq_relative(cotangent), axis=1)
        w_d = wires.gather_dp(w_down).reshape(units, width)

    kept = []
    outs = []
    for n in range(sequences):
        if fused:
            normed, qkv, pre = all_normed[n], all_qkv[n], all_pre[n]
            mixed, log_total = all_mixed[n], all_log[n]
        else:
            normed, qkv, pre = project(
                s_index, x_rel[n], w_in, attn_gain_row, query_gain_row, key_gain_row, cosine, sine, x_count
            )
            mixed, log_total = attend(s_index, qkv, seq, x_count)
        mixed_rows = mixed.reshape(length, -1)
        other = wires.swap(dot(mixed_rows[part:], w_o).astype(BF16), 1)
        total = wires.sum_x(dot(mixed_rows[:part], w_o) + other.astype(F32))
        residual = total + x_rel[n].reshape(length, width)[:part].astype(F32)
        scale = rms_scale(residual)
        normed_mlp = (residual * scale * mlp_gain_row).astype(BF16)
        normed_mlp = jnp.concatenate([normed_mlp, wires.swap(normed_mlp, 1)], axis=0)
        both = dot(normed_mlp, w_mlp)
        gate, upward = both[:, :units], both[:, units:]
        sigmoid = jax.nn.sigmoid(gate)
        silu = gate * sigmoid
        hidden = (silu * upward).astype(BF16)
        other = wires.swap(dot(hidden[part:], w_d).astype(BF16), 1)
        total = wires.scatter_x(dot(hidden[:part], w_d) + other.astype(F32))
        outs.append((residual[:piece] + total).astype(BF16))

        grad_top = g_rel[n].reshape(length, width)
        grad_hidden = dot_t(grad_top, w_d)
        grad_gate = (grad_hidden * upward * sigmoid * (1.0 + gate * (1.0 - sigmoid))).astype(BF16)
        grad_upward = (grad_hidden * silu).astype(BF16)
        grad_both = jnp.concatenate([grad_gate, grad_upward], axis=1)
        other = wires.swap(dot_t(grad_both[part:], w_mlp).astype(BF16), 1)
        grad_normed = wires.sum_x(dot_t(grad_both[:part], w_mlp) + other.astype(F32))
        scaled = grad_normed * mlp_gain_row
        grad_residual = (
            grad_top[:part].astype(F32)
            + scale * scaled
            - residual * (scale * scale * scale * jnp.mean(scaled * residual, axis=-1, keepdims=True))
        )
        grad_mlp_gain = jnp.sum((grad_normed * residual * scale)[:piece], axis=0)
        branch = grad_residual.astype(BF16)
        branch = jnp.concatenate([branch, wires.swap(branch, 1)], axis=0)
        grad_mixed = dot_t(branch, w_o).astype(BF16).reshape(mixed.shape)
        grad_qkv, grad_query_gain, grad_key_gain = attend_back(
            s_index, qkv, pre, log_total, grad_mixed, query_gain_row, key_gain_row, cosine, sine, seq, x_count
        )
        grad_rows = grad_qkv.reshape(length, -1)
        other = wires.swap(dot_t(grad_rows[part:], w_in).astype(BF16), 1)
        grad_first = wires.scatter_x(dot_t(grad_rows[:part], w_in) + other.astype(F32))
        tokens = hidden_in[n].astype(F32)
        scale = rms_scale(tokens)
        scaled = grad_first * attn_gain_row
        grad_tokens = (
            grad_residual[:piece]
            + scale * scaled
            - tokens * (scale * scale * scale * jnp.mean(scaled * tokens, axis=-1, keepdims=True))
        )
        grad_attn_gain = jnp.sum(grad_first * tokens * scale, axis=0)
        kept.append(
            dict(
                normed=normed.reshape(length, width),
                mixed=mixed_rows,
                normed_mlp=normed_mlp,
                hidden=hidden,
                grad_both=grad_both,
                branch=branch,
                grad_rows=grad_rows,
                grad_tokens=grad_tokens,
                gains=jnp.concatenate(
                    [grad_attn_gain, grad_mlp_gain, grad_query_gain[0], grad_key_gain[0]]
                ),
            )
        )

    def over(name):
        return jnp.concatenate([k[name] for k in kept], axis=0)

    grad_down = t_dot(over("hidden"), g_rel.reshape(-1, width)).astype(BF16)
    grad_down = wires.scatter_dp(grad_down.reshape(dp, down_rows, width)).astype(F32)

    grad_mlp = t_dot(over("normed_mlp"), over("grad_both")).astype(BF16)
    grad_mlp = wires.scatter_dp(grad_mlp.reshape(dp, seq * rows, -1))
    grad_mlp = wires.exchange_seq(grad_mlp.reshape(seq, rows, -1)).astype(F32)

    def from_unit(g):
        return g.reshape(seq, rows, dp, down_rows).transpose(1, 2, 0, 3).reshape(rows, -1)

    grad_gate, grad_up = from_unit(grad_mlp[..., :units]), from_unit(grad_mlp[..., units:])

    grad_out = t_dot(over("mixed"), over("branch")).astype(BF16)
    grad_out = wires.scatter_out(grad_out, heads_kv).astype(F32)

    grad_in = t_dot(over("normed"), over("grad_rows")).astype(BF16)
    grad_in = wires.scatter_dp(grad_in.reshape(dp, seq * rows, -1))
    grad_in = wires.exchange_seq(grad_in.reshape(seq, rows, -1)).astype(F32)
    pieces = [None] * heads_kv
    for t in range(seq):
        for m, j in enumerate(order[t]):
            pieces[j] = grad_in[t, :, m * 4 * HEAD_SIZE : (m + 1) * 4 * HEAD_SIZE]
    grad_query = jnp.concatenate([p[:, : 2 * HEAD_SIZE] for p in pieces], axis=1)
    grad_key = jnp.concatenate([p[:, 2 * HEAD_SIZE : 3 * HEAD_SIZE] for p in pieces], axis=1)
    grad_value = jnp.concatenate([p[:, 3 * HEAD_SIZE :] for p in pieces], axis=1)

    gain_sums = wires.sum_all(sum(k["gains"] for k in kept))
    own = width // count
    grad_attn_gain = lax.dynamic_slice_in_dim(gain_sums, index * own, own)
    grad_mlp_gain = lax.dynamic_slice_in_dim(gain_sums, width + index * own, own)
    return (
        jnp.stack(outs),
        jnp.stack([k["grad_tokens"] for k in kept]),
        grad_attn_gain,
        grad_query,
        grad_key,
        grad_value,
        gain_sums[2 * width : 2 * width + HEAD_SIZE],
        gain_sums[2 * width + HEAD_SIZE :],
        grad_out,
        grad_mlp_gain,
        grad_gate,
        grad_up,
        grad_down,
    )


def solution(mesh):
    rows = P(("dp", "seq"), None)
    line = P(("dp", "seq"))
    tokens = P("dp", "seq", None)
    return jax.shard_map(
        body,
        mesh=mesh,
        in_specs=(tokens, line, rows, rows, rows, P(), P(), rows, line, rows, rows, rows, tokens),
        out_specs=(tokens, tokens, line, rows, rows, rows, P(), P(), rows, line, rows, rows, rows),
        check_vma=False,
    )
```

```python
import functools

import jax
import jax.numpy as jnp
from jax import lax
from jax.experimental import pallas as pl
from jax.experimental.pallas import tpu as pltpu
from jax.sharding import PartitionSpec as P

HEAD_SIZE = 128
EPS = 1e-06
ROPE_THETA = 1000000.0
AXES = ("dp", "seq")
SCALE = HEAD_SIZE ** (-0.5)
F32 = jnp.float32
BF16 = jnp.bfloat16


def log2(n):
    return n.bit_length() - 1


class Wires:
    def __init__(self, dp, seq):
        self.dp, self.seq, self.count = dp, seq, dp * seq
        self.dp_bits, self.seq_bits = log2(dp), log2(seq)
        self.x_count = seq // 2
        y_bits = min(log2(self.x_count), self.dp_bits)
        self.dp_order = list(range(y_bits, self.dp_bits)) + list(range(y_bits))
        self.x_bits = list(range(1, self.seq_bits))
        self.d = lax.axis_index("dp")
        self.s = lax.axis_index("seq")

    def swap(self, value, mask, only=None):
        pairs = [(i, i ^ mask) for i in range(self.count) if only is None or only(i)]
        return lax.ppermute(value, AXES, pairs)

    def dp_swap(self, value, bit, only=None):
        return self.swap(value, (1 << bit) * self.seq, only)

    def bit_d(self, bit):
        return (self.d >> bit) & 1

    def bit_s(self, bit):
        return (self.s >> bit) & 1

    def gather_dp(self, shard):
        pieces = {0: shard}
        for bit in self.dp_order:
            pieces.update({r | (1 << bit): self.dp_swap(v, bit) for r, v in list(pieces.items())})
        full = jnp.zeros((self.dp,) + shard.shape, shard.dtype)
        for r, v in pieces.items():
            full = lax.dynamic_update_index_in_dim(full, v, self.d ^ r, 0)
        return full

    def scatter_dp(self, value):
        rest = value.shape[1:]
        held = list(range(self.dp_bits - 1, -1, -1))
        value = value.reshape((2,) * self.dp_bits + rest)
        for bit in reversed(self.dp_order):
            axis = held.index(bit)
            held.pop(axis)
            mine = lax.dynamic_index_in_dim(value, self.bit_d(bit), axis, keepdims=False)
            other = lax.dynamic_index_in_dim(value, 1 - self.bit_d(bit), axis, keepdims=False)
            got = self.dp_swap(other, bit)
            value = (mine.astype(F32) + got.astype(F32)).astype(BF16)
        return value

    def exchange_seq(self, value):
        rest = value.shape[1:]
        for bit in self.x_bits + [0]:
            value = value.reshape((self.seq >> (bit + 1), 2, 1 << bit) + rest)
            me = self.bit_s(bit)
            mine = lax.dynamic_index_in_dim(value, me, 1, keepdims=False)
            other = lax.dynamic_index_in_dim(value, 1 - me, 1, keepdims=False)
            got = self.swap(other, 1 << bit)
            low = jnp.where(me == 0, mine, got)
            high = jnp.where(me == 0, got, mine)
            value = jnp.stack([low, high], axis=1).reshape((self.seq,) + rest)
        return value

    def gather_seq_relative(self, value):
        pieces = [value]
        for bit in self.x_bits:
            pieces = pieces + [self.swap(v, 1 << bit) for v in pieces]
        return pieces + [self.swap(v, 1) for v in pieces]

    def sum_x(self, value):
        n = self.x_count
        shape = value.shape
        for bit in self.x_bits:
            got = self.swap(value.astype(BF16), 1 << bit).astype(F32)
            blocks = got.reshape((n, shape[0] // n) + shape[1:])
            flip = [i ^ (1 << (bit - 1)) for i in range(n)]
            value = value + jnp.concatenate([blocks[i] for i in flip], axis=0)
        return value

    def scatter_x(self, value):
        n = self.x_count
        for bit in reversed(self.x_bits):
            half = value.shape[0] // 2
            got = self.swap(value[half:].astype(BF16), 1 << bit)
            value = value[:half] + got.astype(F32)
        return value

    def sum_all(self, value):
        for bit in range(log2(self.count)):
            value = value + self.swap(value, 1 << bit)
        return value

    def head_bits(self, heads_kv):
        low = self.dp_bits - log2(heads_kv)
        partner = {0: 1, 1: 0, 2: 2}
        matched = [(low + k, partner[k]) for k in range(self.seq_bits)]
        free = [low + k for k in range(self.seq_bits, log2(heads_kv))]
        return low, matched, free

    def heads_of(self, t, heads_kv):
        low, matched, free = self.head_bits(heads_kv)
        heads = [0]
        for bit, tbit in matched:
            heads = [h | (((t >> tbit) & 1) << (bit - low)) for h in heads]
        for bit in free:
            heads = heads + [h | (1 << (bit - low)) for h in heads]
        return heads

    def matches(self, i, pairs):
        return all(((i // self.seq) >> b) & 1 == (i >> t) & 1 for b, t in pairs)

    def gather_out(self, shard, heads_kv):
        low, matched, free = self.head_bits(heads_kv)
        value = shard
        for bit in self.x_bits + [0]:
            pass
        value = shard[None]
        for bit in [0] + self.x_bits:
            got = self.swap(value, 1 << bit)
            value = self.ordered(value, got, self.bit_s(bit))
        for bit in range(low):
            got = self.dp_swap(value, bit)
            value = self.ordered(value, got, self.bit_d(bit))
        for n, (bit, tbit) in enumerate(matched):
            got = self.dp_swap(value, bit, lambda i: self.matches(i, matched[n:]))
            value = jnp.where(self.bit_d(bit) == self.bit_s(tbit), value, got)
        for bit in free:
            got = self.dp_swap(value, bit)
            value = self.ordered(value, got, self.bit_d(bit))
        return value.reshape((-1,) + shard.shape[1:])

    def ordered(self, own, got, bit):
        return jnp.concatenate(
            [jnp.where(bit == 0, own, got), jnp.where(bit == 0, got, own)], axis=0
        )

    def halves(self, value, bit):
        half = value.shape[0] // 2
        mine = lax.dynamic_slice_in_dim(value, bit * half, half, 0)
        other = lax.dynamic_slice_in_dim(value, (1 - bit) * half, half, 0)
        return mine, other

    def scatter_out(self, value, heads_kv):
        low, matched, free = self.head_bits(heads_kv)
        for bit in reversed(free):
            mine, other = self.halves(value, self.bit_d(bit))
            got = self.dp_swap(other, bit)
            value = (mine.astype(F32) + got.astype(F32)).astype(BF16)
        for n in reversed(range(len(matched))):
            bit, tbit = matched[n]
            got = self.dp_swap(
                value,
                bit,
                lambda i: self.matches(i, matched[n + 1 :]) and not self.matches(i, [matched[n]]),
            )
            value = (value.astype(F32) + got.astype(F32)).astype(BF16)
        for bit in reversed(range(low)):
            mine, other = self.halves(value, self.bit_d(bit))
            got = self.dp_swap(other, bit, lambda i: self.matches(i, matched))
            value = (mine.astype(F32) + got.astype(F32)).astype(BF16)
        todo = dict((tbit, bit) for bit, tbit in matched)
        for tbit in reversed(self.x_bits):
            value = self.hand_out(value, tbit, todo)
        return self.hand_out(value, 0, todo)

    def hand_out(self, value, tbit, todo):
        bit = todo.pop(tbit)
        left = [(b, t) for t, b in todo.items()]
        mine, other = self.halves(value, self.bit_s(tbit))
        got = self.swap(
            other, 1 << tbit, lambda i: self.matches(i, left) and self.matches(i, [(bit, tbit)])
        )
        return jnp.where(self.bit_d(bit) == self.bit_s(tbit), mine, got)


def dot(a, b):
    return lax.dot_general(a, b, (((1,), (0,)), ((), ())), preferred_element_type=F32)


def dot_t(a, b):
    return lax.dot_general(a, b, (((1,), (1,)), ((), ())), preferred_element_type=F32)


def t_dot(a, b):
    return lax.dot_general(a, b, (((0,), (0,)), ((), ())), preferred_element_type=F32)


def rms_scale(rows):
    return lax.rsqrt(jnp.mean(rows * rows, axis=-1, keepdims=True) + EPS)


def rope_tables(length):
    halfway = HEAD_SIZE // 2
    inverse = jnp.power(F32(ROPE_THETA), -(jnp.arange(halfway).astype(F32) * 2.0) / HEAD_SIZE)
    angles = jnp.arange(length).astype(F32)[:, None] * inverse[None, :]
    cosine, sine = jnp.cos(angles), jnp.sin(angles)
    return (
        jnp.concatenate([cosine, cosine], axis=-1),
        jnp.concatenate([-sine, sine], axis=-1),
    )


def place(block, s, x_count):
    return ((block & 1) ^ (s & 1)) * x_count + ((block >> 1) ^ (s >> 1))


def project_kernel(s_ref, x_ref, w_ref, gain_ref, qg_ref, kg_ref, cos_ref, sin_ref, n_ref, qkv_ref, pre_ref):
    x = x_ref[0].astype(F32)
    normed = (x * rms_scale(x) * gain_ref[...]).astype(BF16)
    n_ref[0] = normed
    y = dot(normed, w_ref[...])
    cosine, sine = cos_ref[...], sin_ref[...]
    for j in range(y.shape[1] // (4 * HEAD_SIZE)):
        for part in range(4):
            at = slice((4 * j + part) * HEAD_SIZE, (4 * j + part + 1) * HEAD_SIZE)
            head = y[:, at]
            if part < 3:
                pre_ref[:, (3 * j + part) * HEAD_SIZE : (3 * j + part + 1) * HEAD_SIZE] = head
                gain = qg_ref[...] if part < 2 else kg_ref[...]
                head = head * rms_scale(head) * gain
                head = head * cosine + pltpu.roll(head, HEAD_SIZE // 2, 1) * sine
            qkv_ref[:, at] = head.astype(BF16)


def project(s, x_rel, w, gain, query_gain, key_gain, cosine, sine, x_count):
    blocks, piece, width = x_rel.shape
    length, columns = blocks * piece, w.shape[1]
    heads = columns // (4 * HEAD_SIZE)
    whole = lambda shape: pl.BlockSpec(shape, lambda i, s_ref: (0,) * len(shape))
    rel = pl.BlockSpec((1, piece, width), lambda i, s_ref: (place(i, s_ref[0], x_count), 0, 0))
    table = pl.BlockSpec((piece, HEAD_SIZE), lambda i, s_ref: (i, 0))
    return pl.pallas_call(
        project_kernel,
        name="project",
        out_shape=(
            jax.ShapeDtypeStruct((blocks, piece, width), BF16),
            jax.ShapeDtypeStruct((length, columns), BF16),
            jax.ShapeDtypeStruct((length, 3 * heads * HEAD_SIZE), F32),
        ),
        grid_spec=pltpu.PrefetchScalarGridSpec(
            num_scalar_prefetch=1,
            grid=(blocks,),
            in_specs=[
                rel,
                whole(w.shape),
                whole((1, width)),
                whole((1, HEAD_SIZE)),
                whole((1, HEAD_SIZE)),
                table,
                table,
            ],
            out_specs=[
                rel,
                pl.BlockSpec((piece, columns), lambda i, s_ref: (i, 0)),
                pl.BlockSpec((piece, 3 * heads * HEAD_SIZE), lambda i, s_ref: (i, 0)),
            ],
        ),
        cost_estimate=pl.CostEstimate(
            flops=2 * length * width * columns,
            bytes_accessed=2 * (2 * length * width + width * columns + 4 * length * columns),
            transcendentals=0,
        ),
    )(s, x_rel, w, gain, query_gain, key_gain, cosine, sine)


def masked_exp(k_ref, query, i, piece, offset):
    diagonal = dot_t(k_ref[i * piece : (i + 1) * piece, :], query) * SCALE
    key_at = lax.broadcasted_iota(jnp.int32, (piece, piece), 0)
    query_at = lax.broadcasted_iota(jnp.int32, (piece, piece), 1)
    diagonal = jnp.where(key_at <= query_at, diagonal, -jnp.inf)
    if i == 0:
        scores = diagonal
    else:
        scores = jnp.concatenate(
            [dot_t(k_ref[: i * piece, :], query) * SCALE, diagonal], axis=0
        )
    if offset is None:
        offset = jnp.max(scores, axis=0, keepdims=True)
    return jnp.exp(scores - offset), offset


def forward_kernel(blocks, x_count, s_ref, q_ref, k_ref, v_ref, o_ref, log_ref):
    piece = q_ref.shape[0] // blocks
    values_t = v_ref[...].T
    for i in range(blocks):
        query = q_ref[i * piece : (i + 1) * piece, :]
        exponent, highest = masked_exp(k_ref, query, i, piece, None)
        total = jnp.sum(exponent, axis=0, keepdims=True)
        probs = (exponent * (1.0 / total)).astype(BF16)
        mixed = dot(values_t[:, : (i + 1) * piece], probs)
        o_ref[place(i, s_ref[0], x_count)] = mixed.T.astype(BF16)
        log_ref[0, :, i * piece : (i + 1) * piece] = highest + jnp.log(total)


def attend(s, qkv, blocks, x_count):
    length, columns = qkv.shape
    heads = columns // (2 * HEAD_SIZE)
    piece = length // blocks
    head = lambda part: pl.BlockSpec(
        (length, HEAD_SIZE), lambda h, s_ref: (0, 4 * (h // 2) + (h % 2 if part == 0 else part))
    )
    return pl.pallas_call(
        functools.partial(forward_kernel, blocks, x_count),
        name="attend",
        out_shape=(
            jax.ShapeDtypeStruct((blocks, piece, heads * HEAD_SIZE), BF16),
            jax.ShapeDtypeStruct((heads, 1, length), F32),
        ),
        grid_spec=pltpu.PrefetchScalarGridSpec(
            num_scalar_prefetch=1,
            grid=(heads,),
            in_specs=[head(0), head(2), head(3)],
            out_specs=[
                pl.BlockSpec((blocks, piece, HEAD_SIZE), lambda h, s_ref: (0, 0, h)),
                pl.BlockSpec((1, 1, length), lambda h, s_ref: (h, 0, 0)),
            ],
        ),
        cost_estimate=pl.CostEstimate(
            flops=2 * heads * length * length * HEAD_SIZE * 2,
            bytes_accessed=2 * heads * length * HEAD_SIZE * 4,
            transcendentals=heads * length * length // 2,
        ),
    )(s, qkv, qkv, qkv)


def head_back(grad, pre, gain, cosine, sine):
    turned = grad * cosine - pltpu.roll(grad, HEAD_SIZE // 2, 1) * sine
    scale = rms_scale(pre)
    part = turned * gain
    result = scale * part - pre * (scale * scale * scale * jnp.mean(part * pre, axis=-1, keepdims=True))
    return result, jnp.sum(turned * pre * scale, axis=0, keepdims=True)


def backward_kernel(
    blocks, x_count, s_ref, q_ref, k_ref, v_ref, do_ref, log_ref, qp_ref, kp_ref, qg_ref, kg_ref,
    cos_ref, sin_ref, grad_ref, qgain_ref, kgain_ref, dk_ref, dv_ref,
):
    piece = q_ref.shape[0] // blocks
    second = pl.program_id(1)

    @pl.when((pl.program_id(0) == 0) & (second == 0))
    def _():
        qgain_ref[...] = jnp.zeros_like(qgain_ref)
        kgain_ref[...] = jnp.zeros_like(kgain_ref)

    @pl.when(second == 0)
    def _():
        dk_ref[...] = jnp.zeros_like(dk_ref)
        dv_ref[...] = jnp.zeros_like(dv_ref)

    keys_t = k_ref[...].T
    column = pl.ds(pl.multiple_of(second * HEAD_SIZE, HEAD_SIZE), HEAD_SIZE)
    for i in range(blocks):
        rows = slice(i * piece, (i + 1) * piece)
        end = (i + 1) * piece
        at = place(i, s_ref[0], x_count)
        query = q_ref[rows, :]
        grad_out = do_ref[at]
        probs, _ = masked_exp(k_ref, query, i, piece, log_ref[0, :, rows])
        dv_ref[:end, :] += dot(probs.astype(BF16), grad_out)
        grad_probs = dot_t(v_ref[:end, :], grad_out)
        inner = jnp.sum(probs * grad_probs, axis=0, keepdims=True)
        grad_scores = (probs * (grad_probs - inner)).astype(BF16)
        dk_ref[:end, :] += dot(grad_scores, query)
        grad_query = dot(keys_t[:, :end], grad_scores).T * SCALE
        result, gain = head_back(grad_query, qp_ref[rows, :], qg_ref[...], cos_ref[rows, :], sin_ref[rows, :])
        grad_ref[at, :, column] = result.astype(BF16)
        qgain_ref[...] += gain

    @pl.when(second == 1)
    def _():
        for i in range(blocks):
            rows = slice(i * piece, (i + 1) * piece)
            at = place(i, s_ref[0], x_count)
            result, gain = head_back(
                dk_ref[rows, :] * SCALE, kp_ref[rows, :], kg_ref[...], cos_ref[rows, :], sin_ref[rows, :]
            )
            grad_ref[at, :, 2 * HEAD_SIZE : 3 * HEAD_SIZE] = result.astype(BF16)
            grad_ref[at, :, 3 * HEAD_SIZE :] = dv_ref[rows, :].astype(BF16)
            kgain_ref[...] += gain


def attend_back(s, qkv, pre, log_total, grad_mixed, query_gain, key_gain, cosine, sine, blocks, x_count):
    length, columns = qkv.shape
    heads_kv = columns // (4 * HEAD_SIZE)
    piece = length // blocks
    head = lambda part: pl.BlockSpec(
        (length, HEAD_SIZE), lambda j, g, s_ref: (0, 4 * j + (g if part == 0 else part))
    )
    pre_head = lambda part: pl.BlockSpec(
        (length, HEAD_SIZE), lambda j, g, s_ref: (0, 3 * j + (g if part == 0 else part))
    )
    whole = lambda shape: pl.BlockSpec(shape, lambda j, g, s_ref: (0,) * len(shape))
    return pl.pallas_call(
        functools.partial(backward_kernel, blocks, x_count),
        name="attend_back",
        out_shape=(
            jax.ShapeDtypeStruct((blocks, piece, columns), BF16),
            jax.ShapeDtypeStruct((1, HEAD_SIZE), F32),
            jax.ShapeDtypeStruct((1, HEAD_SIZE), F32),
        ),
        grid_spec=pltpu.PrefetchScalarGridSpec(
            num_scalar_prefetch=1,
            grid=(heads_kv, 2),
            in_specs=[
                head(0),
                head(2),
                head(3),
                pl.BlockSpec((blocks, piece, HEAD_SIZE), lambda j, g, s_ref: (0, 0, 2 * j + g)),
                pl.BlockSpec((1, 1, length), lambda j, g, s_ref: (2 * j + g, 0, 0)),
                pre_head(0),
                pre_head(2),
                whole((1, HEAD_SIZE)),
                whole((1, HEAD_SIZE)),
                whole((length, HEAD_SIZE)),
                whole((length, HEAD_SIZE)),
            ],
            out_specs=[
                pl.BlockSpec((blocks, piece, 4 * HEAD_SIZE), lambda j, g, s_ref: (0, 0, j)),
                whole((1, HEAD_SIZE)),
                whole((1, HEAD_SIZE)),
            ],
            scratch_shapes=[pltpu.VMEM((length, HEAD_SIZE), F32), pltpu.VMEM((length, HEAD_SIZE), F32)],
        ),
        cost_estimate=pl.CostEstimate(
            flops=2 * 2 * heads_kv * length * length * HEAD_SIZE * 5 // 2,
            bytes_accessed=2 * heads_kv * length * HEAD_SIZE * 24,
            transcendentals=heads_kv * length * length,
        ),
    )(s, qkv, qkv, qkv, grad_mixed, log_total, pre, pre, query_gain, key_gain, cosine, sine)


MESH = pl.DeviceIdType.MESH


def flip(index, bit):
    step = 1 << bit
    return index + step - 2 * step * lax.rem(lax.div(index, step), 2)


def bit_of(index, bit):
    return lax.rem(lax.div(index, 1 << bit), 2)


class Links:
    def __init__(self, send, recv):
        self.send, self.recv = send, recv
        self.d, self.s = lax.axis_index("dp"), lax.axis_index("seq")
        self.used = 0
        self.started = []

    def slots(self, n):
        self.used += n
        return self.used - n

    def copy(self, src, dst, slot, **to):
        return pltpu.make_async_remote_copy(
            src_ref=src,
            dst_ref=dst,
            send_sem=self.send.at[slot],
            recv_sem=self.recv.at[slot],
            device_id=to,
            device_id_type=MESH,
        )

    def plan(self, src, dst, slot, when=None, **to):
        copy = self.copy(src, dst, slot, **to)
        self.started.append((copy, when))
        return copy

    def start(self, src, dst, slot, when=None, **to):
        copy = self.plan(src, dst, slot, when, **to)
        if when is None:
            copy.start()
        else:
            pl.when(when)(copy.start)
        return copy

    def finish(self):
        for copy, when in self.started:
            if when is None:
                copy.wait_send()
            else:
                pl.when(when)(copy.wait_send)

    def greet(self, dp_masks, seq_masks):
        barrier = pltpu.get_barrier_semaphore()
        for mask in dp_masks:
            pl.semaphore_signal(
                barrier, inc=1, device_id={"dp": self.dp_at(mask)}, device_id_type=MESH
            )
        for mask in seq_masks:
            pl.semaphore_signal(
                barrier, inc=1, device_id={"seq": self.seq_at(mask)}, device_id_type=MESH
            )
        pl.semaphore_wait(barrier, len(dp_masks) + len(seq_masks))

    def seq_at(self, mask):
        s = self.s
        for bit in range(2):
            if mask >> bit & 1:
                s = flip(s, bit)
        return s

    def dp_at(self, mask):
        d = self.d
        for bit in range(3):
            if mask >> bit & 1:
                d = flip(d, bit)
        return d


class Gather:
    def __init__(self, links, block):
        base = links.slots(8)
        self.copies = {}
        for r, mask in ((0, 1), (0, 2), (0, 4), (2, 1), (4, 2), (4, 1), (6, 1)):
            src = block(links.dp_at(r))
            self.copies[r | mask] = links.plan(src, src, base + (r | mask), dp=links.dp_at(mask))

    def got(self, r):
        self.copies[r].wait_recv()

    def first(self):
        for mask in (4, 2, 1):
            self.copies[mask].start()

    def relay(self, r):
        self.got(r)
        if r == 4:
            self.copies[6].start()
        self.copies[r | 1].start()

    def last(self):
        for r in (1, 3, 5, 7):
            self.got(r)


def first_kernel(
    heads,
    a_ref, c_ref, out_ref, down_ref, x_ref, g_ref, gains_ref, qg_ref, kg_ref, cos_ref, sin_ref,
    xr_ref, gr_ref, wa_ref, wc_ref, wo_ref, wd_ref, n_ref, qkv_ref, pre_ref, o_ref, log_ref, gain_ref,
    w_v, x_v, n_v, qkv_v, pre_v, o_v, got_v, send, recv, local,
):
    links = Links(send, recv)
    d, s = links.d, links.s
    sequences, piece, width = x_ref.shape
    blocks = xr_ref.shape[1]
    length = blocks * piece
    x_bit, core = bit_of(s, 1), bit_of(s, 0)
    z1, z0, y = bit_of(d, 2), bit_of(d, 1), bit_of(d, 0)
    place_of = lambda i: lax.rem((i & 1) + core, 2) * 2 + lax.rem((i >> 1) + x_bit, 2)
    local_used = [0]
    locals_ = {}

    def near(name, src, dst):
        copy = pltpu.make_async_copy(src, dst, local.at[local_used[0]])
        local_used[0] += 1
        copy.start()
        locals_[name] = copy

    links.greet((1, 2, 4), (1, 2, 3))

    def exchange(src, dst):
        base = links.slots(4)
        return [
            links.start(src.at[links.seq_at(k)], dst.at[d, s], base + k, seq=links.seq_at(k))
            for k in (2, 3, 1)
        ]

    gain_slots = links.slots(4)
    gain_own = [
        links.start(gains_ref, got_v.at[d, s], gain_slots + k, seq=links.seq_at(k)) for k in (2, 3, 1)
    ]
    got_v[d, s] = gains_ref[...]
    a_own = exchange(a_ref, wa_ref)
    near("a", a_ref.at[s], wa_ref.at[d, s])

    x_slots, g_slots = links.slots(3 * sequences), links.slots(3 * sequences)

    def spread(own, everywhere, base, n):
        copies = [
            links.start(own.at[n], everywhere.at[n, k], base + 3 * n + k - 1, seq=links.seq_at(3 - k))
            for k in (1, 2)
        ]
        onward = links.plan(everywhere.at[n, 1], everywhere.at[n, 3], base + 3 * n + 2, seq=links.seq_at(1))
        return copies + [onward]

    def pass_on(copies):
        copies[0].wait_recv()
        copies[2].start()

    x_copies = [spread(x_ref, xr_ref, x_slots, 0)]
    c_own = exchange(c_ref, wc_ref)
    near("c", c_ref.at[s], wc_ref.at[d, s])
    for n in range(sequences):
        near(f"x{n}", x_ref.at[n], xr_ref.at[n, 0])
    near("d", down_ref, wd_ref.at[d])

    across, beside = lax.rem(x_bit + y, 2), lax.rem(core + z0, 2)
    out_slots = links.slots(7)
    holder = (across == 0) & (beside == 0)
    out_first = [
        links.start(
            out_ref, wo_ref.at[z1, s], out_slots + k,
            when=(across == k >> 1) & (beside == (k & 1)), seq=links.seq_at(k),
        )
        for k in (1, 2, 3)
    ]
    x_copies += [spread(x_ref, xr_ref, x_slots, n) for n in range(1, sequences)]

    for copy in gain_own + a_own:
        copy.wait_recv()
    locals_["a"].wait()
    gather_a, gather_c, gather_d, gather_gain = (
        Gather(links, lambda at, ref=ref: ref.at[at]) for ref in (wa_ref, wc_ref, wd_ref, got_v)
    )
    gather_gain.first()
    gather_a.first()
    for r in (2, 4, 6):
        gather_gain.relay(r)

    pass_on(x_copies[0])

    @pl.when(holder)
    def _():
        own = pltpu.make_async_copy(out_ref, wo_ref.at[z1, s], local.at[local_used[0]])
        own.start()
        for copy in out_first:
            copy.wait_recv()
        own.wait()

    local_used[0] += 1
    gather_a.relay(2)
    gather_a.relay(4)
    gather_a.relay(6)
    out_y = links.start(wo_ref.at[z1], wo_ref.at[z1], out_slots + 4, when=holder, dp=flip(d, 0))
    for copy in c_own:
        copy.wait_recv()
    locals_["c"].wait()
    gather_c.first()
    g_copies = [spread(g_ref, gr_ref, g_slots, n) for n in range(sequences)]
    for n in range(sequences):
        near(f"g{n}", g_ref.at[n], gr_ref.at[n, 0])
    locals_["d"].wait()
    gather_d.first()

    def wait_x(n):
        locals_[f"x{n}"].wait()
        for copy in x_copies[n][1:]:
            copy.wait_recv()
        near(f"xv{n}", xr_ref.at[n], x_v)
        locals_[f"xv{n}"].wait()

    def project_part(n, meanwhile=()):
        def step(i, carry):
            for k, action in enumerate(meanwhile):
                pl.when(i == k)(action)
            at = place_of(i)
            x = x_v[at].astype(F32)
            normed = (x * rms_scale(x) * gain_ref[0:1, :]).astype(BF16)
            n_v[n, at] = normed
            y_rows = dot(normed, w_v[...].reshape(width, -1))
            rows = pl.ds(pl.multiple_of(i * piece, piece), piece)
            cosine, sine = cos_ref[rows, :], sin_ref[rows, :]
            for j in range(heads // 2):
                for part in range(4):
                    cut = slice((4 * j + part) * HEAD_SIZE, (4 * j + part + 1) * HEAD_SIZE)
                    head = y_rows[:, cut]
                    if part < 3:
                        pre_v[n, rows, (3 * j + part) * HEAD_SIZE : (3 * j + part + 1) * HEAD_SIZE] = head
                        gain = qg_ref[...] if part < 2 else kg_ref[...]
                        head = head * rms_scale(head) * gain
                        head = head * cosine + pltpu.roll(head, HEAD_SIZE // 2, 1) * sine
                    qkv_v[n, rows, cut] = head.astype(BF16)
            return carry

        lax.fori_loop(0, blocks, step, 0)
        near(f"n{n}", n_v.at[n], n_ref.at[n])
        near(f"qkv{n}", qkv_v.at[n], qkv_ref.at[n])
        near(f"pre{n}", pre_v.at[n], pre_ref.at[n])

    def attend_part(n, meanwhile=()):
        def step(h, carry):
            for k, action in enumerate(meanwhile):
                pl.when(h == k)(action)
            j, g = lax.div(h, 2), lax.rem(h, 2)
            lanes = lambda at: pl.ds(pl.multiple_of(at * HEAD_SIZE, HEAD_SIZE), HEAD_SIZE)
            values_t = qkv_v[n, :, lanes(4 * j + 3)].T
            keys = qkv_v.at[n, :, lanes(4 * j + 2)]
            for i in range(blocks):
                query = qkv_v[n, i * piece : (i + 1) * piece, lanes(4 * j + g)]
                exponent, highest = masked_exp(keys, query, i, piece, None)
                total = jnp.sum(exponent, axis=0, keepdims=True)
                probs = (exponent * (1.0 / total)).astype(BF16)
                mixed = dot(values_t[:, : (i + 1) * piece], probs)
                o_v[n, place_of(i), :, lanes(h)] = mixed.T.astype(BF16)
                log_ref[n, h, :, i * piece : (i + 1) * piece] = highest + jnp.log(total)
            return carry

        lax.fori_loop(0, heads, step, 0)

    wait_x(0)
    gather_a.last()
    near("w", wa_ref, w_v)
    locals_["w"].wait()

    gather_gain.last()
    for at in range(got_v.shape[0]):
        gain_ref[:, at * 128 : (at + 1) * 128] = jnp.sum(got_v[at], axis=0)

    out_z1 = links.plan(wo_ref.at[z1], wo_ref.at[z1], out_slots + 5, when=beside == 0, dp=flip(d, 2))
    out_z0 = links.plan(wo_ref, wo_ref, out_slots + 6, when=beside == 0, dp=flip(d, 1))

    def out_next():
        pl.when((across == 1) & (beside == 0))(out_y.wait_recv)
        pl.when(beside == 0)(out_z1.start)

    def out_last():
        @pl.when(beside == 0)
        def _():
            out_z1.wait_recv()
            out_z0.start()

    nothing = lambda: None
    project_part(0, [out_next, lambda: gather_c.relay(2), lambda: pass_on(x_copies[1]), lambda: gather_c.relay(4)])
    attend_part(0, [nothing, out_last, lambda: gather_c.relay(6), lambda: gather_d.relay(2)])
    near("o0", o_v.at[0], o_ref.at[0])
    for n in range(1, sequences):
        wait_x(n)
        project_part(n, [lambda: gather_d.relay(4), nothing, lambda: pass_on(g_copies[0])])
        attend_part(n, [lambda: gather_d.relay(6), lambda: pass_on(g_copies[1])])
        near(f"o{n}", o_v.at[n], o_ref.at[n])
    gather_c.last()
    gather_d.last()
    pl.when(beside == 1)(out_z0.wait_recv)
    for pair in g_copies:
        for copy in pair[1:]:
            copy.wait_recv()
    for n in range(sequences):
        for name in ("g", "n", "qkv", "pre", "o"):
            locals_[f"{name}{n}"].wait()
    links.finish()


def first(a, c, w_out, w_down, x, g, gains, query_gain, key_gain, cosine, sine, dp, heads):
    blocks, rows, columns = a.shape
    sequences, piece, width = x.shape
    length = blocks * piece
    hbm = pl.BlockSpec(memory_space=pl.ANY)
    vmem = pl.BlockSpec(memory_space=pltpu.VMEM)
    shape = jax.ShapeDtypeStruct
    pre_columns = columns // 4 * 3
    slots = 96
    return pl.pallas_call(
        functools.partial(first_kernel, heads),
        name="first",
        out_shape=(
            shape((sequences, blocks, piece, width), BF16),
            shape((sequences, blocks, piece, width), BF16),
            shape((dp, blocks, rows, columns), BF16),
            shape((dp, blocks, rows, c.shape[2]), BF16),
            shape((2, blocks) + w_out.shape, BF16),
            shape((dp,) + w_down.shape, BF16),
            shape((sequences, blocks, piece, width), BF16),
            shape((sequences, length, columns), BF16),
            shape((sequences, length, pre_columns), F32),
            shape((sequences, blocks, piece, heads * HEAD_SIZE), BF16),
            shape((sequences, heads, 1, length), F32),
            shape((8, width), F32),
        ),
        in_specs=[vmem] * 11,
        out_specs=[hbm] * 10 + [vmem] * 2,
        scratch_shapes=[
            pltpu.VMEM((dp, blocks, rows, columns), BF16),
            pltpu.VMEM((blocks, piece, width), BF16),
            pltpu.VMEM((sequences, blocks, piece, width), BF16),
            pltpu.VMEM((sequences, length, columns), BF16),
            pltpu.VMEM((sequences, length, pre_columns), F32),
            pltpu.VMEM((sequences, blocks, piece, heads * HEAD_SIZE), BF16),
            pltpu.VMEM((dp, blocks, 8, width // dp), F32),
            pltpu.SemaphoreType.DMA((slots,)),
            pltpu.SemaphoreType.DMA((slots,)),
            pltpu.SemaphoreType.DMA((24,)),
        ],
        compiler_params=pltpu.CompilerParams(
            collective_id=0, has_side_effects=True, vmem_limit_bytes=60 * 1024 * 1024
        ),
    )(a, c, w_out, w_down, x, g, gains, query_gain, key_gain, cosine, sine)


def body(
    hidden_in,
    attn_gain,
    w_query,
    key_weight,
    value_weight,
    query_gain,
    key_gain,
    w_out,
    mlp_gain,
    w_gate,
    w_up,
    w_down,
    cotangent,
):
    wires = Wires(lax.axis_size("dp"), lax.axis_size("seq"))
    dp, seq, x_count = wires.dp, wires.seq, wires.x_count
    count = wires.count
    sequences, piece, width = hidden_in.shape
    length = seq * piece
    part = x_count * piece
    heads_kv = key_weight.shape[1] // HEAD_SIZE
    s_index = wires.s.reshape(1).astype(jnp.int32)
    cosine, sine = rope_tables(length)
    query_gain_row = query_gain.astype(F32).reshape(1, -1)
    key_gain_row = key_gain.astype(F32).reshape(1, -1)

    index = wires.d * seq + wires.s
    own_gains = jnp.stack([attn_gain, mlp_gain])
    rows = w_query.shape[0]
    by_head = jnp.concatenate(
        [
            w_query.reshape(rows, heads_kv, -1),
            key_weight.reshape(rows, heads_kv, -1),
            value_weight.reshape(rows, heads_kv, -1),
        ],
        axis=2,
    )
    order = [wires.heads_of(t, heads_kv) for t in range(seq)]
    package_in = jnp.stack(
        [jnp.concatenate([by_head[:, j] for j in order[t]], axis=1) for t in range(seq)]
    )
    down_rows = w_down.shape[0]

    def by_unit(w):
        return w.reshape(rows, dp, seq, down_rows).transpose(2, 0, 1, 3).reshape(seq, rows, -1)

    units = dp * down_rows
    package_mlp = jnp.concatenate([by_unit(w_gate), by_unit(w_up)], axis=2)

    fused = (dp, seq) == (8, 4) and width == 128 * dp and rows % 16 == 0 and down_rows % 16 == 0
    if fused:
        gains = jnp.zeros((8, seq, width // count), F32)
        gains = lax.dynamic_update_slice(gains, own_gains.astype(F32)[:, None], (0, wires.s, 0))
        (
            x_rel, g_rel, w_in, w_mlp, w_o, w_d, all_normed, all_qkv, all_pre, all_mixed, all_log, gains
        ) = first(
            package_in, package_mlp, w_out, w_down, hidden_in, cotangent, gains.reshape(8, -1),
            query_gain_row, key_gain_row, cosine, sine, dp, 2 * heads_kv // seq,
        )
        w_in, w_mlp = w_in.reshape(width, -1), w_mlp.reshape(width, -1)
        w_o, w_d = w_o.reshape(-1, width), w_d.reshape(units, width)
        attn_gain_row, mlp_gain_row = gains[:1], gains[1:2]
    else:
        gains = jnp.zeros((2, count, width // count), BF16)
        gains = lax.dynamic_update_slice(gains, own_gains[:, None], (0, index, 0))
        gains = wires.sum_all(gains.reshape(2, width)).astype(F32)
        attn_gain_row, mlp_gain_row = gains[:1], gains[1:]
        package = wires.exchange_seq(package_in).reshape(seq * rows, -1)
        w_in = wires.gather_dp(package).reshape(width, -1)
        x_rel = jnp.stack(wires.gather_seq_relative(hidden_in), axis=1)
        w_o = wires.gather_out(w_out, heads_kv)
        package = wires.exchange_seq(package_mlp).reshape(seq * rows, -1)
        w_mlp = wires.gather_dp(package).reshape(width, -1)
        g_rel = jnp.stack(wires.gather_seq_relative(cotangent), axis=1)
        w_d = wires.gather_dp(w_down).reshape(units, width)

    kept = []
    outs = []
    for n in range(sequences):
        if fused:
            normed, qkv, pre = all_normed[n], all_qkv[n], all_pre[n]
            mixed, log_total = all_mixed[n], all_log[n]
        else:
            normed, qkv, pre = project(
                s_index, x_rel[n], w_in, attn_gain_row, query_gain_row, key_gain_row, cosine, sine, x_count
            )
            mixed, log_total = attend(s_index, qkv, seq, x_count)
        mixed_rows = mixed.reshape(length, -1)
        other = wires.swap(dot(mixed_rows[part:], w_o).astype(BF16), 1)
        total = wires.sum_x(dot(mixed_rows[:part], w_o) + other.astype(F32))
        residual = total + x_rel[n].reshape(length, width)[:part].astype(F32)
        scale = rms_scale(residual)
        normed_mlp = (residual * scale * mlp_gain_row).astype(BF16)
        normed_mlp = jnp.concatenate([normed_mlp, wires.swap(normed_mlp, 1)], axis=0)
        both = dot(normed_mlp, w_mlp)
        gate, upward = both[:, :units], both[:, units:]
        sigmoid = jax.nn.sigmoid(gate)
        silu = gate * sigmoid
        hidden = (silu * upward).astype(BF16)
        other = wires.swap(dot(hidden[part:], w_d).astype(BF16), 1)
        total = wires.scatter_x(dot(hidden[:part], w_d) + other.astype(F32))
        outs.append((residual[:piece] + total).astype(BF16))

        grad_top = g_rel[n].reshape(length, width)
        grad_hidden = dot_t(grad_top, w_d)
        grad_gate = (grad_hidden * upward * sigmoid * (1.0 + gate * (1.0 - sigmoid))).astype(BF16)
        grad_upward = (grad_hidden * silu).astype(BF16)
        grad_both = jnp.concatenate([grad_gate, grad_upward], axis=1)
        other = wires.swap(dot_t(grad_both[part:], w_mlp).astype(BF16), 1)
        grad_normed = wires.sum_x(dot_t(grad_both[:part], w_mlp) + other.astype(F32))
        scaled = grad_normed * mlp_gain_row
        grad_residual = (
            grad_top[:part].astype(F32)
            + scale * scaled
            - residual * (scale * scale * scale * jnp.mean(scaled * residual, axis=-1, keepdims=True))
        )
        grad_mlp_gain = jnp.sum((grad_normed * residual * scale)[:piece], axis=0)
        branch = grad_residual.astype(BF16)
        branch = jnp.concatenate([branch, wires.swap(branch, 1)], axis=0)
        grad_mixed = dot_t(branch, w_o).astype(BF16).reshape(mixed.shape)
        grad_qkv, grad_query_gain, grad_key_gain = attend_back(
            s_index, qkv, pre, log_total, grad_mixed, query_gain_row, key_gain_row, cosine, sine, seq, x_count
        )
        grad_rows = grad_qkv.reshape(length, -1)
        other = wires.swap(dot_t(grad_rows[part:], w_in).astype(BF16), 1)
        grad_first = wires.scatter_x(dot_t(grad_rows[:part], w_in) + other.astype(F32))
        tokens = hidden_in[n].astype(F32)
        scale = rms_scale(tokens)
        scaled = grad_first * attn_gain_row
        grad_tokens = (
            grad_residual[:piece]
            + scale * scaled
            - tokens * (scale * scale * scale * jnp.mean(scaled * tokens, axis=-1, keepdims=True))
        )
        grad_attn_gain = jnp.sum(grad_first * tokens * scale, axis=0)
        kept.append(
            dict(
                normed=normed.reshape(length, width),
                mixed=mixed_rows,
                normed_mlp=normed_mlp,
                hidden=hidden,
                grad_both=grad_both,
                branch=branch,
                grad_rows=grad_rows,
                grad_tokens=grad_tokens,
                gains=jnp.concatenate(
                    [grad_attn_gain, grad_mlp_gain, grad_query_gain[0], grad_key_gain[0]]
                ),
            )
        )

    def over(name):
        return jnp.concatenate([k[name] for k in kept], axis=0)

    grad_down = t_dot(over("hidden"), g_rel.reshape(-1, width)).astype(BF16)
    grad_down = wires.scatter_dp(grad_down.reshape(dp, down_rows, width)).astype(F32)

    grad_mlp = t_dot(over("normed_mlp"), over("grad_both")).astype(BF16)
    grad_mlp = wires.scatter_dp(grad_mlp.reshape(dp, seq * rows, -1))
    grad_mlp = wires.exchange_seq(grad_mlp.reshape(seq, rows, -1)).astype(F32)

    def from_unit(g):
        return g.reshape(seq, rows, dp, down_rows).transpose(1, 2, 0, 3).reshape(rows, -1)

    grad_gate, grad_up = from_unit(grad_mlp[..., :units]), from_unit(grad_mlp[..., units:])

    grad_out = t_dot(over("mixed"), over("branch")).astype(BF16)
    grad_out = wires.scatter_out(grad_out, heads_kv).astype(F32)

    grad_in = t_dot(over("normed"), over("grad_rows")).astype(BF16)
    grad_in = wires.scatter_dp(grad_in.reshape(dp, seq * rows, -1))
    grad_in = wires.exchange_seq(grad_in.reshape(seq, rows, -1)).astype(F32)
    pieces = [None] * heads_kv
    for t in range(seq):
        for m, j in enumerate(order[t]):
            pieces[j] = grad_in[t, :, m * 4 * HEAD_SIZE : (m + 1) * 4 * HEAD_SIZE]
    grad_query = jnp.concatenate([p[:, : 2 * HEAD_SIZE] for p in pieces], axis=1)
    grad_key = jnp.concatenate([p[:, 2 * HEAD_SIZE : 3 * HEAD_SIZE] for p in pieces], axis=1)
    grad_value = jnp.concatenate([p[:, 3 * HEAD_SIZE :] for p in pieces], axis=1)

    gain_sums = wires.sum_all(sum(k["gains"] for k in kept))
    own = width // count
    grad_attn_gain = lax.dynamic_slice_in_dim(gain_sums, index * own, own)
    grad_mlp_gain = lax.dynamic_slice_in_dim(gain_sums, width + index * own, own)
    return (
        jnp.stack(outs),
        jnp.stack([k["grad_tokens"] for k in kept]),
        grad_attn_gain,
        grad_query,
        grad_key,
        grad_value,
        gain_sums[2 * width : 2 * width + HEAD_SIZE],
        gain_sums[2 * width + HEAD_SIZE :],
        grad_out,
        grad_mlp_gain,
        grad_gate,
        grad_up,
        grad_down,
    )


def solution(mesh):
    rows = P(("dp", "seq"), None)
    line = P(("dp", "seq"))
    tokens = P("dp", "seq", None)
    return jax.shard_map(
        body,
        mesh=mesh,
        in_specs=(tokens, line, rows, rows, rows, P(), P(), rows, line, rows, rows, rows, tokens),
        out_specs=(tokens, tokens, line, rows, rows, rows, P(), P(), rows, line, rows, rows, rows),
        check_vma=False,
    )
```

```python
import functools

import jax
import jax.numpy as jnp
from jax import lax
from jax.experimental import pallas as pl
from jax.experimental.pallas import tpu as pltpu
from jax.sharding import PartitionSpec as P

HEAD_SIZE = 128
EPS = 1e-06
ROPE_THETA = 1000000.0
AXES = ("dp", "seq")
SCALE = HEAD_SIZE ** (-0.5)
F32 = jnp.float32
BF16 = jnp.bfloat16


def log2(n):
    return n.bit_length() - 1


class Wires:
    def __init__(self, dp, seq):
        self.dp, self.seq, self.count = dp, seq, dp * seq
        self.dp_bits, self.seq_bits = log2(dp), log2(seq)
        self.x_count = seq // 2
        y_bits = min(log2(self.x_count), self.dp_bits)
        self.dp_order = list(range(y_bits, self.dp_bits)) + list(range(y_bits))
        self.x_bits = list(range(1, self.seq_bits))
        self.d = lax.axis_index("dp")
        self.s = lax.axis_index("seq")

    def swap(self, value, mask, only=None):
        pairs = [(i, i ^ mask) for i in range(self.count) if only is None or only(i)]
        return lax.ppermute(value, AXES, pairs)

    def dp_swap(self, value, bit, only=None):
        return self.swap(value, (1 << bit) * self.seq, only)

    def bit_d(self, bit):
        return (self.d >> bit) & 1

    def bit_s(self, bit):
        return (self.s >> bit) & 1

    def gather_dp(self, shard):
        pieces = {0: shard}
        for bit in self.dp_order:
            pieces.update({r | (1 << bit): self.dp_swap(v, bit) for r, v in list(pieces.items())})
        full = jnp.zeros((self.dp,) + shard.shape, shard.dtype)
        for r, v in pieces.items():
            full = lax.dynamic_update_index_in_dim(full, v, self.d ^ r, 0)
        return full

    def scatter_dp(self, value):
        rest = value.shape[1:]
        held = list(range(self.dp_bits - 1, -1, -1))
        value = value.reshape((2,) * self.dp_bits + rest)
        for bit in reversed(self.dp_order):
            axis = held.index(bit)
            held.pop(axis)
            mine = lax.dynamic_index_in_dim(value, self.bit_d(bit), axis, keepdims=False)
            other = lax.dynamic_index_in_dim(value, 1 - self.bit_d(bit), axis, keepdims=False)
            got = self.dp_swap(other, bit)
            value = (mine.astype(F32) + got.astype(F32)).astype(BF16)
        return value

    def exchange_seq(self, value):
        rest = value.shape[1:]
        for bit in self.x_bits + [0]:
            value = value.reshape((self.seq >> (bit + 1), 2, 1 << bit) + rest)
            me = self.bit_s(bit)
            mine = lax.dynamic_index_in_dim(value, me, 1, keepdims=False)
            other = lax.dynamic_index_in_dim(value, 1 - me, 1, keepdims=False)
            got = self.swap(other, 1 << bit)
            low = jnp.where(me == 0, mine, got)
            high = jnp.where(me == 0, got, mine)
            value = jnp.stack([low, high], axis=1).reshape((self.seq,) + rest)
        return value

    def gather_seq_relative(self, value):
        pieces = [value]
        for bit in self.x_bits:
            pieces = pieces + [self.swap(v, 1 << bit) for v in pieces]
        return pieces + [self.swap(v, 1) for v in pieces]

    def sum_x(self, value):
        n = self.x_count
        shape = value.shape
        for bit in self.x_bits:
            got = self.swap(value.astype(BF16), 1 << bit).astype(F32)
            blocks = got.reshape((n, shape[0] // n) + shape[1:])
            flip = [i ^ (1 << (bit - 1)) for i in range(n)]
            value = value + jnp.concatenate([blocks[i] for i in flip], axis=0)
        return value

    def scatter_x(self, value):
        n = self.x_count
        for bit in reversed(self.x_bits):
            half = value.shape[0] // 2
            got = self.swap(value[half:].astype(BF16), 1 << bit)
            value = value[:half] + got.astype(F32)
        return value

    def sum_all(self, value):
        for bit in range(log2(self.count)):
            value = value + self.swap(value, 1 << bit)
        return value

    def head_bits(self, heads_kv):
        low = self.dp_bits - log2(heads_kv)
        partner = {0: 1, 1: 0, 2: 2}
        matched = [(low + k, partner[k]) for k in range(self.seq_bits)]
        free = [low + k for k in range(self.seq_bits, log2(heads_kv))]
        return low, matched, free

    def heads_of(self, t, heads_kv):
        low, matched, free = self.head_bits(heads_kv)
        heads = [0]
        for bit, tbit in matched:
            heads = [h | (((t >> tbit) & 1) << (bit - low)) for h in heads]
        for bit in free:
            heads = heads + [h | (1 << (bit - low)) for h in heads]
        return heads

    def matches(self, i, pairs):
        return all(((i // self.seq) >> b) & 1 == (i >> t) & 1 for b, t in pairs)

    def gather_out(self, shard, heads_kv):
        low, matched, free = self.head_bits(heads_kv)
        value = shard
        for bit in self.x_bits + [0]:
            pass
        value = shard[None]
        for bit in [0] + self.x_bits:
            got = self.swap(value, 1 << bit)
            value = self.ordered(value, got, self.bit_s(bit))
        for bit in range(low):
            got = self.dp_swap(value, bit)
            value = self.ordered(value, got, self.bit_d(bit))
        for n, (bit, tbit) in enumerate(matched):
            got = self.dp_swap(value, bit, lambda i: self.matches(i, matched[n:]))
            value = jnp.where(self.bit_d(bit) == self.bit_s(tbit), value, got)
        for bit in free:
            got = self.dp_swap(value, bit)
            value = self.ordered(value, got, self.bit_d(bit))
        return value.reshape((-1,) + shard.shape[1:])

    def ordered(self, own, got, bit):
        return jnp.concatenate(
            [jnp.where(bit == 0, own, got), jnp.where(bit == 0, got, own)], axis=0
        )

    def halves(self, value, bit):
        half = value.shape[0] // 2
        mine = lax.dynamic_slice_in_dim(value, bit * half, half, 0)
        other = lax.dynamic_slice_in_dim(value, (1 - bit) * half, half, 0)
        return mine, other

    def scatter_out(self, value, heads_kv):
        low, matched, free = self.head_bits(heads_kv)
        for bit in reversed(free):
            mine, other = self.halves(value, self.bit_d(bit))
            got = self.dp_swap(other, bit)
            value = (mine.astype(F32) + got.astype(F32)).astype(BF16)
        for n in reversed(range(len(matched))):
            bit, tbit = matched[n]
            got = self.dp_swap(
                value,
                bit,
                lambda i: self.matches(i, matched[n + 1 :]) and not self.matches(i, [matched[n]]),
            )
            value = (value.astype(F32) + got.astype(F32)).astype(BF16)
        for bit in reversed(range(low)):
            mine, other = self.halves(value, self.bit_d(bit))
            got = self.dp_swap(other, bit, lambda i: self.matches(i, matched))
            value = (mine.astype(F32) + got.astype(F32)).astype(BF16)
        todo = dict((tbit, bit) for bit, tbit in matched)
        for tbit in reversed(self.x_bits):
            value = self.hand_out(value, tbit, todo)
        return self.hand_out(value, 0, todo)

    def hand_out(self, value, tbit, todo):
        bit = todo.pop(tbit)
        left = [(b, t) for t, b in todo.items()]
        mine, other = self.halves(value, self.bit_s(tbit))
        got = self.swap(
            other, 1 << tbit, lambda i: self.matches(i, left) and self.matches(i, [(bit, tbit)])
        )
        return jnp.where(self.bit_d(bit) == self.bit_s(tbit), mine, got)


def dot(a, b):
    return lax.dot_general(a, b, (((1,), (0,)), ((), ())), preferred_element_type=F32)


def dot_t(a, b):
    return lax.dot_general(a, b, (((1,), (1,)), ((), ())), preferred_element_type=F32)


def t_dot(a, b):
    return lax.dot_general(a, b, (((0,), (0,)), ((), ())), preferred_element_type=F32)


def rms_scale(rows):
    return lax.rsqrt(jnp.mean(rows * rows, axis=-1, keepdims=True) + EPS)


def rope_tables(length):
    halfway = HEAD_SIZE // 2
    inverse = jnp.power(F32(ROPE_THETA), -(jnp.arange(halfway).astype(F32) * 2.0) / HEAD_SIZE)
    angles = jnp.arange(length).astype(F32)[:, None] * inverse[None, :]
    cosine, sine = jnp.cos(angles), jnp.sin(angles)
    return (
        jnp.concatenate([cosine, cosine], axis=-1),
        jnp.concatenate([-sine, sine], axis=-1),
    )


def place(block, s, x_count):
    return ((block & 1) ^ (s & 1)) * x_count + ((block >> 1) ^ (s >> 1))


def project_kernel(s_ref, x_ref, w_ref, gain_ref, qg_ref, kg_ref, cos_ref, sin_ref, n_ref, qkv_ref, pre_ref):
    x = x_ref[0].astype(F32)
    normed = (x * rms_scale(x) * gain_ref[...]).astype(BF16)
    n_ref[0] = normed
    y = dot(normed, w_ref[...])
    cosine, sine = cos_ref[...], sin_ref[...]
    for j in range(y.shape[1] // (4 * HEAD_SIZE)):
        for part in range(4):
            at = slice((4 * j + part) * HEAD_SIZE, (4 * j + part + 1) * HEAD_SIZE)
            head = y[:, at]
            if part < 3:
                pre_ref[:, (3 * j + part) * HEAD_SIZE : (3 * j + part + 1) * HEAD_SIZE] = head
                gain = qg_ref[...] if part < 2 else kg_ref[...]
                head = head * rms_scale(head) * gain
                head = head * cosine + pltpu.roll(head, HEAD_SIZE // 2, 1) * sine
            qkv_ref[:, at] = head.astype(BF16)


def project(s, x_rel, w, gain, query_gain, key_gain, cosine, sine, x_count):
    blocks, piece, width = x_rel.shape
    length, columns = blocks * piece, w.shape[1]
    heads = columns // (4 * HEAD_SIZE)
    whole = lambda shape: pl.BlockSpec(shape, lambda i, s_ref: (0,) * len(shape))
    rel = pl.BlockSpec((1, piece, width), lambda i, s_ref: (place(i, s_ref[0], x_count), 0, 0))
    table = pl.BlockSpec((piece, HEAD_SIZE), lambda i, s_ref: (i, 0))
    return pl.pallas_call(
        project_kernel,
        name="project",
        out_shape=(
            jax.ShapeDtypeStruct((blocks, piece, width), BF16),
            jax.ShapeDtypeStruct((length, columns), BF16),
            jax.ShapeDtypeStruct((length, 3 * heads * HEAD_SIZE), F32),
        ),
        grid_spec=pltpu.PrefetchScalarGridSpec(
            num_scalar_prefetch=1,
            grid=(blocks,),
            in_specs=[
                rel,
                whole(w.shape),
                whole((1, width)),
                whole((1, HEAD_SIZE)),
                whole((1, HEAD_SIZE)),
                table,
                table,
            ],
            out_specs=[
                rel,
                pl.BlockSpec((piece, columns), lambda i, s_ref: (i, 0)),
                pl.BlockSpec((piece, 3 * heads * HEAD_SIZE), lambda i, s_ref: (i, 0)),
            ],
        ),
        cost_estimate=pl.CostEstimate(
            flops=2 * length * width * columns,
            bytes_accessed=2 * (2 * length * width + width * columns + 4 * length * columns),
            transcendentals=0,
        ),
    )(s, x_rel, w, gain, query_gain, key_gain, cosine, sine)


def masked_exp(k_ref, query, i, piece, offset):
    diagonal = dot_t(k_ref[i * piece : (i + 1) * piece, :], query) * SCALE
    key_at = lax.broadcasted_iota(jnp.int32, (piece, piece), 0)
    query_at = lax.broadcasted_iota(jnp.int32, (piece, piece), 1)
    diagonal = jnp.where(key_at <= query_at, diagonal, -jnp.inf)
    if i == 0:
        scores = diagonal
    else:
        scores = jnp.concatenate(
            [dot_t(k_ref[: i * piece, :], query) * SCALE, diagonal], axis=0
        )
    if offset is None:
        offset = jnp.max(scores, axis=0, keepdims=True)
    return jnp.exp(scores - offset), offset


def forward_kernel(blocks, x_count, s_ref, q_ref, k_ref, v_ref, o_ref, log_ref):
    piece = q_ref.shape[0] // blocks
    values_t = v_ref[...].T
    for i in range(blocks):
        query = q_ref[i * piece : (i + 1) * piece, :]
        exponent, highest = masked_exp(k_ref, query, i, piece, None)
        total = jnp.sum(exponent, axis=0, keepdims=True)
        probs = (exponent * (1.0 / total)).astype(BF16)
        mixed = dot(values_t[:, : (i + 1) * piece], probs)
        o_ref[place(i, s_ref[0], x_count)] = mixed.T.astype(BF16)
        log_ref[0, :, i * piece : (i + 1) * piece] = highest + jnp.log(total)


def attend(s, qkv, blocks, x_count):
    length, columns = qkv.shape
    heads = columns // (2 * HEAD_SIZE)
    piece = length // blocks
    head = lambda part: pl.BlockSpec(
        (length, HEAD_SIZE), lambda h, s_ref: (0, 4 * (h // 2) + (h % 2 if part == 0 else part))
    )
    return pl.pallas_call(
        functools.partial(forward_kernel, blocks, x_count),
        name="attend",
        out_shape=(
            jax.ShapeDtypeStruct((blocks, piece, heads * HEAD_SIZE), BF16),
            jax.ShapeDtypeStruct((heads, 1, length), F32),
        ),
        grid_spec=pltpu.PrefetchScalarGridSpec(
            num_scalar_prefetch=1,
            grid=(heads,),
            in_specs=[head(0), head(2), head(3)],
            out_specs=[
                pl.BlockSpec((blocks, piece, HEAD_SIZE), lambda h, s_ref: (0, 0, h)),
                pl.BlockSpec((1, 1, length), lambda h, s_ref: (h, 0, 0)),
            ],
        ),
        cost_estimate=pl.CostEstimate(
            flops=2 * heads * length * length * HEAD_SIZE * 2,
            bytes_accessed=2 * heads * length * HEAD_SIZE * 4,
            transcendentals=heads * length * length // 2,
        ),
    )(s, qkv, qkv, qkv)


def head_back(grad, pre, gain, cosine, sine):
    turned = grad * cosine - pltpu.roll(grad, HEAD_SIZE // 2, 1) * sine
    scale = rms_scale(pre)
    part = turned * gain
    result = scale * part - pre * (scale * scale * scale * jnp.mean(part * pre, axis=-1, keepdims=True))
    return result, jnp.sum(turned * pre * scale, axis=0, keepdims=True)


def backward_kernel(
    blocks, x_count, s_ref, q_ref, k_ref, v_ref, do_ref, log_ref, qp_ref, kp_ref, qg_ref, kg_ref,
    cos_ref, sin_ref, grad_ref, qgain_ref, kgain_ref, dk_ref, dv_ref,
):
    piece = q_ref.shape[0] // blocks
    second = pl.program_id(1)

    @pl.when((pl.program_id(0) == 0) & (second == 0))
    def _():
        qgain_ref[...] = jnp.zeros_like(qgain_ref)
        kgain_ref[...] = jnp.zeros_like(kgain_ref)

    @pl.when(second == 0)
    def _():
        dk_ref[...] = jnp.zeros_like(dk_ref)
        dv_ref[...] = jnp.zeros_like(dv_ref)

    keys_t = k_ref[...].T
    column = pl.ds(pl.multiple_of(second * HEAD_SIZE, HEAD_SIZE), HEAD_SIZE)
    for i in range(blocks):
        rows = slice(i * piece, (i + 1) * piece)
        end = (i + 1) * piece
        at = place(i, s_ref[0], x_count)
        query = q_ref[rows, :]
        grad_out = do_ref[at]
        probs, _ = masked_exp(k_ref, query, i, piece, log_ref[0, :, rows])
        dv_ref[:end, :] += dot(probs.astype(BF16), grad_out)
        grad_probs = dot_t(v_ref[:end, :], grad_out)
        inner = jnp.sum(probs * grad_probs, axis=0, keepdims=True)
        grad_scores = (probs * (grad_probs - inner)).astype(BF16)
        dk_ref[:end, :] += dot(grad_scores, query)
        grad_query = dot(keys_t[:, :end], grad_scores).T * SCALE
        result, gain = head_back(grad_query, qp_ref[rows, :], qg_ref[...], cos_ref[rows, :], sin_ref[rows, :])
        grad_ref[at, :, column] = result.astype(BF16)
        qgain_ref[...] += gain

    @pl.when(second == 1)
    def _():
        for i in range(blocks):
            rows = slice(i * piece, (i + 1) * piece)
            at = place(i, s_ref[0], x_count)
            result, gain = head_back(
                dk_ref[rows, :] * SCALE, kp_ref[rows, :], kg_ref[...], cos_ref[rows, :], sin_ref[rows, :]
            )
            grad_ref[at, :, 2 * HEAD_SIZE : 3 * HEAD_SIZE] = result.astype(BF16)
            grad_ref[at, :, 3 * HEAD_SIZE :] = dv_ref[rows, :].astype(BF16)
            kgain_ref[...] += gain


def attend_back(s, qkv, pre, log_total, grad_mixed, query_gain, key_gain, cosine, sine, blocks, x_count):
    length, columns = qkv.shape
    heads_kv = columns // (4 * HEAD_SIZE)
    piece = length // blocks
    head = lambda part: pl.BlockSpec(
        (length, HEAD_SIZE), lambda j, g, s_ref: (0, 4 * j + (g if part == 0 else part))
    )
    pre_head = lambda part: pl.BlockSpec(
        (length, HEAD_SIZE), lambda j, g, s_ref: (0, 3 * j + (g if part == 0 else part))
    )
    whole = lambda shape: pl.BlockSpec(shape, lambda j, g, s_ref: (0,) * len(shape))
    return pl.pallas_call(
        functools.partial(backward_kernel, blocks, x_count),
        name="attend_back",
        out_shape=(
            jax.ShapeDtypeStruct((blocks, piece, columns), BF16),
            jax.ShapeDtypeStruct((1, HEAD_SIZE), F32),
            jax.ShapeDtypeStruct((1, HEAD_SIZE), F32),
        ),
        grid_spec=pltpu.PrefetchScalarGridSpec(
            num_scalar_prefetch=1,
            grid=(heads_kv, 2),
            in_specs=[
                head(0),
                head(2),
                head(3),
                pl.BlockSpec((blocks, piece, HEAD_SIZE), lambda j, g, s_ref: (0, 0, 2 * j + g)),
                pl.BlockSpec((1, 1, length), lambda j, g, s_ref: (2 * j + g, 0, 0)),
                pre_head(0),
                pre_head(2),
                whole((1, HEAD_SIZE)),
                whole((1, HEAD_SIZE)),
                whole((length, HEAD_SIZE)),
                whole((length, HEAD_SIZE)),
            ],
            out_specs=[
                pl.BlockSpec((blocks, piece, 4 * HEAD_SIZE), lambda j, g, s_ref: (0, 0, j)),
                whole((1, HEAD_SIZE)),
                whole((1, HEAD_SIZE)),
            ],
            scratch_shapes=[pltpu.VMEM((length, HEAD_SIZE), F32), pltpu.VMEM((length, HEAD_SIZE), F32)],
        ),
        cost_estimate=pl.CostEstimate(
            flops=2 * 2 * heads_kv * length * length * HEAD_SIZE * 5 // 2,
            bytes_accessed=2 * heads_kv * length * HEAD_SIZE * 24,
            transcendentals=heads_kv * length * length,
        ),
    )(s, qkv, qkv, qkv, grad_mixed, log_total, pre, pre, query_gain, key_gain, cosine, sine)


MESH = pl.DeviceIdType.MESH


def flip(index, bit):
    step = 1 << bit
    return index + step - 2 * step * lax.rem(lax.div(index, step), 2)


def bit_of(index, bit):
    return lax.rem(lax.div(index, 1 << bit), 2)


class Links:
    def __init__(self, send, recv):
        self.send, self.recv = send, recv
        self.d, self.s = lax.axis_index("dp"), lax.axis_index("seq")
        self.used = 0
        self.started = []

    def slots(self, n):
        self.used += n
        return self.used - n

    def copy(self, src, dst, slot, **to):
        return pltpu.make_async_remote_copy(
            src_ref=src,
            dst_ref=dst,
            send_sem=self.send.at[slot],
            recv_sem=self.recv.at[slot],
            device_id=to,
            device_id_type=MESH,
        )

    def plan(self, src, dst, slot, when=None, **to):
        copy = self.copy(src, dst, slot, **to)
        self.started.append((copy, when))
        return copy

    def start(self, src, dst, slot, when=None, **to):
        copy = self.plan(src, dst, slot, when, **to)
        if when is None:
            copy.start()
        else:
            pl.when(when)(copy.start)
        return copy

    def finish(self):
        for copy, when in self.started:
            if when is None:
                copy.wait_send()
            else:
                pl.when(when)(copy.wait_send)

    def greet(self, dp_masks, seq_masks):
        barrier = pltpu.get_barrier_semaphore()
        for mask in dp_masks:
            pl.semaphore_signal(
                barrier, inc=1, device_id={"dp": self.dp_at(mask)}, device_id_type=MESH
            )
        for mask in seq_masks:
            pl.semaphore_signal(
                barrier, inc=1, device_id={"seq": self.seq_at(mask)}, device_id_type=MESH
            )
        pl.semaphore_wait(barrier, len(dp_masks) + len(seq_masks))

    def seq_at(self, mask):
        s = self.s
        for bit in range(2):
            if mask >> bit & 1:
                s = flip(s, bit)
        return s

    def dp_at(self, mask):
        d = self.d
        for bit in range(3):
            if mask >> bit & 1:
                d = flip(d, bit)
        return d


class Gather:
    def __init__(self, links, block):
        base = links.slots(8)
        self.copies = {}
        for r, mask in ((0, 1), (0, 2), (0, 4), (2, 1), (4, 2), (4, 1), (6, 1)):
            src = block(links.dp_at(r))
            self.copies[r | mask] = links.plan(src, src, base + (r | mask), dp=links.dp_at(mask))

    def got(self, r):
        self.copies[r].wait_recv()

    def first(self):
        for mask in (4, 2, 1):
            self.copies[mask].start()

    def relay(self, r):
        self.got(r)
        if r == 4:
            self.copies[6].start()
        self.copies[r | 1].start()

    def last(self):
        for r in (1, 3, 5, 7):
            self.got(r)


def first_kernel(
    heads,
    a_ref, c_ref, out_ref, down_ref, x_ref, g_ref, gains_ref, qg_ref, kg_ref, cos_ref, sin_ref,
    xr_ref, gr_ref, wa_ref, wc_ref, wo_ref, wd_ref, n_ref, qkv_ref, pre_ref, o_ref, log_ref, gain_ref,
    w_v, x_v, n_v, qkv_v, pre_v, o_v, got_v, send, recv, local,
):
    links = Links(send, recv)
    d, s = links.d, links.s
    sequences, piece, width = x_ref.shape
    blocks = xr_ref.shape[1]
    length = blocks * piece
    x_bit, core = bit_of(s, 1), bit_of(s, 0)
    z1, z0, y = bit_of(d, 2), bit_of(d, 1), bit_of(d, 0)
    place_of = lambda i: lax.rem((i & 1) + core, 2) * 2 + lax.rem((i >> 1) + x_bit, 2)
    local_used = [0]
    locals_ = {}

    def near(name, src, dst):
        copy = pltpu.make_async_copy(src, dst, local.at[local_used[0]])
        local_used[0] += 1
        copy.start()
        locals_[name] = copy

    links.greet((1, 2, 4), (1, 2, 3))

    def exchange(src, dst):
        base = links.slots(4)
        return [
            links.start(src.at[links.seq_at(k)], dst.at[d, s], base + k, seq=links.seq_at(k))
            for k in (2, 3, 1)
        ]

    gain_slots = links.slots(4)
    gain_own = [
        links.start(gains_ref, got_v.at[d, s], gain_slots + k, seq=links.seq_at(k)) for k in (2, 3, 1)
    ]
    got_v[d, s] = gains_ref[...]
    a_own = exchange(a_ref, wa_ref)
    near("a", a_ref.at[s], wa_ref.at[d, s])

    x_slots, g_slots = links.slots(3 * sequences), links.slots(3 * sequences)

    def spread(own, everywhere, base, n):
        copies = [
            links.start(own.at[n], everywhere.at[n, k], base + 3 * n + k - 1, seq=links.seq_at(3 - k))
            for k in (1, 2)
        ]
        onward = links.plan(everywhere.at[n, 1], everywhere.at[n, 3], base + 3 * n + 2, seq=links.seq_at(1))
        return copies + [onward]

    def pass_on(copies):
        copies[0].wait_recv()
        copies[2].start()

    x_copies = [spread(x_ref, xr_ref, x_slots, 0)]
    c_own = exchange(c_ref, wc_ref)
    near("c", c_ref.at[s], wc_ref.at[d, s])
    for n in range(sequences):
        near(f"x{n}", x_ref.at[n], xr_ref.at[n, 0])
    near("d", down_ref, wd_ref.at[d])

    across, beside = lax.rem(x_bit + y, 2), lax.rem(core + z0, 2)
    out_slots = links.slots(7)
    holder = (across == 0) & (beside == 0)
    out_first = [
        links.start(
            out_ref, wo_ref.at[z1, s], out_slots + k,
            when=(across == k >> 1) & (beside == (k & 1)), seq=links.seq_at(k),
        )
        for k in (1, 2, 3)
    ]
    x_copies += [spread(x_ref, xr_ref, x_slots, n) for n in range(1, sequences)]

    for copy in gain_own + a_own:
        copy.wait_recv()
    locals_["a"].wait()
    gather_a, gather_c, gather_d, gather_gain = (
        Gather(links, lambda at, ref=ref: ref.at[at]) for ref in (wa_ref, wc_ref, wd_ref, got_v)
    )
    gather_gain.first()
    gather_a.first()
    for r in (2, 4, 6):
        gather_gain.relay(r)

    pass_on(x_copies[0])

    @pl.when(holder)
    def _():
        own = pltpu.make_async_copy(out_ref, wo_ref.at[z1, s], local.at[local_used[0]])
        own.start()
        for copy in out_first:
            copy.wait_recv()
        own.wait()

    local_used[0] += 1
    gather_a.relay(2)
    gather_a.relay(4)
    gather_a.relay(6)
    out_y = links.start(wo_ref.at[z1], wo_ref.at[z1], out_slots + 4, when=holder, dp=flip(d, 0))
    for copy in c_own:
        copy.wait_recv()
    locals_["c"].wait()
    gather_c.first()
    g_copies = [spread(g_ref, gr_ref, g_slots, n) for n in range(sequences)]
    for n in range(sequences):
        near(f"g{n}", g_ref.at[n], gr_ref.at[n, 0])
    locals_["d"].wait()
    gather_d.first()

    def wait_x(n):
        locals_[f"x{n}"].wait()
        for copy in x_copies[n][1:]:
            copy.wait_recv()
        near(f"xv{n}", xr_ref.at[n], x_v)
        locals_[f"xv{n}"].wait()

    def project_part(n, meanwhile=()):
        def step(i, carry):
            for k, action in enumerate(meanwhile):
                pl.when(i == k)(action)
            at = place_of(i)
            x = x_v[at].astype(F32)
            normed = (x * rms_scale(x) * gain_ref[0:1, :]).astype(BF16)
            n_v[n, at] = normed
            y_rows = dot(normed, w_v[...].reshape(width, -1))
            rows = pl.ds(pl.multiple_of(i * piece, piece), piece)
            cosine, sine = cos_ref[rows, :], sin_ref[rows, :]
            for j in range(heads // 2):
                for part in range(4):
                    cut = slice((4 * j + part) * HEAD_SIZE, (4 * j + part + 1) * HEAD_SIZE)
                    head = y_rows[:, cut]
                    if part < 3:
                        pre_v[n, rows, (3 * j + part) * HEAD_SIZE : (3 * j + part + 1) * HEAD_SIZE] = head
                        gain = qg_ref[...] if part < 2 else kg_ref[...]
                        head = head * rms_scale(head) * gain
                        head = head * cosine + pltpu.roll(head, HEAD_SIZE // 2, 1) * sine
                    qkv_v[n, rows, cut] = head.astype(BF16)
            return carry

        lax.fori_loop(0, blocks, step, 0)
        near(f"n{n}", n_v.at[n], n_ref.at[n])
        near(f"qkv{n}", qkv_v.at[n], qkv_ref.at[n])
        near(f"pre{n}", pre_v.at[n], pre_ref.at[n])

    def attend_part(n, meanwhile=()):
        def step(h, carry):
            for k, action in enumerate(meanwhile):
                pl.when(h == k)(action)
            j, g = lax.div(h, 2), lax.rem(h, 2)
            lanes = lambda at: pl.ds(pl.multiple_of(at * HEAD_SIZE, HEAD_SIZE), HEAD_SIZE)
            values_t = qkv_v[n, :, lanes(4 * j + 3)].T
            keys = qkv_v.at[n, :, lanes(4 * j + 2)]
            for i in range(blocks):
                query = qkv_v[n, i * piece : (i + 1) * piece, lanes(4 * j + g)]
                exponent, highest = masked_exp(keys, query, i, piece, None)
                total = jnp.sum(exponent, axis=0, keepdims=True)
                probs = (exponent * (1.0 / total)).astype(BF16)
                mixed = dot(values_t[:, : (i + 1) * piece], probs)
                o_v[n, place_of(i), :, lanes(h)] = mixed.T.astype(BF16)
                log_ref[n, h, :, i * piece : (i + 1) * piece] = highest + jnp.log(total)
            return carry

        lax.fori_loop(0, heads, step, 0)

    wait_x(0)
    gather_a.last()
    near("w", wa_ref, w_v)
    locals_["w"].wait()

    gather_gain.last()
    for at in range(got_v.shape[0]):
        gain_ref[:, at * 128 : (at + 1) * 128] = jnp.sum(got_v[at], axis=0)

    out_z1 = links.plan(wo_ref.at[z1], wo_ref.at[z1], out_slots + 5, when=beside == 0, dp=flip(d, 2))
    out_z0 = links.plan(wo_ref, wo_ref, out_slots + 6, when=beside == 0, dp=flip(d, 1))

    def out_next():
        pl.when((across == 1) & (beside == 0))(out_y.wait_recv)
        pl.when(beside == 0)(out_z1.start)

    def out_last():
        @pl.when(beside == 0)
        def _():
            out_z1.wait_recv()
            out_z0.start()

    nothing = lambda: None
    project_part(0, [out_next, lambda: gather_c.relay(2), lambda: pass_on(x_copies[1]), lambda: gather_c.relay(4)])
    attend_part(0, [nothing, out_last, lambda: gather_c.relay(6), lambda: gather_d.relay(2)])
    near("o0", o_v.at[0], o_ref.at[0])
    for n in range(1, sequences):
        wait_x(n)
        project_part(n, [lambda: gather_d.relay(4), nothing, lambda: pass_on(g_copies[0])])
        attend_part(n, [lambda: gather_d.relay(6), lambda: pass_on(g_copies[1])])
        near(f"o{n}", o_v.at[n], o_ref.at[n])
    gather_c.last()
    gather_d.last()
    pl.when(beside == 1)(out_z0.wait_recv)
    for pair in g_copies:
        for copy in pair[1:]:
            copy.wait_recv()
    for n in range(sequences):
        for name in ("g", "n", "qkv", "pre", "o"):
            locals_[f"{name}{n}"].wait()
    links.finish()


def first(a, c, w_out, w_down, x, g, gains, query_gain, key_gain, cosine, sine, dp, heads):
    blocks, rows, columns = a.shape
    sequences, piece, width = x.shape
    length = blocks * piece
    hbm = pl.BlockSpec(memory_space=pl.ANY)
    vmem = pl.BlockSpec(memory_space=pltpu.VMEM)
    shape = jax.ShapeDtypeStruct
    pre_columns = columns // 4 * 3
    slots = 96
    return pl.pallas_call(
        functools.partial(first_kernel, heads),
        name="first",
        out_shape=(
            shape((sequences, blocks, piece, width), BF16),
            shape((sequences, blocks, piece, width), BF16),
            shape((dp, blocks, rows, columns), BF16),
            shape((dp, blocks, rows, c.shape[2]), BF16),
            shape((2, blocks) + w_out.shape, BF16),
            shape((dp,) + w_down.shape, BF16),
            shape((sequences, blocks, piece, width), BF16),
            shape((sequences, length, columns), BF16),
            shape((sequences, length, pre_columns), F32),
            shape((sequences, blocks, piece, heads * HEAD_SIZE), BF16),
            shape((sequences, heads, 1, length), F32),
            shape((8, width), F32),
        ),
        in_specs=[vmem] * 11,
        out_specs=[hbm] * 10 + [vmem] * 2,
        scratch_shapes=[
            pltpu.VMEM((dp, blocks, rows, columns), BF16),
            pltpu.VMEM((blocks, piece, width), BF16),
            pltpu.VMEM((sequences, blocks, piece, width), BF16),
            pltpu.VMEM((sequences, length, columns), BF16),
            pltpu.VMEM((sequences, length, pre_columns), F32),
            pltpu.VMEM((sequences, blocks, piece, heads * HEAD_SIZE), BF16),
            pltpu.VMEM((dp, blocks, 8, width // dp), F32),
            pltpu.SemaphoreType.DMA((slots,)),
            pltpu.SemaphoreType.DMA((slots,)),
            pltpu.SemaphoreType.DMA((24,)),
        ],
        compiler_params=pltpu.CompilerParams(
            collective_id=0, has_side_effects=True, vmem_limit_bytes=60 * 1024 * 1024
        ),
    )(a, c, w_out, w_down, x, g, gains, query_gain, key_gain, cosine, sine)


def mlp_kernel(
    mixed_ref, wo_ref, wc_ref, wd_ref, x_ref, g_ref, gain_ref,
    out_ref, residual_ref, normed_ref, hidden_ref, both_ref, branch_ref, gain_grad_ref,
    res_v, core_s, oc_v, x_s, og_v, n2_v, hidden_v, both_v, dc_v, dg_v, da_v, us_v, uc_v, ux_v, ug_v, ua_v,
    send, recv, local, tokens_sem,
):
    links = Links(send, recv)
    sequences, blocks, piece, width = g_ref.shape
    half = blocks // 2
    units = wd_ref.shape[0]
    core, far = dict(seq=links.seq_at(1)), dict(seq=links.seq_at(2))
    pairs = [(n, k) for n in range(sequences) for k in range(half)]
    slots = {
        name: links.slots(half * sequences)
        for name in ("o_core", "o_far", "normed", "grad_core", "up_core", "grad_far", "branch", "up_far")
    }
    ends = {
        "o_core": lambda n, k: (core_s.at[n, k], oc_v.at[n, k], core),
        "o_far": lambda n, k: (x_s.at[n, k], og_v.at[n, half - 1 - k], far),
        "normed": lambda n, k: (n2_v.at[n, k], n2_v.at[n, half + k], core),
        "grad_core": lambda n, k: (core_s.at[n, k], dc_v.at[n, k], core),
        "up_core": lambda n, k: (us_v.at[n, k], uc_v.at[n, k], core),
        "grad_far": lambda n, k: (x_s.at[n, k], dg_v.at[n, half - 1 - k], far),
        "branch": lambda n, k: (us_v.at[n, k], branch_ref.at[n, half + k], core),
        "up_far": lambda n, k: (ux_v.at[n], ug_v.at[n], far),
    }

    def copy(name, n, k):
        src, dst, to = ends[name](n, k)
        return links.copy(src, dst, slots[name] + half * n + k, **to)

    def arrived(name, n, k):
        copy(name, n, half - 1 - k if name in ("o_far", "grad_far") else k).wait_recv()

    near_copies = []

    def near(src, dst):
        made = pltpu.make_async_copy(src, dst, local.at[len(near_copies)])
        made.start()
        near_copies.append(made)

    links.greet((), (1, 2))
    tokens = [
        pltpu.make_async_copy(x_ref.at[n, pl.ds(0, half)], uc_v.at[n], tokens_sem.at[n])
        for n in range(sequences)
    ]
    for made in tokens:
        made.start()
    gain = gain_ref[...]

    for n in range(sequences):

        def out_part(i, carry):
            b = lax.rem(i + half, blocks)
            y = dot(mixed_ref[n, b], wo_ref[...])

            @pl.when(i < half)
            def _():
                core_s[n, i] = y.astype(BF16)
                copy("o_core", n, i).start()

            @pl.when(i >= half)
            def _():
                res_v[n, i - half] = y

            return carry

        lax.fori_loop(0, blocks, out_part, 0)
        for k in range(half):
            arrived("o_core", n, k)
            total = res_v[n, k] + oc_v[n, k].astype(F32)
            res_v[n, k] = total
            x_s[n, k] = total.astype(BF16)
            copy("o_far", n, k).start()

    def norm(n):
        tokens[n].wait()
        for k in range(half):
            arrived("o_far", n, k)
            residual = res_v[n, k] + og_v[n, k].astype(F32) + uc_v[n, k].astype(F32)
            res_v[n, k] = residual
            n2_v[n, k] = (residual * rms_scale(residual) * gain).astype(BF16)
            copy("normed", n, k).start()

    def feed(n):
        for k in range(half):
            copy("o_core", n, k).wait_send()
            copy("o_far", n, k).wait_send()
            arrived("normed", n, k)

        def step(i, carry):
            b = lax.rem(i + half, blocks)
            both = dot(n2_v[n, b], wc_ref[...])
            gate, upward = both[:, :units], both[:, units:]
            grad_hidden = dot_t(g_ref[n, b], wd_ref[...])
            sigmoid = 1.0 / (1.0 + jnp.exp(-gate))
            silu = gate * sigmoid
            hidden_v[n, b] = (silu * upward).astype(BF16)
            both_v[n, b, :, units:] = (grad_hidden * silu).astype(BF16)
            both_v[n, b, :, :units] = (
                grad_hidden * upward * sigmoid * (1.0 + gate * (1.0 - sigmoid))
            ).astype(BF16)
            grad = dot_t(both_v[n, b], wc_ref[...])

            @pl.when(i < half)
            def _():
                core_s[n, i] = grad.astype(BF16)
                copy("grad_core", n, i).start()

            @pl.when(i >= half)
            def _():
                k = i - half
                arrived_core = copy("grad_core", n, k)
                arrived_core.wait_recv()
                total = grad + dc_v[n, k].astype(F32)
                da_v[n, k] = total
                x_s[n, k] = total.astype(BF16)
                copy("grad_far", n, k).start()

            up = dot(hidden_v[n, b], wd_ref[...])

            @pl.when(i < half)
            def _():
                us_v[n, i] = up.astype(BF16)
                copy("up_core", n, i).start()

            @pl.when(i >= half)
            def _():
                copy("up_core", n, i - half).wait_recv()

            @pl.when(i == half)
            def _():
                ua_v[n] = res_v[n, 0] + (up + uc_v[n, 0].astype(F32))

            @pl.when(i == half + 1)
            def _():
                ux_v[n] = (up + uc_v[n, 1].astype(F32)).astype(BF16)
                copy("up_far", n, 0).start()

            return carry

        lax.fori_loop(0, blocks, step, 0)
        near(n2_v.at[n], normed_ref.at[n])
        near(hidden_v.at[n], hidden_ref.at[n])
        near(both_v.at[n], both_ref.at[n])

    def back(n):
        for k in range(half):
            copy("up_core", n, k).wait_send()
        for k in range(half):
            arrived("grad_far", n, k)
            grad = da_v[n, k] + dg_v[n, k].astype(F32)
            residual = res_v[n, k]
            scale = rms_scale(residual)
            scaled = grad * gain
            grad_residual = (
                g_ref[n, k].astype(F32)
                + scale * scaled
                - residual * (scale * scale * scale * jnp.mean(scaled * residual, axis=-1, keepdims=True))
            )
            us_v[n, k] = grad_residual.astype(BF16)
            copy("branch", n, k).start()
            near(us_v.at[n, k], branch_ref.at[n, k])
            if k == 0:
                part = jnp.sum(grad * residual * scale, axis=0, keepdims=True)
                gain_grad_ref[...] = part if n == 0 else gain_grad_ref[...] + part
                da_v[n, 0] = grad_residual
                near(da_v.at[n, 0], residual_ref.at[n])
        copy("up_far", n, 0).wait_recv()
        oc_v[n, 0] = (ua_v[n] + ug_v[n].astype(F32)).astype(BF16)
        near(oc_v.at[n, 0], out_ref.at[n])

    for n in range(sequences):
        norm(n)
        feed(n)
    for n in range(sequences):
        back(n)
    for n, k in pairs:
        arrived("branch", n, k)
    for n, k in pairs:
        for name in ("normed", "grad_core", "grad_far", "branch"):
            copy(name, n, k).wait_send()
    for n in range(sequences):
        copy("up_far", n, 0).wait_send()
    for made in near_copies:
        made.wait()


def feed_forward(mixed, w_o, w_mlp, w_d, x_rel, g_rel, gain):
    sequences, blocks, piece, width = g_rel.shape
    half = blocks // 2
    units = w_d.shape[0]
    hbm = pl.BlockSpec(memory_space=pl.ANY)
    vmem = pl.BlockSpec(memory_space=pltpu.VMEM)
    shape = jax.ShapeDtypeStruct
    part = lambda dtype: pltpu.VMEM((sequences, half, piece, width), dtype)
    one = lambda dtype: pltpu.VMEM((sequences, piece, width), dtype)
    return pl.pallas_call(
        mlp_kernel,
        name="feed_forward",
        out_shape=(
            shape((sequences, piece, width), BF16),
            shape((sequences, piece, width), F32),
            shape((sequences, blocks, piece, width), BF16),
            shape((sequences, blocks, piece, units), BF16),
            shape((sequences, blocks, piece, 2 * units), BF16),
            shape((sequences, blocks, piece, width), BF16),
            shape((1, width), F32),
        ),
        in_specs=[vmem] * 4 + [hbm, vmem, vmem],
        out_specs=[hbm] * 6 + [vmem],
        scratch_shapes=[
            part(F32),
            part(BF16),
            part(BF16),
            part(BF16),
            part(BF16),
            pltpu.VMEM((sequences, blocks, piece, width), BF16),
            pltpu.VMEM((sequences, blocks, piece, units), BF16),
            pltpu.VMEM((sequences, blocks, piece, 2 * units), BF16),
            part(BF16),
            part(BF16),
            part(F32),
            part(BF16),
            part(BF16),
            one(BF16),
            one(BF16),
            one(F32),
            pltpu.SemaphoreType.DMA((16 * sequences,)),
            pltpu.SemaphoreType.DMA((16 * sequences,)),
            pltpu.SemaphoreType.DMA((16,)),
            pltpu.SemaphoreType.DMA((sequences,)),
        ],
        compiler_params=pltpu.CompilerParams(
            collective_id=1, has_side_effects=True, vmem_limit_bytes=67043328
        ),
    )(mixed, w_o, w_mlp, w_d, x_rel, g_rel, gain)


class Scatter:
    def __init__(self, links, src, first, second, third, done=None):
        d = links.d
        self.z1, self.z0, self.y = bit_of(d, 2), bit_of(d, 1), bit_of(d, 0)
        self.src, self.first, self.second, self.third = src, first, second, third
        base = links.slots(7)
        self.over_y = links.plan(src.at[:, :, 1 - self.y], first, base, dp=flip(d, 0))
        self.over_z0 = links.plan(first.at[:, 1 - self.z0], second, base + 1, dp=flip(d, 1))
        self.over_z1 = links.plan(second.at[1 - self.z1], third, base + 2, dp=flip(d, 2))
        self.done, self.s = done, links.s
        if done is not None:
            self.share = [
                links.plan(third.at[links.seq_at(k)], done.at[links.s], base + 3 + k, seq=links.seq_at(k))
                for k in (2, 3, 1)
            ]

    def start(self):
        self.over_y.start()

    def sum_y(self):
        self.over_y.wait_recv()

        def step(i, carry):
            a, b = lax.div(i, 2), lax.rem(i, 2)
            mine = self.src[a, b, self.y].astype(F32)
            self.first[a, b] = (mine + self.first[a, b].astype(F32)).astype(BF16)
            return carry

        lax.fori_loop(0, 4, step, 0)
        self.over_z0.start()

    def sum_z0(self):
        self.over_z0.wait_recv()

        def step(a, carry):
            mine = self.first[a, self.z0].astype(F32)
            self.second[a] = (mine + self.second[a].astype(F32)).astype(BF16)
            return carry

        lax.fori_loop(0, 2, step, 0)
        self.over_z1.start()

    def sum_z1(self):
        self.over_z1.wait_recv()
        mine = self.second[self.z1].astype(F32)
        self.third[...] = (mine + self.third[...].astype(F32)).astype(BF16)
        if self.done is not None:
            for copy in self.share:
                copy.start()
            self.done[self.s] = self.third[self.s]

    def end(self):
        for copy in self.share:
            copy.wait_recv()


def last_kernel(
    down_ref, mlp_ref, og_ref, branch_ref, wo_ref, qkv_ref, pre_ref, log_ref, w_ref, normed_ref,
    x_ref, residual_ref, gain_ref, mlp_gain_ref, qg_ref, kg_ref, cos_ref, sin_ref,
    tokens_ref, down_out, mlp_out, out_out, in_out, sums_ref,
    d1, d2, c1, c2, c3, o1, o2, o3, a_v, a1, a2, a3,
    do_v, gr_v, dk_v, dv_v, core_s, core_r, far_s, far_r, acc_v, total_v, got_v,
    send, recv, local,
):
    links = Links(send, recv)
    d, s = links.d, links.s
    sequences, blocks, piece, width = branch_ref.shape
    half = blocks // 2
    heads = log_ref.shape[1]
    heads_kv = heads // 2
    x_bit, core = bit_of(s, 1), bit_of(s, 0)
    z1, z0, y = bit_of(d, 2), bit_of(d, 1), bit_of(d, 0)
    place_of = lambda i: lax.rem((i & 1) + core, 2) * 2 + lax.rem((i >> 1) + x_bit, 2)
    across, beside = lax.rem(x_bit + y, 2), lax.rem(core + z0, 2)
    holder = (across == 0) & (beside == 0)
    lanes = lambda at: pl.ds(pl.multiple_of(at * HEAD_SIZE, HEAD_SIZE), HEAD_SIZE)
    nothing = lambda: None

    down = Scatter(links, down_ref, d1, d2, down_out)
    mlp = Scatter(links, mlp_ref, c1, c2, c3, mlp_out)
    ins = [
        Scatter(links, a_v.at[j], a1.at[j], a2.at[j], a3.at[j], in_out.at[j]) for j in range(heads_kv)
    ]
    base = links.slots(7)
    out_z0 = links.plan(og_ref, o1, base, when=beside == 1, dp=flip(d, 1))
    out_z1 = links.plan(o1.at[1 - z1], o2, base + 1, when=beside == 0, dp=flip(d, 2))
    out_y = links.plan(o2, o3, base + 2, when=(beside == 0) & (across == 1), dp=flip(d, 0))
    out_share = {
        k: links.plan(o3.at[links.seq_at(k)], out_out, base + 3 + k, when=holder, seq=links.seq_at(k))
        for k in (1, 2, 3)
    }

    def out_sum_z0():
        @pl.when(beside == 0)
        def _():
            out_z0.wait_recv()

            def step(i, carry):
                a, b = lax.div(i, blocks), lax.rem(i, blocks)
                o1[a, b] = (og_ref[a, b].astype(F32) + o1[a, b].astype(F32)).astype(BF16)
                return carry

            lax.fori_loop(0, 2 * blocks, step, 0)
            out_z1.start()

    def out_sum_z1():
        @pl.when(beside == 0)
        def _():
            out_z1.wait_recv()

            def step(b, carry):
                o2[b] = (o1[z1, b].astype(F32) + o2[b].astype(F32)).astype(BF16)
                return carry

            lax.fori_loop(0, blocks, step, 0)

        pl.when((beside == 0) & (across == 1))(out_y.start)

    def out_sum_y():
        @pl.when(holder)
        def _():
            out_y.wait_recv()

            def step(b, carry):
                o3[b] = (o2[b].astype(F32) + o3[b].astype(F32)).astype(BF16)
                return carry

            lax.fori_loop(0, blocks, step, 0)
            for copy in out_share.values():
                copy.start()
            out_out[...] = o3[s]

    links.greet((1, 2, 4), (1, 2, 3))
    upper = pltpu.make_async_copy(residual_ref, tokens_ref, local.at[0])
    upper.start()
    mlp.start()
    down.start()
    pl.when(beside == 1)(out_z0.start)
    total_v[0] = jnp.zeros_like(total_v[0])
    for r in range(width // 128):
        total_v[0, 8 + r : 9 + r, :] = mlp_gain_ref[:, r * 128 : (r + 1) * 128]

    def mixed_back(i, carry):
        n, b = lax.div(i, blocks), lax.rem(i, blocks)
        do_v[n, b] = dot_t(branch_ref[n, b], wo_ref[...]).astype(BF16)
        return carry

    lax.fori_loop(0, sequences * blocks, mixed_back, 0)

    slots = [links.slots(half * sequences), links.slots(sequences)]
    core_copies = {
        (n, k): links.plan(core_s.at[n, k], core_r.at[n, k], slots[0] + half * n + k, seq=links.seq_at(1))
        for n in range(sequences)
        for k in range(half)
    }
    far_copies = [
        links.plan(far_s.at[n], far_r.at[n], slots[1] + n, seq=links.seq_at(2)) for n in range(sequences)
    ]

    def input_part(n):
        def step(i, carry):
            b = lax.rem(i + half, blocks)
            grad = dot_t(gr_v[n, b], w_ref[...])
            for k in range(half):

                @pl.when(i == k)
                def _():
                    core_s[n, k] = grad.astype(BF16)
                    core_copies[n, k].start()

                @pl.when(i == half + k)
                def _():
                    core_copies[n, k].wait_recv()
                    total = grad + core_r[n, k].astype(F32)
                    if k == 0:
                        acc_v[n] = total
                    else:
                        far_s[n] = total.astype(BF16)
                        far_copies[n].start()

            return carry

        lax.fori_loop(0, blocks, step, 0)

    def input_end(n):
        far_copies[n].wait_recv()
        grad = acc_v[n] + far_r[n].astype(F32)
        tokens = x_ref[n].astype(F32)
        scale = rms_scale(tokens)
        scaled = grad * gain_ref[...]
        tokens_ref[n] = (
            tokens_ref[n]
            + scale * scaled
            - tokens * (scale * scale * scale * jnp.mean(scaled * tokens, axis=-1, keepdims=True))
        )
        part = jnp.sum(grad * tokens * scale, axis=0, keepdims=True)
        for r in range(width // 128):
            total_v[0, r : r + 1, :] += part[:, r * 128 : (r + 1) * 128]

    def attention(j, meanwhile):
        def step(t, carry):
            for k, action in enumerate(meanwhile):
                pl.when(t == k)(action)
            n, g = lax.div(t, 2), lax.rem(t, 2)

            @pl.when(g == 0)
            def _():
                dk_v[...] = jnp.zeros_like(dk_v)
                dv_v[...] = jnp.zeros_like(dv_v)

            keys, values = qkv_ref.at[n, :, lanes(4 * j + 2)], qkv_ref.at[n, :, lanes(4 * j + 3)]
            keys_t = keys[...].T
            for i in range(blocks):
                rows = slice(i * piece, (i + 1) * piece)
                end = (i + 1) * piece
                at = place_of(i)
                query = qkv_ref[n, rows, lanes(4 * j + g)]
                grad_out = do_v[n, at, :, lanes(2 * j + g)]
                probs, _ = masked_exp(keys, query, i, piece, log_ref[n, 2 * j + g, :, rows])
                dv_v[:end, :] += dot(probs.astype(BF16), grad_out)
                grad_probs = dot_t(values[:end, :], grad_out)
                inner = jnp.sum(probs * grad_probs, axis=0, keepdims=True)
                grad_scores = (probs * (grad_probs - inner)).astype(BF16)
                dk_v[:end, :] += dot(grad_scores, query)
                grad_query = dot(keys_t[:, :end], grad_scores).T * SCALE
                result, gain = head_back(
                    grad_query, pre_ref[n, rows, lanes(3 * j + g)], qg_ref[...], cos_ref[rows, :], sin_ref[rows, :]
                )
                gr_v[n, at, :, lanes(4 * j + g)] = result.astype(BF16)
                total_v[0, 16:17, :] += gain

            @pl.when(g == 1)
            def _():
                for i in range(blocks):
                    rows = slice(i * piece, (i + 1) * piece)
                    at = place_of(i)
                    result, gain = head_back(
                        dk_v[rows, :] * SCALE, pre_ref[n, rows, lanes(3 * j + 2)], kg_ref[...],
                        cos_ref[rows, :], sin_ref[rows, :],
                    )
                    gr_v[n, at, :, lanes(4 * j + 2)] = result.astype(BF16)
                    gr_v[n, at, :, lanes(4 * j + 3)] = dv_v[rows, :].astype(BF16)
                    total_v[0, 17:18, :] += gain

            return carry

        lax.fori_loop(0, 2 * sequences, step, 0)

    def weight_in(j):
        wide = 4 * HEAD_SIZE
        chunk = 2 * width // 8

        def step(m, carry):
            cut = pl.ds(pl.multiple_of(m * chunk, chunk), chunk)
            total = None
            for n in range(sequences):
                left = normed_ref[n, :, :, cut].reshape(blocks * piece, chunk)
                right = gr_v[n, :, :, j * wide : (j + 1) * wide].reshape(blocks * piece, wide)
                term = t_dot(left, right)
                total = term if total is None else total + term
            a_v[j, lax.div(m, 2), lax.rem(m, 2)] = total.astype(BF16).reshape(a_v.shape[3:])
            return carry

        lax.fori_loop(0, width // chunk, step, 0)
        ins[j].start()

    attention(0, [nothing, nothing, out_sum_z0])
    weight_in(0)
    attention(1, [out_sum_z1, mlp.sum_y, lambda: input_part(0)])
    input_part(1)
    weight_in(1)
    down.sum_y()
    mlp.sum_z0()
    upper.wait()
    for n in range(sequences):
        input_end(n)

    gain_slots = links.slots(5)
    gain_to = [dict(seq=links.seq_at(1)), dict(seq=links.seq_at(2))] + [dict(dp=flip(d, b)) for b in range(3)]
    gain_copies = [
        links.plan(total_v.at[k], got_v.at[k], gain_slots + k, **gain_to[k]) for k in range(5)
    ]

    def gain_stage(k):
        gain_copies[k].wait_recv()
        if k == 4:
            sums_ref[...] = total_v[4] + got_v[4]
        else:
            total_v[k + 1] = total_v[k] + got_v[k]
            gain_copies[k + 1].start()

    gain_copies[0].start()
    ins[0].sum_y()
    gain_stage(0)
    down.sum_z0()
    gain_stage(1)
    out_sum_y()
    mlp.sum_z1()
    gain_stage(2)
    ins[0].sum_z0()
    down.sum_z1()
    gain_stage(3)
    ins[0].sum_z1()
    ins[1].sum_y()
    gain_stage(4)
    ins[1].sum_z0()
    ins[1].sum_z1()
    for k, copy in out_share.items():
        pl.when((across == k >> 1) & (beside == (k & 1)))(copy.wait_recv)
    mlp.end()
    for scatter in ins:
        scatter.end()
    links.finish()


def last(
    down, mlp, out, branch, w_o, qkv, pre, log_total, w_in, normed, x, residual,
    gain, mlp_gain_grad, query_gain, key_gain, cosine, sine,
):
    sequences, blocks, piece, width = branch.shape
    length = blocks * piece
    rows, wide = mlp.shape[-2], mlp.shape[-1]
    down_rows = down.shape[-2]
    out_rows = out.shape[-2]
    heads_kv = qkv.shape[-1] // (4 * HEAD_SIZE)
    vmem = pl.BlockSpec(memory_space=pltpu.VMEM)
    shape = jax.ShapeDtypeStruct
    b16 = lambda *dims: pltpu.VMEM(dims, BF16)
    f32 = lambda *dims: pltpu.VMEM(dims, F32)
    part = (blocks, rows, 4 * HEAD_SIZE)
    return pl.pallas_call(
        last_kernel,
        name="last",
        out_shape=(
            shape((sequences, piece, width), F32),
            shape((down_rows, width), BF16),
            shape((blocks, rows, wide), BF16),
            shape((out_rows, width), BF16),
            shape((heads_kv,) + part, BF16),
            shape((24, 128), F32),
        ),
        in_specs=[vmem] * 11 + [pl.BlockSpec(memory_space=pl.ANY)] + [vmem] * 6,
        out_specs=[vmem] * 6,
        scratch_shapes=[
            b16(2, 2, down_rows, width),
            b16(2, down_rows, width),
            b16(2, 2, blocks, rows, wide),
            b16(2, blocks, rows, wide),
            b16(blocks, rows, wide),
            b16(2, blocks, out_rows, width),
            b16(blocks, out_rows, width),
            b16(blocks, out_rows, width),
            b16(heads_kv, 2, 2, 2, *part),
            b16(heads_kv, 2, 2, *part),
            b16(heads_kv, 2, *part),
            b16(heads_kv, *part),
            b16(sequences, blocks, piece, 2 * heads_kv * HEAD_SIZE),
            b16(sequences, blocks, piece, width),
            f32(length, HEAD_SIZE),
            f32(length, HEAD_SIZE),
            b16(sequences, blocks // 2, piece, width),
            b16(sequences, blocks // 2, piece, width),
            b16(sequences, piece, width),
            b16(sequences, piece, width),
            f32(sequences, piece, width),
            f32(5, 24, 128),
            f32(5, 24, 128),
            pltpu.SemaphoreType.DMA((64,)),
            pltpu.SemaphoreType.DMA((64,)),
            pltpu.SemaphoreType.DMA((1,)),
        ],
        compiler_params=pltpu.CompilerParams(
            collective_id=2, has_side_effects=True, vmem_limit_bytes=67043328
        ),
    )(
        down, mlp, out, branch, w_o, qkv, pre, log_total, w_in, normed, x, residual,
        gain, mlp_gain_grad, query_gain, key_gain, cosine, sine,
    )


def body(
    hidden_in,
    attn_gain,
    w_query,
    key_weight,
    value_weight,
    query_gain,
    key_gain,
    w_out,
    mlp_gain,
    w_gate,
    w_up,
    w_down,
    cotangent,
):
    wires = Wires(lax.axis_size("dp"), lax.axis_size("seq"))
    dp, seq, x_count = wires.dp, wires.seq, wires.x_count
    count = wires.count
    sequences, piece, width = hidden_in.shape
    length = seq * piece
    part = x_count * piece
    heads_kv = key_weight.shape[1] // HEAD_SIZE
    s_index = wires.s.reshape(1).astype(jnp.int32)
    cosine, sine = rope_tables(length)
    query_gain_row = query_gain.astype(F32).reshape(1, -1)
    key_gain_row = key_gain.astype(F32).reshape(1, -1)

    index = wires.d * seq + wires.s
    own_gains = jnp.stack([attn_gain, mlp_gain])
    rows = w_query.shape[0]
    by_head = jnp.concatenate(
        [
            w_query.reshape(rows, heads_kv, -1),
            key_weight.reshape(rows, heads_kv, -1),
            value_weight.reshape(rows, heads_kv, -1),
        ],
        axis=2,
    )
    order = [wires.heads_of(t, heads_kv) for t in range(seq)]
    package_in = jnp.stack(
        [jnp.concatenate([by_head[:, j] for j in order[t]], axis=1) for t in range(seq)]
    )
    down_rows = w_down.shape[0]

    def by_unit(w):
        return w.reshape(rows, dp, seq, down_rows).transpose(2, 0, 1, 3).reshape(seq, rows, -1)

    units = dp * down_rows
    package_mlp = jnp.concatenate([by_unit(w_gate), by_unit(w_up)], axis=2)

    fused = (dp, seq, heads_kv) == (8, 4, 8) and width == 128 * dp and rows % 16 == 0 and down_rows % 16 == 0
    if fused:
        gains = jnp.zeros((8, seq, width // count), F32)
        gains = lax.dynamic_update_slice(gains, own_gains.astype(F32)[:, None], (0, wires.s, 0))
        (
            x_rel, g_rel, w_in, w_mlp, w_o, w_d, all_normed, all_qkv, all_pre, all_mixed, all_log, gains
        ) = first(
            package_in, package_mlp, w_out, w_down, hidden_in, cotangent, gains.reshape(8, -1),
            query_gain_row, key_gain_row, cosine, sine, dp, 2 * heads_kv // seq,
        )
        w_in, w_mlp = w_in.reshape(width, -1), w_mlp.reshape(width, -1)
        w_o, w_d = w_o.reshape(-1, width), w_d.reshape(units, width)
        attn_gain_row, mlp_gain_row = gains[:1], gains[1:2]
        (
            all_out, all_grad_residual, all_normed_mlp, all_hidden, all_grad_both, all_branch, mlp_gain_grad
        ) = feed_forward(all_mixed, w_o, w_mlp, w_d, x_rel, g_rel, mlp_gain_row)
    else:
        gains = jnp.zeros((2, count, width // count), BF16)
        gains = lax.dynamic_update_slice(gains, own_gains[:, None], (0, index, 0))
        gains = wires.sum_all(gains.reshape(2, width)).astype(F32)
        attn_gain_row, mlp_gain_row = gains[:1], gains[1:]
        package = wires.exchange_seq(package_in).reshape(seq * rows, -1)
        w_in = wires.gather_dp(package).reshape(width, -1)
        x_rel = jnp.stack(wires.gather_seq_relative(hidden_in), axis=1)
        w_o = wires.gather_out(w_out, heads_kv)
        package = wires.exchange_seq(package_mlp).reshape(seq * rows, -1)
        w_mlp = wires.gather_dp(package).reshape(width, -1)
        g_rel = jnp.stack(wires.gather_seq_relative(cotangent), axis=1)
        w_d = wires.gather_dp(w_down).reshape(units, width)

    kept = []
    outs = []
    for n in range(0 if fused else sequences):
        normed, qkv, pre = project(
            s_index, x_rel[n], w_in, attn_gain_row, query_gain_row, key_gain_row, cosine, sine, x_count
        )
        mixed, log_total = attend(s_index, qkv, seq, x_count)
        mixed_rows = mixed.reshape(length, -1)
        other = wires.swap(dot(mixed_rows[part:], w_o).astype(BF16), 1)
        total = wires.sum_x(dot(mixed_rows[:part], w_o) + other.astype(F32))
        residual = total + x_rel[n].reshape(length, width)[:part].astype(F32)
        scale = rms_scale(residual)
        normed_mlp = (residual * scale * mlp_gain_row).astype(BF16)
        normed_mlp = jnp.concatenate([normed_mlp, wires.swap(normed_mlp, 1)], axis=0)
        both = dot(normed_mlp, w_mlp)
        gate, upward = both[:, :units], both[:, units:]
        sigmoid = jax.nn.sigmoid(gate)
        silu = gate * sigmoid
        hidden = (silu * upward).astype(BF16)
        other = wires.swap(dot(hidden[part:], w_d).astype(BF16), 1)
        total = wires.scatter_x(dot(hidden[:part], w_d) + other.astype(F32))
        outs.append((residual[:piece] + total).astype(BF16))

        grad_top = g_rel[n].reshape(length, width)
        grad_hidden = dot_t(grad_top, w_d)
        grad_gate = (grad_hidden * upward * sigmoid * (1.0 + gate * (1.0 - sigmoid))).astype(BF16)
        grad_upward = (grad_hidden * silu).astype(BF16)
        grad_both = jnp.concatenate([grad_gate, grad_upward], axis=1)
        other = wires.swap(dot_t(grad_both[part:], w_mlp).astype(BF16), 1)
        grad_normed = wires.sum_x(dot_t(grad_both[:part], w_mlp) + other.astype(F32))
        scaled = grad_normed * mlp_gain_row
        grad_residual = (
            grad_top[:part].astype(F32)
            + scale * scaled
            - residual * (scale * scale * scale * jnp.mean(scaled * residual, axis=-1, keepdims=True))
        )
        grad_mlp_gain = jnp.sum((grad_normed * residual * scale)[:piece], axis=0)
        branch = grad_residual.astype(BF16)
        branch = jnp.concatenate([branch, wires.swap(branch, 1)], axis=0)
        grad_mixed = dot_t(branch, w_o).astype(BF16).reshape(mixed.shape)
        grad_qkv, grad_query_gain, grad_key_gain = attend_back(
            s_index, qkv, pre, log_total, grad_mixed, query_gain_row, key_gain_row, cosine, sine, seq, x_count
        )
        grad_rows = grad_qkv.reshape(length, -1)
        other = wires.swap(dot_t(grad_rows[part:], w_in).astype(BF16), 1)
        grad_first = wires.scatter_x(dot_t(grad_rows[:part], w_in) + other.astype(F32))
        tokens = hidden_in[n].astype(F32)
        scale = rms_scale(tokens)
        scaled = grad_first * attn_gain_row
        grad_tokens = (
            grad_residual[:piece]
            + scale * scaled
            - tokens * (scale * scale * scale * jnp.mean(scaled * tokens, axis=-1, keepdims=True))
        )
        grad_attn_gain = jnp.sum(grad_first * tokens * scale, axis=0)
        kept.append(
            dict(
                normed=normed.reshape(length, width),
                mixed=mixed_rows,
                normed_mlp=normed_mlp,
                hidden=hidden,
                grad_both=grad_both,
                branch=branch,
                grad_rows=grad_rows,
                grad_tokens=grad_tokens,
                gains=jnp.concatenate(
                    [grad_attn_gain, grad_mlp_gain, grad_query_gain[0], grad_key_gain[0]]
                ),
            )
        )

    def from_unit(g):
        return g.reshape(seq, rows, dp, down_rows).transpose(1, 2, 0, 3).reshape(rows, -1)

    if fused:
        flat = lambda value: value.reshape(sequences * length, -1)
        grad_mlp = t_dot(flat(all_normed_mlp), flat(all_grad_both)).astype(BF16)
        grad_down = t_dot(flat(all_hidden), flat(g_rel)).astype(BF16)
        grad_out = t_dot(flat(all_mixed), flat(all_branch)).astype(BF16)
        grad_tokens, grad_down, grad_mlp, grad_out, grad_in, gain_sums = last(
            grad_down.reshape(2, 2, 2, down_rows, width),
            grad_mlp.reshape(2, 2, 2, seq, rows, -1),
            grad_out.reshape(2, seq, -1, width),
            all_branch, w_o, all_qkv, all_pre, all_log, w_in, all_normed, hidden_in, all_grad_residual,
            attn_gain_row, mlp_gain_grad, query_gain_row, key_gain_row, cosine, sine,
        )
        grad_down, grad_mlp, grad_out = grad_down.astype(F32), grad_mlp.astype(F32), grad_out.astype(F32)
        grad_in = grad_in.astype(F32).transpose(1, 2, 0, 3).reshape(seq, rows, -1)
        gain_sums = gain_sums.reshape(-1)[: 2 * width + 2 * HEAD_SIZE]
        hidden_out = all_out
    else:
        def over(name):
            return jnp.concatenate([k[name] for k in kept], axis=0)

        grad_down = t_dot(over("hidden"), g_rel.reshape(-1, width)).astype(BF16)
        grad_down = wires.scatter_dp(grad_down.reshape(dp, down_rows, width)).astype(F32)

        grad_mlp = t_dot(over("normed_mlp"), over("grad_both")).astype(BF16)
        grad_mlp = wires.scatter_dp(grad_mlp.reshape(dp, seq * rows, -1))
        grad_mlp = wires.exchange_seq(grad_mlp.reshape(seq, rows, -1)).astype(F32)


        grad_out = t_dot(over("mixed"), over("branch")).astype(BF16)
        grad_out = wires.scatter_out(grad_out, heads_kv).astype(F32)

        grad_in = t_dot(over("normed"), over("grad_rows")).astype(BF16)
        grad_in = wires.scatter_dp(grad_in.reshape(dp, seq * rows, -1))
        grad_in = wires.exchange_seq(grad_in.reshape(seq, rows, -1)).astype(F32)
        gain_sums = wires.sum_all(sum(k["gains"] for k in kept))
        grad_tokens = jnp.stack([k["grad_tokens"] for k in kept])
        hidden_out = jnp.stack(outs)

    grad_gate, grad_up = from_unit(grad_mlp[..., :units]), from_unit(grad_mlp[..., units:])
    pieces = [None] * heads_kv
    for t in range(seq):
        for m, j in enumerate(order[t]):
            pieces[j] = grad_in[t, :, m * 4 * HEAD_SIZE : (m + 1) * 4 * HEAD_SIZE]
    grad_query = jnp.concatenate([p[:, : 2 * HEAD_SIZE] for p in pieces], axis=1)
    grad_key = jnp.concatenate([p[:, 2 * HEAD_SIZE : 3 * HEAD_SIZE] for p in pieces], axis=1)
    grad_value = jnp.concatenate([p[:, 3 * HEAD_SIZE :] for p in pieces], axis=1)

    own = width // count
    grad_attn_gain = lax.dynamic_slice_in_dim(gain_sums, index * own, own)
    grad_mlp_gain = lax.dynamic_slice_in_dim(gain_sums, width + index * own, own)
    return (
        hidden_out,
        grad_tokens,
        grad_attn_gain,
        grad_query,
        grad_key,
        grad_value,
        gain_sums[2 * width : 2 * width + HEAD_SIZE],
        gain_sums[2 * width + HEAD_SIZE :],
        grad_out,
        grad_mlp_gain,
        grad_gate,
        grad_up,
        grad_down,
    )


def solution(mesh):
    rows = P(("dp", "seq"), None)
    line = P(("dp", "seq"))
    tokens = P("dp", "seq", None)
    return jax.shard_map(
        body,
        mesh=mesh,
        in_specs=(tokens, line, rows, rows, rows, P(), P(), rows, line, rows, rows, rows, tokens),
        out_specs=(tokens, tokens, line, rows, rows, rows, P(), P(), rows, line, rows, rows, rows),
        check_vma=False,
    )
```

```python
import functools

import jax
import jax.numpy as jnp
from jax import lax
from jax.experimental import pallas as pl
from jax.experimental.pallas import tpu as pltpu
from jax.sharding import PartitionSpec as P

HEAD_SIZE = 128
EPS = 1e-06
ROPE_THETA = 1000000.0
AXES = ("dp", "seq")
SCALE = HEAD_SIZE ** (-0.5)
F32 = jnp.float32
BF16 = jnp.bfloat16


def log2(n):
    return n.bit_length() - 1


class Wires:
    def __init__(self, dp, seq):
        self.dp, self.seq, self.count = dp, seq, dp * seq
        self.dp_bits, self.seq_bits = log2(dp), log2(seq)
        self.x_count = seq // 2
        y_bits = min(log2(self.x_count), self.dp_bits)
        self.dp_order = list(range(y_bits, self.dp_bits)) + list(range(y_bits))
        self.x_bits = list(range(1, self.seq_bits))
        self.d = lax.axis_index("dp")
        self.s = lax.axis_index("seq")

    def swap(self, value, mask, only=None):
        pairs = [(i, i ^ mask) for i in range(self.count) if only is None or only(i)]
        return lax.ppermute(value, AXES, pairs)

    def dp_swap(self, value, bit, only=None):
        return self.swap(value, (1 << bit) * self.seq, only)

    def bit_d(self, bit):
        return (self.d >> bit) & 1

    def bit_s(self, bit):
        return (self.s >> bit) & 1

    def gather_dp(self, shard):
        pieces = {0: shard}
        for bit in self.dp_order:
            pieces.update({r | (1 << bit): self.dp_swap(v, bit) for r, v in list(pieces.items())})
        full = jnp.zeros((self.dp,) + shard.shape, shard.dtype)
        for r, v in pieces.items():
            full = lax.dynamic_update_index_in_dim(full, v, self.d ^ r, 0)
        return full

    def scatter_dp(self, value):
        rest = value.shape[1:]
        held = list(range(self.dp_bits - 1, -1, -1))
        value = value.reshape((2,) * self.dp_bits + rest)
        for bit in reversed(self.dp_order):
            axis = held.index(bit)
            held.pop(axis)
            mine = lax.dynamic_index_in_dim(value, self.bit_d(bit), axis, keepdims=False)
            other = lax.dynamic_index_in_dim(value, 1 - self.bit_d(bit), axis, keepdims=False)
            got = self.dp_swap(other, bit)
            value = (mine.astype(F32) + got.astype(F32)).astype(BF16)
        return value

    def exchange_seq(self, value):
        rest = value.shape[1:]
        for bit in self.x_bits + [0]:
            value = value.reshape((self.seq >> (bit + 1), 2, 1 << bit) + rest)
            me = self.bit_s(bit)
            mine = lax.dynamic_index_in_dim(value, me, 1, keepdims=False)
            other = lax.dynamic_index_in_dim(value, 1 - me, 1, keepdims=False)
            got = self.swap(other, 1 << bit)
            low = jnp.where(me == 0, mine, got)
            high = jnp.where(me == 0, got, mine)
            value = jnp.stack([low, high], axis=1).reshape((self.seq,) + rest)
        return value

    def gather_seq_relative(self, value):
        pieces = [value]
        for bit in self.x_bits:
            pieces = pieces + [self.swap(v, 1 << bit) for v in pieces]
        return pieces + [self.swap(v, 1) for v in pieces]

    def sum_x(self, value):
        n = self.x_count
        shape = value.shape
        for bit in self.x_bits:
            got = self.swap(value.astype(BF16), 1 << bit).astype(F32)
            blocks = got.reshape((n, shape[0] // n) + shape[1:])
            flip = [i ^ (1 << (bit - 1)) for i in range(n)]
            value = value + jnp.concatenate([blocks[i] for i in flip], axis=0)
        return value

    def scatter_x(self, value):
        n = self.x_count
        for bit in reversed(self.x_bits):
            half = value.shape[0] // 2
            got = self.swap(value[half:].astype(BF16), 1 << bit)
            value = value[:half] + got.astype(F32)
        return value

    def sum_all(self, value):
        for bit in range(log2(self.count)):
            value = value + self.swap(value, 1 << bit)
        return value

    def head_bits(self, heads_kv):
        low = self.dp_bits - log2(heads_kv)
        partner = {0: 1, 1: 0, 2: 2}
        matched = [(low + k, partner[k]) for k in range(self.seq_bits)]
        free = [low + k for k in range(self.seq_bits, log2(heads_kv))]
        return low, matched, free

    def heads_of(self, t, heads_kv):
        low, matched, free = self.head_bits(heads_kv)
        heads = [0]
        for bit, tbit in matched:
            heads = [h | (((t >> tbit) & 1) << (bit - low)) for h in heads]
        for bit in free:
            heads = heads + [h | (1 << (bit - low)) for h in heads]
        return heads

    def matches(self, i, pairs):
        return all(((i // self.seq) >> b) & 1 == (i >> t) & 1 for b, t in pairs)

    def gather_out(self, shard, heads_kv):
        low, matched, free = self.head_bits(heads_kv)
        value = shard
        for bit in self.x_bits + [0]:
            pass
        value = shard[None]
        for bit in [0] + self.x_bits:
            got = self.swap(value, 1 << bit)
            value = self.ordered(value, got, self.bit_s(bit))
        for bit in range(low):
            got = self.dp_swap(value, bit)
            value = self.ordered(value, got, self.bit_d(bit))
        for n, (bit, tbit) in enumerate(matched):
            got = self.dp_swap(value, bit, lambda i: self.matches(i, matched[n:]))
            value = jnp.where(self.bit_d(bit) == self.bit_s(tbit), value, got)
        for bit in free:
            got = self.dp_swap(value, bit)
            value = self.ordered(value, got, self.bit_d(bit))
        return value.reshape((-1,) + shard.shape[1:])

    def ordered(self, own, got, bit):
        return jnp.concatenate(
            [jnp.where(bit == 0, own, got), jnp.where(bit == 0, got, own)], axis=0
        )

    def halves(self, value, bit):
        half = value.shape[0] // 2
        mine = lax.dynamic_slice_in_dim(value, bit * half, half, 0)
        other = lax.dynamic_slice_in_dim(value, (1 - bit) * half, half, 0)
        return mine, other

    def scatter_out(self, value, heads_kv):
        low, matched, free = self.head_bits(heads_kv)
        for bit in reversed(free):
            mine, other = self.halves(value, self.bit_d(bit))
            got = self.dp_swap(other, bit)
            value = (mine.astype(F32) + got.astype(F32)).astype(BF16)
        for n in reversed(range(len(matched))):
            bit, tbit = matched[n]
            got = self.dp_swap(
                value,
                bit,
                lambda i: self.matches(i, matched[n + 1 :]) and not self.matches(i, [matched[n]]),
            )
            value = (value.astype(F32) + got.astype(F32)).astype(BF16)
        for bit in reversed(range(low)):
            mine, other = self.halves(value, self.bit_d(bit))
            got = self.dp_swap(other, bit, lambda i: self.matches(i, matched))
            value = (mine.astype(F32) + got.astype(F32)).astype(BF16)
        todo = dict((tbit, bit) for bit, tbit in matched)
        for tbit in reversed(self.x_bits):
            value = self.hand_out(value, tbit, todo)
        return self.hand_out(value, 0, todo)

    def hand_out(self, value, tbit, todo):
        bit = todo.pop(tbit)
        left = [(b, t) for t, b in todo.items()]
        mine, other = self.halves(value, self.bit_s(tbit))
        got = self.swap(
            other, 1 << tbit, lambda i: self.matches(i, left) and self.matches(i, [(bit, tbit)])
        )
        return jnp.where(self.bit_d(bit) == self.bit_s(tbit), mine, got)


def dot(a, b):
    return lax.dot_general(a, b, (((1,), (0,)), ((), ())), preferred_element_type=F32)


def dot_t(a, b):
    return lax.dot_general(a, b, (((1,), (1,)), ((), ())), preferred_element_type=F32)


def t_dot(a, b):
    return lax.dot_general(a, b, (((0,), (0,)), ((), ())), preferred_element_type=F32)


def rms_scale(rows):
    return lax.rsqrt(jnp.mean(rows * rows, axis=-1, keepdims=True) + EPS)


def rope_tables(length):
    halfway = HEAD_SIZE // 2
    inverse = jnp.power(F32(ROPE_THETA), -(jnp.arange(halfway).astype(F32) * 2.0) / HEAD_SIZE)
    angles = jnp.arange(length).astype(F32)[:, None] * inverse[None, :]
    cosine, sine = jnp.cos(angles), jnp.sin(angles)
    return (
        jnp.concatenate([cosine, cosine], axis=-1),
        jnp.concatenate([-sine, sine], axis=-1),
    )


def place(block, s, x_count):
    return ((block & 1) ^ (s & 1)) * x_count + ((block >> 1) ^ (s >> 1))


def project_kernel(s_ref, x_ref, w_ref, gain_ref, qg_ref, kg_ref, cos_ref, sin_ref, n_ref, qkv_ref, pre_ref):
    x = x_ref[0].astype(F32)
    normed = (x * rms_scale(x) * gain_ref[...]).astype(BF16)
    n_ref[0] = normed
    y = dot(normed, w_ref[...])
    cosine, sine = cos_ref[...], sin_ref[...]
    for j in range(y.shape[1] // (4 * HEAD_SIZE)):
        for part in range(4):
            at = slice((4 * j + part) * HEAD_SIZE, (4 * j + part + 1) * HEAD_SIZE)
            head = y[:, at]
            if part < 3:
                pre_ref[:, (3 * j + part) * HEAD_SIZE : (3 * j + part + 1) * HEAD_SIZE] = head
                gain = qg_ref[...] if part < 2 else kg_ref[...]
                head = head * rms_scale(head) * gain
                head = head * cosine + pltpu.roll(head, HEAD_SIZE // 2, 1) * sine
            qkv_ref[:, at] = head.astype(BF16)


def project(s, x_rel, w, gain, query_gain, key_gain, cosine, sine, x_count):
    blocks, piece, width = x_rel.shape
    length, columns = blocks * piece, w.shape[1]
    heads = columns // (4 * HEAD_SIZE)
    whole = lambda shape: pl.BlockSpec(shape, lambda i, s_ref: (0,) * len(shape))
    rel = pl.BlockSpec((1, piece, width), lambda i, s_ref: (place(i, s_ref[0], x_count), 0, 0))
    table = pl.BlockSpec((piece, HEAD_SIZE), lambda i, s_ref: (i, 0))
    return pl.pallas_call(
        project_kernel,
        name="project",
        out_shape=(
            jax.ShapeDtypeStruct((blocks, piece, width), BF16),
            jax.ShapeDtypeStruct((length, columns), BF16),
            jax.ShapeDtypeStruct((length, 3 * heads * HEAD_SIZE), F32),
        ),
        grid_spec=pltpu.PrefetchScalarGridSpec(
            num_scalar_prefetch=1,
            grid=(blocks,),
            in_specs=[
                rel,
                whole(w.shape),
                whole((1, width)),
                whole((1, HEAD_SIZE)),
                whole((1, HEAD_SIZE)),
                table,
                table,
            ],
            out_specs=[
                rel,
                pl.BlockSpec((piece, columns), lambda i, s_ref: (i, 0)),
                pl.BlockSpec((piece, 3 * heads * HEAD_SIZE), lambda i, s_ref: (i, 0)),
            ],
        ),
        cost_estimate=pl.CostEstimate(
            flops=2 * length * width * columns,
            bytes_accessed=2 * (2 * length * width + width * columns + 4 * length * columns),
            transcendentals=0,
        ),
    )(s, x_rel, w, gain, query_gain, key_gain, cosine, sine)


def masked_exp(k_ref, query, i, piece, offset):
    diagonal = dot_t(k_ref[i * piece : (i + 1) * piece, :], query) * SCALE
    key_at = lax.broadcasted_iota(jnp.int32, (piece, piece), 0)
    query_at = lax.broadcasted_iota(jnp.int32, (piece, piece), 1)
    diagonal = jnp.where(key_at <= query_at, diagonal, -jnp.inf)
    if i == 0:
        scores = diagonal
    else:
        scores = jnp.concatenate(
            [dot_t(k_ref[: i * piece, :], query) * SCALE, diagonal], axis=0
        )
    if offset is None:
        offset = jnp.max(scores, axis=0, keepdims=True)
    return jnp.exp(scores - offset), offset


def forward_kernel(blocks, x_count, s_ref, q_ref, k_ref, v_ref, o_ref, log_ref):
    piece = q_ref.shape[0] // blocks
    values_t = v_ref[...].T
    for i in range(blocks):
        query = q_ref[i * piece : (i + 1) * piece, :]
        exponent, highest = masked_exp(k_ref, query, i, piece, None)
        total = jnp.sum(exponent, axis=0, keepdims=True)
        probs = (exponent * (1.0 / total)).astype(BF16)
        mixed = dot(values_t[:, : (i + 1) * piece], probs)
        o_ref[place(i, s_ref[0], x_count)] = mixed.T.astype(BF16)
        log_ref[0, :, i * piece : (i + 1) * piece] = highest + jnp.log(total)


def attend(s, qkv, blocks, x_count):
    length, columns = qkv.shape
    heads = columns // (2 * HEAD_SIZE)
    piece = length // blocks
    head = lambda part: pl.BlockSpec(
        (length, HEAD_SIZE), lambda h, s_ref: (0, 4 * (h // 2) + (h % 2 if part == 0 else part))
    )
    return pl.pallas_call(
        functools.partial(forward_kernel, blocks, x_count),
        name="attend",
        out_shape=(
            jax.ShapeDtypeStruct((blocks, piece, heads * HEAD_SIZE), BF16),
            jax.ShapeDtypeStruct((heads, 1, length), F32),
        ),
        grid_spec=pltpu.PrefetchScalarGridSpec(
            num_scalar_prefetch=1,
            grid=(heads,),
            in_specs=[head(0), head(2), head(3)],
            out_specs=[
                pl.BlockSpec((blocks, piece, HEAD_SIZE), lambda h, s_ref: (0, 0, h)),
                pl.BlockSpec((1, 1, length), lambda h, s_ref: (h, 0, 0)),
            ],
        ),
        cost_estimate=pl.CostEstimate(
            flops=2 * heads * length * length * HEAD_SIZE * 2,
            bytes_accessed=2 * heads * length * HEAD_SIZE * 4,
            transcendentals=heads * length * length // 2,
        ),
    )(s, qkv, qkv, qkv)


def head_back(grad, pre, gain, cosine, sine):
    turned = grad * cosine - pltpu.roll(grad, HEAD_SIZE // 2, 1) * sine
    scale = rms_scale(pre)
    part = turned * gain
    result = scale * part - pre * (scale * scale * scale * jnp.mean(part * pre, axis=-1, keepdims=True))
    return result, jnp.sum(turned * pre * scale, axis=0, keepdims=True)


def backward_kernel(
    blocks, x_count, s_ref, q_ref, k_ref, v_ref, do_ref, log_ref, qp_ref, kp_ref, qg_ref, kg_ref,
    cos_ref, sin_ref, grad_ref, qgain_ref, kgain_ref, dk_ref, dv_ref,
):
    piece = q_ref.shape[0] // blocks
    second = pl.program_id(1)

    @pl.when((pl.program_id(0) == 0) & (second == 0))
    def _():
        qgain_ref[...] = jnp.zeros_like(qgain_ref)
        kgain_ref[...] = jnp.zeros_like(kgain_ref)

    @pl.when(second == 0)
    def _():
        dk_ref[...] = jnp.zeros_like(dk_ref)
        dv_ref[...] = jnp.zeros_like(dv_ref)

    keys_t = k_ref[...].T
    column = pl.ds(pl.multiple_of(second * HEAD_SIZE, HEAD_SIZE), HEAD_SIZE)
    for i in range(blocks):
        rows = slice(i * piece, (i + 1) * piece)
        end = (i + 1) * piece
        at = place(i, s_ref[0], x_count)
        query = q_ref[rows, :]
        grad_out = do_ref[at]
        probs, _ = masked_exp(k_ref, query, i, piece, log_ref[0, :, rows])
        dv_ref[:end, :] += dot(probs.astype(BF16), grad_out)
        grad_probs = dot_t(v_ref[:end, :], grad_out)
        inner = jnp.sum(probs * grad_probs, axis=0, keepdims=True)
        grad_scores = (probs * (grad_probs - inner)).astype(BF16)
        dk_ref[:end, :] += dot(grad_scores, query)
        grad_query = dot(keys_t[:, :end], grad_scores).T * SCALE
        result, gain = head_back(grad_query, qp_ref[rows, :], qg_ref[...], cos_ref[rows, :], sin_ref[rows, :])
        grad_ref[at, :, column] = result.astype(BF16)
        qgain_ref[...] += gain

    @pl.when(second == 1)
    def _():
        for i in range(blocks):
            rows = slice(i * piece, (i + 1) * piece)
            at = place(i, s_ref[0], x_count)
            result, gain = head_back(
                dk_ref[rows, :] * SCALE, kp_ref[rows, :], kg_ref[...], cos_ref[rows, :], sin_ref[rows, :]
            )
            grad_ref[at, :, 2 * HEAD_SIZE : 3 * HEAD_SIZE] = result.astype(BF16)
            grad_ref[at, :, 3 * HEAD_SIZE :] = dv_ref[rows, :].astype(BF16)
            kgain_ref[...] += gain


def attend_back(s, qkv, pre, log_total, grad_mixed, query_gain, key_gain, cosine, sine, blocks, x_count):
    length, columns = qkv.shape
    heads_kv = columns // (4 * HEAD_SIZE)
    piece = length // blocks
    head = lambda part: pl.BlockSpec(
        (length, HEAD_SIZE), lambda j, g, s_ref: (0, 4 * j + (g if part == 0 else part))
    )
    pre_head = lambda part: pl.BlockSpec(
        (length, HEAD_SIZE), lambda j, g, s_ref: (0, 3 * j + (g if part == 0 else part))
    )
    whole = lambda shape: pl.BlockSpec(shape, lambda j, g, s_ref: (0,) * len(shape))
    return pl.pallas_call(
        functools.partial(backward_kernel, blocks, x_count),
        name="attend_back",
        out_shape=(
            jax.ShapeDtypeStruct((blocks, piece, columns), BF16),
            jax.ShapeDtypeStruct((1, HEAD_SIZE), F32),
            jax.ShapeDtypeStruct((1, HEAD_SIZE), F32),
        ),
        grid_spec=pltpu.PrefetchScalarGridSpec(
            num_scalar_prefetch=1,
            grid=(heads_kv, 2),
            in_specs=[
                head(0),
                head(2),
                head(3),
                pl.BlockSpec((blocks, piece, HEAD_SIZE), lambda j, g, s_ref: (0, 0, 2 * j + g)),
                pl.BlockSpec((1, 1, length), lambda j, g, s_ref: (2 * j + g, 0, 0)),
                pre_head(0),
                pre_head(2),
                whole((1, HEAD_SIZE)),
                whole((1, HEAD_SIZE)),
                whole((length, HEAD_SIZE)),
                whole((length, HEAD_SIZE)),
            ],
            out_specs=[
                pl.BlockSpec((blocks, piece, 4 * HEAD_SIZE), lambda j, g, s_ref: (0, 0, j)),
                whole((1, HEAD_SIZE)),
                whole((1, HEAD_SIZE)),
            ],
            scratch_shapes=[pltpu.VMEM((length, HEAD_SIZE), F32), pltpu.VMEM((length, HEAD_SIZE), F32)],
        ),
        cost_estimate=pl.CostEstimate(
            flops=2 * 2 * heads_kv * length * length * HEAD_SIZE * 5 // 2,
            bytes_accessed=2 * heads_kv * length * HEAD_SIZE * 24,
            transcendentals=heads_kv * length * length,
        ),
    )(s, qkv, qkv, qkv, grad_mixed, log_total, pre, pre, query_gain, key_gain, cosine, sine)


MESH = pl.DeviceIdType.MESH


def flip(index, bit):
    step = 1 << bit
    return index + step - 2 * step * lax.rem(lax.div(index, step), 2)


def bit_of(index, bit):
    return lax.rem(lax.div(index, 1 << bit), 2)


class Links:
    def __init__(self, send, recv):
        self.send, self.recv = send, recv
        self.d, self.s = lax.axis_index("dp"), lax.axis_index("seq")
        self.used = 0
        self.started = []

    def slots(self, n):
        self.used += n
        return self.used - n

    def copy(self, src, dst, slot, **to):
        return pltpu.make_async_remote_copy(
            src_ref=src,
            dst_ref=dst,
            send_sem=self.send.at[slot],
            recv_sem=self.recv.at[slot],
            device_id=to,
            device_id_type=MESH,
        )

    def plan(self, src, dst, slot, when=None, **to):
        copy = self.copy(src, dst, slot, **to)
        self.started.append((copy, when))
        return copy

    def start(self, src, dst, slot, when=None, **to):
        copy = self.plan(src, dst, slot, when, **to)
        if when is None:
            copy.start()
        else:
            pl.when(when)(copy.start)
        return copy

    def finish(self):
        for copy, when in self.started:
            if when is None:
                copy.wait_send()
            else:
                pl.when(when)(copy.wait_send)

    def greet(self, dp_masks, seq_masks):
        barrier = pltpu.get_barrier_semaphore()
        for mask in dp_masks:
            pl.semaphore_signal(
                barrier, inc=1, device_id={"dp": self.dp_at(mask)}, device_id_type=MESH
            )
        for mask in seq_masks:
            pl.semaphore_signal(
                barrier, inc=1, device_id={"seq": self.seq_at(mask)}, device_id_type=MESH
            )
        pl.semaphore_wait(barrier, len(dp_masks) + len(seq_masks))

    def seq_at(self, mask):
        s = self.s
        for bit in range(2):
            if mask >> bit & 1:
                s = flip(s, bit)
        return s

    def dp_at(self, mask):
        d = self.d
        for bit in range(3):
            if mask >> bit & 1:
                d = flip(d, bit)
        return d


class Gather:
    def __init__(self, links, block):
        base = links.slots(8)
        self.copies = {}
        for r, mask in ((0, 1), (0, 2), (0, 4), (2, 1), (4, 2), (4, 1), (6, 1)):
            src = block(links.dp_at(r))
            self.copies[r | mask] = links.plan(src, src, base + (r | mask), dp=links.dp_at(mask))

    def got(self, r):
        self.copies[r].wait_recv()

    def first(self):
        for mask in (4, 2, 1):
            self.copies[mask].start()

    def relay(self, r):
        self.got(r)
        if r == 4:
            self.copies[6].start()
        self.copies[r | 1].start()

    def last(self):
        for r in (1, 3, 5, 7):
            self.got(r)


def first_kernel(
    heads,
    a_ref, c_ref, out_ref, down_ref, x_ref, g_ref, gains_ref, qg_ref, kg_ref, cos_ref, sin_ref,
    xr_ref, gr_ref, wa_ref, wc_ref, wo_ref, wd_ref, n_ref, qkv_ref, pre_ref, o_ref, residual_ref, log_ref, gain_ref,
    w_v, x_v, n_v, qkv_v, pre_v, o_v, got_v, wo_v, res_v, core_s, core_r, far_s, far_r, send, recv, local,
):
    links = Links(send, recv)
    d, s = links.d, links.s
    sequences, piece, width = x_ref.shape
    blocks = xr_ref.shape[1]
    half = blocks // 2
    length = blocks * piece
    x_bit, core = bit_of(s, 1), bit_of(s, 0)
    z1, z0, y = bit_of(d, 2), bit_of(d, 1), bit_of(d, 0)
    place_of = lambda i: lax.rem((i & 1) + core, 2) * 2 + lax.rem((i >> 1) + x_bit, 2)
    local_used = [0]
    locals_ = {}

    def near(name, src, dst):
        copy = pltpu.make_async_copy(src, dst, local.at[local_used[0]])
        local_used[0] += 1
        copy.start()
        locals_[name] = copy

    links.greet((1, 2, 4), (1, 2, 3))

    def exchange(src, dst):
        base = links.slots(4)
        return [
            links.start(src.at[links.seq_at(k)], dst.at[d, s], base + k, seq=links.seq_at(k))
            for k in (2, 3, 1)
        ]

    gain_slots = links.slots(4)
    gain_own = [
        links.start(gains_ref, got_v.at[d, s], gain_slots + k, seq=links.seq_at(k)) for k in (2, 3, 1)
    ]
    got_v[d, s] = gains_ref[...]
    a_own = exchange(a_ref, wa_ref)
    near("a", a_ref.at[s], wa_ref.at[d, s])

    x_slots, g_slots = links.slots(3 * sequences), links.slots(3 * sequences)

    def spread(own, everywhere, base, n):
        copies = [
            links.start(own.at[n], everywhere.at[n, k], base + 3 * n + k - 1, seq=links.seq_at(3 - k))
            for k in (1, 2)
        ]
        onward = links.plan(everywhere.at[n, 1], everywhere.at[n, 3], base + 3 * n + 2, seq=links.seq_at(1))
        return copies + [onward]

    def pass_on(copies):
        copies[0].wait_recv()
        copies[2].start()

    across, beside = lax.rem(x_bit + y, 2), lax.rem(core + z0, 2)
    out_slots = links.slots(7)
    holder = (across == 0) & (beside == 0)
    out_first = [
        links.start(
            out_ref, wo_ref.at[z1, s], out_slots + k,
            when=(across == k >> 1) & (beside == (k & 1)), seq=links.seq_at(k),
        )
        for k in (1, 2, 3)
    ]
    x_copies = [spread(x_ref, xr_ref, x_slots, 0)]
    c_own = exchange(c_ref, wc_ref)
    near("c", c_ref.at[s], wc_ref.at[d, s])
    for n in range(sequences):
        near(f"x{n}", x_ref.at[n], xr_ref.at[n, 0])
    near("d", down_ref, wd_ref.at[d])
    x_copies += [spread(x_ref, xr_ref, x_slots, n) for n in range(1, sequences)]

    for copy in gain_own + a_own:
        copy.wait_recv()
    locals_["a"].wait()
    gather_a, gather_c, gather_d, gather_gain = (
        Gather(links, lambda at, ref=ref: ref.at[at]) for ref in (wa_ref, wc_ref, wd_ref, got_v)
    )
    out_y = links.plan(wo_ref.at[z1], wo_ref.at[z1], out_slots + 4, when=holder, dp=flip(d, 0))
    out_z1 = links.plan(wo_ref.at[z1], wo_ref.at[z1], out_slots + 5, when=beside == 0, dp=flip(d, 2))
    out_z0 = links.plan(wo_ref, wo_ref, out_slots + 6, when=beside == 0, dp=flip(d, 1))

    def out_next():
        pl.when((across == 1) & (beside == 0))(out_y.wait_recv)
        pl.when(beside == 0)(out_z1.start)

    def out_last():
        @pl.when(beside == 0)
        def _():
            out_z1.wait_recv()
            out_z0.start()

    gather_gain.first()
    gather_a.first()

    @pl.when(holder)
    def _():
        own = pltpu.make_async_copy(out_ref, wo_ref.at[z1, s], local.at[local_used[0]])
        own.start()
        for copy in out_first:
            copy.wait_recv()
        own.wait()
        out_y.start()

    local_used[0] += 1
    for r in (2, 4, 6):
        gather_gain.relay(r)
    pass_on(x_copies[0])
    gather_a.relay(2)
    out_next()
    gather_a.relay(4)
    for copy in c_own:
        copy.wait_recv()
    locals_["c"].wait()
    gather_c.first()
    gather_a.relay(6)
    g_copies = [spread(g_ref, gr_ref, g_slots, n) for n in range(sequences)]
    for n in range(sequences):
        near(f"g{n}", g_ref.at[n], gr_ref.at[n, 0])
    locals_["d"].wait()
    gather_d.first()

    def wait_x(n):
        locals_[f"x{n}"].wait()
        for copy in x_copies[n][1:]:
            copy.wait_recv()
        near(f"xv{n}", xr_ref.at[n], x_v.at[n])
        locals_[f"xv{n}"].wait()

    def project_part(n, meanwhile=()):
        def step(i, carry):
            for k, action in enumerate(meanwhile):
                pl.when(i == k)(action)
            at = place_of(i)
            x = x_v[n, at].astype(F32)
            normed = (x * rms_scale(x) * gain_ref[0:1, :]).astype(BF16)
            n_v[n, at] = normed
            y_rows = dot(normed, w_v[...].reshape(width, -1))
            rows = pl.ds(pl.multiple_of(i * piece, piece), piece)
            cosine, sine = cos_ref[rows, :], sin_ref[rows, :]
            for j in range(heads // 2):
                for part in range(4):
                    cut = slice((4 * j + part) * HEAD_SIZE, (4 * j + part + 1) * HEAD_SIZE)
                    head = y_rows[:, cut]
                    if part < 3:
                        pre_v[n, rows, (3 * j + part) * HEAD_SIZE : (3 * j + part + 1) * HEAD_SIZE] = head
                        gain = qg_ref[...] if part < 2 else kg_ref[...]
                        head = head * rms_scale(head) * gain
                        head = head * cosine + pltpu.roll(head, HEAD_SIZE // 2, 1) * sine
                    qkv_v[n, rows, cut] = head.astype(BF16)
            return carry

        lax.fori_loop(0, blocks, step, 0)
        near(f"n{n}", n_v.at[n], n_ref.at[n])
        near(f"qkv{n}", qkv_v.at[n], qkv_ref.at[n])
        near(f"pre{n}", pre_v.at[n], pre_ref.at[n])

    def attend_part(n, meanwhile=()):
        def step(h, carry):
            for k, action in enumerate(meanwhile):
                pl.when(h == k)(action)
            j, g = lax.div(h, 2), lax.rem(h, 2)
            lanes = lambda at: pl.ds(pl.multiple_of(at * HEAD_SIZE, HEAD_SIZE), HEAD_SIZE)
            values_t = qkv_v[n, :, lanes(4 * j + 3)].T
            keys = qkv_v.at[n, :, lanes(4 * j + 2)]
            for i in range(blocks):
                query = qkv_v[n, i * piece : (i + 1) * piece, lanes(4 * j + g)]
                exponent, highest = masked_exp(keys, query, i, piece, None)
                total = jnp.sum(exponent, axis=0, keepdims=True)
                probs = (exponent * (1.0 / total)).astype(BF16)
                mixed = dot(values_t[:, : (i + 1) * piece], probs)
                o_v[n, place_of(i), :, lanes(h)] = mixed.T.astype(BF16)
                log_ref[n, h, :, i * piece : (i + 1) * piece] = highest + jnp.log(total)
            return carry

        lax.fori_loop(0, heads, step, 0)

    wait_x(0)
    gather_a.last()
    near("w", wa_ref, w_v)
    locals_["w"].wait()

    gather_gain.last()
    for at in range(got_v.shape[0]):
        gain_ref[:, at * 128 : (at + 1) * 128] = jnp.sum(got_v[at], axis=0)

    core_slots, far_slots = links.slots(half * sequences), links.slots(half * sequences)
    core_copies = {
        (n, k): links.plan(core_s.at[n, k], core_r.at[n, k], core_slots + half * n + k, seq=links.seq_at(1))
        for n in range(sequences)
        for k in range(half)
    }
    far_copies = {
        (n, k): links.plan(far_s.at[n, k], far_r.at[n, half - 1 - k], far_slots + half * n + k, seq=links.seq_at(2))
        for n in range(sequences)
        for k in range(half)
    }

    def out_part(n):
        if n == 0:
            pl.when(beside == 1)(out_z0.wait_recv)
            near("wo", wo_ref, wo_v)
            locals_["wo"].wait()

        def step(i, carry):
            b = lax.rem(i + half, blocks)
            part = dot(o_v[n, b], wo_v[...].reshape(-1, width))
            for k in range(half):

                @pl.when(i == k)
                def _():
                    core_s[n, k] = part.astype(BF16)
                    core_copies[n, k].start()

                @pl.when(i == half + k)
                def _():
                    core_copies[n, k].wait_recv()
                    total = part + core_r[n, k].astype(F32)
                    res_v[n, k] = total
                    far_s[n, k] = total.astype(BF16)
                    far_copies[n, k].start()

            return carry

        lax.fori_loop(0, blocks, step, 0)

    def residual(n):
        for k in range(half):
            far_copies[n, half - 1 - k].wait_recv()
            res_v[n, k] = res_v[n, k] + far_r[n, k].astype(F32) + x_v[n, k].astype(F32)
        near(f"res{n}", res_v.at[n], residual_ref.at[n])

    nothing = lambda: None
    project_part(0, [nothing, lambda: gather_c.relay(2), lambda: pass_on(x_copies[1]), out_last])
    attend_part(0, [lambda: gather_c.relay(4)])
    near("o0", o_v.at[0], o_ref.at[0])
    for n in range(1, sequences):
        wait_x(n)
        out_part(n - 1)
        project_part(n, [lambda: gather_c.relay(6), nothing, lambda: pass_on(g_copies[0])])
        attend_part(n, [nothing, nothing, lambda: pass_on(g_copies[1])])
        near(f"o{n}", o_v.at[n], o_ref.at[n])
    out_part(sequences - 1)
    for r in (2, 4, 6):
        gather_d.relay(r)
    for n in range(sequences):
        residual(n)
    gather_c.last()
    gather_d.last()
    for pair in g_copies:
        for copy in pair[1:]:
            copy.wait_recv()
    for n in range(sequences):
        for name in ("g", "n", "qkv", "pre", "o", "res"):
            locals_[f"{name}{n}"].wait()
    links.finish()


def first(a, c, w_out, w_down, x, g, gains, query_gain, key_gain, cosine, sine, dp, heads):
    blocks, rows, columns = a.shape
    sequences, piece, width = x.shape
    length = blocks * piece
    hbm = pl.BlockSpec(memory_space=pl.ANY)
    vmem = pl.BlockSpec(memory_space=pltpu.VMEM)
    shape = jax.ShapeDtypeStruct
    pre_columns = columns // 4 * 3
    slots = 96
    return pl.pallas_call(
        functools.partial(first_kernel, heads),
        name="first",
        out_shape=(
            shape((sequences, blocks, piece, width), BF16),
            shape((sequences, blocks, piece, width), BF16),
            shape((dp, blocks, rows, columns), BF16),
            shape((dp, blocks, rows, c.shape[2]), BF16),
            shape((2, blocks) + w_out.shape, BF16),
            shape((dp,) + w_down.shape, BF16),
            shape((sequences, blocks, piece, width), BF16),
            shape((sequences, length, columns), BF16),
            shape((sequences, length, pre_columns), F32),
            shape((sequences, blocks, piece, heads * HEAD_SIZE), BF16),
            shape((sequences, blocks // 2, piece, width), F32),
            shape((sequences, heads, 1, length), F32),
            shape((8, width), F32),
        ),
        in_specs=[vmem] * 11,
        out_specs=[hbm] * 11 + [vmem] * 2,
        scratch_shapes=[
            pltpu.VMEM((dp, blocks, rows, columns), BF16),
            pltpu.VMEM((sequences, blocks, piece, width), BF16),
            pltpu.VMEM((sequences, blocks, piece, width), BF16),
            pltpu.VMEM((sequences, length, columns), BF16),
            pltpu.VMEM((sequences, length, pre_columns), F32),
            pltpu.VMEM((sequences, blocks, piece, heads * HEAD_SIZE), BF16),
            pltpu.VMEM((dp, blocks, 8, width // dp), F32),
            pltpu.VMEM((2, blocks) + w_out.shape, BF16),
            pltpu.VMEM((sequences, blocks // 2, piece, width), F32),
            pltpu.VMEM((sequences, blocks // 2, piece, width), BF16),
            pltpu.VMEM((sequences, blocks // 2, piece, width), BF16),
            pltpu.VMEM((sequences, blocks // 2, piece, width), BF16),
            pltpu.VMEM((sequences, blocks // 2, piece, width), BF16),
            pltpu.SemaphoreType.DMA((slots,)),
            pltpu.SemaphoreType.DMA((slots,)),
            pltpu.SemaphoreType.DMA((32,)),
        ],
        compiler_params=pltpu.CompilerParams(
            collective_id=0, has_side_effects=True, vmem_limit_bytes=60 * 1024 * 1024
        ),
    )(a, c, w_out, w_down, x, g, gains, query_gain, key_gain, cosine, sine)


def mlp_kernel(
    res_ref, wc_ref, wd_ref, g_ref, gain_ref,
    own_ref, far_ref, residual_ref, branch_ref, down_ref, mlp_ref, gain_grad_ref,
    core_s, x_s, n2_v, hidden_v, both_v, dc_v, dg_v, da_v, us_v, uc_v, ux_v, ua_v,
    send, recv, local,
):
    links = Links(send, recv)
    sequences, blocks, piece, width = g_ref.shape
    half = blocks // 2
    units = wd_ref.shape[0]
    core, far = dict(seq=links.seq_at(1)), dict(seq=links.seq_at(2))
    pairs = [(n, k) for n in range(sequences) for k in range(half)]
    slots = {
        name: links.slots(half * sequences)
        for name in ("normed", "grad_core", "up_core", "grad_far", "branch")
    }
    ends = {
        "normed": lambda n, k: (n2_v.at[n, k], n2_v.at[n, half + k], core),
        "grad_core": lambda n, k: (core_s.at[n, k], dc_v.at[n, k], core),
        "up_core": lambda n, k: (us_v.at[n, k], uc_v.at[n, k], core),
        "grad_far": lambda n, k: (x_s.at[n, k], dg_v.at[n, half - 1 - k], far),
        "branch": lambda n, k: (us_v.at[n, k], branch_ref.at[n, half + k], core),
    }

    def copy(name, n, k):
        src, dst, to = ends[name](n, k)
        return links.copy(src, dst, slots[name] + half * n + k, **to)

    def arrived(name, n, k):
        copy(name, n, half - 1 - k if name == "grad_far" else k).wait_recv()

    near_copies = []

    def near(src, dst):
        made = pltpu.make_async_copy(src, dst, local.at[len(near_copies)])
        made.start()
        near_copies.append(made)

    links.greet((), (1, 2))
    gain = gain_ref[...]

    def norm(n):
        for k in range(half):
            residual = res_ref[n, k]
            n2_v[n, k] = (residual * rms_scale(residual) * gain).astype(BF16)
            copy("normed", n, k).start()

    def feed(n):
        for k in range(half):
            arrived("normed", n, k)

        def step(i, carry):
            b = lax.rem(i + half, blocks)
            both = dot(n2_v[n, b], wc_ref[...])
            gate, upward = both[:, :units], both[:, units:]
            grad_hidden = dot_t(g_ref[n, b], wd_ref[...])
            sigmoid = 1.0 / (1.0 + jnp.exp(-gate))
            silu = gate * sigmoid
            hidden_v[n, b] = (silu * upward).astype(BF16)
            both_v[n, b, :, units:] = (grad_hidden * silu).astype(BF16)
            both_v[n, b, :, :units] = (
                grad_hidden * upward * sigmoid * (1.0 + gate * (1.0 - sigmoid))
            ).astype(BF16)
            grad = dot_t(both_v[n, b], wc_ref[...])

            @pl.when(i < half)
            def _():
                core_s[n, i] = grad.astype(BF16)
                copy("grad_core", n, i).start()

            @pl.when(i >= half)
            def _():
                k = i - half
                arrived_core = copy("grad_core", n, k)
                arrived_core.wait_recv()
                total = grad + dc_v[n, k].astype(F32)
                da_v[n, k] = total
                x_s[n, k] = total.astype(BF16)
                copy("grad_far", n, k).start()

            up = dot(hidden_v[n, b], wd_ref[...])

            @pl.when(i < half)
            def _():
                us_v[n, i] = up.astype(BF16)
                copy("up_core", n, i).start()

            @pl.when(i >= half)
            def _():
                copy("up_core", n, i - half).wait_recv()

            @pl.when(i == half)
            def _():
                ua_v[n] = res_ref[n, 0] + (up + uc_v[n, 0].astype(F32))

            @pl.when(i == half + 1)
            def _():
                ux_v[n] = (up + uc_v[n, 1].astype(F32)).astype(BF16)

            return carry

        lax.fori_loop(0, blocks, step, 0)
        near(ua_v.at[n], own_ref.at[n])
        near(ux_v.at[n], far_ref.at[n])

    def back(n):
        for k in range(half):
            copy("up_core", n, k).wait_send()
        for k in range(half):
            arrived("grad_far", n, k)
            grad = da_v[n, k] + dg_v[n, k].astype(F32)
            residual = res_ref[n, k]
            scale = rms_scale(residual)
            scaled = grad * gain
            grad_residual = (
                g_ref[n, k].astype(F32)
                + scale * scaled
                - residual * (scale * scale * scale * jnp.mean(scaled * residual, axis=-1, keepdims=True))
            )
            us_v[n, k] = grad_residual.astype(BF16)
            copy("branch", n, k).start()
            near(us_v.at[n, k], branch_ref.at[n, k])
            if k == 0:
                part = jnp.sum(grad * residual * scale, axis=0, keepdims=True)
                gain_grad_ref[...] = part if n == 0 else gain_grad_ref[...] + part
                da_v[n, 0] = grad_residual
                near(da_v.at[n, 0], residual_ref.at[n])

    def weight_grads():
        chunk = 2 * width // 8
        flat = lambda value: value.reshape(-1, value.shape[-1])

        def rows(left_v, right, out):
            def step(m, carry):
                cut = pl.ds(pl.multiple_of(m * chunk, chunk), chunk)
                total = None
                for n in range(sequences):
                    term = t_dot(flat(left_v[n, :, :, cut]), flat(right[n]))
                    total = term if total is None else total + term
                out[cut, :] = total.astype(BF16)
                return carry

            lax.fori_loop(0, out.shape[0] // chunk, step, 0)

        rows(hidden_v, g_ref, down_ref)
        rows(n2_v, both_v, mlp_ref)

    for n in range(sequences):
        norm(n)
    for n in range(sequences):
        feed(n)
    for n in range(sequences - 1):
        back(n)
    weight_grads()
    back(sequences - 1)
    for n, k in pairs:
        arrived("branch", n, k)
    for n, k in pairs:
        for name in ("normed", "grad_core", "grad_far", "branch"):
            copy(name, n, k).wait_send()
    for made in near_copies:
        made.wait()


def feed_forward(residual, w_mlp, w_d, g_rel, gain):
    sequences, blocks, piece, width = g_rel.shape
    half = blocks // 2
    units = w_d.shape[0]
    hbm = pl.BlockSpec(memory_space=pl.ANY)
    vmem = pl.BlockSpec(memory_space=pltpu.VMEM)
    shape = jax.ShapeDtypeStruct
    part = lambda dtype: pltpu.VMEM((sequences, half, piece, width), dtype)
    one = lambda dtype: pltpu.VMEM((sequences, piece, width), dtype)
    return pl.pallas_call(
        mlp_kernel,
        name="feed_forward",
        out_shape=(
            shape((sequences, piece, width), F32),
            shape((sequences, piece, width), BF16),
            shape((sequences, piece, width), F32),
            shape((sequences, blocks, piece, width), BF16),
            shape((units, width), BF16),
            shape((width, 2 * units), BF16),
            shape((1, width), F32),
        ),
        in_specs=[vmem] * 5,
        out_specs=[hbm] * 4 + [vmem] * 3,
        scratch_shapes=[
            part(BF16),
            part(BF16),
            pltpu.VMEM((sequences, blocks, piece, width), BF16),
            pltpu.VMEM((sequences, blocks, piece, units), BF16),
            pltpu.VMEM((sequences, blocks, piece, 2 * units), BF16),
            part(BF16),
            part(BF16),
            part(F32),
            part(BF16),
            part(BF16),
            one(BF16),
            one(F32),
            pltpu.SemaphoreType.DMA((16 * sequences,)),
            pltpu.SemaphoreType.DMA((16 * sequences,)),
            pltpu.SemaphoreType.DMA((16,)),
        ],
        compiler_params=pltpu.CompilerParams(
            collective_id=1, has_side_effects=True, vmem_limit_bytes=67043328
        ),
    )(residual, w_mlp, w_d, g_rel, gain)


class Scatter:
    def __init__(self, links, src, first, second, third, done=None):
        d = links.d
        self.z1, self.z0, self.y = bit_of(d, 2), bit_of(d, 1), bit_of(d, 0)
        self.src, self.first, self.second, self.third = src, first, second, third
        base = links.slots(7)
        self.over_y = links.plan(src.at[:, :, 1 - self.y], first, base, dp=flip(d, 0))
        self.over_z0 = links.plan(first.at[:, 1 - self.z0], second, base + 1, dp=flip(d, 1))
        self.over_z1 = links.plan(second.at[1 - self.z1], third, base + 2, dp=flip(d, 2))
        self.done, self.s = done, links.s
        if done is not None:
            self.share = [
                links.plan(third.at[links.seq_at(k)], done.at[links.s], base + 3 + k, seq=links.seq_at(k))
                for k in (2, 3, 1)
            ]

    def start(self):
        self.over_y.start()

    def sum_y(self):
        self.over_y.wait_recv()

        def step(i, carry):
            a, b = lax.div(i, 2), lax.rem(i, 2)
            mine = self.src[a, b, self.y].astype(F32)
            self.first[a, b] = (mine + self.first[a, b].astype(F32)).astype(BF16)
            return carry

        lax.fori_loop(0, 4, step, 0)
        self.over_z0.start()

    def sum_z0(self):
        self.over_z0.wait_recv()

        def step(a, carry):
            mine = self.first[a, self.z0].astype(F32)
            self.second[a] = (mine + self.second[a].astype(F32)).astype(BF16)
            return carry

        lax.fori_loop(0, 2, step, 0)
        self.over_z1.start()

    def sum_z1(self):
        self.over_z1.wait_recv()
        mine = self.second[self.z1].astype(F32)
        self.third[...] = (mine + self.third[...].astype(F32)).astype(BF16)
        if self.done is not None:
            for copy in self.share:
                copy.start()
            self.done[self.s] = self.third[self.s]

    def end(self):
        for copy in self.share:
            copy.wait_recv()


def last_kernel(
    down_ref, mlp_ref, og_ref, branch_ref, wo_ref, qkv_ref, pre_ref, log_ref, w_ref, normed_ref,
    x_ref, residual_ref, up_ref, gain_ref, mlp_gain_ref, qg_ref, kg_ref, cos_ref, sin_ref,
    up_out, tokens_ref, down_out, mlp_out, out_out, in_out, sums_ref,
    d1, d2, c1, c2, c3, o1, o2, o3, a_v, a1, a2, a3,
    do_v, gr_v, dk_v, dv_v, core_s, core_r, far_s, far_r, acc_v, total_v, got_v,
    send, recv, local,
):
    links = Links(send, recv)
    d, s = links.d, links.s
    sequences, blocks, piece, width = branch_ref.shape
    half = blocks // 2
    heads = log_ref.shape[1]
    heads_kv = heads // 2
    x_bit, core = bit_of(s, 1), bit_of(s, 0)
    z1, z0, y = bit_of(d, 2), bit_of(d, 1), bit_of(d, 0)
    place_of = lambda i: lax.rem((i & 1) + core, 2) * 2 + lax.rem((i >> 1) + x_bit, 2)
    across, beside = lax.rem(x_bit + y, 2), lax.rem(core + z0, 2)
    holder = (across == 0) & (beside == 0)
    lanes = lambda at: pl.ds(pl.multiple_of(at * HEAD_SIZE, HEAD_SIZE), HEAD_SIZE)
    nothing = lambda: None

    down = Scatter(links, down_ref, d1, d2, down_out)
    mlp = Scatter(links, mlp_ref, c1, c2, c3, mlp_out)
    ins = [
        Scatter(links, a_v.at[j], a1.at[j], a2.at[j], a3.at[j], in_out.at[j]) for j in range(heads_kv)
    ]
    base = links.slots(7)
    out_z0 = links.plan(og_ref, o1, base, when=beside == 1, dp=flip(d, 1))
    out_z1 = links.plan(o1.at[1 - z1], o2, base + 1, when=beside == 0, dp=flip(d, 2))
    out_y = links.plan(o2, o3, base + 2, when=(beside == 0) & (across == 1), dp=flip(d, 0))
    out_share = {
        k: links.plan(o3.at[links.seq_at(k)], out_out, base + 3 + k, when=holder, seq=links.seq_at(k))
        for k in (1, 2, 3)
    }

    def out_sum_z0():
        @pl.when(beside == 0)
        def _():
            out_z0.wait_recv()

            def step(i, carry):
                a, b = lax.div(i, blocks), lax.rem(i, blocks)
                o1[a, b] = (og_ref[a, b].astype(F32) + o1[a, b].astype(F32)).astype(BF16)
                return carry

            lax.fori_loop(0, 2 * blocks, step, 0)
            out_z1.start()

    def out_sum_z1():
        @pl.when(beside == 0)
        def _():
            out_z1.wait_recv()

            def step(b, carry):
                o2[b] = (o1[z1, b].astype(F32) + o2[b].astype(F32)).astype(BF16)
                return carry

            lax.fori_loop(0, blocks, step, 0)

        pl.when((beside == 0) & (across == 1))(out_y.start)

    def out_sum_y():
        @pl.when(holder)
        def _():
            out_y.wait_recv()

            def step(b, carry):
                o3[b] = (o2[b].astype(F32) + o3[b].astype(F32)).astype(BF16)
                return carry

            lax.fori_loop(0, blocks, step, 0)
            for copy in out_share.values():
                copy.start()
            out_out[...] = o3[s]

    links.greet((1, 2, 4), (1, 2, 3))
    upper = pltpu.make_async_copy(residual_ref, tokens_ref, local.at[0])
    upper.start()
    up_slot = links.slots(1)
    up_copy = links.start(up_ref, up_out, up_slot, seq=links.seq_at(2))
    mlp.start()
    down.start()
    pl.when(beside == 1)(out_z0.start)
    total_v[0] = jnp.zeros_like(total_v[0])
    for r in range(width // 128):
        total_v[0, 8 + r : 9 + r, :] = mlp_gain_ref[:, r * 128 : (r + 1) * 128]

    def mixed_back(i, carry):
        n, b = lax.div(i, blocks), lax.rem(i, blocks)
        do_v[n, b] = dot_t(branch_ref[n, b], wo_ref[...]).astype(BF16)
        return carry

    lax.fori_loop(0, sequences * blocks, mixed_back, 0)

    slots = [links.slots(half * sequences), links.slots(sequences)]
    core_copies = {
        (n, k): links.plan(core_s.at[n, k], core_r.at[n, k], slots[0] + half * n + k, seq=links.seq_at(1))
        for n in range(sequences)
        for k in range(half)
    }
    far_copies = [
        links.plan(far_s.at[n], far_r.at[n], slots[1] + n, seq=links.seq_at(2)) for n in range(sequences)
    ]

    def input_part(n):
        def step(i, carry):
            b = lax.rem(i + half, blocks)
            grad = dot_t(gr_v[n, b], w_ref[...])
            for k in range(half):

                @pl.when(i == k)
                def _():
                    core_s[n, k] = grad.astype(BF16)
                    core_copies[n, k].start()

                @pl.when(i == half + k)
                def _():
                    core_copies[n, k].wait_recv()
                    total = grad + core_r[n, k].astype(F32)
                    if k == 0:
                        acc_v[n] = total
                    else:
                        far_s[n] = total.astype(BF16)
                        far_copies[n].start()

            return carry

        lax.fori_loop(0, blocks, step, 0)

    def input_end(n):
        far_copies[n].wait_recv()
        grad = acc_v[n] + far_r[n].astype(F32)
        tokens = x_ref[n].astype(F32)
        scale = rms_scale(tokens)
        scaled = grad * gain_ref[...]
        tokens_ref[n] = (
            tokens_ref[n]
            + scale * scaled
            - tokens * (scale * scale * scale * jnp.mean(scaled * tokens, axis=-1, keepdims=True))
        )
        part = jnp.sum(grad * tokens * scale, axis=0, keepdims=True)
        for r in range(width // 128):
            total_v[0, r : r + 1, :] += part[:, r * 128 : (r + 1) * 128]

    def attention(j, meanwhile):
        def step(t, carry):
            for k, action in enumerate(meanwhile):
                pl.when(t == k)(action)
            n, g = lax.div(t, 2), lax.rem(t, 2)

            @pl.when(g == 0)
            def _():
                dk_v[...] = jnp.zeros_like(dk_v)
                dv_v[...] = jnp.zeros_like(dv_v)

            keys, values = qkv_ref.at[n, :, lanes(4 * j + 2)], qkv_ref.at[n, :, lanes(4 * j + 3)]
            keys_t = keys[...].T
            for i in range(blocks):
                rows = slice(i * piece, (i + 1) * piece)
                end = (i + 1) * piece
                at = place_of(i)
                query = qkv_ref[n, rows, lanes(4 * j + g)]
                grad_out = do_v[n, at, :, lanes(2 * j + g)]
                probs, _ = masked_exp(keys, query, i, piece, log_ref[n, 2 * j + g, :, rows])
                dv_v[:end, :] += dot(probs.astype(BF16), grad_out)
                grad_probs = dot_t(values[:end, :], grad_out)
                inner = jnp.sum(probs * grad_probs, axis=0, keepdims=True)
                grad_scores = (probs * (grad_probs - inner)).astype(BF16)
                dk_v[:end, :] += dot(grad_scores, query)
                grad_query = dot(keys_t[:, :end], grad_scores).T * SCALE
                result, gain = head_back(
                    grad_query, pre_ref[n, rows, lanes(3 * j + g)], qg_ref[...], cos_ref[rows, :], sin_ref[rows, :]
                )
                gr_v[n, at, :, lanes(4 * j + g)] = result.astype(BF16)
                total_v[0, 16:17, :] += gain

            @pl.when(g == 1)
            def _():
                for i in range(blocks):
                    rows = slice(i * piece, (i + 1) * piece)
                    at = place_of(i)
                    result, gain = head_back(
                        dk_v[rows, :] * SCALE, pre_ref[n, rows, lanes(3 * j + 2)], kg_ref[...],
                        cos_ref[rows, :], sin_ref[rows, :],
                    )
                    gr_v[n, at, :, lanes(4 * j + 2)] = result.astype(BF16)
                    gr_v[n, at, :, lanes(4 * j + 3)] = dv_v[rows, :].astype(BF16)
                    total_v[0, 17:18, :] += gain

            return carry

        lax.fori_loop(0, 2 * sequences, step, 0)

    def weight_in(j):
        wide = 4 * HEAD_SIZE
        chunk = 2 * width // 8

        def step(m, carry):
            cut = pl.ds(pl.multiple_of(m * chunk, chunk), chunk)
            total = None
            for n in range(sequences):
                left = normed_ref[n, :, :, cut].reshape(blocks * piece, chunk)
                right = gr_v[n, :, :, j * wide : (j + 1) * wide].reshape(blocks * piece, wide)
                term = t_dot(left, right)
                total = term if total is None else total + term
            a_v[j, lax.div(m, 2), lax.rem(m, 2)] = total.astype(BF16).reshape(a_v.shape[3:])
            return carry

        lax.fori_loop(0, width // chunk, step, 0)
        ins[j].start()

    attention(0, [nothing, nothing, out_sum_z0])
    weight_in(0)
    attention(1, [out_sum_z1, mlp.sum_y, lambda: input_part(0)])
    input_part(1)
    weight_in(1)
    down.sum_y()
    mlp.sum_z0()
    upper.wait()
    for n in range(sequences):
        input_end(n)

    gain_slots = links.slots(5)
    gain_to = [dict(seq=links.seq_at(1)), dict(seq=links.seq_at(2))] + [dict(dp=flip(d, b)) for b in range(3)]
    gain_copies = [
        links.plan(total_v.at[k], got_v.at[k], gain_slots + k, **gain_to[k]) for k in range(5)
    ]

    def gain_stage(k):
        gain_copies[k].wait_recv()
        if k == 4:
            sums_ref[...] = total_v[4] + got_v[4]
        else:
            total_v[k + 1] = total_v[k] + got_v[k]
            gain_copies[k + 1].start()

    gain_copies[0].start()
    ins[0].sum_y()
    gain_stage(0)
    down.sum_z0()
    gain_stage(1)
    out_sum_y()
    mlp.sum_z1()
    gain_stage(2)
    ins[0].sum_z0()
    down.sum_z1()
    gain_stage(3)
    ins[0].sum_z1()
    ins[1].sum_y()
    gain_stage(4)
    ins[1].sum_z0()
    ins[1].sum_z1()
    for k, copy in out_share.items():
        pl.when((across == k >> 1) & (beside == (k & 1)))(copy.wait_recv)
    mlp.end()
    up_copy.wait_recv()
    for scatter in ins:
        scatter.end()
    links.finish()


def last(
    down, mlp, out, branch, w_o, qkv, pre, log_total, w_in, normed, x, residual, up,
    gain, mlp_gain_grad, query_gain, key_gain, cosine, sine,
):
    sequences, blocks, piece, width = branch.shape
    length = blocks * piece
    rows, wide = mlp.shape[-2], mlp.shape[-1]
    down_rows = down.shape[-2]
    out_rows = out.shape[-2]
    heads_kv = qkv.shape[-1] // (4 * HEAD_SIZE)
    vmem = pl.BlockSpec(memory_space=pltpu.VMEM)
    shape = jax.ShapeDtypeStruct
    b16 = lambda *dims: pltpu.VMEM(dims, BF16)
    f32 = lambda *dims: pltpu.VMEM(dims, F32)
    hbm = pl.BlockSpec(memory_space=pl.ANY)
    part = (blocks, rows, 4 * HEAD_SIZE)
    return pl.pallas_call(
        last_kernel,
        name="last",
        out_shape=(
            shape(up.shape, up.dtype),
            shape((sequences, piece, width), F32),
            shape((down_rows, width), BF16),
            shape((blocks, rows, wide), BF16),
            shape((out_rows, width), BF16),
            shape((heads_kv,) + part, BF16),
            shape((24, 128), F32),
        ),
        in_specs=[vmem] * 11 + [hbm] * 2 + [vmem] * 6,
        out_specs=[hbm] + [vmem] * 6,
        scratch_shapes=[
            b16(2, 2, down_rows, width),
            b16(2, down_rows, width),
            b16(2, 2, blocks, rows, wide),
            b16(2, blocks, rows, wide),
            b16(blocks, rows, wide),
            b16(2, blocks, out_rows, width),
            b16(blocks, out_rows, width),
            b16(blocks, out_rows, width),
            b16(heads_kv, 2, 2, 2, *part),
            b16(heads_kv, 2, 2, *part),
            b16(heads_kv, 2, *part),
            b16(heads_kv, *part),
            b16(sequences, blocks, piece, 2 * heads_kv * HEAD_SIZE),
            b16(sequences, blocks, piece, width),
            f32(length, HEAD_SIZE),
            f32(length, HEAD_SIZE),
            b16(sequences, blocks // 2, piece, width),
            b16(sequences, blocks // 2, piece, width),
            b16(sequences, piece, width),
            b16(sequences, piece, width),
            f32(sequences, piece, width),
            f32(5, 24, 128),
            f32(5, 24, 128),
            pltpu.SemaphoreType.DMA((64,)),
            pltpu.SemaphoreType.DMA((64,)),
            pltpu.SemaphoreType.DMA((1,)),
        ],
        compiler_params=pltpu.CompilerParams(
            collective_id=2, has_side_effects=True, vmem_limit_bytes=67043328
        ),
    )(
        down, mlp, out, branch, w_o, qkv, pre, log_total, w_in, normed, x, residual, up,
        gain, mlp_gain_grad, query_gain, key_gain, cosine, sine,
    )


def body(
    hidden_in,
    attn_gain,
    w_query,
    key_weight,
    value_weight,
    query_gain,
    key_gain,
    w_out,
    mlp_gain,
    w_gate,
    w_up,
    w_down,
    cotangent,
):
    wires = Wires(lax.axis_size("dp"), lax.axis_size("seq"))
    dp, seq, x_count = wires.dp, wires.seq, wires.x_count
    count = wires.count
    sequences, piece, width = hidden_in.shape
    length = seq * piece
    part = x_count * piece
    heads_kv = key_weight.shape[1] // HEAD_SIZE
    s_index = wires.s.reshape(1).astype(jnp.int32)
    cosine, sine = rope_tables(length)
    query_gain_row = query_gain.astype(F32).reshape(1, -1)
    key_gain_row = key_gain.astype(F32).reshape(1, -1)

    index = wires.d * seq + wires.s
    own_gains = jnp.stack([attn_gain, mlp_gain])
    rows = w_query.shape[0]
    by_head = jnp.concatenate(
        [
            w_query.reshape(rows, heads_kv, -1),
            key_weight.reshape(rows, heads_kv, -1),
            value_weight.reshape(rows, heads_kv, -1),
        ],
        axis=2,
    )
    order = [wires.heads_of(t, heads_kv) for t in range(seq)]
    package_in = jnp.stack(
        [jnp.concatenate([by_head[:, j] for j in order[t]], axis=1) for t in range(seq)]
    )
    down_rows = w_down.shape[0]

    def by_unit(w):
        return w.reshape(rows, dp, seq, down_rows).transpose(2, 0, 1, 3).reshape(seq, rows, -1)

    units = dp * down_rows
    package_mlp = jnp.concatenate([by_unit(w_gate), by_unit(w_up)], axis=2)

    fused = (dp, seq, heads_kv) == (8, 4, 8) and width == 128 * dp and rows % 16 == 0 and down_rows % 16 == 0
    if fused:
        gains = jnp.zeros((8, seq, width // count), F32)
        gains = lax.dynamic_update_slice(gains, own_gains.astype(F32)[:, None], (0, wires.s, 0))
        (
            x_rel, g_rel, w_in, w_mlp, w_o, w_d, all_normed, all_qkv, all_pre, all_mixed, residual, all_log, gains
        ) = first(
            package_in, package_mlp, w_out, w_down, hidden_in, cotangent, gains.reshape(8, -1),
            query_gain_row, key_gain_row, cosine, sine, dp, 2 * heads_kv // seq,
        )
        w_in, w_mlp = w_in.reshape(width, -1), w_mlp.reshape(width, -1)
        w_o, w_d = w_o.reshape(-1, width), w_d.reshape(units, width)
        attn_gain_row, mlp_gain_row = gains[:1], gains[1:2]
        up_own, up_far, all_grad_residual, all_branch, grad_down, grad_mlp, mlp_gain_grad = feed_forward(
            residual, w_mlp, w_d, g_rel, mlp_gain_row
        )
    else:
        gains = jnp.zeros((2, count, width // count), BF16)
        gains = lax.dynamic_update_slice(gains, own_gains[:, None], (0, index, 0))
        gains = wires.sum_all(gains.reshape(2, width)).astype(F32)
        attn_gain_row, mlp_gain_row = gains[:1], gains[1:]
        package = wires.exchange_seq(package_in).reshape(seq * rows, -1)
        w_in = wires.gather_dp(package).reshape(width, -1)
        x_rel = jnp.stack(wires.gather_seq_relative(hidden_in), axis=1)
        w_o = wires.gather_out(w_out, heads_kv)
        package = wires.exchange_seq(package_mlp).reshape(seq * rows, -1)
        w_mlp = wires.gather_dp(package).reshape(width, -1)
        g_rel = jnp.stack(wires.gather_seq_relative(cotangent), axis=1)
        w_d = wires.gather_dp(w_down).reshape(units, width)

    kept = []
    outs = []
    for n in range(0 if fused else sequences):
        normed, qkv, pre = project(
            s_index, x_rel[n], w_in, attn_gain_row, query_gain_row, key_gain_row, cosine, sine, x_count
        )
        mixed, log_total = attend(s_index, qkv, seq, x_count)
        mixed_rows = mixed.reshape(length, -1)
        other = wires.swap(dot(mixed_rows[part:], w_o).astype(BF16), 1)
        total = wires.sum_x(dot(mixed_rows[:part], w_o) + other.astype(F32))
        residual = total + x_rel[n].reshape(length, width)[:part].astype(F32)
        scale = rms_scale(residual)
        normed_mlp = (residual * scale * mlp_gain_row).astype(BF16)
        normed_mlp = jnp.concatenate([normed_mlp, wires.swap(normed_mlp, 1)], axis=0)
        both = dot(normed_mlp, w_mlp)
        gate, upward = both[:, :units], both[:, units:]
        sigmoid = jax.nn.sigmoid(gate)
        silu = gate * sigmoid
        hidden = (silu * upward).astype(BF16)
        other = wires.swap(dot(hidden[part:], w_d).astype(BF16), 1)
        total = wires.scatter_x(dot(hidden[:part], w_d) + other.astype(F32))
        outs.append((residual[:piece] + total).astype(BF16))

        grad_top = g_rel[n].reshape(length, width)
        grad_hidden = dot_t(grad_top, w_d)
        grad_gate = (grad_hidden * upward * sigmoid * (1.0 + gate * (1.0 - sigmoid))).astype(BF16)
        grad_upward = (grad_hidden * silu).astype(BF16)
        grad_both = jnp.concatenate([grad_gate, grad_upward], axis=1)
        other = wires.swap(dot_t(grad_both[part:], w_mlp).astype(BF16), 1)
        grad_normed = wires.sum_x(dot_t(grad_both[:part], w_mlp) + other.astype(F32))
        scaled = grad_normed * mlp_gain_row
        grad_residual = (
            grad_top[:part].astype(F32)
            + scale * scaled
            - residual * (scale * scale * scale * jnp.mean(scaled * residual, axis=-1, keepdims=True))
        )
        grad_mlp_gain = jnp.sum((grad_normed * residual * scale)[:piece], axis=0)
        branch = grad_residual.astype(BF16)
        branch = jnp.concatenate([branch, wires.swap(branch, 1)], axis=0)
        grad_mixed = dot_t(branch, w_o).astype(BF16).reshape(mixed.shape)
        grad_qkv, grad_query_gain, grad_key_gain = attend_back(
            s_index, qkv, pre, log_total, grad_mixed, query_gain_row, key_gain_row, cosine, sine, seq, x_count
        )
        grad_rows = grad_qkv.reshape(length, -1)
        other = wires.swap(dot_t(grad_rows[part:], w_in).astype(BF16), 1)
        grad_first = wires.scatter_x(dot_t(grad_rows[:part], w_in) + other.astype(F32))
        tokens = hidden_in[n].astype(F32)
        scale = rms_scale(tokens)
        scaled = grad_first * attn_gain_row
        grad_tokens = (
            grad_residual[:piece]
            + scale * scaled
            - tokens * (scale * scale * scale * jnp.mean(scaled * tokens, axis=-1, keepdims=True))
        )
        grad_attn_gain = jnp.sum(grad_first * tokens * scale, axis=0)
        kept.append(
            dict(
                normed=normed.reshape(length, width),
                mixed=mixed_rows,
                normed_mlp=normed_mlp,
                hidden=hidden,
                grad_both=grad_both,
                branch=branch,
                grad_rows=grad_rows,
                grad_tokens=grad_tokens,
                gains=jnp.concatenate(
                    [grad_attn_gain, grad_mlp_gain, grad_query_gain[0], grad_key_gain[0]]
                ),
            )
        )

    def from_unit(g):
        return g.reshape(seq, rows, dp, down_rows).transpose(1, 2, 0, 3).reshape(rows, -1)

    if fused:
        flat = lambda value: value.reshape(sequences * length, -1)
        grad_out = t_dot(flat(all_mixed), flat(all_branch)).astype(BF16)
        up, grad_tokens, grad_down, grad_mlp, grad_out, grad_in, gain_sums = last(
            grad_down.reshape(2, 2, 2, down_rows, width),
            grad_mlp.reshape(2, 2, 2, seq, rows, -1),
            grad_out.reshape(2, seq, -1, width),
            all_branch, w_o, all_qkv, all_pre, all_log, w_in, all_normed, hidden_in, all_grad_residual, up_far,
            attn_gain_row, mlp_gain_grad, query_gain_row, key_gain_row, cosine, sine,
        )
        grad_down, grad_mlp, grad_out = grad_down.astype(F32), grad_mlp.astype(F32), grad_out.astype(F32)
        grad_in = grad_in.astype(F32).transpose(1, 2, 0, 3).reshape(seq, rows, -1)
        gain_sums = gain_sums.reshape(-1)[: 2 * width + 2 * HEAD_SIZE]
        hidden_out = (up_own + up.astype(F32)).astype(BF16)
    else:
        def over(name):
            return jnp.concatenate([k[name] for k in kept], axis=0)

        grad_down = t_dot(over("hidden"), g_rel.reshape(-1, width)).astype(BF16)
        grad_down = wires.scatter_dp(grad_down.reshape(dp, down_rows, width)).astype(F32)

        grad_mlp = t_dot(over("normed_mlp"), over("grad_both")).astype(BF16)
        grad_mlp = wires.scatter_dp(grad_mlp.reshape(dp, seq * rows, -1))
        grad_mlp = wires.exchange_seq(grad_mlp.reshape(seq, rows, -1)).astype(F32)


        grad_out = t_dot(over("mixed"), over("branch")).astype(BF16)
        grad_out = wires.scatter_out(grad_out, heads_kv).astype(F32)

        grad_in = t_dot(over("normed"), over("grad_rows")).astype(BF16)
        grad_in = wires.scatter_dp(grad_in.reshape(dp, seq * rows, -1))
        grad_in = wires.exchange_seq(grad_in.reshape(seq, rows, -1)).astype(F32)
        gain_sums = wires.sum_all(sum(k["gains"] for k in kept))
        grad_tokens = jnp.stack([k["grad_tokens"] for k in kept])
        hidden_out = jnp.stack(outs)

    grad_gate, grad_up = from_unit(grad_mlp[..., :units]), from_unit(grad_mlp[..., units:])
    pieces = [None] * heads_kv
    for t in range(seq):
        for m, j in enumerate(order[t]):
            pieces[j] = grad_in[t, :, m * 4 * HEAD_SIZE : (m + 1) * 4 * HEAD_SIZE]
    grad_query = jnp.concatenate([p[:, : 2 * HEAD_SIZE] for p in pieces], axis=1)
    grad_key = jnp.concatenate([p[:, 2 * HEAD_SIZE : 3 * HEAD_SIZE] for p in pieces], axis=1)
    grad_value = jnp.concatenate([p[:, 3 * HEAD_SIZE :] for p in pieces], axis=1)

    own = width // count
    grad_attn_gain = lax.dynamic_slice_in_dim(gain_sums, index * own, own)
    grad_mlp_gain = lax.dynamic_slice_in_dim(gain_sums, width + index * own, own)
    return (
        hidden_out,
        grad_tokens,
        grad_attn_gain,
        grad_query,
        grad_key,
        grad_value,
        gain_sums[2 * width : 2 * width + HEAD_SIZE],
        gain_sums[2 * width + HEAD_SIZE :],
        grad_out,
        grad_mlp_gain,
        grad_gate,
        grad_up,
        grad_down,
    )


def solution(mesh):
    rows = P(("dp", "seq"), None)
    line = P(("dp", "seq"))
    tokens = P("dp", "seq", None)
    return jax.shard_map(
        body,
        mesh=mesh,
        in_specs=(tokens, line, rows, rows, rows, P(), P(), rows, line, rows, rows, rows, tokens),
        out_specs=(tokens, tokens, line, rows, rows, rows, P(), P(), rows, line, rows, rows, rows),
        check_vma=False,
    )
```

```python
import functools

import jax
import jax.numpy as jnp
from jax import lax
from jax.experimental import pallas as pl
from jax.experimental.pallas import tpu as pltpu
from jax.sharding import PartitionSpec as P

HEAD_SIZE = 128
EPS = 1e-06
ROPE_THETA = 1000000.0
AXES = ("dp", "seq")
SCALE = HEAD_SIZE ** (-0.5)
F32 = jnp.float32
BF16 = jnp.bfloat16


def log2(n):
    return n.bit_length() - 1


class Wires:
    def __init__(self, dp, seq):
        self.dp, self.seq, self.count = dp, seq, dp * seq
        self.dp_bits, self.seq_bits = log2(dp), log2(seq)
        self.x_count = seq // 2
        y_bits = min(log2(self.x_count), self.dp_bits)
        self.dp_order = list(range(y_bits, self.dp_bits)) + list(range(y_bits))
        self.x_bits = list(range(1, self.seq_bits))
        self.d = lax.axis_index("dp")
        self.s = lax.axis_index("seq")

    def swap(self, value, mask, only=None):
        pairs = [(i, i ^ mask) for i in range(self.count) if only is None or only(i)]
        return lax.ppermute(value, AXES, pairs)

    def dp_swap(self, value, bit, only=None):
        return self.swap(value, (1 << bit) * self.seq, only)

    def bit_d(self, bit):
        return (self.d >> bit) & 1

    def bit_s(self, bit):
        return (self.s >> bit) & 1

    def gather_dp(self, shard):
        pieces = {0: shard}
        for bit in self.dp_order:
            pieces.update({r | (1 << bit): self.dp_swap(v, bit) for r, v in list(pieces.items())})
        full = jnp.zeros((self.dp,) + shard.shape, shard.dtype)
        for r, v in pieces.items():
            full = lax.dynamic_update_index_in_dim(full, v, self.d ^ r, 0)
        return full

    def scatter_dp(self, value):
        rest = value.shape[1:]
        held = list(range(self.dp_bits - 1, -1, -1))
        value = value.reshape((2,) * self.dp_bits + rest)
        for bit in reversed(self.dp_order):
            axis = held.index(bit)
            held.pop(axis)
            mine = lax.dynamic_index_in_dim(value, self.bit_d(bit), axis, keepdims=False)
            other = lax.dynamic_index_in_dim(value, 1 - self.bit_d(bit), axis, keepdims=False)
            got = self.dp_swap(other, bit)
            value = (mine.astype(F32) + got.astype(F32)).astype(BF16)
        return value

    def exchange_seq(self, value):
        rest = value.shape[1:]
        for bit in self.x_bits + [0]:
            value = value.reshape((self.seq >> (bit + 1), 2, 1 << bit) + rest)
            me = self.bit_s(bit)
            mine = lax.dynamic_index_in_dim(value, me, 1, keepdims=False)
            other = lax.dynamic_index_in_dim(value, 1 - me, 1, keepdims=False)
            got = self.swap(other, 1 << bit)
            low = jnp.where(me == 0, mine, got)
            high = jnp.where(me == 0, got, mine)
            value = jnp.stack([low, high], axis=1).reshape((self.seq,) + rest)
        return value

    def gather_seq_relative(self, value):
        pieces = [value]
        for bit in self.x_bits:
            pieces = pieces + [self.swap(v, 1 << bit) for v in pieces]
        return pieces + [self.swap(v, 1) for v in pieces]

    def sum_x(self, value):
        n = self.x_count
        shape = value.shape
        for bit in self.x_bits:
            got = self.swap(value.astype(BF16), 1 << bit).astype(F32)
            blocks = got.reshape((n, shape[0] // n) + shape[1:])
            flip = [i ^ (1 << (bit - 1)) for i in range(n)]
            value = value + jnp.concatenate([blocks[i] for i in flip], axis=0)
        return value

    def scatter_x(self, value):
        n = self.x_count
        for bit in reversed(self.x_bits):
            half = value.shape[0] // 2
            got = self.swap(value[half:].astype(BF16), 1 << bit)
            value = value[:half] + got.astype(F32)
        return value

    def sum_all(self, value):
        for bit in range(log2(self.count)):
            value = value + self.swap(value, 1 << bit)
        return value

    def head_bits(self, heads_kv):
        low = self.dp_bits - log2(heads_kv)
        partner = {0: 1, 1: 0, 2: 2}
        matched = [(low + k, partner[k]) for k in range(self.seq_bits)]
        free = [low + k for k in range(self.seq_bits, log2(heads_kv))]
        return low, matched, free

    def heads_of(self, t, heads_kv):
        low, matched, free = self.head_bits(heads_kv)
        heads = [0]
        for bit, tbit in matched:
            heads = [h | (((t >> tbit) & 1) << (bit - low)) for h in heads]
        for bit in free:
            heads = heads + [h | (1 << (bit - low)) for h in heads]
        return heads

    def matches(self, i, pairs):
        return all(((i // self.seq) >> b) & 1 == (i >> t) & 1 for b, t in pairs)

    def gather_out(self, shard, heads_kv):
        low, matched, free = self.head_bits(heads_kv)
        value = shard
        for bit in self.x_bits + [0]:
            pass
        value = shard[None]
        for bit in [0] + self.x_bits:
            got = self.swap(value, 1 << bit)
            value = self.ordered(value, got, self.bit_s(bit))
        for bit in range(low):
            got = self.dp_swap(value, bit)
            value = self.ordered(value, got, self.bit_d(bit))
        for n, (bit, tbit) in enumerate(matched):
            got = self.dp_swap(value, bit, lambda i: self.matches(i, matched[n:]))
            value = jnp.where(self.bit_d(bit) == self.bit_s(tbit), value, got)
        for bit in free:
            got = self.dp_swap(value, bit)
            value = self.ordered(value, got, self.bit_d(bit))
        return value.reshape((-1,) + shard.shape[1:])

    def ordered(self, own, got, bit):
        return jnp.concatenate(
            [jnp.where(bit == 0, own, got), jnp.where(bit == 0, got, own)], axis=0
        )

    def halves(self, value, bit):
        half = value.shape[0] // 2
        mine = lax.dynamic_slice_in_dim(value, bit * half, half, 0)
        other = lax.dynamic_slice_in_dim(value, (1 - bit) * half, half, 0)
        return mine, other

    def scatter_out(self, value, heads_kv):
        low, matched, free = self.head_bits(heads_kv)
        for bit in reversed(free):
            mine, other = self.halves(value, self.bit_d(bit))
            got = self.dp_swap(other, bit)
            value = (mine.astype(F32) + got.astype(F32)).astype(BF16)
        for n in reversed(range(len(matched))):
            bit, tbit = matched[n]
            got = self.dp_swap(
                value,
                bit,
                lambda i: self.matches(i, matched[n + 1 :]) and not self.matches(i, [matched[n]]),
            )
            value = (value.astype(F32) + got.astype(F32)).astype(BF16)
        for bit in reversed(range(low)):
            mine, other = self.halves(value, self.bit_d(bit))
            got = self.dp_swap(other, bit, lambda i: self.matches(i, matched))
            value = (mine.astype(F32) + got.astype(F32)).astype(BF16)
        todo = dict((tbit, bit) for bit, tbit in matched)
        for tbit in reversed(self.x_bits):
            value = self.hand_out(value, tbit, todo)
        return self.hand_out(value, 0, todo)

    def hand_out(self, value, tbit, todo):
        bit = todo.pop(tbit)
        left = [(b, t) for t, b in todo.items()]
        mine, other = self.halves(value, self.bit_s(tbit))
        got = self.swap(
            other, 1 << tbit, lambda i: self.matches(i, left) and self.matches(i, [(bit, tbit)])
        )
        return jnp.where(self.bit_d(bit) == self.bit_s(tbit), mine, got)


def dot(a, b):
    return lax.dot_general(a, b, (((1,), (0,)), ((), ())), preferred_element_type=F32)


def dot_t(a, b):
    return lax.dot_general(a, b, (((1,), (1,)), ((), ())), preferred_element_type=F32)


def t_dot(a, b):
    return lax.dot_general(a, b, (((0,), (0,)), ((), ())), preferred_element_type=F32)


def rms_scale(rows):
    return lax.rsqrt(jnp.mean(rows * rows, axis=-1, keepdims=True) + EPS)


def rope_tables(length):
    halfway = HEAD_SIZE // 2
    inverse = jnp.power(F32(ROPE_THETA), -(jnp.arange(halfway).astype(F32) * 2.0) / HEAD_SIZE)
    angles = jnp.arange(length).astype(F32)[:, None] * inverse[None, :]
    cosine, sine = jnp.cos(angles), jnp.sin(angles)
    return (
        jnp.concatenate([cosine, cosine], axis=-1),
        jnp.concatenate([-sine, sine], axis=-1),
    )


def place(block, s, x_count):
    return ((block & 1) ^ (s & 1)) * x_count + ((block >> 1) ^ (s >> 1))


def project_kernel(s_ref, x_ref, w_ref, gain_ref, qg_ref, kg_ref, cos_ref, sin_ref, n_ref, qkv_ref, pre_ref):
    x = x_ref[0].astype(F32)
    normed = (x * rms_scale(x) * gain_ref[...]).astype(BF16)
    n_ref[0] = normed
    y = dot(normed, w_ref[...])
    cosine, sine = cos_ref[...], sin_ref[...]
    for j in range(y.shape[1] // (4 * HEAD_SIZE)):
        for part in range(4):
            at = slice((4 * j + part) * HEAD_SIZE, (4 * j + part + 1) * HEAD_SIZE)
            head = y[:, at]
            if part < 3:
                pre_ref[:, (3 * j + part) * HEAD_SIZE : (3 * j + part + 1) * HEAD_SIZE] = head
                gain = qg_ref[...] if part < 2 else kg_ref[...]
                head = head * rms_scale(head) * gain
                head = head * cosine + pltpu.roll(head, HEAD_SIZE // 2, 1) * sine
            qkv_ref[:, at] = head.astype(BF16)


def project(s, x_rel, w, gain, query_gain, key_gain, cosine, sine, x_count):
    blocks, piece, width = x_rel.shape
    length, columns = blocks * piece, w.shape[1]
    heads = columns // (4 * HEAD_SIZE)
    whole = lambda shape: pl.BlockSpec(shape, lambda i, s_ref: (0,) * len(shape))
    rel = pl.BlockSpec((1, piece, width), lambda i, s_ref: (place(i, s_ref[0], x_count), 0, 0))
    table = pl.BlockSpec((piece, HEAD_SIZE), lambda i, s_ref: (i, 0))
    return pl.pallas_call(
        project_kernel,
        name="project",
        out_shape=(
            jax.ShapeDtypeStruct((blocks, piece, width), BF16),
            jax.ShapeDtypeStruct((length, columns), BF16),
            jax.ShapeDtypeStruct((length, 3 * heads * HEAD_SIZE), F32),
        ),
        grid_spec=pltpu.PrefetchScalarGridSpec(
            num_scalar_prefetch=1,
            grid=(blocks,),
            in_specs=[
                rel,
                whole(w.shape),
                whole((1, width)),
                whole((1, HEAD_SIZE)),
                whole((1, HEAD_SIZE)),
                table,
                table,
            ],
            out_specs=[
                rel,
                pl.BlockSpec((piece, columns), lambda i, s_ref: (i, 0)),
                pl.BlockSpec((piece, 3 * heads * HEAD_SIZE), lambda i, s_ref: (i, 0)),
            ],
        ),
        cost_estimate=pl.CostEstimate(
            flops=2 * length * width * columns,
            bytes_accessed=2 * (2 * length * width + width * columns + 4 * length * columns),
            transcendentals=0,
        ),
    )(s, x_rel, w, gain, query_gain, key_gain, cosine, sine)


def masked_exp(k_ref, query, i, piece, offset):
    diagonal = dot_t(k_ref[i * piece : (i + 1) * piece, :], query) * SCALE
    key_at = lax.broadcasted_iota(jnp.int32, (piece, piece), 0)
    query_at = lax.broadcasted_iota(jnp.int32, (piece, piece), 1)
    diagonal = jnp.where(key_at <= query_at, diagonal, -jnp.inf)
    if i == 0:
        scores = diagonal
    else:
        scores = jnp.concatenate(
            [dot_t(k_ref[: i * piece, :], query) * SCALE, diagonal], axis=0
        )
    if offset is None:
        offset = jnp.max(scores, axis=0, keepdims=True)
    return jnp.exp(scores - offset), offset


def forward_kernel(blocks, x_count, s_ref, q_ref, k_ref, v_ref, o_ref, log_ref):
    piece = q_ref.shape[0] // blocks
    values_t = v_ref[...].T
    for i in range(blocks):
        query = q_ref[i * piece : (i + 1) * piece, :]
        exponent, highest = masked_exp(k_ref, query, i, piece, None)
        total = jnp.sum(exponent, axis=0, keepdims=True)
        probs = (exponent * (1.0 / total)).astype(BF16)
        mixed = dot(values_t[:, : (i + 1) * piece], probs)
        o_ref[place(i, s_ref[0], x_count)] = mixed.T.astype(BF16)
        log_ref[0, :, i * piece : (i + 1) * piece] = highest + jnp.log(total)


def attend(s, qkv, blocks, x_count):
    length, columns = qkv.shape
    heads = columns // (2 * HEAD_SIZE)
    piece = length // blocks
    head = lambda part: pl.BlockSpec(
        (length, HEAD_SIZE), lambda h, s_ref: (0, 4 * (h // 2) + (h % 2 if part == 0 else part))
    )
    return pl.pallas_call(
        functools.partial(forward_kernel, blocks, x_count),
        name="attend",
        out_shape=(
            jax.ShapeDtypeStruct((blocks, piece, heads * HEAD_SIZE), BF16),
            jax.ShapeDtypeStruct((heads, 1, length), F32),
        ),
        grid_spec=pltpu.PrefetchScalarGridSpec(
            num_scalar_prefetch=1,
            grid=(heads,),
            in_specs=[head(0), head(2), head(3)],
            out_specs=[
                pl.BlockSpec((blocks, piece, HEAD_SIZE), lambda h, s_ref: (0, 0, h)),
                pl.BlockSpec((1, 1, length), lambda h, s_ref: (h, 0, 0)),
            ],
        ),
        cost_estimate=pl.CostEstimate(
            flops=2 * heads * length * length * HEAD_SIZE * 2,
            bytes_accessed=2 * heads * length * HEAD_SIZE * 4,
            transcendentals=heads * length * length // 2,
        ),
    )(s, qkv, qkv, qkv)


def head_back(grad, pre, gain, cosine, sine):
    turned = grad * cosine - pltpu.roll(grad, HEAD_SIZE // 2, 1) * sine
    scale = rms_scale(pre)
    part = turned * gain
    result = scale * part - pre * (scale * scale * scale * jnp.mean(part * pre, axis=-1, keepdims=True))
    return result, jnp.sum(turned * pre * scale, axis=0, keepdims=True)


def backward_kernel(
    blocks, x_count, s_ref, q_ref, k_ref, v_ref, do_ref, log_ref, qp_ref, kp_ref, qg_ref, kg_ref,
    cos_ref, sin_ref, grad_ref, qgain_ref, kgain_ref, dk_ref, dv_ref,
):
    piece = q_ref.shape[0] // blocks
    second = pl.program_id(1)

    @pl.when((pl.program_id(0) == 0) & (second == 0))
    def _():
        qgain_ref[...] = jnp.zeros_like(qgain_ref)
        kgain_ref[...] = jnp.zeros_like(kgain_ref)

    @pl.when(second == 0)
    def _():
        dk_ref[...] = jnp.zeros_like(dk_ref)
        dv_ref[...] = jnp.zeros_like(dv_ref)

    keys_t = k_ref[...].T
    column = pl.ds(pl.multiple_of(second * HEAD_SIZE, HEAD_SIZE), HEAD_SIZE)
    for i in range(blocks):
        rows = slice(i * piece, (i + 1) * piece)
        end = (i + 1) * piece
        at = place(i, s_ref[0], x_count)
        query = q_ref[rows, :]
        grad_out = do_ref[at]
        probs, _ = masked_exp(k_ref, query, i, piece, log_ref[0, :, rows])
        dv_ref[:end, :] += dot(probs.astype(BF16), grad_out)
        grad_probs = dot_t(v_ref[:end, :], grad_out)
        inner = jnp.sum(probs * grad_probs, axis=0, keepdims=True)
        grad_scores = (probs * (grad_probs - inner)).astype(BF16)
        dk_ref[:end, :] += dot(grad_scores, query)
        grad_query = dot(keys_t[:, :end], grad_scores).T * SCALE
        result, gain = head_back(grad_query, qp_ref[rows, :], qg_ref[...], cos_ref[rows, :], sin_ref[rows, :])
        grad_ref[at, :, column] = result.astype(BF16)
        qgain_ref[...] += gain

    @pl.when(second == 1)
    def _():
        for i in range(blocks):
            rows = slice(i * piece, (i + 1) * piece)
            at = place(i, s_ref[0], x_count)
            result, gain = head_back(
                dk_ref[rows, :] * SCALE, kp_ref[rows, :], kg_ref[...], cos_ref[rows, :], sin_ref[rows, :]
            )
            grad_ref[at, :, 2 * HEAD_SIZE : 3 * HEAD_SIZE] = result.astype(BF16)
            grad_ref[at, :, 3 * HEAD_SIZE :] = dv_ref[rows, :].astype(BF16)
            kgain_ref[...] += gain


def attend_back(s, qkv, pre, log_total, grad_mixed, query_gain, key_gain, cosine, sine, blocks, x_count):
    length, columns = qkv.shape
    heads_kv = columns // (4 * HEAD_SIZE)
    piece = length // blocks
    head = lambda part: pl.BlockSpec(
        (length, HEAD_SIZE), lambda j, g, s_ref: (0, 4 * j + (g if part == 0 else part))
    )
    pre_head = lambda part: pl.BlockSpec(
        (length, HEAD_SIZE), lambda j, g, s_ref: (0, 3 * j + (g if part == 0 else part))
    )
    whole = lambda shape: pl.BlockSpec(shape, lambda j, g, s_ref: (0,) * len(shape))
    return pl.pallas_call(
        functools.partial(backward_kernel, blocks, x_count),
        name="attend_back",
        out_shape=(
            jax.ShapeDtypeStruct((blocks, piece, columns), BF16),
            jax.ShapeDtypeStruct((1, HEAD_SIZE), F32),
            jax.ShapeDtypeStruct((1, HEAD_SIZE), F32),
        ),
        grid_spec=pltpu.PrefetchScalarGridSpec(
            num_scalar_prefetch=1,
            grid=(heads_kv, 2),
            in_specs=[
                head(0),
                head(2),
                head(3),
                pl.BlockSpec((blocks, piece, HEAD_SIZE), lambda j, g, s_ref: (0, 0, 2 * j + g)),
                pl.BlockSpec((1, 1, length), lambda j, g, s_ref: (2 * j + g, 0, 0)),
                pre_head(0),
                pre_head(2),
                whole((1, HEAD_SIZE)),
                whole((1, HEAD_SIZE)),
                whole((length, HEAD_SIZE)),
                whole((length, HEAD_SIZE)),
            ],
            out_specs=[
                pl.BlockSpec((blocks, piece, 4 * HEAD_SIZE), lambda j, g, s_ref: (0, 0, j)),
                whole((1, HEAD_SIZE)),
                whole((1, HEAD_SIZE)),
            ],
            scratch_shapes=[pltpu.VMEM((length, HEAD_SIZE), F32), pltpu.VMEM((length, HEAD_SIZE), F32)],
        ),
        cost_estimate=pl.CostEstimate(
            flops=2 * 2 * heads_kv * length * length * HEAD_SIZE * 5 // 2,
            bytes_accessed=2 * heads_kv * length * HEAD_SIZE * 24,
            transcendentals=heads_kv * length * length,
        ),
    )(s, qkv, qkv, qkv, grad_mixed, log_total, pre, pre, query_gain, key_gain, cosine, sine)


MESH = pl.DeviceIdType.MESH


def flip(index, bit):
    step = 1 << bit
    return index + step - 2 * step * lax.rem(lax.div(index, step), 2)


def bit_of(index, bit):
    return lax.rem(lax.div(index, 1 << bit), 2)


class Links:
    def __init__(self, send, recv):
        self.send, self.recv = send, recv
        self.d, self.s = lax.axis_index("dp"), lax.axis_index("seq")
        self.used = 0
        self.started = []

    def slots(self, n):
        self.used += n
        return self.used - n

    def copy(self, src, dst, slot, **to):
        return pltpu.make_async_remote_copy(
            src_ref=src,
            dst_ref=dst,
            send_sem=self.send.at[slot],
            recv_sem=self.recv.at[slot],
            device_id=to,
            device_id_type=MESH,
        )

    def plan(self, src, dst, slot, when=None, **to):
        copy = self.copy(src, dst, slot, **to)
        self.started.append((copy, when))
        return copy

    def start(self, src, dst, slot, when=None, **to):
        copy = self.plan(src, dst, slot, when, **to)
        if when is None:
            copy.start()
        else:
            pl.when(when)(copy.start)
        return copy

    def finish(self):
        for copy, when in self.started:
            if when is None:
                copy.wait_send()
            else:
                pl.when(when)(copy.wait_send)

    def greet(self, dp_masks, seq_masks):
        barrier = pltpu.get_barrier_semaphore()
        for mask in dp_masks:
            pl.semaphore_signal(
                barrier, inc=1, device_id={"dp": self.dp_at(mask)}, device_id_type=MESH
            )
        for mask in seq_masks:
            pl.semaphore_signal(
                barrier, inc=1, device_id={"seq": self.seq_at(mask)}, device_id_type=MESH
            )
        pl.semaphore_wait(barrier, len(dp_masks) + len(seq_masks))

    def seq_at(self, mask):
        s = self.s
        for bit in range(2):
            if mask >> bit & 1:
                s = flip(s, bit)
        return s

    def dp_at(self, mask):
        d = self.d
        for bit in range(3):
            if mask >> bit & 1:
                d = flip(d, bit)
        return d


class Gather:
    def __init__(self, links, block):
        base = links.slots(8)
        self.copies = {}
        for r, mask in ((0, 1), (0, 2), (0, 4), (2, 1), (4, 2), (4, 1), (6, 1)):
            src = block(links.dp_at(r))
            self.copies[r | mask] = links.plan(src, src, base + (r | mask), dp=links.dp_at(mask))

    def got(self, r):
        self.copies[r].wait_recv()

    def first(self):
        for mask in (4, 2, 1):
            self.copies[mask].start()

    def relay(self, r):
        self.got(r)
        if r == 4:
            self.copies[6].start()
        self.copies[r | 1].start()

    def last(self):
        for r in (1, 3, 5, 7):
            self.got(r)


def first_kernel(
    heads,
    a_ref, c_ref, out_ref, down_ref, x_ref, g_ref, gains_ref, qg_ref, kg_ref, cos_ref, sin_ref,
    xr_ref, gr_ref, wa_ref, wc_ref, wo_ref, wd_ref, n_ref, qkv_ref, pre_ref, o_ref, residual_ref, far_ref, log_ref, gain_ref,
    w_v, x_v, n_v, qkv_v, pre_v, o_v, got_v, wo_v, res_v, core_s, core_r, far_s, far_r, send, recv, local,
):
    links = Links(send, recv)
    d, s = links.d, links.s
    sequences, piece, width = x_ref.shape
    blocks = xr_ref.shape[1]
    half = blocks // 2
    length = blocks * piece
    x_bit, core = bit_of(s, 1), bit_of(s, 0)
    z1, z0, y = bit_of(d, 2), bit_of(d, 1), bit_of(d, 0)
    place_of = lambda i: lax.rem((i & 1) + core, 2) * 2 + lax.rem((i >> 1) + x_bit, 2)
    local_used = [0]
    locals_ = {}

    def near(name, src, dst):
        copy = pltpu.make_async_copy(src, dst, local.at[local_used[0]])
        local_used[0] += 1
        copy.start()
        locals_[name] = copy

    links.greet((1, 2, 4), (1, 2, 3))

    def exchange(src, dst):
        base = links.slots(4)
        return [
            links.start(src.at[links.seq_at(k)], dst.at[d, s], base + k, seq=links.seq_at(k))
            for k in (2, 3, 1)
        ]

    gain_slots = links.slots(4)
    gain_own = [
        links.start(gains_ref, got_v.at[d, s], gain_slots + k, seq=links.seq_at(k)) for k in (2, 3, 1)
    ]
    got_v[d, s] = gains_ref[...]
    a_own = exchange(a_ref, wa_ref)
    near("a", a_ref.at[s], wa_ref.at[d, s])

    x_slots, g_slots = links.slots(3 * sequences), links.slots(3 * sequences)

    def spread(own, everywhere, base, n):
        copies = [
            links.start(own.at[n], everywhere.at[n, k], base + 3 * n + k - 1, seq=links.seq_at(3 - k))
            for k in (1, 2)
        ]
        onward = links.plan(everywhere.at[n, 1], everywhere.at[n, 3], base + 3 * n + 2, seq=links.seq_at(1))
        return copies + [onward]

    def pass_on(copies):
        copies[0].wait_recv()
        copies[2].start()

    across, beside = lax.rem(x_bit + y, 2), lax.rem(core + z0, 2)
    out_slots = links.slots(7)
    holder = (across == 0) & (beside == 0)
    out_first = [
        links.start(
            out_ref, wo_ref.at[z1, s], out_slots + k,
            when=(across == k >> 1) & (beside == (k & 1)), seq=links.seq_at(k),
        )
        for k in (1, 2, 3)
    ]
    x_copies = [spread(x_ref, xr_ref, x_slots, 0)]
    c_own = exchange(c_ref, wc_ref)
    near("c", c_ref.at[s], wc_ref.at[d, s])
    for n in range(sequences):
        near(f"x{n}", x_ref.at[n], xr_ref.at[n, 0])
    near("d", down_ref, wd_ref.at[d])
    x_copies += [spread(x_ref, xr_ref, x_slots, n) for n in range(1, sequences)]

    for copy in gain_own + a_own:
        copy.wait_recv()
    locals_["a"].wait()
    gather_a, gather_c, gather_d, gather_gain = (
        Gather(links, lambda at, ref=ref: ref.at[at]) for ref in (wa_ref, wc_ref, wd_ref, got_v)
    )
    out_y = links.plan(wo_ref.at[z1], wo_ref.at[z1], out_slots + 4, when=holder, dp=flip(d, 0))
    out_z1 = links.plan(wo_ref.at[z1], wo_ref.at[z1], out_slots + 5, when=beside == 0, dp=flip(d, 2))
    out_z0 = links.plan(wo_ref, wo_ref, out_slots + 6, when=beside == 0, dp=flip(d, 1))

    def out_next():
        pl.when((across == 1) & (beside == 0))(out_y.wait_recv)
        pl.when(beside == 0)(out_z1.start)

    def out_last():
        @pl.when(beside == 0)
        def _():
            out_z1.wait_recv()
            out_z0.start()

    gather_gain.first()
    gather_a.first()

    @pl.when(holder)
    def _():
        own = pltpu.make_async_copy(out_ref, wo_ref.at[z1, s], local.at[local_used[0]])
        own.start()
        for copy in out_first:
            copy.wait_recv()
        own.wait()
        out_y.start()

    local_used[0] += 1
    for r in (2, 4, 6):
        gather_gain.relay(r)
    pass_on(x_copies[0])
    gather_a.relay(2)
    out_next()
    gather_a.relay(4)
    for copy in c_own:
        copy.wait_recv()
    locals_["c"].wait()
    gather_c.first()
    gather_a.relay(6)
    g_copies = [spread(g_ref, gr_ref, g_slots, n) for n in range(sequences)]
    for n in range(sequences):
        near(f"g{n}", g_ref.at[n], gr_ref.at[n, 0])
    locals_["d"].wait()
    gather_d.first()

    def wait_x(n):
        locals_[f"x{n}"].wait()
        for copy in x_copies[n][1:]:
            copy.wait_recv()
        near(f"xv{n}", xr_ref.at[n], x_v.at[n])
        locals_[f"xv{n}"].wait()

    def project_part(n, meanwhile=()):
        def step(i, carry):
            for k, action in enumerate(meanwhile):
                pl.when(i == k)(action)
            at = place_of(i)
            x = x_v[n, at].astype(F32)
            normed = (x * rms_scale(x) * gain_ref[0:1, :]).astype(BF16)
            n_v[n, at] = normed
            y_rows = dot(normed, w_v[...].reshape(width, -1))
            rows = pl.ds(pl.multiple_of(i * piece, piece), piece)
            cosine, sine = cos_ref[rows, :], sin_ref[rows, :]
            for j in range(heads // 2):
                for part in range(4):
                    cut = slice((4 * j + part) * HEAD_SIZE, (4 * j + part + 1) * HEAD_SIZE)
                    head = y_rows[:, cut]
                    if part < 3:
                        pre_v[n, rows, (3 * j + part) * HEAD_SIZE : (3 * j + part + 1) * HEAD_SIZE] = head
                        gain = qg_ref[...] if part < 2 else kg_ref[...]
                        head = head * rms_scale(head) * gain
                        head = head * cosine + pltpu.roll(head, HEAD_SIZE // 2, 1) * sine
                    qkv_v[n, rows, cut] = head.astype(BF16)
            return carry

        lax.fori_loop(0, blocks, step, 0)
        near(f"n{n}", n_v.at[n], n_ref.at[n])
        near(f"qkv{n}", qkv_v.at[n], qkv_ref.at[n])
        near(f"pre{n}", pre_v.at[n], pre_ref.at[n])

    def attend_part(n, meanwhile=()):
        def step(h, carry):
            for k, action in enumerate(meanwhile):
                pl.when(h == k)(action)
            j, g = lax.div(h, 2), lax.rem(h, 2)
            lanes = lambda at: pl.ds(pl.multiple_of(at * HEAD_SIZE, HEAD_SIZE), HEAD_SIZE)
            values_t = qkv_v[n, :, lanes(4 * j + 3)].T
            keys = qkv_v.at[n, :, lanes(4 * j + 2)]
            for i in range(blocks):
                query = qkv_v[n, i * piece : (i + 1) * piece, lanes(4 * j + g)]
                exponent, highest = masked_exp(keys, query, i, piece, None)
                total = jnp.sum(exponent, axis=0, keepdims=True)
                probs = (exponent * (1.0 / total)).astype(BF16)
                mixed = dot(values_t[:, : (i + 1) * piece], probs)
                o_v[n, place_of(i), :, lanes(h)] = mixed.T.astype(BF16)
                log_ref[n, h, :, i * piece : (i + 1) * piece] = highest + jnp.log(total)
            return carry

        lax.fori_loop(0, heads, step, 0)

    wait_x(0)
    gather_a.last()
    near("w", wa_ref, w_v)
    locals_["w"].wait()

    gather_gain.last()
    for at in range(got_v.shape[0]):
        gain_ref[:, at * 128 : (at + 1) * 128] = jnp.sum(got_v[at], axis=0)

    core_slots, far_slots = links.slots(half * sequences), links.slots(half * sequences)
    core_copies = {
        (n, k): links.plan(core_s.at[n, k], core_r.at[n, k], core_slots + half * n + k, seq=links.seq_at(1))
        for n in range(sequences)
        for k in range(half)
    }
    far_copies = {
        (n, k): links.plan(far_s.at[n, k], far_r.at[n, half - 1 - k], far_slots + half * n + k, seq=links.seq_at(2))
        for n in range(sequences - 1)
        for k in range(half)
    }

    def out_part(n):
        if n == 0:
            pl.when(beside == 1)(out_z0.wait_recv)
            near("wo", wo_ref, wo_v)
            locals_["wo"].wait()

        def step(i, carry):
            b = lax.rem(i + half, blocks)
            part = dot(o_v[n, b], wo_v[...].reshape(-1, width))
            for k in range(half):

                @pl.when(i == k)
                def _():
                    core_s[n, k] = part.astype(BF16)
                    core_copies[n, k].start()

                @pl.when(i == half + k)
                def _():
                    core_copies[n, k].wait_recv()
                    total = part + core_r[n, k].astype(F32)
                    res_v[n, k] = total
                    far_s[n, k] = total.astype(BF16)
                    if n < sequences - 1:
                        far_copies[n, k].start()

            return carry

        lax.fori_loop(0, blocks, step, 0)

    def residual(n):
        for k in range(half):
            if n < sequences - 1:
                far_copies[n, half - 1 - k].wait_recv()
                res_v[n, k] = res_v[n, k] + far_r[n, k].astype(F32) + x_v[n, k].astype(F32)
            else:
                res_v[n, k] = res_v[n, k] + x_v[n, k].astype(F32)
        near(f"res{n}", res_v.at[n], residual_ref.at[n])
        if n == sequences - 1:
            near("far", far_s.at[n], far_ref)

    nothing = lambda: None
    project_part(0, [nothing, lambda: gather_c.relay(2), lambda: pass_on(x_copies[1]), out_last])
    attend_part(0, [lambda: gather_c.relay(4)])
    near("o0", o_v.at[0], o_ref.at[0])
    for n in range(1, sequences):
        wait_x(n)
        out_part(n - 1)
        project_part(n, [lambda: gather_c.relay(6), nothing, lambda: pass_on(g_copies[0])])
        attend_part(n, [nothing, nothing, lambda: pass_on(g_copies[1])])
        near(f"o{n}", o_v.at[n], o_ref.at[n])
    out_part(sequences - 1)
    for r in (2, 4, 6):
        gather_d.relay(r)
    for n in range(sequences):
        residual(n)
    gather_c.last()
    gather_d.last()
    for pair in g_copies:
        for copy in pair[1:]:
            copy.wait_recv()
    for n in range(sequences):
        for name in ("g", "n", "qkv", "pre", "o", "res"):
            locals_[f"{name}{n}"].wait()
    locals_["far"].wait()
    links.finish()


def first(a, c, w_out, w_down, x, g, gains, query_gain, key_gain, cosine, sine, dp, heads):
    blocks, rows, columns = a.shape
    sequences, piece, width = x.shape
    length = blocks * piece
    hbm = pl.BlockSpec(memory_space=pl.ANY)
    vmem = pl.BlockSpec(memory_space=pltpu.VMEM)
    shape = jax.ShapeDtypeStruct
    pre_columns = columns // 4 * 3
    slots = 96
    return pl.pallas_call(
        functools.partial(first_kernel, heads),
        name="first",
        out_shape=(
            shape((sequences, blocks, piece, width), BF16),
            shape((sequences, blocks, piece, width), BF16),
            shape((dp, blocks, rows, columns), BF16),
            shape((dp, blocks, rows, c.shape[2]), BF16),
            shape((2, blocks) + w_out.shape, BF16),
            shape((dp,) + w_down.shape, BF16),
            shape((sequences, blocks, piece, width), BF16),
            shape((sequences, length, columns), BF16),
            shape((sequences, length, pre_columns), F32),
            shape((sequences, blocks, piece, heads * HEAD_SIZE), BF16),
            shape((sequences, blocks // 2, piece, width), F32),
            shape((blocks // 2, piece, width), BF16),
            shape((sequences, heads, 1, length), F32),
            shape((8, width), F32),
        ),
        in_specs=[vmem] * 11,
        out_specs=[hbm] * 12 + [vmem] * 2,
        scratch_shapes=[
            pltpu.VMEM((dp, blocks, rows, columns), BF16),
            pltpu.VMEM((sequences, blocks, piece, width), BF16),
            pltpu.VMEM((sequences, blocks, piece, width), BF16),
            pltpu.VMEM((sequences, length, columns), BF16),
            pltpu.VMEM((sequences, length, pre_columns), F32),
            pltpu.VMEM((sequences, blocks, piece, heads * HEAD_SIZE), BF16),
            pltpu.VMEM((dp, blocks, 8, width // dp), F32),
            pltpu.VMEM((2, blocks) + w_out.shape, BF16),
            pltpu.VMEM((sequences, blocks // 2, piece, width), F32),
            pltpu.VMEM((sequences, blocks // 2, piece, width), BF16),
            pltpu.VMEM((sequences, blocks // 2, piece, width), BF16),
            pltpu.VMEM((sequences, blocks // 2, piece, width), BF16),
            pltpu.VMEM((sequences, blocks // 2, piece, width), BF16),
            pltpu.SemaphoreType.DMA((slots,)),
            pltpu.SemaphoreType.DMA((slots,)),
            pltpu.SemaphoreType.DMA((32,)),
        ],
        compiler_params=pltpu.CompilerParams(
            collective_id=0, has_side_effects=True, vmem_limit_bytes=60 * 1024 * 1024
        ),
    )(a, c, w_out, w_down, x, g, gains, query_gain, key_gain, cosine, sine)


def mlp_kernel(
    res_ref, last_ref, wc_ref, wd_ref, g_ref, gain_ref,
    own_ref, far_ref, residual_ref, branch_ref, down_ref, mlp_ref, gain_grad_ref,
    res_v, last_v, core_s, x_s, n2_v, hidden_v, both_v, dc_v, dg_v, da_v, us_v, uc_v, ux_v, ua_v,
    send, recv, local,
):
    links = Links(send, recv)
    sequences, blocks, piece, width = g_ref.shape
    half = blocks // 2
    units = wd_ref.shape[0]
    core, far = dict(seq=links.seq_at(1)), dict(seq=links.seq_at(2))
    pairs = [(n, k) for n in range(sequences) for k in range(half)]
    slots = {
        name: links.slots(half * sequences)
        for name in ("normed", "grad_core", "up_core", "grad_far", "branch")
    }
    ends = {
        "normed": lambda n, k: (n2_v.at[n, k], n2_v.at[n, half + k], core),
        "grad_core": lambda n, k: (core_s.at[n, k], dc_v.at[n, k], core),
        "up_core": lambda n, k: (us_v.at[n, k], uc_v.at[n, k], core),
        "grad_far": lambda n, k: (x_s.at[n, k], dg_v.at[n, half - 1 - k], far),
        "branch": lambda n, k: (us_v.at[n, k], branch_ref.at[n, half + k], core),
    }

    def copy(name, n, k):
        src, dst, to = ends[name](n, k)
        return links.copy(src, dst, slots[name] + half * n + k, **to)

    def arrived(name, n, k):
        copy(name, n, half - 1 - k if name == "grad_far" else k).wait_recv()

    near_copies = []

    def near(src, dst):
        made = pltpu.make_async_copy(src, dst, local.at[len(near_copies)])
        made.start()
        near_copies.append(made)

    last_slots = links.slots(half)
    last_copies = [
        links.plan(last_ref.at[k], last_v.at[half - 1 - k], last_slots + k, **far) for k in range(half)
    ]

    links.greet((), (1, 2))
    for made in last_copies:
        made.start()
    gain = gain_ref[...]

    def residual_of(n, k):
        return res_ref[n, k] if n < sequences - 1 else res_v[k]

    def norm(n):
        for k in range(half):
            if n == sequences - 1:
                last_copies[half - 1 - k].wait_recv()
                res_v[k] = res_ref[n, k] + last_v[k].astype(F32)
            residual = residual_of(n, k)
            n2_v[n, k] = (residual * rms_scale(residual) * gain).astype(BF16)
            copy("normed", n, k).start()

    def feed(n):
        for k in range(half):
            arrived("normed", n, k)

        def step(i, carry):
            b = lax.rem(i + half, blocks)
            both = dot(n2_v[n, b], wc_ref[...])
            gate, upward = both[:, :units], both[:, units:]
            grad_hidden = dot_t(g_ref[n, b], wd_ref[...])
            sigmoid = 1.0 / (1.0 + jnp.exp(-gate))
            silu = gate * sigmoid
            hidden_v[n, b] = (silu * upward).astype(BF16)
            both_v[n, b, :, units:] = (grad_hidden * silu).astype(BF16)
            both_v[n, b, :, :units] = (
                grad_hidden * upward * sigmoid * (1.0 + gate * (1.0 - sigmoid))
            ).astype(BF16)
            grad = dot_t(both_v[n, b], wc_ref[...])

            @pl.when(i < half)
            def _():
                core_s[n, i] = grad.astype(BF16)
                copy("grad_core", n, i).start()

            @pl.when(i >= half)
            def _():
                k = i - half
                arrived_core = copy("grad_core", n, k)
                arrived_core.wait_recv()
                total = grad + dc_v[n, k].astype(F32)
                da_v[n, k] = total
                x_s[n, k] = total.astype(BF16)
                copy("grad_far", n, k).start()

            up = dot(hidden_v[n, b], wd_ref[...])

            @pl.when(i < half)
            def _():
                us_v[n, i] = up.astype(BF16)
                copy("up_core", n, i).start()

            @pl.when(i >= half)
            def _():
                copy("up_core", n, i - half).wait_recv()

            @pl.when(i == half)
            def _():
                ua_v[n] = residual_of(n, 0) + (up + uc_v[n, 0].astype(F32))

            @pl.when(i == half + 1)
            def _():
                ux_v[n] = (up + uc_v[n, 1].astype(F32)).astype(BF16)

            return carry

        lax.fori_loop(0, blocks, step, 0)
        near(ua_v.at[n], own_ref.at[n])
        near(ux_v.at[n], far_ref.at[n])

    def back(n):
        for k in range(half):
            copy("up_core", n, k).wait_send()
        for k in range(half):
            arrived("grad_far", n, k)
            grad = da_v[n, k] + dg_v[n, k].astype(F32)
            residual = residual_of(n, k)
            scale = rms_scale(residual)
            scaled = grad * gain
            grad_residual = (
                g_ref[n, k].astype(F32)
                + scale * scaled
                - residual * (scale * scale * scale * jnp.mean(scaled * residual, axis=-1, keepdims=True))
            )
            us_v[n, k] = grad_residual.astype(BF16)
            copy("branch", n, k).start()
            near(us_v.at[n, k], branch_ref.at[n, k])
            if k == 0:
                part = jnp.sum(grad * residual * scale, axis=0, keepdims=True)
                gain_grad_ref[...] = part if n == 0 else gain_grad_ref[...] + part
                da_v[n, 0] = grad_residual
                near(da_v.at[n, 0], residual_ref.at[n])

    def weight_grads():
        chunk = 2 * width // 8
        flat = lambda value: value.reshape(-1, value.shape[-1])

        def rows(left_v, right, out):
            def step(m, carry):
                cut = pl.ds(pl.multiple_of(m * chunk, chunk), chunk)
                total = None
                for n in range(sequences):
                    term = t_dot(flat(left_v[n, :, :, cut]), flat(right[n]))
                    total = term if total is None else total + term
                out[cut, :] = total.astype(BF16)
                return carry

            lax.fori_loop(0, out.shape[0] // chunk, step, 0)

        rows(hidden_v, g_ref, down_ref)
        rows(n2_v, both_v, mlp_ref)

    for n in range(sequences):
        norm(n)
        feed(n)
    for n in range(sequences - 1):
        back(n)
    weight_grads()
    back(sequences - 1)
    for n, k in pairs:
        arrived("branch", n, k)
    for n, k in pairs:
        for name in ("normed", "grad_core", "grad_far", "branch"):
            copy(name, n, k).wait_send()
    links.finish()
    for made in near_copies:
        made.wait()


def feed_forward(residual, last_far, w_mlp, w_d, g_rel, gain):
    sequences, blocks, piece, width = g_rel.shape
    half = blocks // 2
    units = w_d.shape[0]
    hbm = pl.BlockSpec(memory_space=pl.ANY)
    vmem = pl.BlockSpec(memory_space=pltpu.VMEM)
    shape = jax.ShapeDtypeStruct
    part = lambda dtype: pltpu.VMEM((sequences, half, piece, width), dtype)
    one = lambda dtype: pltpu.VMEM((sequences, piece, width), dtype)
    return pl.pallas_call(
        mlp_kernel,
        name="feed_forward",
        out_shape=(
            shape((sequences, piece, width), F32),
            shape((sequences, piece, width), BF16),
            shape((sequences, piece, width), F32),
            shape((sequences, blocks, piece, width), BF16),
            shape((units, width), BF16),
            shape((width, 2 * units), BF16),
            shape((1, width), F32),
        ),
        in_specs=[vmem] * 6,
        out_specs=[hbm] * 4 + [vmem] * 3,
        scratch_shapes=[
            pltpu.VMEM((half, piece, width), F32),
            pltpu.VMEM((half, piece, width), BF16),
            part(BF16),
            part(BF16),
            pltpu.VMEM((sequences, blocks, piece, width), BF16),
            pltpu.VMEM((sequences, blocks, piece, units), BF16),
            pltpu.VMEM((sequences, blocks, piece, 2 * units), BF16),
            part(BF16),
            part(BF16),
            part(F32),
            part(BF16),
            part(BF16),
            one(BF16),
            one(F32),
            pltpu.SemaphoreType.DMA((16 * sequences,)),
            pltpu.SemaphoreType.DMA((16 * sequences,)),
            pltpu.SemaphoreType.DMA((16,)),
        ],
        compiler_params=pltpu.CompilerParams(
            collective_id=1, has_side_effects=True, vmem_limit_bytes=67043328
        ),
    )(residual, last_far, w_mlp, w_d, g_rel, gain)


class Scatter:
    def __init__(self, links, src, first, second, third, done=None):
        d = links.d
        self.z1, self.z0, self.y = bit_of(d, 2), bit_of(d, 1), bit_of(d, 0)
        self.src, self.first, self.second, self.third = src, first, second, third
        base = links.slots(7)
        self.over_y = links.plan(src.at[:, :, 1 - self.y], first, base, dp=flip(d, 0))
        self.over_z0 = links.plan(first.at[:, 1 - self.z0], second, base + 1, dp=flip(d, 1))
        self.over_z1 = links.plan(second.at[1 - self.z1], third, base + 2, dp=flip(d, 2))
        self.done, self.s = done, links.s
        if done is not None:
            self.share = [
                links.plan(third.at[links.seq_at(k)], done.at[links.s], base + 3 + k, seq=links.seq_at(k))
                for k in (2, 3, 1)
            ]

    def start(self):
        self.over_y.start()

    def sum_y(self):
        self.over_y.wait_recv()

        def step(i, carry):
            a, b = lax.div(i, 2), lax.rem(i, 2)
            mine = self.src[a, b, self.y].astype(F32)
            self.first[a, b] = (mine + self.first[a, b].astype(F32)).astype(BF16)
            return carry

        lax.fori_loop(0, 4, step, 0)
        self.over_z0.start()

    def sum_z0(self):
        self.over_z0.wait_recv()

        def step(a, carry):
            mine = self.first[a, self.z0].astype(F32)
            self.second[a] = (mine + self.second[a].astype(F32)).astype(BF16)
            return carry

        lax.fori_loop(0, 2, step, 0)
        self.over_z1.start()

    def sum_z1(self):
        self.over_z1.wait_recv()
        mine = self.second[self.z1].astype(F32)
        self.third[...] = (mine + self.third[...].astype(F32)).astype(BF16)
        if self.done is not None:
            for copy in self.share:
                copy.start()
            self.done[self.s] = self.third[self.s]

    def end(self):
        for copy in self.share:
            copy.wait_recv()


def last_kernel(
    down_ref, mlp_ref, mixed_h, branch_h, wo_ref, qkv_h, pre_h, log_ref, w_h, normed_h,
    x_ref, residual_ref, up_ref, gain_ref, mlp_gain_ref, qg_ref, kg_ref, cos_ref, sin_ref,
    up_out, tokens_ref, down_out, mlp_out, out_out, in_out, sums_ref,
    rows_v, mixed_ref, qkv_ref, pre_ref, w_ref, og_ref, d1, d2, c1, c2, c3, o1, o2, o3, a_v, a1, a2, a3,
    do_v, gr_v, dk_v, dv_v, core_s, core_r, far_s, far_r, acc_v, total_v, got_v,
    send, recv, local,
):
    links = Links(send, recv)
    d, s = links.d, links.s
    sequences, blocks, piece, width = rows_v.shape
    half = blocks // 2
    heads = log_ref.shape[1]
    heads_kv = heads // 2
    x_bit, core = bit_of(s, 1), bit_of(s, 0)
    z1, z0, y = bit_of(d, 2), bit_of(d, 1), bit_of(d, 0)
    place_of = lambda i: lax.rem((i & 1) + core, 2) * 2 + lax.rem((i >> 1) + x_bit, 2)
    across, beside = lax.rem(x_bit + y, 2), lax.rem(core + z0, 2)
    holder = (across == 0) & (beside == 0)
    lanes = lambda at: pl.ds(pl.multiple_of(at * HEAD_SIZE, HEAD_SIZE), HEAD_SIZE)
    nothing = lambda: None

    down = Scatter(links, down_ref, d1, d2, down_out)
    mlp = Scatter(links, mlp_ref, c1, c2, c3, mlp_out)
    ins = [
        Scatter(links, a_v.at[j], a1.at[j], a2.at[j], a3.at[j], in_out.at[j]) for j in range(heads_kv)
    ]
    base = links.slots(7)
    out_z0 = links.plan(og_ref, o1, base, when=beside == 1, dp=flip(d, 1))
    out_z1 = links.plan(o1.at[1 - z1], o2, base + 1, when=beside == 0, dp=flip(d, 2))
    out_y = links.plan(o2, o3, base + 2, when=(beside == 0) & (across == 1), dp=flip(d, 0))
    out_share = {
        k: links.plan(o3.at[links.seq_at(k)], out_out, base + 3 + k, when=holder, seq=links.seq_at(k))
        for k in (1, 2, 3)
    }

    def out_sum_z0():
        @pl.when(beside == 0)
        def _():
            out_z0.wait_recv()

            def step(i, carry):
                a, b = lax.div(i, blocks), lax.rem(i, blocks)
                o1[a, b] = (og_ref[a, b].astype(F32) + o1[a, b].astype(F32)).astype(BF16)
                return carry

            lax.fori_loop(0, 2 * blocks, step, 0)
            out_z1.start()

    def out_sum_z1():
        @pl.when(beside == 0)
        def _():
            out_z1.wait_recv()

            def step(b, carry):
                o2[b] = (o1[z1, b].astype(F32) + o2[b].astype(F32)).astype(BF16)
                return carry

            lax.fori_loop(0, blocks, step, 0)

        pl.when((beside == 0) & (across == 1))(out_y.start)

    def out_sum_y():
        @pl.when(holder)
        def _():
            out_y.wait_recv()

            def step(b, carry):
                o3[b] = (o2[b].astype(F32) + o3[b].astype(F32)).astype(BF16)
                return carry

            lax.fori_loop(0, blocks, step, 0)
            for copy in out_share.values():
                copy.start()
            out_out[...] = o3[s]

    links.greet((1, 2, 4), (1, 2, 3))
    loads = {
        name: pltpu.make_async_copy(src, dst, local.at[k])
        for k, (name, src, dst) in enumerate(
            (
                ("mixed", mixed_h, mixed_ref),
                ("branch", branch_h, rows_v),
                ("qkv", qkv_h, qkv_ref),
                ("pre", pre_h, pre_ref),
                ("w", w_h, w_ref),
                ("residual", residual_ref, tokens_ref),
                ("normed", normed_h, rows_v),
            )
        )
    }
    for name in ("mixed", "branch", "qkv", "pre", "w", "residual"):
        loads[name].start()
    up_slot = links.slots(1)
    up_copy = links.start(up_ref, up_out, up_slot, seq=links.seq_at(2))
    mlp.start()
    down.start()
    total_v[0] = jnp.zeros_like(total_v[0])
    for r in range(width // 128):
        total_v[0, 8 + r : 9 + r, :] = mlp_gain_ref[:, r * 128 : (r + 1) * 128]

    def weight_out(h, carry):
        cut = pl.ds(pl.multiple_of(h * 2 * HEAD_SIZE, 2 * HEAD_SIZE), 2 * HEAD_SIZE)
        total = None
        for n in range(sequences):
            term = t_dot(
                mixed_ref[n, :, :, cut].reshape(blocks * piece, 2 * HEAD_SIZE),
                rows_v[n].reshape(blocks * piece, width),
            )
            total = term if total is None else total + term
        og_ref[h] = total.astype(BF16).reshape(og_ref.shape[1:])
        return carry

    def mixed_back(i, carry):
        n, b = lax.div(i, blocks), lax.rem(i, blocks)
        do_v[n, b] = dot_t(rows_v[n, b], wo_ref[...]).astype(BF16)
        return carry

    loads["mixed"].wait()
    loads["branch"].wait()
    lax.fori_loop(0, heads_kv, weight_out, 0)
    pl.when(beside == 1)(out_z0.start)
    lax.fori_loop(0, sequences * blocks, mixed_back, 0)
    loads["normed"].start()

    slots = [links.slots(half * sequences), links.slots(sequences)]
    core_copies = {
        (n, k): links.plan(core_s.at[n, k], core_r.at[n, k], slots[0] + half * n + k, seq=links.seq_at(1))
        for n in range(sequences)
        for k in range(half)
    }
    far_copies = [
        links.plan(far_s.at[n], far_r.at[n], slots[1] + n, seq=links.seq_at(2)) for n in range(sequences)
    ]

    def input_part(n):
        def step(i, carry):
            b = lax.rem(i + half, blocks)
            grad = dot_t(gr_v[n, b], w_ref[...])
            for k in range(half):

                @pl.when(i == k)
                def _():
                    core_s[n, k] = grad.astype(BF16)
                    core_copies[n, k].start()

                @pl.when(i == half + k)
                def _():
                    core_copies[n, k].wait_recv()
                    total = grad + core_r[n, k].astype(F32)
                    if k == 0:
                        acc_v[n] = total
                    else:
                        far_s[n] = total.astype(BF16)
                        far_copies[n].start()

            return carry

        lax.fori_loop(0, blocks, step, 0)

    def input_end(n):
        far_copies[n].wait_recv()
        grad = acc_v[n] + far_r[n].astype(F32)
        tokens = x_ref[n].astype(F32)
        scale = rms_scale(tokens)
        scaled = grad * gain_ref[...]
        tokens_ref[n] = (
            tokens_ref[n]
            + scale * scaled
            - tokens * (scale * scale * scale * jnp.mean(scaled * tokens, axis=-1, keepdims=True))
        )
        part = jnp.sum(grad * tokens * scale, axis=0, keepdims=True)
        for r in range(width // 128):
            total_v[0, r : r + 1, :] += part[:, r * 128 : (r + 1) * 128]

    def attention(j, meanwhile):
        def step(t, carry):
            for k, action in enumerate(meanwhile):
                pl.when(t == k)(action)
            n, g = lax.div(t, 2), lax.rem(t, 2)

            @pl.when(g == 0)
            def _():
                dk_v[...] = jnp.zeros_like(dk_v)
                dv_v[...] = jnp.zeros_like(dv_v)

            keys, values = qkv_ref.at[n, :, lanes(4 * j + 2)], qkv_ref.at[n, :, lanes(4 * j + 3)]
            keys_t = keys[...].T
            for i in range(blocks):
                rows = slice(i * piece, (i + 1) * piece)
                end = (i + 1) * piece
                at = place_of(i)
                query = qkv_ref[n, rows, lanes(4 * j + g)]
                grad_out = do_v[n, at, :, lanes(2 * j + g)]
                probs, _ = masked_exp(keys, query, i, piece, log_ref[n, 2 * j + g, :, rows])
                dv_v[:end, :] += dot(probs.astype(BF16), grad_out)
                grad_probs = dot_t(values[:end, :], grad_out)
                inner = jnp.sum(probs * grad_probs, axis=0, keepdims=True)
                grad_scores = (probs * (grad_probs - inner)).astype(BF16)
                dk_v[:end, :] += dot(grad_scores, query)
                grad_query = dot(keys_t[:, :end], grad_scores).T * SCALE
                result, gain = head_back(
                    grad_query, pre_ref[n, rows, lanes(3 * j + g)], qg_ref[...], cos_ref[rows, :], sin_ref[rows, :]
                )
                gr_v[n, at, :, lanes(4 * j + g)] = result.astype(BF16)
                total_v[0, 16:17, :] += gain

            @pl.when(g == 1)
            def _():
                for i in range(blocks):
                    rows = slice(i * piece, (i + 1) * piece)
                    at = place_of(i)
                    result, gain = head_back(
                        dk_v[rows, :] * SCALE, pre_ref[n, rows, lanes(3 * j + 2)], kg_ref[...],
                        cos_ref[rows, :], sin_ref[rows, :],
                    )
                    gr_v[n, at, :, lanes(4 * j + 2)] = result.astype(BF16)
                    gr_v[n, at, :, lanes(4 * j + 3)] = dv_v[rows, :].astype(BF16)
                    total_v[0, 17:18, :] += gain

            return carry

        lax.fori_loop(0, 2 * sequences, step, 0)

    def weight_in(j):
        wide = 4 * HEAD_SIZE
        chunk = 2 * width // 8

        def step(m, carry):
            cut = pl.ds(pl.multiple_of(m * chunk, chunk), chunk)
            total = None
            for n in range(sequences):
                left = rows_v[n, :, :, cut].reshape(blocks * piece, chunk)
                right = gr_v[n, :, :, j * wide : (j + 1) * wide].reshape(blocks * piece, wide)
                term = t_dot(left, right)
                total = term if total is None else total + term
            a_v[j, lax.div(m, 2), lax.rem(m, 2)] = total.astype(BF16).reshape(a_v.shape[3:])
            return carry

        lax.fori_loop(0, width // chunk, step, 0)
        ins[j].start()

    loads["qkv"].wait()
    loads["pre"].wait()
    attention(0, [nothing, nothing, out_sum_z0])
    loads["normed"].wait()
    loads["w"].wait()
    weight_in(0)
    attention(1, [out_sum_z1, mlp.sum_y, lambda: input_part(0)])
    input_part(1)
    weight_in(1)
    down.sum_y()
    mlp.sum_z0()
    loads["residual"].wait()
    for n in range(sequences):
        input_end(n)

    gain_slots = links.slots(5)
    gain_to = [dict(seq=links.seq_at(1)), dict(seq=links.seq_at(2))] + [dict(dp=flip(d, b)) for b in range(3)]
    gain_copies = [
        links.plan(total_v.at[k], got_v.at[k], gain_slots + k, **gain_to[k]) for k in range(5)
    ]

    def gain_stage(k):
        gain_copies[k].wait_recv()
        if k == 4:
            sums_ref[...] = total_v[4] + got_v[4]
        else:
            total_v[k + 1] = total_v[k] + got_v[k]
            gain_copies[k + 1].start()

    gain_copies[0].start()
    ins[0].sum_y()
    gain_stage(0)
    down.sum_z0()
    gain_stage(1)
    out_sum_y()
    mlp.sum_z1()
    gain_stage(2)
    ins[0].sum_z0()
    down.sum_z1()
    gain_stage(3)
    ins[0].sum_z1()
    ins[1].sum_y()
    gain_stage(4)
    ins[1].sum_z0()
    ins[1].sum_z1()
    for k, copy in out_share.items():
        pl.when((across == k >> 1) & (beside == (k & 1)))(copy.wait_recv)
    mlp.end()
    up_copy.wait_recv()
    for scatter in ins:
        scatter.end()
    links.finish()


def last(
    down, mlp, mixed, branch, w_o, qkv, pre, log_total, w_in, normed, x, residual, up,
    gain, mlp_gain_grad, query_gain, key_gain, cosine, sine,
):
    sequences, blocks, piece, width = branch.shape
    length = blocks * piece
    rows, wide = mlp.shape[-2], mlp.shape[-1]
    down_rows = down.shape[-2]
    heads_kv = qkv.shape[-1] // (4 * HEAD_SIZE)
    out_rows = w_o.shape[0] // (heads_kv * blocks)
    vmem = pl.BlockSpec(memory_space=pltpu.VMEM)
    shape = jax.ShapeDtypeStruct
    b16 = lambda *dims: pltpu.VMEM(dims, BF16)
    f32 = lambda *dims: pltpu.VMEM(dims, F32)
    hbm = pl.BlockSpec(memory_space=pl.ANY)
    part = (blocks, rows, 4 * HEAD_SIZE)
    return pl.pallas_call(
        last_kernel,
        name="last",
        out_shape=(
            shape(up.shape, up.dtype),
            shape((sequences, piece, width), F32),
            shape((down_rows, width), BF16),
            shape((blocks, rows, wide), BF16),
            shape((out_rows, width), BF16),
            shape((heads_kv,) + part, BF16),
            shape((24, 128), F32),
        ),
        in_specs=[vmem] * 2 + [hbm] * 2 + [vmem] + [hbm] * 2 + [vmem] + [hbm] * 2 + [vmem] + [hbm] * 2 + [vmem] * 6,
        out_specs=[hbm] + [vmem] * 6,
        scratch_shapes=[
            b16(*normed.shape),
            b16(*mixed.shape),
            b16(*qkv.shape),
            f32(*pre.shape),
            b16(*w_in.shape),
            b16(heads_kv, blocks, out_rows, width),
            b16(2, 2, down_rows, width),
            b16(2, down_rows, width),
            b16(2, 2, blocks, rows, wide),
            b16(2, blocks, rows, wide),
            b16(blocks, rows, wide),
            b16(2, blocks, out_rows, width),
            b16(blocks, out_rows, width),
            b16(blocks, out_rows, width),
            b16(heads_kv, 2, 2, 2, *part),
            b16(heads_kv, 2, 2, *part),
            b16(heads_kv, 2, *part),
            b16(heads_kv, *part),
            b16(sequences, blocks, piece, 2 * heads_kv * HEAD_SIZE),
            b16(sequences, blocks, piece, width),
            f32(length, HEAD_SIZE),
            f32(length, HEAD_SIZE),
            b16(sequences, blocks // 2, piece, width),
            b16(sequences, blocks // 2, piece, width),
            b16(sequences, piece, width),
            b16(sequences, piece, width),
            f32(sequences, piece, width),
            f32(5, 24, 128),
            f32(5, 24, 128),
            pltpu.SemaphoreType.DMA((64,)),
            pltpu.SemaphoreType.DMA((64,)),
            pltpu.SemaphoreType.DMA((8,)),
        ],
        compiler_params=pltpu.CompilerParams(
            collective_id=2, has_side_effects=True, vmem_limit_bytes=67043328
        ),
    )(
        down, mlp, mixed, branch, w_o, qkv, pre, log_total, w_in, normed, x, residual, up,
        gain, mlp_gain_grad, query_gain, key_gain, cosine, sine,
    )


def body(
    hidden_in,
    attn_gain,
    w_query,
    key_weight,
    value_weight,
    query_gain,
    key_gain,
    w_out,
    mlp_gain,
    w_gate,
    w_up,
    w_down,
    cotangent,
):
    wires = Wires(lax.axis_size("dp"), lax.axis_size("seq"))
    dp, seq, x_count = wires.dp, wires.seq, wires.x_count
    count = wires.count
    sequences, piece, width = hidden_in.shape
    length = seq * piece
    part = x_count * piece
    heads_kv = key_weight.shape[1] // HEAD_SIZE
    s_index = wires.s.reshape(1).astype(jnp.int32)
    cosine, sine = rope_tables(length)
    query_gain_row = query_gain.astype(F32).reshape(1, -1)
    key_gain_row = key_gain.astype(F32).reshape(1, -1)

    index = wires.d * seq + wires.s
    own_gains = jnp.stack([attn_gain, mlp_gain])
    rows = w_query.shape[0]
    by_head = jnp.concatenate(
        [
            w_query.reshape(rows, heads_kv, -1),
            key_weight.reshape(rows, heads_kv, -1),
            value_weight.reshape(rows, heads_kv, -1),
        ],
        axis=2,
    )
    order = [wires.heads_of(t, heads_kv) for t in range(seq)]
    package_in = jnp.stack(
        [jnp.concatenate([by_head[:, j] for j in order[t]], axis=1) for t in range(seq)]
    )
    down_rows = w_down.shape[0]

    def by_unit(w):
        return w.reshape(rows, dp, seq, down_rows).transpose(2, 0, 1, 3).reshape(seq, rows, -1)

    units = dp * down_rows
    package_mlp = jnp.concatenate([by_unit(w_gate), by_unit(w_up)], axis=2)

    fused = (dp, seq, heads_kv) == (8, 4, 8) and width == 128 * dp and rows % 16 == 0 and down_rows % 16 == 0
    if fused:
        gains = jnp.zeros((8, seq, width // count), F32)
        gains = lax.dynamic_update_slice(gains, own_gains.astype(F32)[:, None], (0, wires.s, 0))
        (
            x_rel, g_rel, w_in, w_mlp, w_o, w_d, all_normed, all_qkv, all_pre, all_mixed, residual, residual_far, all_log, gains
        ) = first(
            package_in, package_mlp, w_out, w_down, hidden_in, cotangent, gains.reshape(8, -1),
            query_gain_row, key_gain_row, cosine, sine, dp, 2 * heads_kv // seq,
        )
        w_in, w_mlp = w_in.reshape(width, -1), w_mlp.reshape(width, -1)
        w_o, w_d = w_o.reshape(-1, width), w_d.reshape(units, width)
        attn_gain_row, mlp_gain_row = gains[:1], gains[1:2]
        up_own, up_far, all_grad_residual, all_branch, grad_down, grad_mlp, mlp_gain_grad = feed_forward(
            residual, residual_far, w_mlp, w_d, g_rel, mlp_gain_row
        )
    else:
        gains = jnp.zeros((2, count, width // count), BF16)
        gains = lax.dynamic_update_slice(gains, own_gains[:, None], (0, index, 0))
        gains = wires.sum_all(gains.reshape(2, width)).astype(F32)
        attn_gain_row, mlp_gain_row = gains[:1], gains[1:]
        package = wires.exchange_seq(package_in).reshape(seq * rows, -1)
        w_in = wires.gather_dp(package).reshape(width, -1)
        x_rel = jnp.stack(wires.gather_seq_relative(hidden_in), axis=1)
        w_o = wires.gather_out(w_out, heads_kv)
        package = wires.exchange_seq(package_mlp).reshape(seq * rows, -1)
        w_mlp = wires.gather_dp(package).reshape(width, -1)
        g_rel = jnp.stack(wires.gather_seq_relative(cotangent), axis=1)
        w_d = wires.gather_dp(w_down).reshape(units, width)

    kept = []
    outs = []
    for n in range(0 if fused else sequences):
        normed, qkv, pre = project(
            s_index, x_rel[n], w_in, attn_gain_row, query_gain_row, key_gain_row, cosine, sine, x_count
        )
        mixed, log_total = attend(s_index, qkv, seq, x_count)
        mixed_rows = mixed.reshape(length, -1)
        other = wires.swap(dot(mixed_rows[part:], w_o).astype(BF16), 1)
        total = wires.sum_x(dot(mixed_rows[:part], w_o) + other.astype(F32))
        residual = total + x_rel[n].reshape(length, width)[:part].astype(F32)
        scale = rms_scale(residual)
        normed_mlp = (residual * scale * mlp_gain_row).astype(BF16)
        normed_mlp = jnp.concatenate([normed_mlp, wires.swap(normed_mlp, 1)], axis=0)
        both = dot(normed_mlp, w_mlp)
        gate, upward = both[:, :units], both[:, units:]
        sigmoid = jax.nn.sigmoid(gate)
        silu = gate * sigmoid
        hidden = (silu * upward).astype(BF16)
        other = wires.swap(dot(hidden[part:], w_d).astype(BF16), 1)
        total = wires.scatter_x(dot(hidden[:part], w_d) + other.astype(F32))
        outs.append((residual[:piece] + total).astype(BF16))

        grad_top = g_rel[n].reshape(length, width)
        grad_hidden = dot_t(grad_top, w_d)
        grad_gate = (grad_hidden * upward * sigmoid * (1.0 + gate * (1.0 - sigmoid))).astype(BF16)
        grad_upward = (grad_hidden * silu).astype(BF16)
        grad_both = jnp.concatenate([grad_gate, grad_upward], axis=1)
        other = wires.swap(dot_t(grad_both[part:], w_mlp).astype(BF16), 1)
        grad_normed = wires.sum_x(dot_t(grad_both[:part], w_mlp) + other.astype(F32))
        scaled = grad_normed * mlp_gain_row
        grad_residual = (
            grad_top[:part].astype(F32)
            + scale * scaled
            - residual * (scale * scale * scale * jnp.mean(scaled * residual, axis=-1, keepdims=True))
        )
        grad_mlp_gain = jnp.sum((grad_normed * residual * scale)[:piece], axis=0)
        branch = grad_residual.astype(BF16)
        branch = jnp.concatenate([branch, wires.swap(branch, 1)], axis=0)
        grad_mixed = dot_t(branch, w_o).astype(BF16).reshape(mixed.shape)
        grad_qkv, grad_query_gain, grad_key_gain = attend_back(
            s_index, qkv, pre, log_total, grad_mixed, query_gain_row, key_gain_row, cosine, sine, seq, x_count
        )
        grad_rows = grad_qkv.reshape(length, -1)
        other = wires.swap(dot_t(grad_rows[part:], w_in).astype(BF16), 1)
        grad_first = wires.scatter_x(dot_t(grad_rows[:part], w_in) + other.astype(F32))
        tokens = hidden_in[n].astype(F32)
        scale = rms_scale(tokens)
        scaled = grad_first * attn_gain_row
        grad_tokens = (
            grad_residual[:piece]
            + scale * scaled
            - tokens * (scale * scale * scale * jnp.mean(scaled * tokens, axis=-1, keepdims=True))
        )
        grad_attn_gain = jnp.sum(grad_first * tokens * scale, axis=0)
        kept.append(
            dict(
                normed=normed.reshape(length, width),
                mixed=mixed_rows,
                normed_mlp=normed_mlp,
                hidden=hidden,
                grad_both=grad_both,
                branch=branch,
                grad_rows=grad_rows,
                grad_tokens=grad_tokens,
                gains=jnp.concatenate(
                    [grad_attn_gain, grad_mlp_gain, grad_query_gain[0], grad_key_gain[0]]
                ),
            )
        )

    def from_unit(g):
        return g.reshape(seq, rows, dp, down_rows).transpose(1, 2, 0, 3).reshape(rows, -1)

    if fused:
        up, grad_tokens, grad_down, grad_mlp, grad_out, grad_in, gain_sums = last(
            grad_down.reshape(2, 2, 2, down_rows, width),
            grad_mlp.reshape(2, 2, 2, seq, rows, -1),
            all_mixed, all_branch, w_o, all_qkv, all_pre, all_log, w_in, all_normed, hidden_in, all_grad_residual, up_far,
            attn_gain_row, mlp_gain_grad, query_gain_row, key_gain_row, cosine, sine,
        )
        grad_down, grad_mlp, grad_out = grad_down.astype(F32), grad_mlp.astype(F32), grad_out.astype(F32)
        grad_in = grad_in.astype(F32).transpose(1, 2, 0, 3).reshape(seq, rows, -1)
        gain_sums = gain_sums.reshape(-1)[: 2 * width + 2 * HEAD_SIZE]
        hidden_out = (up_own + up.astype(F32)).astype(BF16)
    else:
        def over(name):
            return jnp.concatenate([k[name] for k in kept], axis=0)

        grad_down = t_dot(over("hidden"), g_rel.reshape(-1, width)).astype(BF16)
        grad_down = wires.scatter_dp(grad_down.reshape(dp, down_rows, width)).astype(F32)

        grad_mlp = t_dot(over("normed_mlp"), over("grad_both")).astype(BF16)
        grad_mlp = wires.scatter_dp(grad_mlp.reshape(dp, seq * rows, -1))
        grad_mlp = wires.exchange_seq(grad_mlp.reshape(seq, rows, -1)).astype(F32)


        grad_out = t_dot(over("mixed"), over("branch")).astype(BF16)
        grad_out = wires.scatter_out(grad_out, heads_kv).astype(F32)

        grad_in = t_dot(over("normed"), over("grad_rows")).astype(BF16)
        grad_in = wires.scatter_dp(grad_in.reshape(dp, seq * rows, -1))
        grad_in = wires.exchange_seq(grad_in.reshape(seq, rows, -1)).astype(F32)
        gain_sums = wires.sum_all(sum(k["gains"] for k in kept))
        grad_tokens = jnp.stack([k["grad_tokens"] for k in kept])
        hidden_out = jnp.stack(outs)

    grad_gate, grad_up = from_unit(grad_mlp[..., :units]), from_unit(grad_mlp[..., units:])
    pieces = [None] * heads_kv
    for t in range(seq):
        for m, j in enumerate(order[t]):
            pieces[j] = grad_in[t, :, m * 4 * HEAD_SIZE : (m + 1) * 4 * HEAD_SIZE]
    grad_query = jnp.concatenate([p[:, : 2 * HEAD_SIZE] for p in pieces], axis=1)
    grad_key = jnp.concatenate([p[:, 2 * HEAD_SIZE : 3 * HEAD_SIZE] for p in pieces], axis=1)
    grad_value = jnp.concatenate([p[:, 3 * HEAD_SIZE :] for p in pieces], axis=1)

    own = width // count
    grad_attn_gain = lax.dynamic_slice_in_dim(gain_sums, index * own, own)
    grad_mlp_gain = lax.dynamic_slice_in_dim(gain_sums, width + index * own, own)
    return (
        hidden_out,
        grad_tokens,
        grad_attn_gain,
        grad_query,
        grad_key,
        grad_value,
        gain_sums[2 * width : 2 * width + HEAD_SIZE],
        gain_sums[2 * width + HEAD_SIZE :],
        grad_out,
        grad_mlp_gain,
        grad_gate,
        grad_up,
        grad_down,
    )


def solution(mesh):
    rows = P(("dp", "seq"), None)
    line = P(("dp", "seq"))
    tokens = P("dp", "seq", None)
    return jax.shard_map(
        body,
        mesh=mesh,
        in_specs=(tokens, line, rows, rows, rows, P(), P(), rows, line, rows, rows, rows, tokens),
        out_specs=(tokens, tokens, line, rows, rows, rows, P(), P(), rows, line, rows, rows, rows),
        check_vma=False,
    )
```

```python
import functools

import jax
import jax.numpy as jnp
from jax import lax
from jax.experimental import pallas as pl
from jax.experimental.pallas import tpu as pltpu
from jax.sharding import PartitionSpec as P

HEAD_SIZE = 128
EPS = 1e-06
ROPE_THETA = 1000000.0
AXES = ("dp", "seq")
SCALE = HEAD_SIZE ** (-0.5)
F32 = jnp.float32
BF16 = jnp.bfloat16


def log2(n):
    return n.bit_length() - 1


class Wires:
    def __init__(self, dp, seq):
        self.dp, self.seq, self.count = dp, seq, dp * seq
        self.dp_bits, self.seq_bits = log2(dp), log2(seq)
        self.x_count = seq // 2
        y_bits = min(log2(self.x_count), self.dp_bits)
        self.dp_order = list(range(y_bits, self.dp_bits)) + list(range(y_bits))
        self.x_bits = list(range(1, self.seq_bits))
        self.d = lax.axis_index("dp")
        self.s = lax.axis_index("seq")

    def swap(self, value, mask, only=None):
        pairs = [(i, i ^ mask) for i in range(self.count) if only is None or only(i)]
        return lax.ppermute(value, AXES, pairs)

    def dp_swap(self, value, bit, only=None):
        return self.swap(value, (1 << bit) * self.seq, only)

    def bit_d(self, bit):
        return (self.d >> bit) & 1

    def bit_s(self, bit):
        return (self.s >> bit) & 1

    def gather_dp(self, shard):
        pieces = {0: shard}
        for bit in self.dp_order:
            pieces.update({r | (1 << bit): self.dp_swap(v, bit) for r, v in list(pieces.items())})
        full = jnp.zeros((self.dp,) + shard.shape, shard.dtype)
        for r, v in pieces.items():
            full = lax.dynamic_update_index_in_dim(full, v, self.d ^ r, 0)
        return full

    def scatter_dp(self, value):
        rest = value.shape[1:]
        held = list(range(self.dp_bits - 1, -1, -1))
        value = value.reshape((2,) * self.dp_bits + rest)
        for bit in reversed(self.dp_order):
            axis = held.index(bit)
            held.pop(axis)
            mine = lax.dynamic_index_in_dim(value, self.bit_d(bit), axis, keepdims=False)
            other = lax.dynamic_index_in_dim(value, 1 - self.bit_d(bit), axis, keepdims=False)
            got = self.dp_swap(other, bit)
            value = (mine.astype(F32) + got.astype(F32)).astype(BF16)
        return value

    def exchange_seq(self, value):
        rest = value.shape[1:]
        for bit in self.x_bits + [0]:
            value = value.reshape((self.seq >> (bit + 1), 2, 1 << bit) + rest)
            me = self.bit_s(bit)
            mine = lax.dynamic_index_in_dim(value, me, 1, keepdims=False)
            other = lax.dynamic_index_in_dim(value, 1 - me, 1, keepdims=False)
            got = self.swap(other, 1 << bit)
            low = jnp.where(me == 0, mine, got)
            high = jnp.where(me == 0, got, mine)
            value = jnp.stack([low, high], axis=1).reshape((self.seq,) + rest)
        return value

    def gather_seq_relative(self, value):
        pieces = [value]
        for bit in self.x_bits:
            pieces = pieces + [self.swap(v, 1 << bit) for v in pieces]
        return pieces + [self.swap(v, 1) for v in pieces]

    def sum_x(self, value):
        n = self.x_count
        shape = value.shape
        for bit in self.x_bits:
            got = self.swap(value.astype(BF16), 1 << bit).astype(F32)
            blocks = got.reshape((n, shape[0] // n) + shape[1:])
            flip = [i ^ (1 << (bit - 1)) for i in range(n)]
            value = value + jnp.concatenate([blocks[i] for i in flip], axis=0)
        return value

    def scatter_x(self, value):
        n = self.x_count
        for bit in reversed(self.x_bits):
            half = value.shape[0] // 2
            got = self.swap(value[half:].astype(BF16), 1 << bit)
            value = value[:half] + got.astype(F32)
        return value

    def sum_all(self, value):
        for bit in range(log2(self.count)):
            value = value + self.swap(value, 1 << bit)
        return value

    def head_bits(self, heads_kv):
        low = self.dp_bits - log2(heads_kv)
        partner = {0: 1, 1: 0, 2: 2}
        matched = [(low + k, partner[k]) for k in range(self.seq_bits)]
        free = [low + k for k in range(self.seq_bits, log2(heads_kv))]
        return low, matched, free

    def heads_of(self, t, heads_kv):
        low, matched, free = self.head_bits(heads_kv)
        heads = [0]
        for bit, tbit in matched:
            heads = [h | (((t >> tbit) & 1) << (bit - low)) for h in heads]
        for bit in free:
            heads = heads + [h | (1 << (bit - low)) for h in heads]
        return heads

    def matches(self, i, pairs):
        return all(((i // self.seq) >> b) & 1 == (i >> t) & 1 for b, t in pairs)

    def gather_out(self, shard, heads_kv):
        low, matched, free = self.head_bits(heads_kv)
        value = shard
        for bit in self.x_bits + [0]:
            pass
        value = shard[None]
        for bit in [0] + self.x_bits:
            got = self.swap(value, 1 << bit)
            value = self.ordered(value, got, self.bit_s(bit))
        for bit in range(low):
            got = self.dp_swap(value, bit)
            value = self.ordered(value, got, self.bit_d(bit))
        for n, (bit, tbit) in enumerate(matched):
            got = self.dp_swap(value, bit, lambda i: self.matches(i, matched[n:]))
            value = jnp.where(self.bit_d(bit) == self.bit_s(tbit), value, got)
        for bit in free:
            got = self.dp_swap(value, bit)
            value = self.ordered(value, got, self.bit_d(bit))
        return value.reshape((-1,) + shard.shape[1:])

    def ordered(self, own, got, bit):
        return jnp.concatenate(
            [jnp.where(bit == 0, own, got), jnp.where(bit == 0, got, own)], axis=0
        )

    def halves(self, value, bit):
        half = value.shape[0] // 2
        mine = lax.dynamic_slice_in_dim(value, bit * half, half, 0)
        other = lax.dynamic_slice_in_dim(value, (1 - bit) * half, half, 0)
        return mine, other

    def scatter_out(self, value, heads_kv):
        low, matched, free = self.head_bits(heads_kv)
        for bit in reversed(free):
            mine, other = self.halves(value, self.bit_d(bit))
            got = self.dp_swap(other, bit)
            value = (mine.astype(F32) + got.astype(F32)).astype(BF16)
        for n in reversed(range(len(matched))):
            bit, tbit = matched[n]
            got = self.dp_swap(
                value,
                bit,
                lambda i: self.matches(i, matched[n + 1 :]) and not self.matches(i, [matched[n]]),
            )
            value = (value.astype(F32) + got.astype(F32)).astype(BF16)
        for bit in reversed(range(low)):
            mine, other = self.halves(value, self.bit_d(bit))
            got = self.dp_swap(other, bit, lambda i: self.matches(i, matched))
            value = (mine.astype(F32) + got.astype(F32)).astype(BF16)
        todo = dict((tbit, bit) for bit, tbit in matched)
        for tbit in reversed(self.x_bits):
            value = self.hand_out(value, tbit, todo)
        return self.hand_out(value, 0, todo)

    def hand_out(self, value, tbit, todo):
        bit = todo.pop(tbit)
        left = [(b, t) for t, b in todo.items()]
        mine, other = self.halves(value, self.bit_s(tbit))
        got = self.swap(
            other, 1 << tbit, lambda i: self.matches(i, left) and self.matches(i, [(bit, tbit)])
        )
        return jnp.where(self.bit_d(bit) == self.bit_s(tbit), mine, got)


def dot(a, b):
    return lax.dot_general(a, b, (((1,), (0,)), ((), ())), preferred_element_type=F32)


def dot_t(a, b):
    return lax.dot_general(a, b, (((1,), (1,)), ((), ())), preferred_element_type=F32)


def t_dot(a, b):
    return lax.dot_general(a, b, (((0,), (0,)), ((), ())), preferred_element_type=F32)


def rms_scale(rows):
    return lax.rsqrt(jnp.mean(rows * rows, axis=-1, keepdims=True) + EPS)


def rope_tables(length):
    halfway = HEAD_SIZE // 2
    inverse = jnp.power(F32(ROPE_THETA), -(jnp.arange(halfway).astype(F32) * 2.0) / HEAD_SIZE)
    angles = jnp.arange(length).astype(F32)[:, None] * inverse[None, :]
    cosine, sine = jnp.cos(angles), jnp.sin(angles)
    return (
        jnp.concatenate([cosine, cosine], axis=-1),
        jnp.concatenate([-sine, sine], axis=-1),
    )


def place(block, s, x_count):
    return ((block & 1) ^ (s & 1)) * x_count + ((block >> 1) ^ (s >> 1))


def project_kernel(s_ref, x_ref, w_ref, gain_ref, qg_ref, kg_ref, cos_ref, sin_ref, n_ref, qkv_ref, pre_ref):
    x = x_ref[0].astype(F32)
    normed = (x * rms_scale(x) * gain_ref[...]).astype(BF16)
    n_ref[0] = normed
    y = dot(normed, w_ref[...])
    cosine, sine = cos_ref[...], sin_ref[...]
    for j in range(y.shape[1] // (4 * HEAD_SIZE)):
        for part in range(4):
            at = slice((4 * j + part) * HEAD_SIZE, (4 * j + part + 1) * HEAD_SIZE)
            head = y[:, at]
            if part < 3:
                pre_ref[:, (3 * j + part) * HEAD_SIZE : (3 * j + part + 1) * HEAD_SIZE] = head
                gain = qg_ref[...] if part < 2 else kg_ref[...]
                head = head * rms_scale(head) * gain
                head = head * cosine + pltpu.roll(head, HEAD_SIZE // 2, 1) * sine
            qkv_ref[:, at] = head.astype(BF16)


def project(s, x_rel, w, gain, query_gain, key_gain, cosine, sine, x_count):
    blocks, piece, width = x_rel.shape
    length, columns = blocks * piece, w.shape[1]
    heads = columns // (4 * HEAD_SIZE)
    whole = lambda shape: pl.BlockSpec(shape, lambda i, s_ref: (0,) * len(shape))
    rel = pl.BlockSpec((1, piece, width), lambda i, s_ref: (place(i, s_ref[0], x_count), 0, 0))
    table = pl.BlockSpec((piece, HEAD_SIZE), lambda i, s_ref: (i, 0))
    return pl.pallas_call(
        project_kernel,
        name="project",
        out_shape=(
            jax.ShapeDtypeStruct((blocks, piece, width), BF16),
            jax.ShapeDtypeStruct((length, columns), BF16),
            jax.ShapeDtypeStruct((length, 3 * heads * HEAD_SIZE), F32),
        ),
        grid_spec=pltpu.PrefetchScalarGridSpec(
            num_scalar_prefetch=1,
            grid=(blocks,),
            in_specs=[
                rel,
                whole(w.shape),
                whole((1, width)),
                whole((1, HEAD_SIZE)),
                whole((1, HEAD_SIZE)),
                table,
                table,
            ],
            out_specs=[
                rel,
                pl.BlockSpec((piece, columns), lambda i, s_ref: (i, 0)),
                pl.BlockSpec((piece, 3 * heads * HEAD_SIZE), lambda i, s_ref: (i, 0)),
            ],
        ),
        cost_estimate=pl.CostEstimate(
            flops=2 * length * width * columns,
            bytes_accessed=2 * (2 * length * width + width * columns + 4 * length * columns),
            transcendentals=0,
        ),
    )(s, x_rel, w, gain, query_gain, key_gain, cosine, sine)


def masked_exp(k_ref, query, i, piece, offset):
    diagonal = dot_t(k_ref[i * piece : (i + 1) * piece, :], query) * SCALE
    key_at = lax.broadcasted_iota(jnp.int32, (piece, piece), 0)
    query_at = lax.broadcasted_iota(jnp.int32, (piece, piece), 1)
    diagonal = jnp.where(key_at <= query_at, diagonal, -jnp.inf)
    if i == 0:
        scores = diagonal
    else:
        scores = jnp.concatenate(
            [dot_t(k_ref[: i * piece, :], query) * SCALE, diagonal], axis=0
        )
    if offset is None:
        offset = jnp.max(scores, axis=0, keepdims=True)
    return jnp.exp(scores - offset), offset


def forward_kernel(blocks, x_count, s_ref, q_ref, k_ref, v_ref, o_ref, log_ref):
    piece = q_ref.shape[0] // blocks
    values_t = v_ref[...].T
    for i in range(blocks):
        query = q_ref[i * piece : (i + 1) * piece, :]
        exponent, highest = masked_exp(k_ref, query, i, piece, None)
        total = jnp.sum(exponent, axis=0, keepdims=True)
        probs = (exponent * (1.0 / total)).astype(BF16)
        mixed = dot(values_t[:, : (i + 1) * piece], probs)
        o_ref[place(i, s_ref[0], x_count)] = mixed.T.astype(BF16)
        log_ref[0, :, i * piece : (i + 1) * piece] = highest + jnp.log(total)


def attend(s, qkv, blocks, x_count):
    length, columns = qkv.shape
    heads = columns // (2 * HEAD_SIZE)
    piece = length // blocks
    head = lambda part: pl.BlockSpec(
        (length, HEAD_SIZE), lambda h, s_ref: (0, 4 * (h // 2) + (h % 2 if part == 0 else part))
    )
    return pl.pallas_call(
        functools.partial(forward_kernel, blocks, x_count),
        name="attend",
        out_shape=(
            jax.ShapeDtypeStruct((blocks, piece, heads * HEAD_SIZE), BF16),
            jax.ShapeDtypeStruct((heads, 1, length), F32),
        ),
        grid_spec=pltpu.PrefetchScalarGridSpec(
            num_scalar_prefetch=1,
            grid=(heads,),
            in_specs=[head(0), head(2), head(3)],
            out_specs=[
                pl.BlockSpec((blocks, piece, HEAD_SIZE), lambda h, s_ref: (0, 0, h)),
                pl.BlockSpec((1, 1, length), lambda h, s_ref: (h, 0, 0)),
            ],
        ),
        cost_estimate=pl.CostEstimate(
            flops=2 * heads * length * length * HEAD_SIZE * 2,
            bytes_accessed=2 * heads * length * HEAD_SIZE * 4,
            transcendentals=heads * length * length // 2,
        ),
    )(s, qkv, qkv, qkv)


def head_back(grad, pre, gain, cosine, sine):
    turned = grad * cosine - pltpu.roll(grad, HEAD_SIZE // 2, 1) * sine
    scale = rms_scale(pre)
    part = turned * gain
    result = scale * part - pre * (scale * scale * scale * jnp.mean(part * pre, axis=-1, keepdims=True))
    return result, jnp.sum(turned * pre * scale, axis=0, keepdims=True)


def backward_kernel(
    blocks, x_count, s_ref, q_ref, k_ref, v_ref, do_ref, log_ref, qp_ref, kp_ref, qg_ref, kg_ref,
    cos_ref, sin_ref, grad_ref, qgain_ref, kgain_ref, dk_ref, dv_ref,
):
    piece = q_ref.shape[0] // blocks
    second = pl.program_id(1)

    @pl.when((pl.program_id(0) == 0) & (second == 0))
    def _():
        qgain_ref[...] = jnp.zeros_like(qgain_ref)
        kgain_ref[...] = jnp.zeros_like(kgain_ref)

    @pl.when(second == 0)
    def _():
        dk_ref[...] = jnp.zeros_like(dk_ref)
        dv_ref[...] = jnp.zeros_like(dv_ref)

    keys_t = k_ref[...].T
    column = pl.ds(pl.multiple_of(second * HEAD_SIZE, HEAD_SIZE), HEAD_SIZE)
    for i in range(blocks):
        rows = slice(i * piece, (i + 1) * piece)
        end = (i + 1) * piece
        at = place(i, s_ref[0], x_count)
        query = q_ref[rows, :]
        grad_out = do_ref[at]
        probs, _ = masked_exp(k_ref, query, i, piece, log_ref[0, :, rows])
        dv_ref[:end, :] += dot(probs.astype(BF16), grad_out)
        grad_probs = dot_t(v_ref[:end, :], grad_out)
        inner = jnp.sum(probs * grad_probs, axis=0, keepdims=True)
        grad_scores = (probs * (grad_probs - inner)).astype(BF16)
        dk_ref[:end, :] += dot(grad_scores, query)
        grad_query = dot(keys_t[:, :end], grad_scores).T * SCALE
        result, gain = head_back(grad_query, qp_ref[rows, :], qg_ref[...], cos_ref[rows, :], sin_ref[rows, :])
        grad_ref[at, :, column] = result.astype(BF16)
        qgain_ref[...] += gain

    @pl.when(second == 1)
    def _():
        for i in range(blocks):
            rows = slice(i * piece, (i + 1) * piece)
            at = place(i, s_ref[0], x_count)
            result, gain = head_back(
                dk_ref[rows, :] * SCALE, kp_ref[rows, :], kg_ref[...], cos_ref[rows, :], sin_ref[rows, :]
            )
            grad_ref[at, :, 2 * HEAD_SIZE : 3 * HEAD_SIZE] = result.astype(BF16)
            grad_ref[at, :, 3 * HEAD_SIZE :] = dv_ref[rows, :].astype(BF16)
            kgain_ref[...] += gain


def attend_back(s, qkv, pre, log_total, grad_mixed, query_gain, key_gain, cosine, sine, blocks, x_count):
    length, columns = qkv.shape
    heads_kv = columns // (4 * HEAD_SIZE)
    piece = length // blocks
    head = lambda part: pl.BlockSpec(
        (length, HEAD_SIZE), lambda j, g, s_ref: (0, 4 * j + (g if part == 0 else part))
    )
    pre_head = lambda part: pl.BlockSpec(
        (length, HEAD_SIZE), lambda j, g, s_ref: (0, 3 * j + (g if part == 0 else part))
    )
    whole = lambda shape: pl.BlockSpec(shape, lambda j, g, s_ref: (0,) * len(shape))
    return pl.pallas_call(
        functools.partial(backward_kernel, blocks, x_count),
        name="attend_back",
        out_shape=(
            jax.ShapeDtypeStruct((blocks, piece, columns), BF16),
            jax.ShapeDtypeStruct((1, HEAD_SIZE), F32),
            jax.ShapeDtypeStruct((1, HEAD_SIZE), F32),
        ),
        grid_spec=pltpu.PrefetchScalarGridSpec(
            num_scalar_prefetch=1,
            grid=(heads_kv, 2),
            in_specs=[
                head(0),
                head(2),
                head(3),
                pl.BlockSpec((blocks, piece, HEAD_SIZE), lambda j, g, s_ref: (0, 0, 2 * j + g)),
                pl.BlockSpec((1, 1, length), lambda j, g, s_ref: (2 * j + g, 0, 0)),
                pre_head(0),
                pre_head(2),
                whole((1, HEAD_SIZE)),
                whole((1, HEAD_SIZE)),
                whole((length, HEAD_SIZE)),
                whole((length, HEAD_SIZE)),
            ],
            out_specs=[
                pl.BlockSpec((blocks, piece, 4 * HEAD_SIZE), lambda j, g, s_ref: (0, 0, j)),
                whole((1, HEAD_SIZE)),
                whole((1, HEAD_SIZE)),
            ],
            scratch_shapes=[pltpu.VMEM((length, HEAD_SIZE), F32), pltpu.VMEM((length, HEAD_SIZE), F32)],
        ),
        cost_estimate=pl.CostEstimate(
            flops=2 * 2 * heads_kv * length * length * HEAD_SIZE * 5 // 2,
            bytes_accessed=2 * heads_kv * length * HEAD_SIZE * 24,
            transcendentals=heads_kv * length * length,
        ),
    )(s, qkv, qkv, qkv, grad_mixed, log_total, pre, pre, query_gain, key_gain, cosine, sine)


MESH = pl.DeviceIdType.MESH


def flip(index, bit):
    step = 1 << bit
    return index + step - 2 * step * lax.rem(lax.div(index, step), 2)


def bit_of(index, bit):
    return lax.rem(lax.div(index, 1 << bit), 2)


class Links:
    def __init__(self, send, recv):
        self.send, self.recv = send, recv
        self.d, self.s = lax.axis_index("dp"), lax.axis_index("seq")
        self.used = 0
        self.started = []

    def slots(self, n):
        self.used += n
        return self.used - n

    def copy(self, src, dst, slot, **to):
        return pltpu.make_async_remote_copy(
            src_ref=src,
            dst_ref=dst,
            send_sem=self.send.at[slot],
            recv_sem=self.recv.at[slot],
            device_id=to,
            device_id_type=MESH,
        )

    def plan(self, src, dst, slot, when=None, **to):
        copy = self.copy(src, dst, slot, **to)
        self.started.append((copy, when))
        return copy

    def start(self, src, dst, slot, when=None, **to):
        copy = self.plan(src, dst, slot, when, **to)
        if when is None:
            copy.start()
        else:
            pl.when(when)(copy.start)
        return copy

    def finish(self):
        for copy, when in self.started:
            if when is None:
                copy.wait_send()
            else:
                pl.when(when)(copy.wait_send)

    def greet(self, dp_masks, seq_masks):
        barrier = pltpu.get_barrier_semaphore()
        for mask in dp_masks:
            pl.semaphore_signal(
                barrier, inc=1, device_id={"dp": self.dp_at(mask)}, device_id_type=MESH
            )
        for mask in seq_masks:
            pl.semaphore_signal(
                barrier, inc=1, device_id={"seq": self.seq_at(mask)}, device_id_type=MESH
            )
        pl.semaphore_wait(barrier, len(dp_masks) + len(seq_masks))

    def seq_at(self, mask):
        s = self.s
        for bit in range(2):
            if mask >> bit & 1:
                s = flip(s, bit)
        return s

    def dp_at(self, mask):
        d = self.d
        for bit in range(3):
            if mask >> bit & 1:
                d = flip(d, bit)
        return d


class Gather:
    def __init__(self, links, block):
        base = links.slots(8)
        self.copies = {}
        for r, mask in ((0, 1), (0, 2), (0, 4), (2, 1), (4, 2), (4, 1), (6, 1)):
            src = block(links.dp_at(r))
            self.copies[r | mask] = links.plan(src, src, base + (r | mask), dp=links.dp_at(mask))

    def got(self, r):
        self.copies[r].wait_recv()

    def first(self):
        for mask in (2, 4, 1):
            self.copies[mask].start()

    def relay(self, r):
        self.got(r)
        if r == 4:
            self.copies[6].start()
        self.copies[r | 1].start()

    def last(self):
        for r in (1, 3, 5, 7):
            self.got(r)


def first_kernel(
    heads,
    a_ref, c_ref, out_ref, down_ref, x_ref, g_ref, gains_ref, qg_ref, kg_ref, cos_ref, sin_ref,
    xr_ref, gr_ref, wa_ref, wc_ref, wo_ref, wd_ref, n_ref, qkv_ref, pre_ref, o_ref, residual_ref, far_ref, log_ref, gain_ref,
    w_v, x_v, n_v, qkv_v, pre_v, o_v, got_v, wo_v, res_v, core_s, core_r, far_s, far_r, send, recv, local,
):
    links = Links(send, recv)
    d, s = links.d, links.s
    sequences, piece, width = x_ref.shape
    blocks = xr_ref.shape[1]
    half = blocks // 2
    length = blocks * piece
    x_bit, core = bit_of(s, 1), bit_of(s, 0)
    z1, z0, y = bit_of(d, 2), bit_of(d, 1), bit_of(d, 0)
    place_of = lambda i: lax.rem((i & 1) + core, 2) * 2 + lax.rem((i >> 1) + x_bit, 2)
    local_used = [0]
    locals_ = {}

    def near(name, src, dst):
        copy = pltpu.make_async_copy(src, dst, local.at[local_used[0]])
        local_used[0] += 1
        copy.start()
        locals_[name] = copy

    links.greet((1, 2, 4), (1, 2, 3))

    def exchange(src, dst):
        base = links.slots(4)
        return [
            links.start(src.at[links.seq_at(k)], dst.at[d, s], base + k, seq=links.seq_at(k))
            for k in (2, 3, 1)
        ]

    gain_slots = links.slots(4)
    gain_own = [
        links.start(gains_ref, got_v.at[d, s], gain_slots + k, seq=links.seq_at(k)) for k in (2, 3, 1)
    ]
    got_v[d, s] = gains_ref[...]
    a_own = exchange(a_ref, wa_ref)
    near("a", a_ref.at[s], wa_ref.at[d, s])

    x_slots, g_slots = links.slots(3 * sequences), links.slots(3 * sequences)

    def spread(own, everywhere, base, n):
        copies = [
            links.start(own.at[n], everywhere.at[n, k], base + 3 * n + k - 1, seq=links.seq_at(3 - k))
            for k in (1, 2)
        ]
        onward = links.plan(everywhere.at[n, 1], everywhere.at[n, 3], base + 3 * n + 2, seq=links.seq_at(1))
        return copies + [onward]

    def pass_on(copies):
        copies[0].wait_recv()
        copies[2].start()

    across, beside = lax.rem(x_bit + y, 2), lax.rem(core + z0, 2)
    out_slots = links.slots(7)
    holder = (across == 0) & (beside == 0)
    out_first = [
        links.start(
            out_ref, wo_ref.at[z1, s], out_slots + k,
            when=(across == k >> 1) & (beside == (k & 1)), seq=links.seq_at(k),
        )
        for k in (1, 2, 3)
    ]
    x_copies = [spread(x_ref, xr_ref, x_slots, 0)]
    c_own = exchange(c_ref, wc_ref)
    near("c", c_ref.at[s], wc_ref.at[d, s])
    for n in range(sequences):
        near(f"x{n}", x_ref.at[n], xr_ref.at[n, 0])
    near("d", down_ref, wd_ref.at[d])
    x_copies += [spread(x_ref, xr_ref, x_slots, n) for n in range(1, sequences)]

    for copy in gain_own + a_own:
        copy.wait_recv()
    locals_["a"].wait()
    gather_a, gather_c, gather_d, gather_gain = (
        Gather(links, lambda at, ref=ref: ref.at[at]) for ref in (wa_ref, wc_ref, wd_ref, got_v)
    )
    out_y = links.plan(wo_ref.at[z1], wo_ref.at[z1], out_slots + 4, when=holder, dp=flip(d, 0))
    out_z1 = links.plan(wo_ref.at[z1], wo_ref.at[z1], out_slots + 5, when=beside == 0, dp=flip(d, 2))
    out_z0 = links.plan(wo_ref, wo_ref, out_slots + 6, when=beside == 0, dp=flip(d, 1))

    def out_next():
        pl.when((across == 1) & (beside == 0))(out_y.wait_recv)
        pl.when(beside == 0)(out_z1.start)

    def out_last():
        @pl.when(beside == 0)
        def _():
            out_z1.wait_recv()
            out_z0.start()

    gather_gain.first()
    gather_a.first()

    @pl.when(holder)
    def _():
        own = pltpu.make_async_copy(out_ref, wo_ref.at[z1, s], local.at[local_used[0]])
        own.start()
        for copy in out_first:
            copy.wait_recv()
        own.wait()
        out_y.start()

    local_used[0] += 1
    for r in (2, 4, 6):
        gather_gain.relay(r)
    pass_on(x_copies[0])
    gather_a.relay(2)
    out_next()
    gather_a.relay(4)
    for copy in c_own:
        copy.wait_recv()
    locals_["c"].wait()
    gather_c.first()
    gather_a.relay(6)
    g_copies = [spread(g_ref, gr_ref, g_slots, n) for n in range(sequences)]
    for n in range(sequences):
        near(f"g{n}", g_ref.at[n], gr_ref.at[n, 0])
    locals_["d"].wait()
    gather_d.first()

    def wait_x(n):
        locals_[f"x{n}"].wait()
        for copy in x_copies[n][1:]:
            copy.wait_recv()
        near(f"xv{n}", xr_ref.at[n], x_v.at[n])
        locals_[f"xv{n}"].wait()

    def project_part(n, meanwhile=()):
        def step(i, carry):
            for k, action in enumerate(meanwhile):
                pl.when(i == k)(action)
            at = place_of(i)
            x = x_v[n, at].astype(F32)
            normed = (x * rms_scale(x) * gain_ref[0:1, :]).astype(BF16)
            n_v[n, at] = normed
            y_rows = dot(normed, w_v[...].reshape(width, -1))
            rows = pl.ds(pl.multiple_of(i * piece, piece), piece)
            cosine, sine = cos_ref[rows, :], sin_ref[rows, :]
            for j in range(heads // 2):
                for part in range(4):
                    cut = slice((4 * j + part) * HEAD_SIZE, (4 * j + part + 1) * HEAD_SIZE)
                    head = y_rows[:, cut]
                    if part < 3:
                        pre_v[n, rows, (3 * j + part) * HEAD_SIZE : (3 * j + part + 1) * HEAD_SIZE] = head
                        gain = qg_ref[...] if part < 2 else kg_ref[...]
                        head = head * rms_scale(head) * gain
                        head = head * cosine + pltpu.roll(head, HEAD_SIZE // 2, 1) * sine
                    qkv_v[n, rows, cut] = head.astype(BF16)
            return carry

        lax.fori_loop(0, blocks, step, 0)
        near(f"n{n}", n_v.at[n], n_ref.at[n])
        near(f"qkv{n}", qkv_v.at[n], qkv_ref.at[n])
        near(f"pre{n}", pre_v.at[n], pre_ref.at[n])

    def attend_part(n, meanwhile=()):
        def step(h, carry):
            for k, action in enumerate(meanwhile):
                pl.when(h == k)(action)
            j, g = lax.div(h, 2), lax.rem(h, 2)
            lanes = lambda at: pl.ds(pl.multiple_of(at * HEAD_SIZE, HEAD_SIZE), HEAD_SIZE)
            values_t = qkv_v[n, :, lanes(4 * j + 3)].T
            keys = qkv_v.at[n, :, lanes(4 * j + 2)]
            for i in range(blocks):
                query = qkv_v[n, i * piece : (i + 1) * piece, lanes(4 * j + g)]
                exponent, highest = masked_exp(keys, query, i, piece, None)
                total = jnp.sum(exponent, axis=0, keepdims=True)
                probs = (exponent * (1.0 / total)).astype(BF16)
                mixed = dot(values_t[:, : (i + 1) * piece], probs)
                o_v[n, place_of(i), :, lanes(h)] = mixed.T.astype(BF16)
                log_ref[n, h, :, i * piece : (i + 1) * piece] = highest + jnp.log(total)
            return carry

        lax.fori_loop(0, heads, step, 0)

    wait_x(0)
    gather_a.last()
    near("w", wa_ref, w_v)
    locals_["w"].wait()

    gather_gain.last()
    for at in range(got_v.shape[0]):
        gain_ref[:, at * 128 : (at + 1) * 128] = jnp.sum(got_v[at], axis=0)

    core_slots, far_slots = links.slots(half * sequences), links.slots(half * sequences)
    core_copies = {
        (n, k): links.plan(core_s.at[n, k], core_r.at[n, k], core_slots + half * n + k, seq=links.seq_at(1))
        for n in range(sequences)
        for k in range(half)
    }
    far_copies = {
        (n, k): links.plan(far_s.at[n, k], far_r.at[n, half - 1 - k], far_slots + half * n + k, seq=links.seq_at(2))
        for n in range(sequences - 1)
        for k in range(half)
    }

    def out_part(n):
        if n == 0:
            pl.when(beside == 1)(out_z0.wait_recv)
            near("wo", wo_ref, wo_v)
            locals_["wo"].wait()

        def step(i, carry):
            b = lax.rem(i + half, blocks)
            part = dot(o_v[n, b], wo_v[...].reshape(-1, width))
            for k in range(half):

                @pl.when(i == k)
                def _():
                    core_s[n, k] = part.astype(BF16)
                    core_copies[n, k].start()

                @pl.when(i == half + k)
                def _():
                    core_copies[n, k].wait_recv()
                    total = part + core_r[n, k].astype(F32)
                    res_v[n, k] = total
                    far_s[n, k] = total.astype(BF16)
                    if n < sequences - 1:
                        far_copies[n, k].start()

            return carry

        lax.fori_loop(0, blocks, step, 0)

    def residual(n):
        for k in range(half):
            if n < sequences - 1:
                far_copies[n, half - 1 - k].wait_recv()
                res_v[n, k] = res_v[n, k] + far_r[n, k].astype(F32) + x_v[n, k].astype(F32)
            else:
                res_v[n, k] = res_v[n, k] + x_v[n, k].astype(F32)
        near(f"res{n}", res_v.at[n], residual_ref.at[n])
        if n == sequences - 1:
            near("far", far_s.at[n], far_ref)

    nothing = lambda: None
    project_part(0, [nothing, lambda: gather_c.relay(2), lambda: pass_on(x_copies[1]), out_last])
    attend_part(0, [lambda: gather_c.relay(4)])
    near("o0", o_v.at[0], o_ref.at[0])
    for n in range(1, sequences):
        wait_x(n)
        out_part(n - 1)
        project_part(n, [lambda: gather_c.relay(6), nothing, lambda: pass_on(g_copies[0])])
        attend_part(n, [nothing, nothing, lambda: pass_on(g_copies[1])])
        near(f"o{n}", o_v.at[n], o_ref.at[n])
    out_part(sequences - 1)
    for r in (2, 4, 6):
        gather_d.relay(r)
    for n in range(sequences):
        residual(n)
    gather_c.last()
    gather_d.last()
    for pair in g_copies:
        for copy in pair[1:]:
            copy.wait_recv()
    for n in range(sequences):
        for name in ("g", "n", "qkv", "pre", "o", "res"):
            locals_[f"{name}{n}"].wait()
    locals_["far"].wait()
    links.finish()


def first(a, c, w_out, w_down, x, g, gains, query_gain, key_gain, cosine, sine, dp, heads):
    blocks, rows, columns = a.shape
    sequences, piece, width = x.shape
    length = blocks * piece
    hbm = pl.BlockSpec(memory_space=pl.ANY)
    vmem = pl.BlockSpec(memory_space=pltpu.VMEM)
    shape = jax.ShapeDtypeStruct
    pre_columns = columns // 4 * 3
    slots = 96
    return pl.pallas_call(
        functools.partial(first_kernel, heads),
        name="first",
        out_shape=(
            shape((sequences, blocks, piece, width), BF16),
            shape((sequences, blocks, piece, width), BF16),
            shape((dp, blocks, rows, columns), BF16),
            shape((dp, blocks, rows, c.shape[2]), BF16),
            shape((2, blocks) + w_out.shape, BF16),
            shape((dp,) + w_down.shape, BF16),
            shape((sequences, blocks, piece, width), BF16),
            shape((sequences, length, columns), BF16),
            shape((sequences, length, pre_columns), F32),
            shape((sequences, blocks, piece, heads * HEAD_SIZE), BF16),
            shape((sequences, blocks // 2, piece, width), F32),
            shape((blocks // 2, piece, width), BF16),
            shape((sequences, heads, 1, length), F32),
            shape((8, width), F32),
        ),
        in_specs=[vmem] * 11,
        out_specs=[hbm] * 12 + [vmem] * 2,
        scratch_shapes=[
            pltpu.VMEM((dp, blocks, rows, columns), BF16),
            pltpu.VMEM((sequences, blocks, piece, width), BF16),
            pltpu.VMEM((sequences, blocks, piece, width), BF16),
            pltpu.VMEM((sequences, length, columns), BF16),
            pltpu.VMEM((sequences, length, pre_columns), F32),
            pltpu.VMEM((sequences, blocks, piece, heads * HEAD_SIZE), BF16),
            pltpu.VMEM((dp, blocks, 8, width // dp), F32),
            pltpu.VMEM((2, blocks) + w_out.shape, BF16),
            pltpu.VMEM((sequences, blocks // 2, piece, width), F32),
            pltpu.VMEM((sequences, blocks // 2, piece, width), BF16),
            pltpu.VMEM((sequences, blocks // 2, piece, width), BF16),
            pltpu.VMEM((sequences, blocks // 2, piece, width), BF16),
            pltpu.VMEM((sequences, blocks // 2, piece, width), BF16),
            pltpu.SemaphoreType.DMA((slots,)),
            pltpu.SemaphoreType.DMA((slots,)),
            pltpu.SemaphoreType.DMA((32,)),
        ],
        compiler_params=pltpu.CompilerParams(
            collective_id=0, has_side_effects=True, vmem_limit_bytes=60 * 1024 * 1024
        ),
    )(a, c, w_out, w_down, x, g, gains, query_gain, key_gain, cosine, sine)


def mlp_kernel(
    res_ref, last_ref, wc_ref, wd_ref, g_ref, gain_ref,
    own_ref, far_ref, residual_ref, branch_ref, down_ref, mlp_ref, gain_grad_ref,
    res_v, last_v, core_s, x_s, n2_v, hidden_v, both_v, dc_v, dg_v, da_v, us_v, uc_v, ux_v, ua_v,
    send, recv, local,
):
    links = Links(send, recv)
    sequences, blocks, piece, width = g_ref.shape
    half = blocks // 2
    units = wd_ref.shape[0]
    core, far = dict(seq=links.seq_at(1)), dict(seq=links.seq_at(2))
    pairs = [(n, k) for n in range(sequences) for k in range(half)]
    slots = {
        name: links.slots(half * sequences)
        for name in ("normed", "grad_core", "up_core", "grad_far", "branch")
    }
    ends = {
        "normed": lambda n, k: (n2_v.at[n, k], n2_v.at[n, half + k], core),
        "grad_core": lambda n, k: (core_s.at[n, k], dc_v.at[n, k], core),
        "up_core": lambda n, k: (us_v.at[n, k], uc_v.at[n, k], core),
        "grad_far": lambda n, k: (x_s.at[n, k], dg_v.at[n, half - 1 - k], far),
        "branch": lambda n, k: (us_v.at[n, k], branch_ref.at[n, half + k], core),
    }

    def copy(name, n, k):
        src, dst, to = ends[name](n, k)
        return links.copy(src, dst, slots[name] + half * n + k, **to)

    def arrived(name, n, k):
        copy(name, n, half - 1 - k if name == "grad_far" else k).wait_recv()

    near_copies = []

    def near(src, dst):
        made = pltpu.make_async_copy(src, dst, local.at[len(near_copies)])
        made.start()
        near_copies.append(made)

    last_slots = links.slots(half)
    last_copies = [
        links.plan(last_ref.at[k], last_v.at[half - 1 - k], last_slots + k, **far) for k in range(half)
    ]

    links.greet((), (1, 2))
    for made in last_copies:
        made.start()
    gain = gain_ref[...]

    def residual_of(n, k):
        return res_ref[n, k] if n < sequences - 1 else res_v[k]

    def norm(n):
        for k in range(half):
            if n == sequences - 1:
                last_copies[half - 1 - k].wait_recv()
                res_v[k] = res_ref[n, k] + last_v[k].astype(F32)
            residual = residual_of(n, k)
            n2_v[n, k] = (residual * rms_scale(residual) * gain).astype(BF16)
            copy("normed", n, k).start()

    def feed(n):
        for k in range(half):
            arrived("normed", n, k)

        def step(i, carry):
            b = lax.rem(i + half, blocks)
            both = dot(n2_v[n, b], wc_ref[...])
            gate, upward = both[:, :units], both[:, units:]
            grad_hidden = dot_t(g_ref[n, b], wd_ref[...])
            sigmoid = 1.0 / (1.0 + jnp.exp(-gate))
            silu = gate * sigmoid
            hidden_v[n, b] = (silu * upward).astype(BF16)
            both_v[n, b, :, units:] = (grad_hidden * silu).astype(BF16)
            both_v[n, b, :, :units] = (
                grad_hidden * upward * sigmoid * (1.0 + gate * (1.0 - sigmoid))
            ).astype(BF16)
            grad = dot_t(both_v[n, b], wc_ref[...])

            @pl.when(i < half)
            def _():
                core_s[n, i] = grad.astype(BF16)
                copy("grad_core", n, i).start()

            @pl.when(i >= half)
            def _():
                k = i - half
                arrived_core = copy("grad_core", n, k)
                arrived_core.wait_recv()
                total = grad + dc_v[n, k].astype(F32)
                da_v[n, k] = total
                x_s[n, k] = total.astype(BF16)
                copy("grad_far", n, k).start()

            up = dot(hidden_v[n, b], wd_ref[...])

            @pl.when(i < half)
            def _():
                us_v[n, i] = up.astype(BF16)
                copy("up_core", n, i).start()

            @pl.when(i >= half)
            def _():
                copy("up_core", n, i - half).wait_recv()

            @pl.when(i == half)
            def _():
                ua_v[n] = residual_of(n, 0) + (up + uc_v[n, 0].astype(F32))

            @pl.when(i == half + 1)
            def _():
                ux_v[n] = (up + uc_v[n, 1].astype(F32)).astype(BF16)

            return carry

        lax.fori_loop(0, blocks, step, 0)
        near(ua_v.at[n], own_ref.at[n])
        near(ux_v.at[n], far_ref.at[n])

    def back(n):
        for k in range(half):
            copy("up_core", n, k).wait_send()
        for k in range(half):
            arrived("grad_far", n, k)
            grad = da_v[n, k] + dg_v[n, k].astype(F32)
            residual = residual_of(n, k)
            scale = rms_scale(residual)
            scaled = grad * gain
            grad_residual = (
                g_ref[n, k].astype(F32)
                + scale * scaled
                - residual * (scale * scale * scale * jnp.mean(scaled * residual, axis=-1, keepdims=True))
            )
            us_v[n, k] = grad_residual.astype(BF16)
            copy("branch", n, k).start()
            near(us_v.at[n, k], branch_ref.at[n, k])
            if k == 0:
                part = jnp.sum(grad * residual * scale, axis=0, keepdims=True)
                gain_grad_ref[...] = part if n == 0 else gain_grad_ref[...] + part
                da_v[n, 0] = grad_residual
                near(da_v.at[n, 0], residual_ref.at[n])

    def weight_grads():
        chunk = 2 * width // 8
        flat = lambda value: value.reshape(-1, value.shape[-1])

        def rows(left_v, right, out):
            def step(m, carry):
                cut = pl.ds(pl.multiple_of(m * chunk, chunk), chunk)
                total = None
                for n in range(sequences):
                    term = t_dot(flat(left_v[n, :, :, cut]), flat(right[n]))
                    total = term if total is None else total + term
                out[cut, :] = total.astype(BF16)
                return carry

            lax.fori_loop(0, out.shape[0] // chunk, step, 0)

        rows(hidden_v, g_ref, down_ref)
        rows(n2_v, both_v, mlp_ref)

    for n in range(sequences):
        norm(n)
        feed(n)
    for n in range(sequences - 1):
        back(n)
    weight_grads()
    back(sequences - 1)
    for n, k in pairs:
        arrived("branch", n, k)
    for n, k in pairs:
        for name in ("normed", "grad_core", "grad_far", "branch"):
            copy(name, n, k).wait_send()
    links.finish()
    for made in near_copies:
        made.wait()


def feed_forward(residual, last_far, w_mlp, w_d, g_rel, gain):
    sequences, blocks, piece, width = g_rel.shape
    half = blocks // 2
    units = w_d.shape[0]
    hbm = pl.BlockSpec(memory_space=pl.ANY)
    vmem = pl.BlockSpec(memory_space=pltpu.VMEM)
    shape = jax.ShapeDtypeStruct
    part = lambda dtype: pltpu.VMEM((sequences, half, piece, width), dtype)
    one = lambda dtype: pltpu.VMEM((sequences, piece, width), dtype)
    return pl.pallas_call(
        mlp_kernel,
        name="feed_forward",
        out_shape=(
            shape((sequences, piece, width), F32),
            shape((sequences, piece, width), BF16),
            shape((sequences, piece, width), F32),
            shape((sequences, blocks, piece, width), BF16),
            shape((units, width), BF16),
            shape((width, 2 * units), BF16),
            shape((1, width), F32),
        ),
        in_specs=[vmem] * 6,
        out_specs=[hbm] * 4 + [vmem] * 3,
        scratch_shapes=[
            pltpu.VMEM((half, piece, width), F32),
            pltpu.VMEM((half, piece, width), BF16),
            part(BF16),
            part(BF16),
            pltpu.VMEM((sequences, blocks, piece, width), BF16),
            pltpu.VMEM((sequences, blocks, piece, units), BF16),
            pltpu.VMEM((sequences, blocks, piece, 2 * units), BF16),
            part(BF16),
            part(BF16),
            part(F32),
            part(BF16),
            part(BF16),
            one(BF16),
            one(F32),
            pltpu.SemaphoreType.DMA((16 * sequences,)),
            pltpu.SemaphoreType.DMA((16 * sequences,)),
            pltpu.SemaphoreType.DMA((16,)),
        ],
        compiler_params=pltpu.CompilerParams(
            collective_id=1, has_side_effects=True, vmem_limit_bytes=67043328
        ),
    )(residual, last_far, w_mlp, w_d, g_rel, gain)


class Scatter:
    def __init__(self, links, src, first, second, third, done=None):
        d = links.d
        self.z1, self.z0, self.y = bit_of(d, 2), bit_of(d, 1), bit_of(d, 0)
        self.src, self.first, self.second, self.third = src, first, second, third
        base = links.slots(7)
        self.over_y = links.plan(src.at[:, :, 1 - self.y], first, base, dp=flip(d, 0))
        self.over_z0 = links.plan(first.at[:, 1 - self.z0], second, base + 1, dp=flip(d, 1))
        self.over_z1 = links.plan(second.at[1 - self.z1], third, base + 2, dp=flip(d, 2))
        self.done, self.s = done, links.s
        if done is not None:
            self.share = [
                links.plan(third.at[links.seq_at(k)], done.at[links.s], base + 3 + k, seq=links.seq_at(k))
                for k in (2, 3, 1)
            ]

    def start(self):
        self.over_y.start()

    def sum_y(self):
        self.over_y.wait_recv()

        def step(i, carry):
            a, b = lax.div(i, 2), lax.rem(i, 2)
            mine = self.src[a, b, self.y].astype(F32)
            self.first[a, b] = (mine + self.first[a, b].astype(F32)).astype(BF16)
            return carry

        lax.fori_loop(0, 4, step, 0)
        self.over_z0.start()

    def sum_z0(self):
        self.over_z0.wait_recv()

        def step(a, carry):
            mine = self.first[a, self.z0].astype(F32)
            self.second[a] = (mine + self.second[a].astype(F32)).astype(BF16)
            return carry

        lax.fori_loop(0, 2, step, 0)
        self.over_z1.start()

    def sum_z1(self):
        self.over_z1.wait_recv()
        mine = self.second[self.z1].astype(F32)
        self.third[...] = (mine + self.third[...].astype(F32)).astype(BF16)
        if self.done is not None:
            for copy in self.share:
                copy.start()
            self.done[self.s] = self.third[self.s]

    def end(self):
        for copy in self.share:
            copy.wait_recv()


def last_kernel(
    down_ref, mlp_ref, mixed_h, branch_h, wo_ref, qkv_h, pre_h, log_ref, w_h, normed_h,
    x_ref, residual_ref, up_ref, gain_ref, mlp_gain_ref, qg_ref, kg_ref, cos_ref, sin_ref,
    up_out, tokens_ref, down_out, mlp_out, out_out, in_out, sums_ref,
    rows_v, mixed_ref, qkv_ref, pre_ref, w_ref, og_ref, d1, d2, c1, c2, c3, o1, o2, o3, a_v, a1, a2, a3,
    do_v, gr_v, dk_v, dv_v, core_s, core_r, far_s, far_r, acc_v, total_v, got_v,
    send, recv, local,
):
    links = Links(send, recv)
    d, s = links.d, links.s
    sequences, blocks, piece, width = rows_v.shape
    half = blocks // 2
    heads = log_ref.shape[1]
    heads_kv = heads // 2
    x_bit, core = bit_of(s, 1), bit_of(s, 0)
    z1, z0, y = bit_of(d, 2), bit_of(d, 1), bit_of(d, 0)
    place_of = lambda i: lax.rem((i & 1) + core, 2) * 2 + lax.rem((i >> 1) + x_bit, 2)
    across, beside = lax.rem(x_bit + y, 2), lax.rem(core + z0, 2)
    holder = (across == 0) & (beside == 0)
    lanes = lambda at: pl.ds(pl.multiple_of(at * HEAD_SIZE, HEAD_SIZE), HEAD_SIZE)
    nothing = lambda: None

    down = Scatter(links, down_ref, d1, d2, down_out)
    mlp = Scatter(links, mlp_ref, c1, c2, c3, mlp_out)
    ins = [
        Scatter(links, a_v.at[j], a1.at[j], a2.at[j], a3.at[j], in_out.at[j]) for j in range(heads_kv)
    ]
    base = links.slots(7)
    out_z0 = links.plan(og_ref, o1, base, when=beside == 1, dp=flip(d, 1))
    out_z1 = links.plan(o1.at[1 - z1], o2, base + 1, when=beside == 0, dp=flip(d, 2))
    out_y = links.plan(o2, o3, base + 2, when=(beside == 0) & (across == 1), dp=flip(d, 0))
    out_share = {
        k: links.plan(o3.at[links.seq_at(k)], out_out, base + 3 + k, when=holder, seq=links.seq_at(k))
        for k in (1, 2, 3)
    }

    def out_sum_z0():
        @pl.when(beside == 0)
        def _():
            out_z0.wait_recv()

            def step(i, carry):
                a, b = lax.div(i, blocks), lax.rem(i, blocks)
                o1[a, b] = (og_ref[a, b].astype(F32) + o1[a, b].astype(F32)).astype(BF16)
                return carry

            lax.fori_loop(0, 2 * blocks, step, 0)
            out_z1.start()

    def out_sum_z1():
        @pl.when(beside == 0)
        def _():
            out_z1.wait_recv()

            def step(b, carry):
                o2[b] = (o1[z1, b].astype(F32) + o2[b].astype(F32)).astype(BF16)
                return carry

            lax.fori_loop(0, blocks, step, 0)

        pl.when((beside == 0) & (across == 1))(out_y.start)

    def out_sum_y():
        @pl.when(holder)
        def _():
            out_y.wait_recv()

            def step(b, carry):
                o3[b] = (o2[b].astype(F32) + o3[b].astype(F32)).astype(BF16)
                return carry

            lax.fori_loop(0, blocks, step, 0)
            for copy in out_share.values():
                copy.start()
            out_out[...] = o3[s]

    links.greet((1, 2, 4), (1, 2, 3))
    loads = {
        name: pltpu.make_async_copy(src, dst, local.at[k])
        for k, (name, src, dst) in enumerate(
            (
                ("mixed", mixed_h, mixed_ref),
                ("branch", branch_h, rows_v),
                ("qkv", qkv_h, qkv_ref),
                ("pre", pre_h, pre_ref),
                ("w", w_h, w_ref),
                ("residual", residual_ref, tokens_ref),
                ("normed", normed_h, rows_v),
            )
        )
    }
    for name in ("mixed", "branch", "qkv", "pre", "w", "residual"):
        loads[name].start()
    up_slot = links.slots(1)
    up_copy = links.start(up_ref, up_out, up_slot, seq=links.seq_at(2))
    mlp.start()
    down.start()
    total_v[0] = jnp.zeros_like(total_v[0])
    for r in range(width // 128):
        total_v[0, 8 + r : 9 + r, :] = mlp_gain_ref[:, r * 128 : (r + 1) * 128]

    def weight_out(h, carry):
        cut = pl.ds(pl.multiple_of(h * 2 * HEAD_SIZE, 2 * HEAD_SIZE), 2 * HEAD_SIZE)
        total = None
        for n in range(sequences):
            term = t_dot(
                mixed_ref[n, :, :, cut].reshape(blocks * piece, 2 * HEAD_SIZE),
                rows_v[n].reshape(blocks * piece, width),
            )
            total = term if total is None else total + term
        og_ref[h] = total.astype(BF16).reshape(og_ref.shape[1:])
        return carry

    def mixed_back(i, carry):
        n, b = lax.div(i, blocks), lax.rem(i, blocks)
        do_v[n, b] = dot_t(rows_v[n, b], wo_ref[...]).astype(BF16)
        return carry

    loads["mixed"].wait()
    loads["branch"].wait()
    lax.fori_loop(0, heads_kv, weight_out, 0)
    pl.when(beside == 1)(out_z0.start)
    lax.fori_loop(0, sequences * blocks, mixed_back, 0)
    loads["normed"].start()

    slots = [links.slots(half * sequences), links.slots(sequences)]
    core_copies = {
        (n, k): links.plan(core_s.at[n, k], core_r.at[n, k], slots[0] + half * n + k, seq=links.seq_at(1))
        for n in range(sequences)
        for k in range(half)
    }
    far_copies = [
        links.plan(far_s.at[n], far_r.at[n], slots[1] + n, seq=links.seq_at(2)) for n in range(sequences)
    ]

    def input_part(n):
        def step(i, carry):
            b = lax.rem(i + half, blocks)
            grad = dot_t(gr_v[n, b], w_ref[...])
            for k in range(half):

                @pl.when(i == k)
                def _():
                    core_s[n, k] = grad.astype(BF16)
                    core_copies[n, k].start()

                @pl.when(i == half + k)
                def _():
                    core_copies[n, k].wait_recv()
                    total = grad + core_r[n, k].astype(F32)
                    if k == 0:
                        acc_v[n] = total
                    else:
                        far_s[n] = total.astype(BF16)
                        far_copies[n].start()

            return carry

        lax.fori_loop(0, blocks, step, 0)

    def input_end(n):
        far_copies[n].wait_recv()
        grad = acc_v[n] + far_r[n].astype(F32)
        tokens = x_ref[n].astype(F32)
        scale = rms_scale(tokens)
        scaled = grad * gain_ref[...]
        tokens_ref[n] = (
            tokens_ref[n]
            + scale * scaled
            - tokens * (scale * scale * scale * jnp.mean(scaled * tokens, axis=-1, keepdims=True))
        )
        part = jnp.sum(grad * tokens * scale, axis=0, keepdims=True)
        for r in range(width // 128):
            total_v[0, r : r + 1, :] += part[:, r * 128 : (r + 1) * 128]

    def attention(j, meanwhile):
        def step(t, carry):
            for k, action in enumerate(meanwhile):
                pl.when(t == k)(action)
            n, g = lax.div(t, 2), lax.rem(t, 2)

            @pl.when(g == 0)
            def _():
                dk_v[...] = jnp.zeros_like(dk_v)
                dv_v[...] = jnp.zeros_like(dv_v)

            keys, values = qkv_ref.at[n, :, lanes(4 * j + 2)], qkv_ref.at[n, :, lanes(4 * j + 3)]
            keys_t = keys[...].T
            for i in range(blocks):
                rows = slice(i * piece, (i + 1) * piece)
                end = (i + 1) * piece
                at = place_of(i)
                query = qkv_ref[n, rows, lanes(4 * j + g)]
                grad_out = do_v[n, at, :, lanes(2 * j + g)]
                probs, _ = masked_exp(keys, query, i, piece, log_ref[n, 2 * j + g, :, rows])
                dv_v[:end, :] += dot(probs.astype(BF16), grad_out)
                grad_probs = dot_t(values[:end, :], grad_out)
                inner = jnp.sum(probs * grad_probs, axis=0, keepdims=True)
                grad_scores = (probs * (grad_probs - inner)).astype(BF16)
                dk_v[:end, :] += dot(grad_scores, query)
                grad_query = dot(keys_t[:, :end], grad_scores).T * SCALE
                result, gain = head_back(
                    grad_query, pre_ref[n, rows, lanes(3 * j + g)], qg_ref[...], cos_ref[rows, :], sin_ref[rows, :]
                )
                gr_v[n, at, :, lanes(4 * j + g)] = result.astype(BF16)
                total_v[0, 16:17, :] += gain

            @pl.when(g == 1)
            def _():
                for i in range(blocks):
                    rows = slice(i * piece, (i + 1) * piece)
                    at = place_of(i)
                    result, gain = head_back(
                        dk_v[rows, :] * SCALE, pre_ref[n, rows, lanes(3 * j + 2)], kg_ref[...],
                        cos_ref[rows, :], sin_ref[rows, :],
                    )
                    gr_v[n, at, :, lanes(4 * j + 2)] = result.astype(BF16)
                    gr_v[n, at, :, lanes(4 * j + 3)] = dv_v[rows, :].astype(BF16)
                    total_v[0, 17:18, :] += gain

            return carry

        lax.fori_loop(0, 2 * sequences, step, 0)

    def weight_in(j):
        wide = 4 * HEAD_SIZE
        chunk = 2 * width // 8

        def step(m, carry):
            cut = pl.ds(pl.multiple_of(m * chunk, chunk), chunk)
            total = None
            for n in range(sequences):
                left = rows_v[n, :, :, cut].reshape(blocks * piece, chunk)
                right = gr_v[n, :, :, j * wide : (j + 1) * wide].reshape(blocks * piece, wide)
                term = t_dot(left, right)
                total = term if total is None else total + term
            a_v[j, lax.div(m, 2), lax.rem(m, 2)] = total.astype(BF16).reshape(a_v.shape[3:])
            return carry

        lax.fori_loop(0, width // chunk, step, 0)
        ins[j].start()

    loads["qkv"].wait()
    loads["pre"].wait()
    attention(0, [nothing, nothing, out_sum_z0])
    loads["normed"].wait()
    loads["w"].wait()
    weight_in(0)
    attention(1, [out_sum_z1, mlp.sum_y, lambda: input_part(0)])
    input_part(1)
    weight_in(1)
    down.sum_y()
    mlp.sum_z0()
    loads["residual"].wait()
    for n in range(sequences):
        input_end(n)

    gain_slots = links.slots(5)
    gain_to = [dict(seq=links.seq_at(1)), dict(seq=links.seq_at(2))] + [dict(dp=flip(d, b)) for b in range(3)]
    gain_copies = [
        links.plan(total_v.at[k], got_v.at[k], gain_slots + k, **gain_to[k]) for k in range(5)
    ]

    def gain_stage(k):
        gain_copies[k].wait_recv()
        if k == 4:
            sums_ref[...] = total_v[4] + got_v[4]
        else:
            total_v[k + 1] = total_v[k] + got_v[k]
            gain_copies[k + 1].start()

    gain_copies[0].start()
    ins[0].sum_y()
    gain_stage(0)
    down.sum_z0()
    gain_stage(1)
    out_sum_y()
    mlp.sum_z1()
    gain_stage(2)
    ins[0].sum_z0()
    down.sum_z1()
    gain_stage(3)
    ins[0].sum_z1()
    ins[1].sum_y()
    gain_stage(4)
    ins[1].sum_z0()
    ins[1].sum_z1()
    for k, copy in out_share.items():
        pl.when((across == k >> 1) & (beside == (k & 1)))(copy.wait_recv)
    mlp.end()
    up_copy.wait_recv()
    for scatter in ins:
        scatter.end()
    links.finish()


def last(
    down, mlp, mixed, branch, w_o, qkv, pre, log_total, w_in, normed, x, residual, up,
    gain, mlp_gain_grad, query_gain, key_gain, cosine, sine,
):
    sequences, blocks, piece, width = branch.shape
    length = blocks * piece
    rows, wide = mlp.shape[-2], mlp.shape[-1]
    down_rows = down.shape[-2]
    heads_kv = qkv.shape[-1] // (4 * HEAD_SIZE)
    out_rows = w_o.shape[0] // (heads_kv * blocks)
    vmem = pl.BlockSpec(memory_space=pltpu.VMEM)
    shape = jax.ShapeDtypeStruct
    b16 = lambda *dims: pltpu.VMEM(dims, BF16)
    f32 = lambda *dims: pltpu.VMEM(dims, F32)
    hbm = pl.BlockSpec(memory_space=pl.ANY)
    part = (blocks, rows, 4 * HEAD_SIZE)
    return pl.pallas_call(
        last_kernel,
        name="last",
        out_shape=(
            shape(up.shape, up.dtype),
            shape((sequences, piece, width), F32),
            shape((down_rows, width), BF16),
            shape((blocks, rows, wide), BF16),
            shape((out_rows, width), BF16),
            shape((heads_kv,) + part, BF16),
            shape((24, 128), F32),
        ),
        in_specs=[vmem] * 2 + [hbm] * 2 + [vmem] + [hbm] * 2 + [vmem] + [hbm] * 2 + [vmem] + [hbm] * 2 + [vmem] * 6,
        out_specs=[hbm] + [vmem] * 6,
        scratch_shapes=[
            b16(*normed.shape),
            b16(*mixed.shape),
            b16(*qkv.shape),
            f32(*pre.shape),
            b16(*w_in.shape),
            b16(heads_kv, blocks, out_rows, width),
            b16(2, 2, down_rows, width),
            b16(2, down_rows, width),
            b16(2, 2, blocks, rows, wide),
            b16(2, blocks, rows, wide),
            b16(blocks, rows, wide),
            b16(2, blocks, out_rows, width),
            b16(blocks, out_rows, width),
            b16(blocks, out_rows, width),
            b16(heads_kv, 2, 2, 2, *part),
            b16(heads_kv, 2, 2, *part),
            b16(heads_kv, 2, *part),
            b16(heads_kv, *part),
            b16(sequences, blocks, piece, 2 * heads_kv * HEAD_SIZE),
            b16(sequences, blocks, piece, width),
            f32(length, HEAD_SIZE),
            f32(length, HEAD_SIZE),
            b16(sequences, blocks // 2, piece, width),
            b16(sequences, blocks // 2, piece, width),
            b16(sequences, piece, width),
            b16(sequences, piece, width),
            f32(sequences, piece, width),
            f32(5, 24, 128),
            f32(5, 24, 128),
            pltpu.SemaphoreType.DMA((64,)),
            pltpu.SemaphoreType.DMA((64,)),
            pltpu.SemaphoreType.DMA((8,)),
        ],
        compiler_params=pltpu.CompilerParams(
            collective_id=2, has_side_effects=True, vmem_limit_bytes=67043328
        ),
    )(
        down, mlp, mixed, branch, w_o, qkv, pre, log_total, w_in, normed, x, residual, up,
        gain, mlp_gain_grad, query_gain, key_gain, cosine, sine,
    )


def body(
    hidden_in,
    attn_gain,
    w_query,
    key_weight,
    value_weight,
    query_gain,
    key_gain,
    w_out,
    mlp_gain,
    w_gate,
    w_up,
    w_down,
    cotangent,
):
    wires = Wires(lax.axis_size("dp"), lax.axis_size("seq"))
    dp, seq, x_count = wires.dp, wires.seq, wires.x_count
    count = wires.count
    sequences, piece, width = hidden_in.shape
    length = seq * piece
    part = x_count * piece
    heads_kv = key_weight.shape[1] // HEAD_SIZE
    s_index = wires.s.reshape(1).astype(jnp.int32)
    cosine, sine = rope_tables(length)
    query_gain_row = query_gain.astype(F32).reshape(1, -1)
    key_gain_row = key_gain.astype(F32).reshape(1, -1)

    index = wires.d * seq + wires.s
    own_gains = jnp.stack([attn_gain, mlp_gain])
    rows = w_query.shape[0]
    by_head = jnp.concatenate(
        [
            w_query.reshape(rows, heads_kv, -1),
            key_weight.reshape(rows, heads_kv, -1),
            value_weight.reshape(rows, heads_kv, -1),
        ],
        axis=2,
    )
    order = [wires.heads_of(t, heads_kv) for t in range(seq)]
    package_in = jnp.stack(
        [jnp.concatenate([by_head[:, j] for j in order[t]], axis=1) for t in range(seq)]
    )
    down_rows = w_down.shape[0]

    def by_unit(w):
        return w.reshape(rows, dp, seq, down_rows).transpose(2, 0, 1, 3).reshape(seq, rows, -1)

    units = dp * down_rows
    package_mlp = jnp.concatenate([by_unit(w_gate), by_unit(w_up)], axis=2)

    fused = (dp, seq, heads_kv) == (8, 4, 8) and width == 128 * dp and rows % 16 == 0 and down_rows % 16 == 0
    if fused:
        gains = jnp.zeros((8, seq, width // count), F32)
        gains = lax.dynamic_update_slice(gains, own_gains.astype(F32)[:, None], (0, wires.s, 0))
        (
            x_rel, g_rel, w_in, w_mlp, w_o, w_d, all_normed, all_qkv, all_pre, all_mixed, residual, residual_far, all_log, gains
        ) = first(
            package_in, package_mlp, w_out, w_down, hidden_in, cotangent, gains.reshape(8, -1),
            query_gain_row, key_gain_row, cosine, sine, dp, 2 * heads_kv // seq,
        )
        w_in, w_mlp = w_in.reshape(width, -1), w_mlp.reshape(width, -1)
        w_o, w_d = w_o.reshape(-1, width), w_d.reshape(units, width)
        attn_gain_row, mlp_gain_row = gains[:1], gains[1:2]
        up_own, up_far, all_grad_residual, all_branch, grad_down, grad_mlp, mlp_gain_grad = feed_forward(
            residual, residual_far, w_mlp, w_d, g_rel, mlp_gain_row
        )
    else:
        gains = jnp.zeros((2, count, width // count), BF16)
        gains = lax.dynamic_update_slice(gains, own_gains[:, None], (0, index, 0))
        gains = wires.sum_all(gains.reshape(2, width)).astype(F32)
        attn_gain_row, mlp_gain_row = gains[:1], gains[1:]
        package = wires.exchange_seq(package_in).reshape(seq * rows, -1)
        w_in = wires.gather_dp(package).reshape(width, -1)
        x_rel = jnp.stack(wires.gather_seq_relative(hidden_in), axis=1)
        w_o = wires.gather_out(w_out, heads_kv)
        package = wires.exchange_seq(package_mlp).reshape(seq * rows, -1)
        w_mlp = wires.gather_dp(package).reshape(width, -1)
        g_rel = jnp.stack(wires.gather_seq_relative(cotangent), axis=1)
        w_d = wires.gather_dp(w_down).reshape(units, width)

    kept = []
    outs = []
    for n in range(0 if fused else sequences):
        normed, qkv, pre = project(
            s_index, x_rel[n], w_in, attn_gain_row, query_gain_row, key_gain_row, cosine, sine, x_count
        )
        mixed, log_total = attend(s_index, qkv, seq, x_count)
        mixed_rows = mixed.reshape(length, -1)
        other = wires.swap(dot(mixed_rows[part:], w_o).astype(BF16), 1)
        total = wires.sum_x(dot(mixed_rows[:part], w_o) + other.astype(F32))
        residual = total + x_rel[n].reshape(length, width)[:part].astype(F32)
        scale = rms_scale(residual)
        normed_mlp = (residual * scale * mlp_gain_row).astype(BF16)
        normed_mlp = jnp.concatenate([normed_mlp, wires.swap(normed_mlp, 1)], axis=0)
        both = dot(normed_mlp, w_mlp)
        gate, upward = both[:, :units], both[:, units:]
        sigmoid = jax.nn.sigmoid(gate)
        silu = gate * sigmoid
        hidden = (silu * upward).astype(BF16)
        other = wires.swap(dot(hidden[part:], w_d).astype(BF16), 1)
        total = wires.scatter_x(dot(hidden[:part], w_d) + other.astype(F32))
        outs.append((residual[:piece] + total).astype(BF16))

        grad_top = g_rel[n].reshape(length, width)
        grad_hidden = dot_t(grad_top, w_d)
        grad_gate = (grad_hidden * upward * sigmoid * (1.0 + gate * (1.0 - sigmoid))).astype(BF16)
        grad_upward = (grad_hidden * silu).astype(BF16)
        grad_both = jnp.concatenate([grad_gate, grad_upward], axis=1)
        other = wires.swap(dot_t(grad_both[part:], w_mlp).astype(BF16), 1)
        grad_normed = wires.sum_x(dot_t(grad_both[:part], w_mlp) + other.astype(F32))
        scaled = grad_normed * mlp_gain_row
        grad_residual = (
            grad_top[:part].astype(F32)
            + scale * scaled
            - residual * (scale * scale * scale * jnp.mean(scaled * residual, axis=-1, keepdims=True))
        )
        grad_mlp_gain = jnp.sum((grad_normed * residual * scale)[:piece], axis=0)
        branch = grad_residual.astype(BF16)
        branch = jnp.concatenate([branch, wires.swap(branch, 1)], axis=0)
        grad_mixed = dot_t(branch, w_o).astype(BF16).reshape(mixed.shape)
        grad_qkv, grad_query_gain, grad_key_gain = attend_back(
            s_index, qkv, pre, log_total, grad_mixed, query_gain_row, key_gain_row, cosine, sine, seq, x_count
        )
        grad_rows = grad_qkv.reshape(length, -1)
        other = wires.swap(dot_t(grad_rows[part:], w_in).astype(BF16), 1)
        grad_first = wires.scatter_x(dot_t(grad_rows[:part], w_in) + other.astype(F32))
        tokens = hidden_in[n].astype(F32)
        scale = rms_scale(tokens)
        scaled = grad_first * attn_gain_row
        grad_tokens = (
            grad_residual[:piece]
            + scale * scaled
            - tokens * (scale * scale * scale * jnp.mean(scaled * tokens, axis=-1, keepdims=True))
        )
        grad_attn_gain = jnp.sum(grad_first * tokens * scale, axis=0)
        kept.append(
            dict(
                normed=normed.reshape(length, width),
                mixed=mixed_rows,
                normed_mlp=normed_mlp,
                hidden=hidden,
                grad_both=grad_both,
                branch=branch,
                grad_rows=grad_rows,
                grad_tokens=grad_tokens,
                gains=jnp.concatenate(
                    [grad_attn_gain, grad_mlp_gain, grad_query_gain[0], grad_key_gain[0]]
                ),
            )
        )

    def from_unit(g):
        return g.reshape(seq, rows, dp, down_rows).transpose(1, 2, 0, 3).reshape(rows, -1)

    if fused:
        up, grad_tokens, grad_down, grad_mlp, grad_out, grad_in, gain_sums = last(
            grad_down.reshape(2, 2, 2, down_rows, width),
            grad_mlp.reshape(2, 2, 2, seq, rows, -1),
            all_mixed, all_branch, w_o, all_qkv, all_pre, all_log, w_in, all_normed, hidden_in, all_grad_residual, up_far,
            attn_gain_row, mlp_gain_grad, query_gain_row, key_gain_row, cosine, sine,
        )
        grad_down, grad_mlp, grad_out = grad_down.astype(F32), grad_mlp.astype(F32), grad_out.astype(F32)
        grad_in = grad_in.astype(F32).transpose(1, 2, 0, 3).reshape(seq, rows, -1)
        gain_sums = gain_sums.reshape(-1)[: 2 * width + 2 * HEAD_SIZE]
        hidden_out = (up_own + up.astype(F32)).astype(BF16)
    else:
        def over(name):
            return jnp.concatenate([k[name] for k in kept], axis=0)

        grad_down = t_dot(over("hidden"), g_rel.reshape(-1, width)).astype(BF16)
        grad_down = wires.scatter_dp(grad_down.reshape(dp, down_rows, width)).astype(F32)

        grad_mlp = t_dot(over("normed_mlp"), over("grad_both")).astype(BF16)
        grad_mlp = wires.scatter_dp(grad_mlp.reshape(dp, seq * rows, -1))
        grad_mlp = wires.exchange_seq(grad_mlp.reshape(seq, rows, -1)).astype(F32)


        grad_out = t_dot(over("mixed"), over("branch")).astype(BF16)
        grad_out = wires.scatter_out(grad_out, heads_kv).astype(F32)

        grad_in = t_dot(over("normed"), over("grad_rows")).astype(BF16)
        grad_in = wires.scatter_dp(grad_in.reshape(dp, seq * rows, -1))
        grad_in = wires.exchange_seq(grad_in.reshape(seq, rows, -1)).astype(F32)
        gain_sums = wires.sum_all(sum(k["gains"] for k in kept))
        grad_tokens = jnp.stack([k["grad_tokens"] for k in kept])
        hidden_out = jnp.stack(outs)

    grad_gate, grad_up = from_unit(grad_mlp[..., :units]), from_unit(grad_mlp[..., units:])
    pieces = [None] * heads_kv
    for t in range(seq):
        for m, j in enumerate(order[t]):
            pieces[j] = grad_in[t, :, m * 4 * HEAD_SIZE : (m + 1) * 4 * HEAD_SIZE]
    grad_query = jnp.concatenate([p[:, : 2 * HEAD_SIZE] for p in pieces], axis=1)
    grad_key = jnp.concatenate([p[:, 2 * HEAD_SIZE : 3 * HEAD_SIZE] for p in pieces], axis=1)
    grad_value = jnp.concatenate([p[:, 3 * HEAD_SIZE :] for p in pieces], axis=1)

    own = width // count
    grad_attn_gain = lax.dynamic_slice_in_dim(gain_sums, index * own, own)
    grad_mlp_gain = lax.dynamic_slice_in_dim(gain_sums, width + index * own, own)
    return (
        hidden_out,
        grad_tokens,
        grad_attn_gain,
        grad_query,
        grad_key,
        grad_value,
        gain_sums[2 * width : 2 * width + HEAD_SIZE],
        gain_sums[2 * width + HEAD_SIZE :],
        grad_out,
        grad_mlp_gain,
        grad_gate,
        grad_up,
        grad_down,
    )


def solution(mesh):
    rows = P(("dp", "seq"), None)
    line = P(("dp", "seq"))
    tokens = P("dp", "seq", None)
    return jax.shard_map(
        body,
        mesh=mesh,
        in_specs=(tokens, line, rows, rows, rows, P(), P(), rows, line, rows, rows, rows, tokens),
        out_specs=(tokens, tokens, line, rows, rows, rows, P(), P(), rows, line, rows, rows, rows),
        check_vma=False,
    )
```
